32 devices in a mesh: macro: 4 (over y, x), micro: 8 (over z, core).
Axes of the slice: x: 2, y: 2, z: 4, core: 2. Of those that a mesh axis runs over, the one named last changes fastest.
Arguments:
- displacement: float32 [3, 8, 16, 256], P(None, 'macro', 'micro'), may hold values from -6 to 6
- load: float32 [3, 8, 16, 256], P(None, 'macro', 'micro'), may hold values from -6 to 6
- routes: int32 [4, 8, 1024, 1], P('macro', 'micro'), may hold values from 0 to 7; in each aligned block of 1024 rows (0 to 1023, 1024 to 2047, ..., all dimensions but the last counted through in order) at most 256 rows name the same one
- counts: int32 [4, 8, 1024], P('macro', 'micro'), may hold values from 1 to 4
- stiffness: bfloat16 [8, 512, 512], P('micro'), may hold values from -0.5 to 2.5, as said below
- precond: bfloat16 [8, 512, 512], P('micro'), may hold values from -0.5 to 2.5, as said below
- forcing: bfloat16 [8, 6, 512], P('micro'), may hold values from -2.5 to 2.5
- coupling: bfloat16 [8, 512, 6], P('micro'), may hold values from -0.25 to 0.25
- lame_first: float32 [8], P('micro'), may hold values from 0.5 to 2
- lame_shear: float32 [8], P('micro'), may hold values from 0.5 to 2
Outputs:
- increment: float32 [3, 8, 16, 256], P(None, 'macro', 'micro')
- residual: float32 [3, 8, 16, 256], P(None, 'macro', 'micro')
The draws below stay inside these ranges and needn't reach their ends.
Inputs may be any that keep to these rules, and one draw needn't show every extreme that they name: `routes`: among the points of one block (one device's points), no owner is named by more than 256 points, a bound that some block reaches. `stiffness`: Symmetric. `precond`: Symmetric.
All inputs are finite; a program needn't handle non-finite values.
Results may differ from the reference program's by a relative error of at most 0.002.
Values sent between devices are 32-bit elements; how exact they have to be, the bound alone decides.
A program may use at most 64 MiB of HBM per device.

```python
import math
import jax
import jax.numpy as jnp
import numpy as np
from jax import lax

CX = 2
CY = 2
MODES = 512
ITMAX = 4
ITERS = 5
P_DEV = 1024
CAP = 256
MODELS = 8
NX = 8
NY = 16
NZ = 256
N_MACRO = 4
N_MICRO = 8


def model_scale(key):
    return jnp.exp(jax.random.uniform(jax.random.fold_in(key, 7), (MODELS,), jnp.float32, math.log(0.7), math.log(1.4)))


def model_matrix(key, scale):
    gauss = jax.random.truncated_normal(key, -4.0, 4.0, (MODELS, MODES, MODES), jnp.float32) / jnp.sqrt(MODES * 1.0)
    symmetric = (gauss + jnp.swapaxes(gauss, 1, 2)) / 2.9
    identity = jnp.eye(MODES, dtype=jnp.float32)
    return scale[:, None, None] * (identity[None] + 0.45 * symmetric)


def draw_stiffness(key, part):
    scale = model_scale(key)
    return model_matrix(jax.random.fold_in(key, 11), scale).astype(jnp.bfloat16)


def draw_precond(key, part):
    scale = model_scale(key)
    return model_matrix(jax.random.fold_in(key, 13), 1.0 / scale).astype(jnp.bfloat16)


def plant(values, stream_key, least, top_value):
    shape = values.shape
    spot = [jax.random.randint(jax.random.fold_in(stream_key, axis), (), 0, shape[axis]) for axis in range(len(shape))]
    values = values.at[tuple(spot)].set(least)
    longest = shape.index(max(shape))
    spot[longest] = (spot[longest] + 1) % shape[longest]
    return values.at[tuple(spot)].set(top_value)


def block_levels(key, shape, pieces, smallest, largest):
    def one(axis_at, shards_of):
        heights = jax.random.uniform(jax.random.fold_in(jax.random.fold_in(key, 6), axis_at), (shards_of,), jnp.float32, smallest / len(pieces), largest / len(pieces))
        return jnp.repeat(jnp.exp(heights), shape[axis_at] // shards_of).reshape((-1,) + (1,) * (len(shape) - axis_at - 1))

    loudness = one(*pieces[0])
    for cut in pieces[1:]:
        loudness = loudness * one(*cut)
    return loudness


def deal_out(key, own, number, rows, amount, top, reach, lean):
    sequence = jax.random.permutation(key, amount)
    packed, common = shares(amount, rows * top, reach, lean, True), shares(amount, rows * top, reach, lean, False)
    places = jnp.arange(amount)

    def named(sizes, rotation):
        used = int((sizes > 0).sum())
        fixed = max(1, used // 4)
        shifted = fixed + (places - fixed + rotation * (used - fixed)) % max(1, amount - fixed)
        return jnp.zeros((amount,), jnp.int32).at[sequence[jnp.where(places < fixed, places, shifted)]].set(jnp.asarray(sizes, jnp.int32))

    sizes = jnp.where(number % 4 == 0, named(packed, number // 4), named(common, number - number // 4 - 1))
    mixed = jax.random.permutation(jax.random.fold_in(own, 3), amount)
    source_of, taker = mixed[0:amount // 2 * 2:2], mixed[1:amount // 2 * 2:2]
    room = jnp.minimum(sizes[source_of] - 1, reach - sizes[taker]) // 2
    room = jnp.where((source_of == sequence[0]) | (taker == sequence[0]) | (sizes[taker] == 0), 0, jnp.maximum(room, 0))
    shifted = jax.random.randint(jax.random.fold_in(own, 4), (amount // 2,), 0, 1 << 20) % (room + 1)
    sizes = sizes.at[source_of].add(-shifted).at[taker].add(shifted)
    members = jnp.searchsorted(jnp.cumsum(sizes), jnp.arange(rows * top), side="right").astype(jnp.int32)
    table = members.reshape(top, rows).T
    table = table[jax.random.permutation(jax.random.fold_in(own, 1), rows)]
    rotation = jax.random.randint(jax.random.fold_in(own, 2), (rows, 1), 0, top)
    return jnp.take_along_axis(table, (jnp.arange(top)[None, :] + rotation) % top, axis=1)


def shares(amount, total, reach, lean, full):
    loads = [(1 << 20) // math.isqrt(grade ** lean) + 1 for grade in range(1, amount + 1)]
    largest = reach if full else min(reach, max(-(-total // amount), total * loads[0] // sum(loads)))
    least = 1 if total - largest >= amount - 1 else 0
    holding, spare = [largest] + [least] * (amount - 1), total - largest - least * (amount - 1)
    while spare > 0:
        candidates = [i for i in range(1, amount) if holding[i] < largest] or [i for i in range(1, amount) if holding[i] < reach]
        whole, budget = sum([loads[i] for i in candidates]), spare
        for i in candidates:
            more = min(reach - holding[i], max(1, budget * loads[i] // whole), spare)
            holding[i] = holding[i] + more
            spare = spare - more
    return np.array(holding)


def normal_values(key, dims, spread, reach, cuts=(), held_as=jnp.bfloat16):
    values = jax.random.normal(key, dims, jnp.float32) * spread
    if len(cuts) > 0:
        values = block_levels(key, dims, cuts, -0.22, 0.18) * values
    return jnp.clip(values, min=-reach, max=reach).astype(held_as)


def setup_inputs(seed: int = 0) -> dict:
    keys = jax.random.split(jax.random.key(seed), 11)
    displacement = normal_values(keys[0], (3, NX, NY, NZ), 1.0, 6.0, ((1, 4), (2, 8)), jnp.float32)
    load = normal_values(keys[1], (3, NX, NY, NZ), 1.0, 6.0, ((1, 4), (2, 8)), jnp.float32)
    routes_keys = jax.random.split(jax.random.fold_in(keys[2], 1), N_MACRO * N_MICRO * P_DEV // P_DEV)
    routes_turns = jax.random.permutation(jax.random.fold_in(keys[2], 3), N_MACRO * N_MICRO * P_DEV // P_DEV)
    routes = jax.vmap(lambda own, number: deal_out(jax.random.fold_in(keys[2], 2), own, number, P_DEV, N_MICRO, 1, CAP, 2))(routes_keys, routes_turns).reshape((N_MACRO, N_MICRO, P_DEV, 1))
    counts = plant(jax.random.randint(keys[3], (N_MACRO, N_MICRO, P_DEV), 1, ITMAX + 1), jax.random.fold_in(keys[3], 1), 1, ITMAX).astype(jnp.int32)
    stiffness = draw_stiffness(jax.random.fold_in(keys[10], 71), 0)
    precond = draw_precond(jax.random.fold_in(keys[10], 71), 0)
    forcing = normal_values(keys[6], (MODELS, 6, MODES), 6 ** -0.5, 2.5, ((0, 8),))
    coupling = normal_values(keys[7], (MODELS, MODES, 6), MODES ** -0.5, 0.25, ((0, 8),))
    lame_first = jnp.clip(jnp.exp(math.log(2.0) - 1.3862944 * jax.random.uniform(keys[8], (MODELS,), jnp.float32) ** block_levels(keys[8], (MODELS,), ((0, 8),), -0.2, 0.2)), 0.5, 2.0)
    lame_shear = jnp.clip(jnp.exp(math.log(2.0) - 1.3862944 * jax.random.uniform(keys[9], (MODELS,), jnp.float32) ** block_levels(keys[9], (MODELS,), ((0, 8),), -0.2, 0.2)), 0.5, 2.0)
    return {"displacement": displacement, "load": load, "routes": routes, "counts": counts, "stiffness": stiffness, "precond": precond, "forcing": forcing, "coupling": coupling, "lame_first": lame_first, "lame_shear": lame_shear}


BETA = 0.1
OMEGA = 0.8
MASS = 0.1
VOIGT = ((0, 5, 4), (5, 1, 3), (4, 3, 2))
ALL_PAIRS = tuple((first_axis, second_axis) for first_axis in range(6) for second_axis in range(6))


def element_strain(nodes):
    count_x = nodes.shape[1] - 1
    count_y = nodes.shape[2] - 1
    count_z = nodes.shape[3]
    padded = jnp.pad(nodes, ((0, 0), (0, 0), (0, 0), (0, 1)))
    zeros = jnp.zeros((3, count_x, count_y, count_z), jnp.float32)
    grad_x, grad_y, grad_z = zeros, zeros, zeros
    for corner_x in (0, 1):
        for corner_y in (0, 1):
            for corner_z in (0, 1):
                piece = padded[:, corner_x:corner_x + count_x, corner_y:corner_y + count_y, corner_z:corner_z + count_z]
                grad_x = grad_x + (0.25 * (2 * corner_x - 1)) * piece
                grad_y = grad_y + (0.25 * (2 * corner_y - 1)) * piece
                grad_z = grad_z + (0.25 * (2 * corner_z - 1)) * piece
    return jnp.stack([grad_x[0], grad_y[1], grad_z[2], grad_z[1] + grad_y[2], grad_z[0] + grad_x[2], grad_y[0] + grad_x[1]])


def node_force(stress):
    count_x, count_y, count_z = stress.shape[1], stress.shape[2], stress.shape[3]
    forces = jnp.zeros((3, count_x + 1, count_y + 1, count_z + 1), jnp.float32)
    for corner_x in (0, 1):
        for corner_y in (0, 1):
            for corner_z in (0, 1):
                signs = (2 * corner_x - 1, 2 * corner_y - 1, 2 * corner_z - 1)
                parts = []
                for component in range(3):
                    table = VOIGT[component]
                    parts.append(0.25 * (signs[0] * stress[table[0]] + signs[1] * stress[table[1]] + signs[2] * stress[table[2]]))
                contrib = jnp.stack(parts)
                forces = forces + jnp.pad(contrib, ((0, 0), (corner_x, 1 - corner_x), (corner_y, 1 - corner_y), (corner_z, 1 - corner_z)))
    return forces


def micro_solve(strain, sweeps, stiffness, precond, forcing, coupling, lame_first, lame_shear, pairs):
    strain_half = strain.astype(jnp.bfloat16)
    modal_load = lax.dot_general(strain_half, forcing, (((0,), (0,)), ((), ())), preferred_element_type=jnp.float32)
    modes = jnp.zeros_like(modal_load)
    for sweep in range(ITMAX):
        misfit = jnp.dot(modes.astype(jnp.bfloat16), stiffness, preferred_element_type=jnp.float32) + BETA * jnp.tanh(modes) - modal_load
        update = modes - OMEGA * jnp.dot(misfit.astype(jnp.bfloat16), precond, preferred_element_type=jnp.float32)
        modes = jnp.where((sweeps[0] > sweep)[:, None], update, modes)
    trace = strain[0] + strain[1] + strain[2]
    elastic = jnp.stack([lame_first * trace + 2.0 * lame_shear * strain[0], lame_first * trace + 2.0 * lame_shear * strain[1], lame_first * trace + 2.0 * lame_shear * strain[2], lame_shear * strain[3], lame_shear * strain[4], lame_shear * strain[5]])
    stress = elastic + lax.dot_general(coupling, modes.astype(jnp.bfloat16), (((0,), (1,)), ((), ())), preferred_element_type=jnp.float32)
    slope = 1.0 - jnp.tanh(modes) ** 2
    wide = coupling.astype(jnp.float32)
    products = jnp.stack([wide[:, pair[0]] * wide[:, pair[1]] for pair in pairs], axis=1)
    extra = lax.dot_general(products, slope, (((0,), (1,)), ((), ())), precision=lax.Precision.HIGHEST, preferred_element_type=jnp.float32)
    base = jnp.stack([lame_first * float(pair[0] < 3 and pair[1] < 3) + lame_shear * (2.0 * float(pair[0] == pair[1] and pair[0] < 3) + float(pair[0] == pair[1] and pair[0] >= 3)) for pair in pairs])
    return jnp.concatenate([stress, extra + base[:, None]], axis=0)


def operate(field, tangent):
    padded = jnp.pad(field, ((0, 0), (0, 1), (0, 1), (0, 0)))
    strain = element_strain(padded)
    stress = jnp.sum(tangent * strain[None], axis=1)
    return MASS * field + node_force(stress)[:, :-1, :-1, :-1]


def reference(displacement, load, routes, counts, stiffness, precond, forcing, coupling, lame_first, lame_shear):
    strain_all = element_strain(jnp.pad(displacement, ((0, 0), (0, 1), (0, 1), (0, 0))))
    points = strain_all.reshape(6, N_MACRO, CX, N_MICRO, CY, NZ).transpose(0, 1, 3, 2, 4, 5).reshape(6, N_MACRO, N_MICRO, P_DEV)
    owner_of = routes[..., 0]
    onehot = (owner_of[..., None] == jnp.arange(N_MICRO, dtype=jnp.int32)).astype(jnp.int32)
    ranks = jnp.sum((jnp.cumsum(onehot, axis=2) - 1) * onehot, axis=-1)
    target = (owner_of * CAP + ranks).astype(jnp.int32)
    macro_index = jnp.arange(N_MACRO, dtype=jnp.int32)[:, None, None]
    source_index = jnp.arange(N_MICRO, dtype=jnp.int32)[None, :, None]
    strain_buffer = jnp.zeros((6, N_MACRO, N_MICRO, N_MICRO * CAP), jnp.float32).at[:, macro_index, source_index, target].set(points)
    sweep_buffer = jnp.zeros((N_MACRO, N_MICRO, N_MICRO * CAP), jnp.int32).at[macro_index, source_index, target].set(counts)
    strain_owner = strain_buffer.reshape(6, N_MACRO, N_MICRO, N_MICRO, CAP).transpose(3, 0, 1, 2, 4).reshape(N_MICRO, 6, N_MACRO * N_MICRO * CAP)
    sweep_owner = sweep_buffer.reshape(N_MACRO, N_MICRO, N_MICRO, CAP).transpose(2, 0, 1, 3).reshape(N_MICRO, 1, N_MACRO * N_MICRO * CAP)

    def solve_owner(bundle):
        return micro_solve(bundle[0], bundle[1], bundle[2], bundle[3], bundle[4], bundle[5], bundle[6], bundle[7], ALL_PAIRS)

    results = lax.map(solve_owner, (strain_owner, sweep_owner, stiffness, precond, forcing, coupling, lame_first, lame_shear))
    back = results.reshape(N_MICRO, 42, N_MACRO, N_MICRO, CAP).transpose(1, 2, 3, 0, 4).reshape(42, N_MACRO, N_MICRO, N_MICRO * CAP)
    picked = jnp.take_along_axis(back, target[None], axis=3)
    values = picked.reshape(42, N_MACRO, N_MICRO, CX, CY, NZ).transpose(0, 1, 3, 2, 4, 5).reshape(42, NX, NY, NZ)
    stress = values[:6]
    tangent = values[6:].reshape(6, 6, NX, NY, NZ)
    rhs = load - node_force(stress)[:, :-1, :-1, :-1]
    increment = jnp.zeros_like(rhs)
    residual, direction = rhs, rhs
    norm_now = jnp.sum(residual * residual)
    for step in range(ITERS):
        image = operate(direction, tangent)
        alpha = norm_now / jnp.sum(direction * image)
        increment = increment + alpha * direction
        residual = residual - alpha * image
        norm_next = jnp.sum(residual * residual)
        direction = residual + (norm_next / norm_now) * direction
        norm_now = norm_next
    return increment, residual
```

```python
import jax
import jax.numpy as jnp
from jax import lax
from jax.experimental import pallas as pl
from jax.experimental.pallas import tpu as pltpu
from jax.sharding import PartitionSpec as P

ITMAX = 4
ITERS = 5


BETA = 0.1
OMEGA = 0.8
MASS = 0.1
VOIGT = ((0, 5, 4), (5, 1, 3), (4, 3, 2))
PAIRS = tuple((first, second) for first in range(6) for second in range(first, 6))
PAIR_AT = {pair: at for at, pair in enumerate(PAIRS)}
AROUND = tuple((dx, dy) for dx in (-1, 0, 1) for dy in (-1, 0, 1) if (dx, dy) != (0, 0))
MESH = pl.DeviceIdType.MESH


def with_halo(block, sides, width):
    for axis, dim in sides:
        count = lax.axis_size(axis)
        forward = [(i, i + 1) for i in range(count - 1)]
        backward = [(target, source) for source, target in forward]
        low = lax.ppermute(
            lax.slice_in_dim(block, block.shape[dim] - width, None, axis=dim), axis, forward
        )
        high = lax.ppermute(lax.slice_in_dim(block, 0, width, axis=dim), axis, backward)
        block = jnp.concatenate([low, block, high], axis=dim)
    return block


def passed_along(value, axis, steps):
    count = lax.axis_size(axis)
    initial, last = (max(0, -steps), min(count, count - steps))
    return lax.ppermute(value, axis, [(source, source + steps) for source in range(initial, last)])


def element_strain(nodes):
    count_x = nodes.shape[1] - 1
    count_y = nodes.shape[2] - 1
    count_z = nodes.shape[3]
    padded = jnp.pad(nodes, ((0, 0), (0, 0), (0, 0), (0, 1)))
    zeros = jnp.zeros((3, count_x, count_y, count_z), jnp.float32)
    grad_x, grad_y, grad_z = (zeros, zeros, zeros)
    for corner_x in (0, 1):
        for corner_y in (0, 1):
            for corner_z in (0, 1):
                piece = padded[
                    :,
                    corner_x : corner_x + count_x,
                    corner_y : corner_y + count_y,
                    corner_z : corner_z + count_z,
                ]
                grad_x = grad_x + 0.25 * (2 * corner_x - 1) * piece
                grad_y = grad_y + 0.25 * (2 * corner_y - 1) * piece
                grad_z = grad_z + 0.25 * (2 * corner_z - 1) * piece
    return jnp.stack(
        [
            grad_x[0],
            grad_y[1],
            grad_z[2],
            grad_z[1] + grad_y[2],
            grad_z[0] + grad_x[2],
            grad_y[0] + grad_x[1],
        ]
    )


def node_force(stress):
    count_x, count_y, count_z = (stress.shape[1], stress.shape[2], stress.shape[3])
    forces = jnp.zeros((3, count_x + 1, count_y + 1, count_z + 1), jnp.float32)
    for corner_x in (0, 1):
        for corner_y in (0, 1):
            for corner_z in (0, 1):
                signs = (2 * corner_x - 1, 2 * corner_y - 1, 2 * corner_z - 1)
                parts = []
                for component in range(3):
                    table = VOIGT[component]
                    parts.append(
                        0.25
                        * (
                            signs[0] * stress[table[0]]
                            + signs[1] * stress[table[1]]
                            + signs[2] * stress[table[2]]
                        )
                    )
                contrib = jnp.stack(parts)
                forces = forces + jnp.pad(
                    contrib,
                    (
                        (0, 0),
                        (corner_x, 1 - corner_x),
                        (corner_y, 1 - corner_y),
                        (corner_z, 1 - corner_z),
                    ),
                )
    return forces


def micro_kernel(bundle_ref, stiff_ref, pre_ref, force_ref, couple_ref, product_ref, coef_ref, out_ref):
    bundle = bundle_ref[...]
    sweeps = bundle[6:7]
    modal_load = jnp.dot(
        force_ref[...], bundle.astype(jnp.bfloat16), preferred_element_type=jnp.float32
    )
    modes = None
    for sweep in range(ITMAX):
        misfit = -modal_load
        if modes is not None:
            misfit = (
                jnp.dot(
                    stiff_ref[...], modes.astype(jnp.bfloat16), preferred_element_type=jnp.float32
                )
                + BETA * jnp.tanh(modes)
                - modal_load
            )
        change = OMEGA * jnp.dot(
            pre_ref[...], misfit.astype(jnp.bfloat16), preferred_element_type=jnp.float32
        )
        before = jnp.zeros_like(change) if modes is None else modes
        modes = jnp.where(sweeps > sweep, before - change, before)
    bent = jnp.tanh(modes)
    slope = 1.0 - bent * bent
    trace = bundle[0:1] + bundle[1:2] + bundle[2:3]
    rows = coef_ref.shape[0]
    tall = jnp.concatenate(
        [bundle, jnp.zeros((rows - bundle.shape[0], bundle.shape[1]), jnp.float32)], axis=0
    )
    coef = coef_ref[...]
    total = coef[:, 0:1] * trace + coef[:, 1:2] * tall + coef[:, 2:3]
    total = total + jnp.dot(
        couple_ref[...], modes.astype(jnp.bfloat16), preferred_element_type=jnp.float32
    )
    total = total + jnp.dot(
        product_ref[...], slope.astype(jnp.bfloat16), preferred_element_type=jnp.float32
    )
    out_ref[...] = total[: out_ref.shape[0]]


def micro_solve(bundle, stiffness, precond, forcing, coupling, lame_first, lame_shear, pairs):
    size, points = stiffness.shape[0], bundle.shape[1]
    tile = 512 if points % 512 == 0 else points
    count = 6 + len(pairs)
    rows = -(-count // 8) * 8
    force = jnp.pad(forcing.T, ((0, 0), (0, 2)))
    wide = coupling.astype(jnp.float32).T
    products = jnp.stack([wide[first] * wide[second] for first, second in pairs])
    products = jnp.pad(products.astype(jnp.bfloat16), ((6, rows - count), (0, 0)))
    couple = jnp.pad(coupling.T, ((0, rows - 6), (0, 0)))
    on_trace = jnp.array([1.0] * 3 + [0.0] * (rows - 3), jnp.float32)
    on_shear = jnp.array([2.0] * 3 + [1.0] * 3 + [0.0] * (rows - 6), jnp.float32)
    base_first = [0.0] * 6 + [float(i < 3 and j < 3) for i, j in pairs] + [0.0] * (rows - count)
    base_shear = (
        [0.0] * 6
        + [float(i == j) * (2.0 if i < 3 else 1.0) for i, j in pairs]
        + [0.0] * (rows - count)
    )
    base = lame_first * jnp.array(base_first, jnp.float32) + lame_shear * jnp.array(
        base_shear, jnp.float32
    )
    coef = jnp.stack([lame_first * on_trace, lame_shear * on_shear, base], axis=1)

    def whole(shape):
        return pl.BlockSpec(shape, lambda i: (0, 0))

    return pl.pallas_call(
        micro_kernel,
        grid=(points // tile,),
        out_shape=jax.ShapeDtypeStruct((count, points), jnp.float32),
        in_specs=[
            pl.BlockSpec((8, tile), lambda i: (0, i)),
            whole((size, size)),
            whole((size, size)),
            whole((size, 8)),
            whole((rows, size)),
            whole((rows, size)),
            whole((rows, 3)),
        ],
        out_specs=pl.BlockSpec((count, tile), lambda i: (0, i)),
        name="micro_solve",
    )(bundle, stiffness, precond, force, couple, products, coef)


def extend(field):
    return with_halo(field, (("macro", 1), ("micro", 2)), 1)


def cg_kernel(
    sizes,
    load_ref,
    elem_ref,
    inc_ref,
    res_ref,
    basis,
    send_halo,
    halo,
    part,
    got_micro,
    middle,
    got_macro,
    send_sem,
    recv_sem,
    micro_send,
    micro_recv,
    macro_send,
    macro_recv,
):
    count_x, count_y, n_macro, n_micro = sizes
    wide = count_y + 2
    rows, lanes = load_ref.shape[1], load_ref.shape[2]
    a, b = lax.axis_index("macro"), lax.axis_index("micro")

    def inside(dx, dy):
        test = None
        for place, step, count in ((a, dx, n_macro), (b, dy, n_micro)):
            if step != 0:
                good = (place > 0) if step < 0 else (place < count - 1)
                test = good if test is None else jnp.logical_and(test, good)
        return test

    barrier = pltpu.get_barrier_semaphore()
    for step in range(1, n_micro):
        pl.semaphore_signal(
            barrier, inc=1, device_id=(a, lax.rem(b + step, n_micro)), device_id_type=MESH
        )
    for step in range(1, n_macro):
        pl.semaphore_signal(
            barrier, inc=1, device_id=(lax.rem(a + step, n_macro), b), device_id_type=MESH
        )
    corners = [(dx, dy) for dx, dy in AROUND if dx != 0 and dy != 0]
    for dx, dy in corners:
        pl.semaphore_signal(
            barrier,
            inc=1,
            device_id=(lax.rem(a + dx + n_macro, n_macro), lax.rem(b + dy + n_micro, n_micro)),
            device_id_type=MESH,
        )
    for at, (dx, dy) in enumerate(AROUND):

        @pl.when(jnp.logical_not(inside(dx, dy)))
        def _():
            for it in range(ITERS):
                halo[it, at] = jnp.zeros(halo.shape[2:], jnp.float32)

    def near(step, count):
        return {0: list(range(1, count + 1)), -1: [1], 1: [count]}[step]

    def far(step, count):
        return {0: list(range(1, count + 1)), -1: [0], 1: [count + 1]}[step]

    def places(at, pick):
        dx, dy = AROUND[at]
        return [i * wide + j for i in pick(dx, count_x) for j in pick(dy, count_y)]

    def hop(it, at):
        dx, dy = AROUND[at]
        other = len(AROUND) - 1 - at
        return pltpu.make_async_remote_copy(
            src_ref=send_halo.at[it, at],
            dst_ref=halo.at[it, other],
            send_sem=send_sem.at[it, at],
            recv_sem=recv_sem.at[it, other],
            device_id=(a + dx, b + dy),
            device_id_type=MESH,
        )

    def halo_start(it):
        for at, (dx, dy) in enumerate(AROUND):

            @pl.when(inside(dx, dy))
            def _():
                mine = places(at, near)
                for c in range(3):
                    for k, row in enumerate(mine):
                        send_halo[it, at, pl.ds(c * len(mine) + k, 1)] = basis[it, c, pl.ds(row, 1)]
                hop(it, at).start()

    def halo_finish(it):
        for at, (dx, dy) in enumerate(AROUND):

            @pl.when(inside(dx, dy))
            def _():
                hop(it, at).wait_send()
                pltpu.make_async_remote_copy(
                    src_ref=send_halo.at[it, at],
                    dst_ref=halo.at[it, at],
                    send_sem=send_sem.at[it, at],
                    recv_sem=recv_sem.at[it, at],
                    device_id=(a + dx, b + dy),
                    device_id_type=MESH,
                ).wait_recv()

        for at in range(len(AROUND)):
            theirs = places(at, far)
            for c in range(3):
                for k, row in enumerate(theirs):
                    basis[it, c, pl.ds(row, 1)] = halo[it, at, pl.ds(c * len(theirs) + k, 1)]

    row_at = lax.broadcasted_iota(jnp.int32, (rows, lanes), 0)
    lane_at = lax.broadcasted_iota(jnp.int32, (rows, lanes), 1)
    own = row_at < 0
    for i in range(1, count_x + 1):
        low = i * wide + 1
        own = jnp.logical_or(own, jnp.logical_and(row_at >= low, row_at < low + count_y))

    def up(value, axis):
        if axis == 2:
            moved = pltpu.roll(value, lanes - 1, 1)
            return jnp.where(lane_at == lanes - 1, 0.0, moved)
        return pltpu.roll(value, rows - (wide if axis == 0 else 1), 0)

    def down(value, axis):
        if axis == 2:
            return jnp.where(lane_at == 0, 0.0, pltpu.roll(value, 1, 1))
        return pltpu.roll(value, wide if axis == 0 else 1, 0)

    def strain_of(it):
        grads = []
        for c in range(3):
            value = basis[it, c]
            moved = up(value, 2)
            total, gap = value + moved, moved - value
            total_up, gap_up = up(total, 1), up(gap, 1)
            flat, slope_y, slope_z = total + total_up, total_up - total, gap + gap_up
            grads.append(
                (
                    0.25 * (up(flat, 0) - flat),
                    0.25 * (up(slope_y, 0) + slope_y),
                    0.25 * (up(slope_z, 0) + slope_z),
                )
            )
        return [
            grads[0][0],
            grads[1][1],
            grads[2][2],
            grads[1][2] + grads[2][1],
            grads[0][2] + grads[2][0],
            grads[0][1] + grads[1][0],
        ]

    def force_of(stress, c):
        first, second, third = (stress[VOIGT[c][d]] for d in range(3))
        first = first + down(first, 2)
        second = second + down(second, 2)
        third = down(third, 2) - third
        first = first + down(first, 1)
        rest = down(second, 1) - second + third + down(third, 1)
        return 0.25 * (down(first, 0) - first + rest + down(rest, 0))

    def applied(it):
        strain = strain_of(it)
        stress = []
        for i in range(6):
            value = None
            for j in range(6):
                term = elem_ref[6 + PAIR_AT[(min(i, j), max(i, j))]] * strain[j]
                value = term if value is None else value + term
            stress.append(value)
        return [
            jnp.where(own, MASS * basis[it, c] + force_of(stress, c), 0.0) for c in range(3)
        ]

    def product(first, second):
        total = None
        for c in range(3):
            term = first[c] * second[c]
            total = term if total is None else total + term
        total = jnp.sum(jnp.where(own, total, 0.0), axis=0, keepdims=True)
        value = total[:, :128]
        for at in range(128, lanes, 128):
            value = value + total[:, at : at + 128]
        return value

    def stacked(pieces):
        tile_row = lax.broadcasted_iota(jnp.int32, (part.shape[1], 128), 0)
        value = jnp.zeros((part.shape[1], 128), jnp.float32)
        for at, piece in enumerate(pieces):
            value = jnp.where(tile_row == at, piece, value)
        return value

    def gather_start(it, src, dst, count, me, send, recv, device):
        copies = []
        for step in range(1, count):
            copy = pltpu.make_async_remote_copy(
                src_ref=src.at[it],
                dst_ref=dst.at[it, me],
                send_sem=send.at[it, step - 1],
                recv_sem=recv.at[it, step - 1],
                device_id=device(lax.rem(me + step, count)),
                device_id_type=MESH,
            )
            copy.start()
            copies.append(copy)
        dst[it, me] = src[it]
        return copies

    def gather_finish(it, copies, dst, count):
        for copy in copies:
            copy.wait()
        total = dst[it, 0]
        for at in range(1, count):
            total = total + dst[it, at]
        return total

    def micro_start(it):
        return gather_start(
            it, part, got_micro, n_micro, b, micro_send, micro_recv, lambda other: (a, other)
        )

    def macro_start(it):
        return gather_start(
            it, middle, got_macro, n_macro, a, macro_send, macro_recv, lambda other: (other, b)
        )

    stress = [elem_ref[i] for i in range(6)]
    for c in range(3):
        basis[0, c] = jnp.where(own, load_ref[c] - force_of(stress, c), 0.0)
    pl.semaphore_wait(barrier, n_micro - 1 + n_macro - 1 + len(corners))
    halo_start(0)
    halo_finish(0)
    first = applied(0)
    for c in range(3):
        basis[1, c] = first[c]
    halo_start(1)
    part[0] = stacked([product([basis[0, c] for c in range(3)], [basis[0, c] for c in range(3)]),
                       product(first, first)])
    copies = micro_start(0)
    halo_finish(1)
    second = applied(1)
    for c in range(3):
        basis[2, c] = second[c]
    halo_start(2)
    middle[0] = gather_finish(0, copies, got_micro, n_micro)
    copies = macro_start(0)
    halo_finish(2)
    totals = jnp.sum(gather_finish(0, copies, got_macro, n_macro), axis=1, keepdims=True)
    shift = jnp.sqrt(totals[1:2] / totals[0:1])
    scale = 1.0 / shift
    for c in range(3):
        u0, w1, w2 = basis[0, c], basis[1, c] * scale, basis[2, c] * (scale * scale)
        basis[1, c] = w1 - u0
        basis[2, c] = (w2 - w1) - (w1 - u0)

    def field(it):
        return [basis[it, c] for c in range(3)]

    def step(it):
        grown = applied(it)
        return [grown[c] * scale - jnp.where(own, basis[it, c], 0.0) for c in range(3)]

    moments = []
    for it in range(2, ITERS):
        grown = step(it)
        if it + 1 < ITERS:
            for c in range(3):
                basis[it + 1, c] = grown[c]
            halo_start(it + 1)
            if it == 2:
                for k in range(3):
                    moments.append(product(field(k), field(k)))
                    moments.append(product(field(k), field(k + 1)))
            else:
                moments.append(product(field(it), field(it)))
                moments.append(product(field(it), field(it + 1)))
            halo_finish(it + 1)
    moments.append(product(field(ITERS - 1), field(ITERS - 1)))
    moments.append(product(field(ITERS - 1), grown))
    part[1] = stacked(moments)
    copies = micro_start(1)
    middle[1] = gather_finish(1, copies, got_micro, n_micro)
    copies = macro_start(1)
    totals = jnp.sum(gather_finish(1, copies, got_macro, n_macro), axis=1, keepdims=True)
    held = [totals[k : k + 1] for k in range(2 * ITERS)]

    def inner(first, second, extra=0):
        gathered = {}
        for i, x in enumerate(first):
            for j, y in enumerate(second):
                gathered.setdefault(i + j, []).append(x * y)
        value = None
        for degree, terms in gathered.items():
            total = terms[0]
            for term in terms[1:]:
                total = total + term
            total = total * held[degree + extra]
            value = total if value is None else value + total
        return value

    one = jnp.ones((1, 1), jnp.float32)
    left, toward, done = [one], [one], []
    norm = held[0]
    for it in range(ITERS):
        energy = inner(toward, toward) + inner(toward, toward, 1)
        size = norm / energy
        done = [x + size * scale * p for x, p in zip(done + [0.0], toward)]
        raised = [
            (toward[k] if k < len(toward) else 0.0) + (toward[k - 1] if k > 0 else 0.0)
            for k in range(len(toward) + 1)
        ]
        left = [
            (left[k] if k < len(left) else 0.0) - size * raised[k] for k in range(len(raised))
        ]
        if it + 1 < ITERS:
            fresh = inner(left, left)
            ratio = fresh / norm
            toward = [
                left[k] + (ratio * toward[k] if k < len(toward) else 0.0)
                for k in range(len(left))
            ]
            norm = fresh
    for c in range(3):
        fields = [basis[k, c] for k in range(ITERS)] + [grown[c]]
        moved, rest = None, None
        for k in range(ITERS + 1):
            if k < len(done):
                term = done[k] * fields[k]
                moved = term if moved is None else moved + term
            term = left[k] * fields[k]
            rest = term if rest is None else rest + term
        for i in range(count_x):
            low = (i + 1) * wide + 1
            inc_ref[c, i] = moved[low : low + count_y]
            res_ref[c, i] = rest[low : low + count_y]


def conjugate_gradients(load, elements):
    _, count_x, count_y, count_z = load.shape
    n_macro, n_micro = lax.axis_size("macro"), lax.axis_size("micro")
    flat = (count_x + 2) * (count_y + 2)
    rows = -(-flat // 8) * 8

    def laid(value, high):
        value = jnp.pad(value, ((0, 0), (1 - high, 1), (1 - high, 1), (0, 0)))
        value = value.reshape(value.shape[0], flat, count_z)
        return jnp.pad(value, ((0, 0), (0, rows - flat), (0, 0)))

    side = -(-3 * max(count_x, count_y) // 8) * 8
    around = pltpu.VMEM((ITERS, len(AROUND), side, count_z), jnp.float32)
    dma = pltpu.SemaphoreType.DMA

    def body(*refs):
        cg_kernel((count_x, count_y, n_macro, n_micro), *refs)

    vmem = pl.BlockSpec(memory_space=pltpu.VMEM)
    return pl.pallas_call(
        body,
        out_shape=[jax.ShapeDtypeStruct(load.shape, jnp.float32)] * 2,
        in_specs=[vmem, vmem],
        out_specs=[vmem, vmem],
        scratch_shapes=[
            pltpu.VMEM((ITERS, 3, rows, count_z), jnp.float32),
            around,
            around,
            pltpu.VMEM((2, 16, 128), jnp.float32),
            pltpu.VMEM((2, n_micro, 16, 128), jnp.float32),
            pltpu.VMEM((2, 16, 128), jnp.float32),
            pltpu.VMEM((2, n_macro, 16, 128), jnp.float32),
            dma((ITERS, len(AROUND))),
            dma((ITERS, len(AROUND))),
            dma((2, n_micro - 1)),
            dma((2, n_micro - 1)),
            dma((2, n_macro - 1)),
            dma((2, n_macro - 1)),
        ],
        compiler_params=pltpu.CompilerParams(collective_id=0, has_side_effects=True),
        name="conjugate_gradients",
    )(laid(load, 0), laid(elements, 1))


def shards(
    displacement,
    load,
    routes,
    counts,
    stiffness,
    precond,
    forcing,
    coupling,
    lame_first,
    lame_shear,
):
    count_x, count_y, count_z = (
        displacement.shape[1],
        displacement.shape[2],
        displacement.shape[3],
    )
    points = count_x * count_y * count_z
    owners = lax.axis_size("micro")
    capacity = max(2, 2 * points // owners)
    strain_ext = element_strain(extend(displacement))
    strain_points = strain_ext[:, 1:, 1:].reshape(6, points)
    owner_of = routes.reshape(points)
    sweeps_of = counts.reshape(points)
    onehot = (owner_of[:, None] == jnp.arange(owners, dtype=jnp.int32)[None, :]).astype(jnp.int32)
    ranks = jnp.sum((jnp.cumsum(onehot, axis=0) - 1) * onehot, axis=1)
    target = owner_of * capacity + ranks
    bundle = jnp.concatenate([strain_points, sweeps_of.astype(jnp.float32)[None]], axis=0)
    bundle = jnp.pad(bundle, ((0, 1), (0, 0)))
    send = jnp.zeros((8, owners * capacity), jnp.float32).at[:, target].set(
        bundle, unique_indices=True, mode="promise_in_bounds"
    )
    got = lax.all_to_all(send, "micro", split_axis=1, concat_axis=1, tiled=True)
    rows = micro_solve(
        got,
        stiffness[0],
        precond[0],
        forcing[0],
        coupling[0],
        lame_first[0],
        lame_shear[0],
        PAIRS,
    )
    back = lax.all_to_all(rows, "micro", split_axis=1, concat_axis=1, tiled=True)
    values = jnp.take(back, target, axis=1, unique_indices=True, mode="clip")
    values = values.reshape(back.shape[0], count_x, count_y, count_z)
    left_x = passed_along(values[:, -1:], "macro", 1)
    values = jnp.concatenate([left_x, values], axis=1)
    left_y = passed_along(values[:, :, -1:], "micro", 1)
    values = jnp.concatenate([left_y, values], axis=2)
    return tuple(conjugate_gradients(load, values))


def solution(mesh):
    in_specs = (
        P(None, "macro", "micro", None),
        P(None, "macro", "micro", None),
        P("macro", "micro", None, None),
        P("macro", "micro", None),
        P("micro", None, None),
        P("micro", None, None),
        P("micro", None, None),
        P("micro", None, None),
        P("micro"),
        P("micro"),
    )
    out_specs = (P(None, "macro", "micro", None), P(None, "macro", "micro", None))
    return jax.shard_map(shards, mesh=mesh, in_specs=in_specs, out_specs=out_specs, check_vma=False)
```

```python
import jax
import jax.numpy as jnp
from jax import lax
from jax.experimental import pallas as pl
from jax.experimental.pallas import tpu as pltpu
from jax.sharding import PartitionSpec as P

ITMAX = 4
ITERS = 5


BETA = 0.1
OMEGA = 0.8
MASS = 0.1
VOIGT = ((0, 5, 4), (5, 1, 3), (4, 3, 2))
PAIRS = tuple((first, second) for first in range(6) for second in range(first, 6))
PAIR_AT = {pair: at for at, pair in enumerate(PAIRS)}
AROUND = tuple((dx, dy) for dx in (-1, 0, 1) for dy in (-1, 0, 1) if (dx, dy) != (0, 0))
MESH = pl.DeviceIdType.MESH


def place_of(at, count):
    turned = jnp.where(at < 2, at, count + 1 - at)
    return lax.rem(jnp.where(turned % 2 == 1, (turned + 1) // 2, count - turned // 2), count)


def newton_kernel(
    sizes,
    disp_ref,
    load_ref,
    routes_ref,
    counts_ref,
    stiff_hbm,
    pre_hbm,
    force_ref,
    couple_ref,
    first_ref,
    shear_ref,
    inc_ref,
    res_ref,
    stiff,
    pre,
    force_t,
    couple,
    products,
    wide_products,
    spots,
    near_disp,
    bundle,
    route_out,
    route_in,
    back_out,
    back_in,
    values,
    beside,
    elem,
    basis,
    send_halo,
    halo,
    part,
    got_micro,
    middle,
    got_macro,
    last_part,
    last_all,
    weight_sem,
    disp_send,
    disp_recv,
    route_send,
    route_recv,
    back_send,
    back_recv,
    side_send,
    side_recv,
    send_sem,
    recv_sem,
    micro_send,
    micro_recv,
    macro_send,
    macro_recv,
    last_send,
    last_recv,
):
    count_x, count_y, lanes, n_macro, n_micro = sizes
    wide = count_y + 2
    rows = basis.shape[2]
    slots = spots.shape[1]
    points = spots.shape[2]
    groups = points // 128
    size = stiff.shape[0]
    tall = couple.shape[0]
    total = n_macro * n_micro
    a, b = lax.axis_index("macro"), lax.axis_index("micro")
    me = a * n_micro + b

    def device(other):
        return (other // n_micro, lax.rem(other, n_micro))

    def inside(dx, dy):
        test = None
        for place, step, count in ((a, dx, n_macro), (b, dy, n_micro)):
            if step != 0:
                good = (place > 0) if step < 0 else (place < count - 1)
                test = good if test is None else jnp.logical_and(test, good)
        return test

    barrier = pltpu.get_barrier_semaphore()

    def greet(step, carry):
        pl.semaphore_signal(
            barrier, inc=1, device_id=device(lax.rem(me + step, total)), device_id_type=MESH
        )
        return carry

    lax.fori_loop(1, total, greet, 0)
    weights = [
        pltpu.make_async_copy(stiff_hbm, stiff, weight_sem.at[0]),
        pltpu.make_async_copy(pre_hbm, pre, weight_sem.at[1]),
    ]
    for copy in weights:
        copy.start()

    force = force_ref[...].astype(jnp.float32)
    force = jnp.concatenate([force, jnp.zeros((2, size), jnp.float32)], axis=0)
    force_t[...] = force.T.astype(jnp.bfloat16)
    wide_products[...] = jnp.zeros((tall, size), jnp.float32)
    coupling = couple_ref[...].astype(jnp.float32)
    wide_products[pl.ds(0, 6)] = coupling
    couple[...] = wide_products[...].astype(jnp.bfloat16)
    wide_products[pl.ds(0, 6)] = jnp.zeros((6, size), jnp.float32)
    for at, (first, second) in enumerate(PAIRS):
        wide_products[pl.ds(6 + at, 1)] = coupling[first : first + 1] * coupling[second : second + 1]
    products[...] = wide_products[...].astype(jnp.bfloat16)

    route = routes_ref[...]
    row_of = lax.broadcasted_iota(jnp.int32, (128, 128), 0)
    column_of = lax.broadcasted_iota(jnp.int32, (128, 128), 1)
    until = jnp.where(row_of <= column_of, 1.0, 0.0).astype(jnp.bfloat16)
    named = [jnp.where(route == owner, 1.0, 0.0) for owner in range(n_micro)]
    named = jnp.concatenate(named, axis=0).astype(jnp.bfloat16)
    inner_rank = jnp.dot(named, until, preferred_element_type=jnp.float32)
    whole = jnp.dot(
        named, jnp.ones((128, 128), jnp.bfloat16), preferred_element_type=jnp.float32
    ).astype(jnp.bfloat16)
    span = n_micro * groups
    row_of = lax.broadcasted_iota(jnp.int32, (span, span), 0)
    column_of = lax.broadcasted_iota(jnp.int32, (span, span), 1)
    ahead = jnp.logical_and(column_of < row_of, column_of // groups == row_of // groups)
    before = jnp.dot(
        jnp.where(ahead, 1.0, 0.0).astype(jnp.bfloat16), whole, preferred_element_type=jnp.float32
    )
    ranks = inner_rank + before - 1.0
    rank = jnp.zeros((groups, 128), jnp.float32)
    for owner in range(n_micro):
        rank = jnp.where(route == owner, ranks[owner * groups : (owner + 1) * groups], rank)
    slot_at = lax.broadcasted_iota(jnp.int32, (slots, 128), 0).astype(jnp.float32)

    def spot(owner, carry):
        local = jnp.where(route == owner, rank, -1.0)
        for g in range(groups):
            hit = jnp.where(local[g : g + 1] == slot_at, 1.0, 0.0)
            spots[owner, :, g * 128 : (g + 1) * 128] = hit.astype(jnp.bfloat16)
        return carry

    lax.fori_loop(0, n_micro, spot, 0)

    for it in range(basis.shape[0]):
        for c in range(3):
            basis[it, c] = jnp.zeros((rows, lanes), jnp.float32)
    elem[...] = jnp.zeros(elem.shape, jnp.float32)
    values[...] = jnp.zeros(values.shape, jnp.float32)
    bundle[...] = jnp.zeros(bundle.shape, jnp.float32)
    for g in range(groups):
        bundle[6:7, g * 128 : (g + 1) * 128] = counts_ref[g : g + 1].astype(jnp.float32)

    for at, (dx, dy) in enumerate(AROUND):

        @pl.when(jnp.logical_not(inside(dx, dy)))
        def _():
            for it in range(ITERS):
                halo[it, at] = jnp.zeros(halo.shape[2:], jnp.float32)

    after = ((1, 0), (0, 1), (1, 1))
    for at, (dx, dy) in enumerate(after):

        @pl.when(jnp.logical_not(inside(dx, dy)))
        def _():
            near_disp[at] = jnp.zeros(near_disp.shape[1:], jnp.float32)

    owned = [(i, j) for i in range(count_x) for j in range(count_y)]
    column_at = {place: at for at, place in enumerate(owned)}
    handed = [((1, 0), (count_x - 1, j), (0, j + 1)) for j in range(count_y)]
    handed += [((0, 1), (i, count_y - 1), (i + 1, 0)) for i in range(count_x)]
    handed += [((1, 1), (count_x - 1, count_y - 1), (0, 0))]
    for at, ((dx, dy), _, _) in enumerate(handed):

        @pl.when(jnp.logical_not(inside(-dx, -dy)))
        def _():
            beside[at] = jnp.zeros(beside.shape[1:], jnp.float32)

    pl.semaphore_wait(barrier, total - 1)

    def show(at):
        dx, dy = after[at]
        return pltpu.make_async_remote_copy(
            src_ref=disp_ref,
            dst_ref=near_disp.at[at],
            send_sem=disp_send.at[at],
            recv_sem=disp_recv.at[at],
            device_id=(a - dx, b - dy),
            device_id_type=MESH,
        )

    for at, (dx, dy) in enumerate(after):

        @pl.when(inside(-dx, -dy))
        def _():
            show(at).start()

    for c in range(3):
        for i, j in owned:
            basis[0, c, pl.ds((i + 1) * wide + j + 1, 1)] = disp_ref[c, i, j : j + 1]
    for at, (dx, dy) in enumerate(after):

        @pl.when(inside(-dx, -dy))
        def _():
            show(at).wait_send()

        @pl.when(inside(dx, dy))
        def _():
            pltpu.make_async_remote_copy(
                src_ref=disp_ref,
                dst_ref=near_disp.at[at],
                send_sem=disp_send.at[at],
                recv_sem=disp_recv.at[at],
                device_id=(a + dx, b + dy),
                device_id_type=MESH,
            ).wait_recv()

    for c in range(3):
        for j in range(count_y):
            basis[0, c, pl.ds((count_x + 1) * wide + j + 1, 1)] = near_disp[0, c, 0, j : j + 1]
        for i in range(count_x):
            basis[0, c, pl.ds((i + 1) * wide + count_y + 1, 1)] = near_disp[1, c, i, 0:1]
        basis[0, c, pl.ds((count_x + 1) * wide + count_y + 1, 1)] = near_disp[2, c, 0, 0:1]

    row_at = lax.broadcasted_iota(jnp.int32, (rows, lanes), 0)
    lane_at = lax.broadcasted_iota(jnp.int32, (rows, lanes), 1)
    own = row_at < 0
    for i in range(1, count_x + 1):
        low = i * wide + 1
        own = jnp.logical_or(own, jnp.logical_and(row_at >= low, row_at < low + count_y))

    def up(value, axis):
        if axis == 2:
            moved = pltpu.roll(value, lanes - 1, 1)
            return jnp.where(lane_at == lanes - 1, 0.0, moved)
        return pltpu.roll(value, rows - (wide if axis == 0 else 1), 0)

    def down(value, axis):
        if axis == 2:
            return jnp.where(lane_at == 0, 0.0, pltpu.roll(value, 1, 1))
        return pltpu.roll(value, wide if axis == 0 else 1, 0)

    def strain_of(it):
        grads = []
        for c in range(3):
            value = basis[it, c]
            moved = up(value, 2)
            total, gap = value + moved, moved - value
            total_up, gap_up = up(total, 1), up(gap, 1)
            flat, slope_y, slope_z = total + total_up, total_up - total, gap + gap_up
            grads.append(
                (
                    0.25 * (up(flat, 0) - flat),
                    0.25 * (up(slope_y, 0) + slope_y),
                    0.25 * (up(slope_z, 0) + slope_z),
                )
            )
        return [
            grads[0][0],
            grads[1][1],
            grads[2][2],
            grads[1][2] + grads[2][1],
            grads[0][2] + grads[2][0],
            grads[0][1] + grads[1][0],
        ]

    strain = strain_of(0)
    for at, (i, j) in enumerate(owned):
        low = (i + 1) * wide + j + 1
        for k in range(6):
            bundle[k : k + 1, at * lanes : (at + 1) * lanes] = strain[k][low : low + 1]
    exact = bundle[...]
    high = exact.astype(jnp.bfloat16).astype(jnp.float32)
    both = jnp.concatenate([high, exact - high], axis=0).astype(jnp.bfloat16)

    def route_copy(other, mine):
        return pltpu.make_async_remote_copy(
            src_ref=route_out.at[other],
            dst_ref=route_in.at[mine],
            send_sem=route_send.at[other],
            recv_sem=route_recv.at[mine],
            device_id=(a, other),
            device_id_type=MESH,
        )

    def hand_out(at, carry):
        other = lax.rem(b + place_of(n_micro - 1 - at, n_micro), n_micro)
        moved = lax.dot_general(
            both, spots[other], (((1,), (1,)), ((), ())), preferred_element_type=jnp.float32
        )
        moved = moved[:8] + moved[8:]

        @pl.when(other != b)
        def _():
            route_out[other] = moved
            route_copy(other, b).start()

        @pl.when(other == b)
        def _():
            route_in[b] = moved

        return carry

    lax.fori_loop(0, n_micro, hand_out, 0)
    for copy in weights:
        copy.wait()

    lame_first, lame_shear = first_ref[0], shear_ref[0]
    tall_at = lax.broadcasted_iota(jnp.int32, (tall, slots), 0)
    on_trace = jnp.where(tall_at < 3, lame_first, 0.0)
    on_strain = jnp.where(tall_at < 3, 2.0 * lame_shear, jnp.where(tall_at < 6, lame_shear, 0.0))
    base = jnp.zeros((tall, slots), jnp.float32)
    for at, (i, j) in enumerate(PAIRS):
        if i == j:
            amount = lame_first + 2.0 * lame_shear if i < 3 else lame_shear
        elif j < 3:
            amount = lame_first
        else:
            continue
        base = jnp.where(tall_at == 6 + at, amount, base)

    def back_copy(other, mine):
        return pltpu.make_async_remote_copy(
            src_ref=back_out.at[other],
            dst_ref=back_in.at[mine],
            send_sem=back_send.at[other],
            recv_sem=back_recv.at[mine],
            device_id=(a, other),
            device_id_type=MESH,
        )

    def solve(at, carry):
        other = lax.rem(b + place_of(at, n_micro), n_micro)

        @pl.when(other != b)
        def _():
            route_copy(b, other).wait_recv()

        points_in = route_in[other]
        sweeps = points_in[6:7]
        modal_load = jnp.dot(
            force_t[...], points_in.astype(jnp.bfloat16), preferred_element_type=jnp.float32
        )
        modes = None
        for sweep in range(ITMAX):
            misfit = -modal_load
            if modes is not None:
                misfit = (
                    jnp.dot(
                        stiff[...], modes.astype(jnp.bfloat16), preferred_element_type=jnp.float32
                    )
                    + BETA * jnp.tanh(modes)
                    - modal_load
                )
            change = jnp.where(sweeps > sweep, OMEGA, 0.0) * jnp.dot(
                pre[...], misfit.astype(jnp.bfloat16), preferred_element_type=jnp.float32
            )
            modes = -change if modes is None else modes - change
        bent = jnp.tanh(modes)
        slope = 1.0 - bent * bent
        trace = points_in[0:1] + points_in[1:2] + points_in[2:3]
        padded = jnp.concatenate(
            [points_in, jnp.zeros((tall - 8, slots), jnp.float32)], axis=0
        )
        answer = on_trace * trace + on_strain * padded + base
        answer = answer + jnp.dot(
            couple[...], modes.astype(jnp.bfloat16), preferred_element_type=jnp.float32
        )
        answer = answer + jnp.dot(
            products[...], slope.astype(jnp.bfloat16), preferred_element_type=jnp.float32
        )

        @pl.when(other != b)
        def _():
            back_out[other] = answer
            back_copy(other, b).start()

        @pl.when(other == b)
        def _():
            back_in[b] = answer

        return carry

    lax.fori_loop(0, n_micro, solve, 0)

    def take_back(at, carry):
        other = lax.rem(b - place_of(at, n_micro) + n_micro, n_micro)

        @pl.when(other != b)
        def _():
            back_copy(b, other).wait_recv()

        exact = back_in[other]
        high = exact.astype(jnp.bfloat16).astype(jnp.float32)
        both = jnp.concatenate([high, exact - high], axis=0).astype(jnp.bfloat16)
        moved = jnp.dot(both, spots[other], preferred_element_type=jnp.float32)
        values[...] += moved[:tall] + moved[tall:]
        return carry

    lax.fori_loop(0, n_micro, take_back, 0)

    def side_copy(at):
        (dx, dy), place, _ = handed[at]
        low = column_at[place] * lanes
        return pltpu.make_async_remote_copy(
            src_ref=values.at[:, pl.ds(low, lanes)],
            dst_ref=beside.at[at],
            send_sem=side_send.at[at],
            recv_sem=side_recv.at[at],
            device_id=(a + dx, b + dy),
            device_id_type=MESH,
        )

    for at, ((dx, dy), _, _) in enumerate(handed):

        @pl.when(inside(dx, dy))
        def _():
            side_copy(at).start()

    def put_column(read, row):
        for v in range(6 + len(PAIRS)):
            elem[v, pl.ds(row, 1)] = read(v)

    for at, (i, j) in enumerate(owned):
        put_column(
            lambda v: values[v : v + 1, at * lanes : (at + 1) * lanes], (i + 1) * wide + j + 1
        )
    for at, ((dx, dy), _, (i, j)) in enumerate(handed):

        @pl.when(inside(dx, dy))
        def _():
            side_copy(at).wait_send()

        @pl.when(inside(-dx, -dy))
        def _():
            pltpu.make_async_remote_copy(
                src_ref=values.at[:, pl.ds(0, lanes)],
                dst_ref=beside.at[at],
                send_sem=side_send.at[at],
                recv_sem=side_recv.at[at],
                device_id=(a - dx, b - dy),
                device_id_type=MESH,
            ).wait_recv()

        put_column(lambda v: beside[at, v : v + 1], i * wide + j)

    def near(step, count):
        return {0: list(range(1, count + 1)), -1: [1], 1: [count]}[step]

    def far(step, count):
        return {0: list(range(1, count + 1)), -1: [0], 1: [count + 1]}[step]

    def places(at, pick):
        dx, dy = AROUND[at]
        return [i * wide + j for i in pick(dx, count_x) for j in pick(dy, count_y)]

    def hop(it, at):
        dx, dy = AROUND[at]
        other = len(AROUND) - 1 - at
        return pltpu.make_async_remote_copy(
            src_ref=send_halo.at[it, at],
            dst_ref=halo.at[it, other],
            send_sem=send_sem.at[it, at],
            recv_sem=recv_sem.at[it, other],
            device_id=(a + dx, b + dy),
            device_id_type=MESH,
        )

    def halo_start(it):
        for at, (dx, dy) in enumerate(AROUND):

            @pl.when(inside(dx, dy))
            def _():
                mine = places(at, near)
                for c in range(3):
                    for k, row in enumerate(mine):
                        send_halo[it, at, pl.ds(c * len(mine) + k, 1)] = basis[it, c, pl.ds(row, 1)]
                hop(it, at).start()

    def halo_finish(it):
        for at, (dx, dy) in enumerate(AROUND):

            @pl.when(inside(dx, dy))
            def _():
                hop(it, at).wait_send()
                pltpu.make_async_remote_copy(
                    src_ref=send_halo.at[it, at],
                    dst_ref=halo.at[it, at],
                    send_sem=send_sem.at[it, at],
                    recv_sem=recv_sem.at[it, at],
                    device_id=(a + dx, b + dy),
                    device_id_type=MESH,
                ).wait_recv()

        for at in range(len(AROUND)):
            theirs = places(at, far)
            for c in range(3):
                for k, row in enumerate(theirs):
                    basis[it, c, pl.ds(row, 1)] = halo[it, at, pl.ds(c * len(theirs) + k, 1)]

    def force_of(stress, c):
        first, second, third = (stress[VOIGT[c][d]] for d in range(3))
        first = first + down(first, 2)
        second = second + down(second, 2)
        third = down(third, 2) - third
        first = first + down(first, 1)
        rest = down(second, 1) - second + third + down(third, 1)
        return 0.25 * (down(first, 0) - first + rest + down(rest, 0))

    def applied(it):
        strain = strain_of(it)
        stress = []
        for i in range(6):
            value = None
            for j in range(6):
                term = elem[6 + PAIR_AT[(min(i, j), max(i, j))]] * strain[j]
                value = term if value is None else value + term
            stress.append(value)
        return [
            jnp.where(own, MASS * basis[it, c] + force_of(stress, c), 0.0) for c in range(3)
        ]

    def product(first, second):
        total = None
        for c in range(3):
            term = first[c] * second[c]
            total = term if total is None else total + term
        total = jnp.sum(jnp.where(own, total, 0.0), axis=0, keepdims=True)
        value = total[:, :128]
        for at in range(128, lanes, 128):
            value = value + total[:, at : at + 128]
        return value

    def stacked(pieces):
        tile_row = lax.broadcasted_iota(jnp.int32, (16, 128), 0)
        value = jnp.zeros((16, 128), jnp.float32)
        for at, piece in enumerate(pieces):
            value = jnp.where(tile_row == at, piece, value)
        return value

    def gather_start(src, dst, count, mine, send, recv, device):
        copies = []
        for step in range(1, count):
            copy = pltpu.make_async_remote_copy(
                src_ref=src,
                dst_ref=dst.at[mine],
                send_sem=send.at[step - 1],
                recv_sem=recv.at[step - 1],
                device_id=device(lax.rem(mine + step, count)),
                device_id_type=MESH,
            )
            copy.start()
            copies.append(copy)
        dst[mine] = src[...]
        return copies

    def gather_finish(copies, dst, count):
        for copy in copies:
            copy.wait()
        total = dst[0]
        for at in range(1, count):
            total = total + dst[at]
        return total

    stress = [elem[i] for i in range(6)]
    zero = jnp.zeros((rows, lanes), jnp.float32)
    for c in range(3):
        padded = jnp.concatenate(
            [jnp.zeros((wide + 1, lanes), jnp.float32)]
            + [
                piece
                for i in range(count_x)
                for piece in (load_ref[c, i], jnp.zeros((2, lanes), jnp.float32))
            ]
            + [jnp.zeros((rows - 1 - wide * (count_x + 1), lanes), jnp.float32)],
            axis=0,
        )
        basis[0, c] = jnp.where(own, padded - force_of(stress, c), zero)
    halo_start(0)
    halo_finish(0)
    grown = applied(0)
    for c in range(3):
        basis[1, c] = grown[c]
    halo_start(1)
    start = [basis[0, c] for c in range(3)]
    part[...] = stacked([product(start, start), product(grown, grown)])
    copies = gather_start(
        part, got_micro, n_micro, b, micro_send, micro_recv, lambda other: (a, other)
    )
    halo_finish(1)
    grown = applied(1)
    for c in range(3):
        basis[2, c] = grown[c]
    halo_start(2)
    middle[...] = gather_finish(copies, got_micro, n_micro)
    copies = gather_start(
        middle, got_macro, n_macro, a, macro_send, macro_recv, lambda other: (other, b)
    )
    halo_finish(2)
    totals = jnp.sum(gather_finish(copies, got_macro, n_macro), axis=1, keepdims=True)
    shift = jnp.sqrt(totals[1:2] / totals[0:1])
    scale = 1.0 / shift
    for c in range(3):
        u0, w1, w2 = basis[0, c], basis[1, c] * scale, basis[2, c] * (scale * scale)
        basis[1, c] = w1 - u0
        basis[2, c] = (w2 - w1) - (w1 - u0)

    def field(it):
        return [basis[it, c] for c in range(3)]

    def step(it):
        grown = applied(it)
        return [grown[c] * scale - jnp.where(own, basis[it, c], 0.0) for c in range(3)]

    moments = []
    for it in range(2, ITERS):
        grown = step(it)
        if it + 1 < ITERS:
            for c in range(3):
                basis[it + 1, c] = grown[c]
            halo_start(it + 1)
            if it == 2:
                for k in range(3):
                    moments.append(product(field(k), field(k)))
                    moments.append(product(field(k), field(k + 1)))
            else:
                moments.append(product(field(it), field(it)))
                moments.append(product(field(it), field(it + 1)))
            halo_finish(it + 1)
    moments.append(product(field(ITERS - 1), field(ITERS - 1)))
    moments.append(product(field(ITERS - 1), grown))
    sums = jnp.sum(stacked(moments), axis=1, keepdims=True)
    diagonal = lax.broadcasted_iota(jnp.int32, (16, 128), 0) == lax.broadcasted_iota(
        jnp.int32, (16, 128), 1
    )
    last_part[...] = jnp.sum(jnp.where(diagonal, sums, 0.0), axis=0, keepdims=True)

    def last_copy(step, other):
        return pltpu.make_async_remote_copy(
            src_ref=last_part,
            dst_ref=last_all.at[me],
            send_sem=last_send.at[step],
            recv_sem=last_recv.at[step],
            device_id=device(other),
            device_id_type=MESH,
        )

    def last_start(step, carry):
        last_copy(step, lax.rem(me + step, total)).start()
        return carry

    def last_wait(step, carry):
        last_copy(step, lax.rem(me + step, total)).wait()
        return carry

    lax.fori_loop(1, total, last_start, 0)
    last_all[me] = last_part[...]
    lax.fori_loop(1, total, last_wait, 0)
    totals = jnp.sum(last_all[...], axis=0)
    held = [totals[:, k : k + 1] for k in range(2 * ITERS)]

    def inner(first, second, extra=0):
        gathered = {}
        for i, x in enumerate(first):
            for j, y in enumerate(second):
                gathered.setdefault(i + j, []).append(x * y)
        value = None
        for degree, terms in gathered.items():
            total = terms[0]
            for term in terms[1:]:
                total = total + term
            total = total * held[degree + extra]
            value = total if value is None else value + total
        return value

    one = jnp.ones((1, 1), jnp.float32)
    left, toward, done = [one], [one], []
    norm = held[0]
    for it in range(ITERS):
        energy = inner(toward, toward) + inner(toward, toward, 1)
        length = norm / energy
        done = [x + length * scale * p for x, p in zip(done + [0.0], toward)]
        raised = [
            (toward[k] if k < len(toward) else 0.0) + (toward[k - 1] if k > 0 else 0.0)
            for k in range(len(toward) + 1)
        ]
        left = [
            (left[k] if k < len(left) else 0.0) - length * raised[k] for k in range(len(raised))
        ]
        if it + 1 < ITERS:
            fresh = inner(left, left)
            ratio = fresh / norm
            toward = [
                left[k] + (ratio * toward[k] if k < len(toward) else 0.0)
                for k in range(len(left))
            ]
            norm = fresh
    for c in range(3):
        fields = [basis[k, c] for k in range(ITERS)] + [grown[c]]
        moved, rest = None, None
        for k in range(ITERS + 1):
            if k < len(done):
                term = done[k] * fields[k]
                moved = term if moved is None else moved + term
            term = left[k] * fields[k]
            rest = term if rest is None else rest + term
        for i in range(count_x):
            low = (i + 1) * wide + 1
            inc_ref[c, i] = moved[low : low + count_y]
            res_ref[c, i] = rest[low : low + count_y]

    def sent(step, carry):
        other = lax.rem(b + step, n_micro)
        route_copy(other, b).wait_send()
        back_copy(other, b).wait_send()
        return carry

    lax.fori_loop(1, n_micro, sent, 0)


def shards(
    displacement,
    load,
    routes,
    counts,
    stiffness,
    precond,
    forcing,
    coupling,
    lame_first,
    lame_shear,
):
    _, count_x, count_y, lanes = displacement.shape
    points = count_x * count_y * lanes
    n_macro, n_micro = lax.axis_size("macro"), lax.axis_size("micro")
    capacity = max(2, 2 * points // n_micro)
    slots = -(-capacity // 128) * 128
    size = stiffness.shape[1]
    tall = -(-(6 + len(PAIRS)) // 8) * 8
    rows = -(-(count_x + 2) * (count_y + 2) // 8) * 8
    side = -(-3 * max(count_x, count_y) // 8) * 8
    total = n_macro * n_micro
    sides = count_x + count_y + 1
    vmem = pl.BlockSpec(memory_space=pltpu.VMEM)
    smem = pl.BlockSpec(memory_space=pltpu.SMEM)
    anywhere = pl.BlockSpec(memory_space=pl.ANY)
    dma = pltpu.SemaphoreType.DMA

    def held(*shape):
        return pltpu.VMEM(shape, jnp.float32)

    def half(*shape):
        return pltpu.VMEM(shape, jnp.bfloat16)

    def body(*refs):
        newton_kernel((count_x, count_y, lanes, n_macro, n_micro), *refs)

    return tuple(
        pl.pallas_call(
            body,
            out_shape=[jax.ShapeDtypeStruct(load.shape, jnp.float32)] * 2,
            in_specs=[vmem] * 4 + [anywhere] * 2 + [vmem] * 2 + [smem] * 2,
            out_specs=[vmem, vmem],
            scratch_shapes=[
                half(size, size),
                half(size, size),
                half(size, 8),
                half(tall, size),
                half(tall, size),
                held(tall, size),
                half(n_micro, slots, points),
                held(3, *displacement.shape),
                held(8, points),
                held(n_micro, 8, slots),
                held(n_micro, 8, slots),
                held(n_micro, tall, slots),
                held(n_micro, tall, slots),
                held(tall, points),
                held(sides, tall, lanes),
                held(6 + len(PAIRS), rows, lanes),
                held(ITERS, 3, rows, lanes),
                held(ITERS, len(AROUND), side, lanes),
                held(ITERS, len(AROUND), side, lanes),
                held(16, 128),
                held(n_micro, 16, 128),
                held(16, 128),
                held(n_macro, 16, 128),
                held(1, 128),
                held(total, 1, 128),
                dma((2,)),
                dma((3,)),
                dma((3,)),
                dma((n_micro,)),
                dma((n_micro,)),
                dma((n_micro,)),
                dma((n_micro,)),
                dma((sides,)),
                dma((sides,)),
                dma((ITERS, len(AROUND))),
                dma((ITERS, len(AROUND))),
                dma((n_micro - 1,)),
                dma((n_micro - 1,)),
                dma((n_macro - 1,)),
                dma((n_macro - 1,)),
                dma((total,)),
                dma((total,)),
            ],
            compiler_params=pltpu.CompilerParams(collective_id=0, has_side_effects=True),
            name="newton_step",
        )(
            displacement,
            load,
            routes.reshape(points // 128, 128),
            counts.reshape(points // 128, 128),
            stiffness[0],
            precond[0],
            forcing[0],
            coupling[0].T,
            lame_first,
            lame_shear,
        )
    )


def solution(mesh):
    in_specs = (
        P(None, "macro", "micro", None),
        P(None, "macro", "micro", None),
        P("macro", "micro", None, None),
        P("macro", "micro", None),
        P("micro", None, None),
        P("micro", None, None),
        P("micro", None, None),
        P("micro", None, None),
        P("micro"),
        P("micro"),
    )
    out_specs = (P(None, "macro", "micro", None), P(None, "macro", "micro", None))
    return jax.shard_map(shards, mesh=mesh, in_specs=in_specs, out_specs=out_specs, check_vma=False)
```

```python
import jax
import jax.numpy as jnp
from jax import lax
from jax.experimental import pallas as pl
from jax.experimental.pallas import tpu as pltpu
from jax.sharding import PartitionSpec as P

ITMAX = 4
ITERS = 5


BETA = 0.1
OMEGA = 0.8
MASS = 0.1
VOIGT = ((0, 5, 4), (5, 1, 3), (4, 3, 2))
PAIRS = tuple((first, second) for first in range(6) for second in range(first, 6))
PAIR_AT = {pair: at for at, pair in enumerate(PAIRS)}
AROUND = tuple((dx, dy) for dx in (-1, 0, 1) for dy in (-1, 0, 1) if (dx, dy) != (0, 0))
MESH = pl.DeviceIdType.MESH


def newton_kernel(
    sizes,
    disp_ref,
    load_ref,
    routes_ref,
    counts_ref,
    stiff_hbm,
    pre_hbm,
    force_ref,
    couple_ref,
    first_ref,
    shear_ref,
    inc_ref,
    res_ref,
    stiff,
    pre,
    force_t,
    couple,
    products,
    wide_products,
    spots,
    near_disp,
    bundle,
    route_out,
    route_in,
    back_out,
    back_in,
    values,
    beside,
    elem,
    basis,
    send_halo,
    halo,
    part,
    got_micro,
    middle,
    got_macro,
    last_part,
    last_all,
    weight_sem,
    disp_send,
    disp_recv,
    route_send,
    route_recv,
    back_send,
    back_recv,
    side_send,
    side_recv,
    send_sem,
    recv_sem,
    micro_send,
    micro_recv,
    macro_send,
    macro_recv,
    last_send,
    last_recv,
):
    count_x, count_y, lanes, n_macro, n_micro = sizes
    wide = count_y + 2
    rows = basis.shape[2]
    points = spots.shape[1]
    slots = spots.shape[0] // n_micro
    pairs = n_micro // 2
    groups = points // 128
    size = stiff.shape[0]
    tall = couple.shape[0]
    total = n_macro * n_micro
    a, b = lax.axis_index("macro"), lax.axis_index("micro")
    me = a * n_micro + b

    def device(other):
        return (other // n_micro, lax.rem(other, n_micro))

    def inside(dx, dy):
        test = None
        for place, step, count in ((a, dx, n_macro), (b, dy, n_micro)):
            if step != 0:
                good = (place > 0) if step < 0 else (place < count - 1)
                test = good if test is None else jnp.logical_and(test, good)
        return test

    barrier = pltpu.get_barrier_semaphore()

    def greet(step, carry):
        pl.semaphore_signal(
            barrier, inc=1, device_id=device(lax.rem(me + step, total)), device_id_type=MESH
        )
        return carry

    lax.fori_loop(1, total, greet, 0)
    weights = [
        pltpu.make_async_copy(stiff_hbm, stiff, weight_sem.at[0]),
        pltpu.make_async_copy(pre_hbm, pre, weight_sem.at[1]),
    ]
    for copy in weights:
        copy.start()

    force = force_ref[...].astype(jnp.float32)
    force = jnp.concatenate([force, jnp.zeros((2, size), jnp.float32)], axis=0)
    force_t[...] = force.T.astype(jnp.bfloat16)
    wide_products[...] = jnp.zeros((tall, size), jnp.float32)
    coupling = couple_ref[...].astype(jnp.float32)
    wide_products[pl.ds(0, 6)] = coupling
    couple[...] = wide_products[...].astype(jnp.bfloat16)
    wide_products[pl.ds(0, 6)] = jnp.zeros((6, size), jnp.float32)
    for at, (first, second) in enumerate(PAIRS):
        wide_products[pl.ds(6 + at, 1)] = coupling[first : first + 1] * coupling[second : second + 1]
    products[...] = wide_products[...].astype(jnp.bfloat16)

    route = routes_ref[...]
    row_of = lax.broadcasted_iota(jnp.int32, (128, 128), 0)
    column_of = lax.broadcasted_iota(jnp.int32, (128, 128), 1)
    until = jnp.where(row_of <= column_of, 1.0, 0.0).astype(jnp.bfloat16)
    named = [jnp.where(route == owner, 1.0, 0.0) for owner in range(n_micro)]
    named = jnp.concatenate(named, axis=0).astype(jnp.bfloat16)
    inner_rank = jnp.dot(named, until, preferred_element_type=jnp.float32)
    whole = jnp.dot(
        named, jnp.ones((128, 128), jnp.bfloat16), preferred_element_type=jnp.float32
    ).astype(jnp.bfloat16)
    span = n_micro * groups
    row_of = lax.broadcasted_iota(jnp.int32, (span, span), 0)
    column_of = lax.broadcasted_iota(jnp.int32, (span, span), 1)
    ahead = jnp.logical_and(column_of < row_of, column_of // groups == row_of // groups)
    before = jnp.dot(
        jnp.where(ahead, 1.0, 0.0).astype(jnp.bfloat16), whole, preferred_element_type=jnp.float32
    )
    ranks = inner_rank + before - 1.0
    rank = jnp.zeros((groups, 128), jnp.float32)
    for owner in range(n_micro):
        rank = jnp.where(route == owner, ranks[owner * groups : (owner + 1) * groups], rank)
    slot_at = lax.broadcasted_iota(jnp.int32, (slots, 128), 0).astype(jnp.float32)

    def spot(owner, carry):
        local = jnp.where(route == owner, rank, -1.0)
        for g in range(groups):
            hit = jnp.where(local[g : g + 1] == slot_at, 1.0, 0.0)
            low = pl.multiple_of(owner * slots, slots)
            spots[pl.ds(low, slots), g * 128 : (g + 1) * 128] = hit.astype(jnp.bfloat16)
        return carry

    lax.fori_loop(0, n_micro, spot, 0)

    for it in range(basis.shape[0]):
        for c in range(3):
            basis[it, c] = jnp.zeros((rows, lanes), jnp.float32)
    elem[...] = jnp.zeros(elem.shape, jnp.float32)
    values[...] = jnp.zeros(values.shape, jnp.float32)
    bundle[...] = jnp.zeros(bundle.shape, jnp.float32)
    for g in range(groups):
        bundle[6:7, g * 128 : (g + 1) * 128] = counts_ref[g : g + 1].astype(jnp.float32)

    for at, (dx, dy) in enumerate(AROUND):

        @pl.when(jnp.logical_not(inside(dx, dy)))
        def _():
            for it in range(ITERS):
                halo[it, at] = jnp.zeros(halo.shape[2:], jnp.float32)

    after = ((1, 0), (0, 1), (1, 1))
    for at, (dx, dy) in enumerate(after):

        @pl.when(jnp.logical_not(inside(dx, dy)))
        def _():
            near_disp[at] = jnp.zeros(near_disp.shape[1:], jnp.float32)

    owned = [(i, j) for i in range(count_x) for j in range(count_y)]
    column_at = {place: at for at, place in enumerate(owned)}
    handed = [((1, 0), (count_x - 1, j), (0, j + 1)) for j in range(count_y)]
    handed += [((0, 1), (i, count_y - 1), (i + 1, 0)) for i in range(count_x)]
    handed += [((1, 1), (count_x - 1, count_y - 1), (0, 0))]
    for at, ((dx, dy), _, _) in enumerate(handed):

        @pl.when(jnp.logical_not(inside(-dx, -dy)))
        def _():
            beside[at] = jnp.zeros(beside.shape[1:], jnp.float32)

    pl.semaphore_wait(barrier, total - 1)

    def show(at):
        dx, dy = after[at]
        return pltpu.make_async_remote_copy(
            src_ref=disp_ref,
            dst_ref=near_disp.at[at],
            send_sem=disp_send.at[at],
            recv_sem=disp_recv.at[at],
            device_id=(a - dx, b - dy),
            device_id_type=MESH,
        )

    for at, (dx, dy) in enumerate(after):

        @pl.when(inside(-dx, -dy))
        def _():
            show(at).start()

    for c in range(3):
        for i, j in owned:
            basis[0, c, pl.ds((i + 1) * wide + j + 1, 1)] = disp_ref[c, i, j : j + 1]
    for at, (dx, dy) in enumerate(after):

        @pl.when(inside(-dx, -dy))
        def _():
            show(at).wait_send()

        @pl.when(inside(dx, dy))
        def _():
            pltpu.make_async_remote_copy(
                src_ref=disp_ref,
                dst_ref=near_disp.at[at],
                send_sem=disp_send.at[at],
                recv_sem=disp_recv.at[at],
                device_id=(a + dx, b + dy),
                device_id_type=MESH,
            ).wait_recv()

    for c in range(3):
        for j in range(count_y):
            basis[0, c, pl.ds((count_x + 1) * wide + j + 1, 1)] = near_disp[0, c, 0, j : j + 1]
        for i in range(count_x):
            basis[0, c, pl.ds((i + 1) * wide + count_y + 1, 1)] = near_disp[1, c, i, 0:1]
        basis[0, c, pl.ds((count_x + 1) * wide + count_y + 1, 1)] = near_disp[2, c, 0, 0:1]

    row_at = lax.broadcasted_iota(jnp.int32, (rows, lanes), 0)
    lane_at = lax.broadcasted_iota(jnp.int32, (rows, lanes), 1)
    own = row_at < 0
    for i in range(1, count_x + 1):
        low = i * wide + 1
        own = jnp.logical_or(own, jnp.logical_and(row_at >= low, row_at < low + count_y))

    def up(value, axis):
        if axis == 2:
            moved = pltpu.roll(value, lanes - 1, 1)
            return jnp.where(lane_at == lanes - 1, 0.0, moved)
        return pltpu.roll(value, rows - (wide if axis == 0 else 1), 0)

    def down(value, axis):
        if axis == 2:
            return jnp.where(lane_at == 0, 0.0, pltpu.roll(value, 1, 1))
        return pltpu.roll(value, wide if axis == 0 else 1, 0)

    def strain_of(it):
        grads = []
        for c in range(3):
            value = basis[it, c]
            moved = up(value, 2)
            total, gap = value + moved, moved - value
            total_up, gap_up = up(total, 1), up(gap, 1)
            flat, slope_y, slope_z = total + total_up, total_up - total, gap + gap_up
            grads.append(
                (
                    0.25 * (up(flat, 0) - flat),
                    0.25 * (up(slope_y, 0) + slope_y),
                    0.25 * (up(slope_z, 0) + slope_z),
                )
            )
        return [
            grads[0][0],
            grads[1][1],
            grads[2][2],
            grads[1][2] + grads[2][1],
            grads[0][2] + grads[2][0],
            grads[0][1] + grads[1][0],
        ]

    strain = strain_of(0)
    for at, (i, j) in enumerate(owned):
        low = (i + 1) * wide + j + 1
        for k in range(6):
            bundle[k : k + 1, at * lanes : (at + 1) * lanes] = strain[k][low : low + 1]
    exact = bundle[...]
    high = exact.astype(jnp.bfloat16).astype(jnp.float32)
    both = jnp.concatenate([high, exact - high], axis=0).astype(jnp.bfloat16)

    def route_copy(other, mine):
        return pltpu.make_async_remote_copy(
            src_ref=route_out.at[other],
            dst_ref=route_in.at[mine],
            send_sem=route_send.at[other],
            recv_sem=route_recv.at[mine],
            device_id=(a, other),
            device_id_type=MESH,
        )

    chip, core = b // 2, lax.rem(b, 2)

    def pair_rows(place):
        return pl.ds(pl.multiple_of(place * (2 * slots), 2 * slots), 2 * slots)

    def hand_out(at, carry):
        place = lax.rem(chip + pairs - 1 - at, pairs)
        moved = lax.dot_general(
            both,
            spots[pair_rows(place)],
            (((1,), (1,)), ((), ())),
            preferred_element_type=jnp.float32,
        )
        moved = moved[:8] + moved[8:]
        for k in range(2):
            other = 2 * place + k
            piece = moved[:, k * slots : (k + 1) * slots]

            @pl.when(other != b)
            def _():
                route_out[other] = piece
                route_copy(other, b).start()

            @pl.when(other == b)
            def _():
                route_in[b] = piece

        return carry

    lax.fori_loop(0, pairs, hand_out, 0)
    for copy in weights:
        copy.wait()

    lame_first, lame_shear = first_ref[0], shear_ref[0]
    tall_at = lax.broadcasted_iota(jnp.int32, (tall, 2 * slots), 0)
    on_trace = jnp.where(tall_at < 3, lame_first, 0.0)
    on_strain = jnp.where(tall_at < 3, 2.0 * lame_shear, jnp.where(tall_at < 6, lame_shear, 0.0))
    base = jnp.zeros((tall, 2 * slots), jnp.float32)
    for at, (i, j) in enumerate(PAIRS):
        if i == j:
            amount = lame_first + 2.0 * lame_shear if i < 3 else lame_shear
        elif j < 3:
            amount = lame_first
        else:
            continue
        base = jnp.where(tall_at == 6 + at, amount, base)

    def back_copy(other, mine):
        return pltpu.make_async_remote_copy(
            src_ref=back_out.at[other],
            dst_ref=back_in.at[mine],
            send_sem=back_send.at[other],
            recv_sem=back_recv.at[mine],
            device_id=(a, other),
            device_id_type=MESH,
        )

    def solve(at, carry):
        place = lax.rem(chip + at, pairs)
        taken = []
        for k in range(2):
            other = 2 * place + k

            @pl.when(other != b)
            def _():
                route_copy(b, other).wait_recv()

            taken.append(route_in[other])
        points_in = jnp.concatenate(taken, axis=1)
        sweeps = points_in[6:7]
        modal_load = jnp.dot(
            force_t[...], points_in.astype(jnp.bfloat16), preferred_element_type=jnp.float32
        )
        modes = None
        for sweep in range(ITMAX):
            if modes is None:
                misfit = (-modal_load).astype(jnp.bfloat16)
            else:
                short = modes.astype(jnp.bfloat16)
                misfit = jnp.dot(stiff[...], short, preferred_element_type=jnp.float32)
                misfit = (misfit - modal_load).astype(jnp.bfloat16)
                misfit = misfit + jnp.tanh(short) * jnp.bfloat16(BETA)
            change = jnp.dot(pre[...], misfit, preferred_element_type=jnp.float32)
            if modes is None:
                modes = -OMEGA * change
            else:
                modes = modes - jnp.where(sweeps > sweep, OMEGA, 0.0) * change
        bent = jnp.tanh(modes)
        slope = 1.0 - bent * bent
        trace = points_in[0:1] + points_in[1:2] + points_in[2:3]
        padded = jnp.concatenate(
            [points_in, jnp.zeros((tall - 8, 2 * slots), jnp.float32)], axis=0
        )
        answer = on_trace * trace + on_strain * padded + base
        answer = answer + jnp.dot(
            couple[...], modes.astype(jnp.bfloat16), preferred_element_type=jnp.float32
        )
        answer = answer + jnp.dot(
            products[...], slope.astype(jnp.bfloat16), preferred_element_type=jnp.float32
        )
        for k in range(2):
            other = 2 * place + k
            piece = answer[:, k * slots : (k + 1) * slots]

            @pl.when(other != b)
            def _():
                back_out[other] = piece
                back_copy(other, b).start()

            @pl.when(other == b)
            def _():
                back_in[b] = piece

        return carry

    lax.fori_loop(0, pairs, solve, 0)

    def take_back(at, carry):
        place = lax.rem(chip + pairs - at, pairs)
        taken = []
        for k in range(2):
            other = 2 * place + k

            @pl.when(other != b)
            def _():
                back_copy(b, other).wait_recv()

            taken.append(back_in[other])
        exact = jnp.concatenate(taken, axis=1)
        high = exact.astype(jnp.bfloat16).astype(jnp.float32)
        both = jnp.concatenate([high, exact - high], axis=0).astype(jnp.bfloat16)
        moved = jnp.dot(both, spots[pair_rows(place)], preferred_element_type=jnp.float32)
        values[...] += moved[:tall] + moved[tall:]
        return carry

    lax.fori_loop(0, pairs, take_back, 0)

    def side_copy(at):
        (dx, dy), place, _ = handed[at]
        low = column_at[place] * lanes
        return pltpu.make_async_remote_copy(
            src_ref=values.at[:, pl.ds(low, lanes)],
            dst_ref=beside.at[at],
            send_sem=side_send.at[at],
            recv_sem=side_recv.at[at],
            device_id=(a + dx, b + dy),
            device_id_type=MESH,
        )

    for at, ((dx, dy), _, _) in enumerate(handed):

        @pl.when(inside(dx, dy))
        def _():
            side_copy(at).start()

    def put_column(read, row):
        for v in range(6 + len(PAIRS)):
            elem[v, pl.ds(row, 1)] = read(v)

    for at, (i, j) in enumerate(owned):
        put_column(
            lambda v: values[v : v + 1, at * lanes : (at + 1) * lanes], (i + 1) * wide + j + 1
        )
    for at, ((dx, dy), _, (i, j)) in enumerate(handed):

        @pl.when(inside(dx, dy))
        def _():
            side_copy(at).wait_send()

        @pl.when(inside(-dx, -dy))
        def _():
            pltpu.make_async_remote_copy(
                src_ref=values.at[:, pl.ds(0, lanes)],
                dst_ref=beside.at[at],
                send_sem=side_send.at[at],
                recv_sem=side_recv.at[at],
                device_id=(a - dx, b - dy),
                device_id_type=MESH,
            ).wait_recv()

        put_column(lambda v: beside[at, v : v + 1], i * wide + j)

    def near(step, count):
        return {0: list(range(1, count + 1)), -1: [1], 1: [count]}[step]

    def far(step, count):
        return {0: list(range(1, count + 1)), -1: [0], 1: [count + 1]}[step]

    def places(at, pick):
        dx, dy = AROUND[at]
        return [i * wide + j for i in pick(dx, count_x) for j in pick(dy, count_y)]

    def hop(it, at):
        dx, dy = AROUND[at]
        other = len(AROUND) - 1 - at
        return pltpu.make_async_remote_copy(
            src_ref=send_halo.at[it, at],
            dst_ref=halo.at[it, other],
            send_sem=send_sem.at[it, at],
            recv_sem=recv_sem.at[it, other],
            device_id=(a + dx, b + dy),
            device_id_type=MESH,
        )

    def halo_start(it):
        for at, (dx, dy) in enumerate(AROUND):

            @pl.when(inside(dx, dy))
            def _():
                mine = places(at, near)
                for c in range(3):
                    for k, row in enumerate(mine):
                        send_halo[it, at, pl.ds(c * len(mine) + k, 1)] = basis[it, c, pl.ds(row, 1)]
                hop(it, at).start()

    def halo_finish(it):
        for at, (dx, dy) in enumerate(AROUND):

            @pl.when(inside(dx, dy))
            def _():
                hop(it, at).wait_send()
                pltpu.make_async_remote_copy(
                    src_ref=send_halo.at[it, at],
                    dst_ref=halo.at[it, at],
                    send_sem=send_sem.at[it, at],
                    recv_sem=recv_sem.at[it, at],
                    device_id=(a + dx, b + dy),
                    device_id_type=MESH,
                ).wait_recv()

        for at in range(len(AROUND)):
            theirs = places(at, far)
            for c in range(3):
                for k, row in enumerate(theirs):
                    basis[it, c, pl.ds(row, 1)] = halo[it, at, pl.ds(c * len(theirs) + k, 1)]

    def force_of(stress, c):
        first, second, third = (stress[VOIGT[c][d]] for d in range(3))
        first = first + down(first, 2)
        second = second + down(second, 2)
        third = down(third, 2) - third
        first = first + down(first, 1)
        rest = down(second, 1) - second + third + down(third, 1)
        return 0.25 * (down(first, 0) - first + rest + down(rest, 0))

    def applied(it):
        strain = strain_of(it)
        stress = []
        for i in range(6):
            value = None
            for j in range(6):
                term = elem[6 + PAIR_AT[(min(i, j), max(i, j))]] * strain[j]
                value = term if value is None else value + term
            stress.append(value)
        return [
            jnp.where(own, MASS * basis[it, c] + force_of(stress, c), 0.0) for c in range(3)
        ]

    def product(first, second):
        total = None
        for c in range(3):
            term = first[c] * second[c]
            total = term if total is None else total + term
        total = jnp.sum(jnp.where(own, total, 0.0), axis=0, keepdims=True)
        value = total[:, :128]
        for at in range(128, lanes, 128):
            value = value + total[:, at : at + 128]
        return value

    def stacked(pieces):
        tile_row = lax.broadcasted_iota(jnp.int32, (16, 128), 0)
        value = jnp.zeros((16, 128), jnp.float32)
        for at, piece in enumerate(pieces):
            value = jnp.where(tile_row == at, piece, value)
        return value

    def gather_start(src, dst, count, mine, send, recv, device):
        copies = []
        for step in range(1, count):
            copy = pltpu.make_async_remote_copy(
                src_ref=src,
                dst_ref=dst.at[mine],
                send_sem=send.at[step - 1],
                recv_sem=recv.at[step - 1],
                device_id=device(lax.rem(mine + step, count)),
                device_id_type=MESH,
            )
            copy.start()
            copies.append(copy)
        dst[mine] = src[...]
        return copies

    def gather_finish(copies, dst, count):
        for copy in copies:
            copy.wait()
        total = dst[0]
        for at in range(1, count):
            total = total + dst[at]
        return total

    stress = [elem[i] for i in range(6)]
    zero = jnp.zeros((rows, lanes), jnp.float32)
    for c in range(3):
        padded = jnp.concatenate(
            [jnp.zeros((wide + 1, lanes), jnp.float32)]
            + [
                piece
                for i in range(count_x)
                for piece in (load_ref[c, i], jnp.zeros((2, lanes), jnp.float32))
            ]
            + [jnp.zeros((rows - 1 - wide * (count_x + 1), lanes), jnp.float32)],
            axis=0,
        )
        basis[0, c] = jnp.where(own, padded - force_of(stress, c), zero)
    halo_start(0)
    halo_finish(0)
    grown = applied(0)
    for c in range(3):
        basis[1, c] = grown[c]
    halo_start(1)
    start = [basis[0, c] for c in range(3)]
    part[...] = stacked([product(start, start), product(grown, grown)])
    copies = gather_start(
        part, got_micro, n_micro, b, micro_send, micro_recv, lambda other: (a, other)
    )
    halo_finish(1)
    grown = applied(1)
    for c in range(3):
        basis[2, c] = grown[c]
    halo_start(2)
    middle[...] = gather_finish(copies, got_micro, n_micro)
    copies = gather_start(
        middle, got_macro, n_macro, a, macro_send, macro_recv, lambda other: (other, b)
    )
    halo_finish(2)
    totals = jnp.sum(gather_finish(copies, got_macro, n_macro), axis=1, keepdims=True)
    shift = jnp.sqrt(totals[1:2] / totals[0:1])
    scale = 1.0 / shift
    for c in range(3):
        u0, w1, w2 = basis[0, c], basis[1, c] * scale, basis[2, c] * (scale * scale)
        basis[1, c] = w1 - u0
        basis[2, c] = (w2 - w1) - (w1 - u0)

    def field(it):
        return [basis[it, c] for c in range(3)]

    def step(it):
        grown = applied(it)
        return [grown[c] * scale - jnp.where(own, basis[it, c], 0.0) for c in range(3)]

    moments = []
    for it in range(2, ITERS):
        grown = step(it)
        if it + 1 < ITERS:
            for c in range(3):
                basis[it + 1, c] = grown[c]
            halo_start(it + 1)
            if it == 2:
                for k in range(3):
                    moments.append(product(field(k), field(k)))
                    moments.append(product(field(k), field(k + 1)))
            else:
                moments.append(product(field(it), field(it)))
                moments.append(product(field(it), field(it + 1)))
            halo_finish(it + 1)
    moments.append(product(field(ITERS - 1), field(ITERS - 1)))
    moments.append(product(field(ITERS - 1), grown))
    sums = jnp.sum(stacked(moments), axis=1, keepdims=True)
    diagonal = lax.broadcasted_iota(jnp.int32, (16, 128), 0) == lax.broadcasted_iota(
        jnp.int32, (16, 128), 1
    )
    last_part[...] = jnp.sum(jnp.where(diagonal, sums, 0.0), axis=0, keepdims=True)

    def last_copy(step, other):
        return pltpu.make_async_remote_copy(
            src_ref=last_part,
            dst_ref=last_all.at[me],
            send_sem=last_send.at[step],
            recv_sem=last_recv.at[step],
            device_id=device(other),
            device_id_type=MESH,
        )

    def last_start(step, carry):
        last_copy(step, lax.rem(me + step, total)).start()
        return carry

    def last_wait(step, carry):
        last_copy(step, lax.rem(me + step, total)).wait()
        return carry

    lax.fori_loop(1, total, last_start, 0)
    last_all[me] = last_part[...]
    lax.fori_loop(1, total, last_wait, 0)
    totals = jnp.sum(last_all[...], axis=0)
    held = [totals[:, k : k + 1] for k in range(2 * ITERS)]

    def inner(first, second, extra=0):
        gathered = {}
        for i, x in enumerate(first):
            for j, y in enumerate(second):
                gathered.setdefault(i + j, []).append(x * y)
        value = None
        for degree, terms in gathered.items():
            total = terms[0]
            for term in terms[1:]:
                total = total + term
            total = total * held[degree + extra]
            value = total if value is None else value + total
        return value

    one = jnp.ones((1, 1), jnp.float32)
    left, toward, done = [one], [one], []
    norm = held[0]
    for it in range(ITERS):
        energy = inner(toward, toward) + inner(toward, toward, 1)
        length = norm / energy
        done = [x + length * scale * p for x, p in zip(done + [0.0], toward)]
        raised = [
            (toward[k] if k < len(toward) else 0.0) + (toward[k - 1] if k > 0 else 0.0)
            for k in range(len(toward) + 1)
        ]
        left = [
            (left[k] if k < len(left) else 0.0) - length * raised[k] for k in range(len(raised))
        ]
        if it + 1 < ITERS:
            fresh = inner(left, left)
            ratio = fresh / norm
            toward = [
                left[k] + (ratio * toward[k] if k < len(toward) else 0.0)
                for k in range(len(left))
            ]
            norm = fresh
    for c in range(3):
        fields = [basis[k, c] for k in range(ITERS)] + [grown[c]]
        moved, rest = None, None
        for k in range(ITERS + 1):
            if k < len(done):
                term = done[k] * fields[k]
                moved = term if moved is None else moved + term
            term = left[k] * fields[k]
            rest = term if rest is None else rest + term
        for i in range(count_x):
            low = (i + 1) * wide + 1
            inc_ref[c, i] = moved[low : low + count_y]
            res_ref[c, i] = rest[low : low + count_y]

    def sent(step, carry):
        other = lax.rem(b + step, n_micro)
        route_copy(other, b).wait_send()
        back_copy(other, b).wait_send()
        return carry

    lax.fori_loop(1, n_micro, sent, 0)


def shards(
    displacement,
    load,
    routes,
    counts,
    stiffness,
    precond,
    forcing,
    coupling,
    lame_first,
    lame_shear,
):
    _, count_x, count_y, lanes = displacement.shape
    points = count_x * count_y * lanes
    n_macro, n_micro = lax.axis_size("macro"), lax.axis_size("micro")
    capacity = max(2, 2 * points // n_micro)
    slots = -(-capacity // 128) * 128
    size = stiffness.shape[1]
    tall = -(-(6 + len(PAIRS)) // 8) * 8
    rows = -(-(count_x + 2) * (count_y + 2) // 8) * 8
    side = -(-3 * max(count_x, count_y) // 8) * 8
    total = n_macro * n_micro
    sides = count_x + count_y + 1
    vmem = pl.BlockSpec(memory_space=pltpu.VMEM)
    smem = pl.BlockSpec(memory_space=pltpu.SMEM)
    anywhere = pl.BlockSpec(memory_space=pl.ANY)
    dma = pltpu.SemaphoreType.DMA

    def held(*shape):
        return pltpu.VMEM(shape, jnp.float32)

    def half(*shape):
        return pltpu.VMEM(shape, jnp.bfloat16)

    def body(*refs):
        newton_kernel((count_x, count_y, lanes, n_macro, n_micro), *refs)

    return tuple(
        pl.pallas_call(
            body,
            out_shape=[jax.ShapeDtypeStruct(load.shape, jnp.float32)] * 2,
            in_specs=[vmem] * 4 + [anywhere] * 2 + [vmem] * 2 + [smem] * 2,
            out_specs=[vmem, vmem],
            scratch_shapes=[
                half(size, size),
                half(size, size),
                half(size, 8),
                half(tall, size),
                half(tall, size),
                held(tall, size),
                half(n_micro * slots, points),
                held(3, *displacement.shape),
                held(8, points),
                held(n_micro, 8, slots),
                held(n_micro, 8, slots),
                held(n_micro, tall, slots),
                held(n_micro, tall, slots),
                held(tall, points),
                held(sides, tall, lanes),
                held(6 + len(PAIRS), rows, lanes),
                held(ITERS, 3, rows, lanes),
                held(ITERS, len(AROUND), side, lanes),
                held(ITERS, len(AROUND), side, lanes),
                held(16, 128),
                held(n_micro, 16, 128),
                held(16, 128),
                held(n_macro, 16, 128),
                held(1, 128),
                held(total, 1, 128),
                dma((2,)),
                dma((3,)),
                dma((3,)),
                dma((n_micro,)),
                dma((n_micro,)),
                dma((n_micro,)),
                dma((n_micro,)),
                dma((sides,)),
                dma((sides,)),
                dma((ITERS, len(AROUND))),
                dma((ITERS, len(AROUND))),
                dma((n_micro - 1,)),
                dma((n_micro - 1,)),
                dma((n_macro - 1,)),
                dma((n_macro - 1,)),
                dma((total,)),
                dma((total,)),
            ],
            compiler_params=pltpu.CompilerParams(collective_id=0, has_side_effects=True),
            name="newton_step",
        )(
            displacement,
            load,
            routes.reshape(points // 128, 128),
            counts.reshape(points // 128, 128),
            stiffness[0],
            precond[0],
            forcing[0],
            coupling[0].T,
            lame_first,
            lame_shear,
        )
    )


def solution(mesh):
    in_specs = (
        P(None, "macro", "micro", None),
        P(None, "macro", "micro", None),
        P("macro", "micro", None, None),
        P("macro", "micro", None),
        P("micro", None, None),
        P("micro", None, None),
        P("micro", None, None),
        P("micro", None, None),
        P("micro"),
        P("micro"),
    )
    out_specs = (P(None, "macro", "micro", None), P(None, "macro", "micro", None))
    return jax.shard_map(shards, mesh=mesh, in_specs=in_specs, out_specs=out_specs, check_vma=False)
```

```python
import jax
import jax.numpy as jnp
from jax import lax
from jax.experimental import pallas as pl
from jax.experimental.pallas import tpu as pltpu
from jax.sharding import PartitionSpec as P

ITMAX = 4
ITERS = 5


BETA = 0.1
OMEGA = 0.8
MASS = 0.1
VOIGT = ((0, 5, 4), (5, 1, 3), (4, 3, 2))
PAIRS = tuple((first, second) for first in range(6) for second in range(first, 6))
PAIR_AT = {pair: at for at, pair in enumerate(PAIRS)}
AROUND = tuple((dx, dy) for dx in (-1, 0, 1) for dy in (-1, 0, 1) if (dx, dy) != (0, 0))
MESH = pl.DeviceIdType.MESH


def newton_kernel(
    sizes,
    disp_ref,
    load_ref,
    routes_ref,
    counts_ref,
    stiff_hbm,
    pre_hbm,
    force_ref,
    couple_ref,
    first_ref,
    shear_ref,
    inc_ref,
    res_ref,
    stiff,
    pre,
    maps,
    couple,
    products,
    wide_products,
    spots,
    near_disp,
    bundle,
    route_out,
    route_in,
    back_out,
    back_in,
    values,
    beside,
    elem,
    basis,
    send_halo,
    halo,
    part,
    got_micro,
    middle,
    got_macro,
    last_part,
    last_all,
    weight_sem,
    disp_send,
    disp_recv,
    route_send,
    route_recv,
    back_send,
    back_recv,
    side_send,
    side_recv,
    send_sem,
    recv_sem,
    micro_send,
    micro_recv,
    macro_send,
    macro_recv,
    last_send,
    last_recv,
):
    count_x, count_y, lanes, n_macro, n_micro = sizes
    wide = count_y + 2
    rows = basis.shape[2]
    points = spots.shape[1]
    slots = spots.shape[0] // n_micro
    pairs = n_micro // 2
    groups = points // 128
    size = stiff.shape[0]
    tall = couple.shape[0]
    total = n_macro * n_micro
    a, b = lax.axis_index("macro"), lax.axis_index("micro")
    me = a * n_micro + b

    def device(other):
        return (other // n_micro, lax.rem(other, n_micro))

    def inside(dx, dy):
        test = None
        for place, step, count in ((a, dx, n_macro), (b, dy, n_micro)):
            if step != 0:
                good = (place > 0) if step < 0 else (place < count - 1)
                test = good if test is None else jnp.logical_and(test, good)
        return test

    barrier = pltpu.get_barrier_semaphore()

    def greet(step, carry):
        pl.semaphore_signal(
            barrier, inc=1, device_id=device(lax.rem(me + step, total)), device_id_type=MESH
        )
        return carry

    lax.fori_loop(1, total, greet, 0)
    weights = [
        pltpu.make_async_copy(stiff_hbm, stiff, weight_sem.at[0]),
        pltpu.make_async_copy(pre_hbm, pre, weight_sem.at[1]),
    ]
    for copy in weights:
        copy.start()

    force = force_ref[...].astype(jnp.float32)
    force = jnp.concatenate([force, jnp.zeros((2, size), jnp.float32)], axis=0)
    load_map = force.T
    wide_products[...] = jnp.zeros((tall, size), jnp.float32)
    coupling = couple_ref[...].astype(jnp.float32)
    wide_products[pl.ds(0, 6)] = coupling
    couple[...] = wide_products[...].astype(jnp.bfloat16)
    wide_products[pl.ds(0, 6)] = jnp.zeros((6, size), jnp.float32)
    for at, (first, second) in enumerate(PAIRS):
        wide_products[pl.ds(6 + at, 1)] = coupling[first : first + 1] * coupling[second : second + 1]
    products[...] = wide_products[...].astype(jnp.bfloat16)

    route = routes_ref[...]
    row_of = lax.broadcasted_iota(jnp.int32, (128, 128), 0)
    column_of = lax.broadcasted_iota(jnp.int32, (128, 128), 1)
    until = jnp.where(row_of <= column_of, 1.0, 0.0).astype(jnp.bfloat16)
    named = [jnp.where(route == owner, 1.0, 0.0) for owner in range(n_micro)]
    named = jnp.concatenate(named, axis=0).astype(jnp.bfloat16)
    inner_rank = jnp.dot(named, until, preferred_element_type=jnp.float32)
    whole = jnp.dot(
        named, jnp.ones((128, 128), jnp.bfloat16), preferred_element_type=jnp.float32
    ).astype(jnp.bfloat16)
    span = n_micro * groups
    row_of = lax.broadcasted_iota(jnp.int32, (span, span), 0)
    column_of = lax.broadcasted_iota(jnp.int32, (span, span), 1)
    ahead = jnp.logical_and(column_of < row_of, column_of // groups == row_of // groups)
    before = jnp.dot(
        jnp.where(ahead, 1.0, 0.0).astype(jnp.bfloat16), whole, preferred_element_type=jnp.float32
    )
    ranks = inner_rank + before - 1.0
    rank = jnp.zeros((groups, 128), jnp.float32)
    for owner in range(n_micro):
        rank = jnp.where(route == owner, ranks[owner * groups : (owner + 1) * groups], rank)
    slot_at = lax.broadcasted_iota(jnp.int32, (slots, 128), 0).astype(jnp.float32)

    def spot(owner, carry):
        local = jnp.where(route == owner, rank, -1.0)
        for g in range(groups):
            hit = jnp.where(local[g : g + 1] == slot_at, 1.0, 0.0)
            low = pl.multiple_of(owner * slots, slots)
            spots[pl.ds(low, slots), g * 128 : (g + 1) * 128] = hit.astype(jnp.bfloat16)
        return carry

    lax.fori_loop(0, n_micro, spot, 0)

    for it in range(basis.shape[0]):
        for c in range(3):
            basis[it, c] = jnp.zeros((rows, lanes), jnp.float32)
    elem[...] = jnp.zeros(elem.shape, jnp.float32)
    values[...] = jnp.zeros(values.shape, jnp.float32)
    bundle[...] = jnp.zeros(bundle.shape, jnp.float32)
    for g in range(groups):
        bundle[6:7, g * 128 : (g + 1) * 128] = counts_ref[g : g + 1].astype(jnp.float32)

    for at, (dx, dy) in enumerate(AROUND):

        @pl.when(jnp.logical_not(inside(dx, dy)))
        def _():
            for it in range(ITERS):
                halo[it, at] = jnp.zeros(halo.shape[2:], jnp.float32)

    after = ((1, 0), (0, 1), (1, 1))
    for at, (dx, dy) in enumerate(after):

        @pl.when(jnp.logical_not(inside(dx, dy)))
        def _():
            near_disp[at] = jnp.zeros(near_disp.shape[1:], jnp.float32)

    owned = [(i, j) for i in range(count_x) for j in range(count_y)]
    column_at = {place: at for at, place in enumerate(owned)}
    handed = [((1, 0), (count_x - 1, j), (0, j + 1)) for j in range(count_y)]
    handed += [((0, 1), (i, count_y - 1), (i + 1, 0)) for i in range(count_x)]
    handed += [((1, 1), (count_x - 1, count_y - 1), (0, 0))]
    for at, ((dx, dy), _, _) in enumerate(handed):

        @pl.when(jnp.logical_not(inside(-dx, -dy)))
        def _():
            beside[at] = jnp.zeros(beside.shape[1:], jnp.float32)

    pl.semaphore_wait(barrier, total - 1)

    def show(at):
        dx, dy = after[at]
        return pltpu.make_async_remote_copy(
            src_ref=disp_ref,
            dst_ref=near_disp.at[at],
            send_sem=disp_send.at[at],
            recv_sem=disp_recv.at[at],
            device_id=(a - dx, b - dy),
            device_id_type=MESH,
        )

    for at, (dx, dy) in enumerate(after):

        @pl.when(inside(-dx, -dy))
        def _():
            show(at).start()

    for copy in weights:
        copy.wait()

    def split(exact):
        high = exact.astype(jnp.bfloat16)
        return jnp.concatenate([high, (exact - high.astype(jnp.float32)).astype(jnp.bfloat16)], axis=1)

    def through(matrix, exact):
        moved = jnp.dot(matrix[...], split(exact), preferred_element_type=jnp.float32)
        return moved[:, :8] + moved[:, 8:]

    first_map = OMEGA * through(pre, load_map)
    misfit_map = through(stiff, first_map) - load_map
    for at, exact in enumerate((first_map, misfit_map, load_map)):
        maps[pl.ds(at * size, size)] = split(exact)
    for c in range(3):
        for i, j in owned:
            basis[0, c, pl.ds((i + 1) * wide + j + 1, 1)] = disp_ref[c, i, j : j + 1]
    for at, (dx, dy) in enumerate(after):

        @pl.when(inside(-dx, -dy))
        def _():
            show(at).wait_send()

        @pl.when(inside(dx, dy))
        def _():
            pltpu.make_async_remote_copy(
                src_ref=disp_ref,
                dst_ref=near_disp.at[at],
                send_sem=disp_send.at[at],
                recv_sem=disp_recv.at[at],
                device_id=(a + dx, b + dy),
                device_id_type=MESH,
            ).wait_recv()

    for c in range(3):
        for j in range(count_y):
            basis[0, c, pl.ds((count_x + 1) * wide + j + 1, 1)] = near_disp[0, c, 0, j : j + 1]
        for i in range(count_x):
            basis[0, c, pl.ds((i + 1) * wide + count_y + 1, 1)] = near_disp[1, c, i, 0:1]
        basis[0, c, pl.ds((count_x + 1) * wide + count_y + 1, 1)] = near_disp[2, c, 0, 0:1]

    row_at = lax.broadcasted_iota(jnp.int32, (rows, lanes), 0)
    lane_at = lax.broadcasted_iota(jnp.int32, (rows, lanes), 1)
    own = row_at < 0
    for i in range(1, count_x + 1):
        low = i * wide + 1
        own = jnp.logical_or(own, jnp.logical_and(row_at >= low, row_at < low + count_y))

    def up(value, axis):
        if axis == 2:
            moved = pltpu.roll(value, lanes - 1, 1)
            return jnp.where(lane_at == lanes - 1, 0.0, moved)
        return pltpu.roll(value, rows - (wide if axis == 0 else 1), 0)

    def down(value, axis):
        if axis == 2:
            return jnp.where(lane_at == 0, 0.0, pltpu.roll(value, 1, 1))
        return pltpu.roll(value, wide if axis == 0 else 1, 0)

    def strain_of(it):
        grads = []
        for c in range(3):
            value = basis[it, c]
            moved = up(value, 2)
            total, gap = value + moved, moved - value
            total_up, gap_up = up(total, 1), up(gap, 1)
            flat, slope_y, slope_z = total + total_up, total_up - total, gap + gap_up
            grads.append(
                (
                    0.25 * (up(flat, 0) - flat),
                    0.25 * (up(slope_y, 0) + slope_y),
                    0.25 * (up(slope_z, 0) + slope_z),
                )
            )
        return [
            grads[0][0],
            grads[1][1],
            grads[2][2],
            grads[1][2] + grads[2][1],
            grads[0][2] + grads[2][0],
            grads[0][1] + grads[1][0],
        ]

    strain = strain_of(0)
    for at, (i, j) in enumerate(owned):
        low = (i + 1) * wide + j + 1
        for k in range(6):
            bundle[k : k + 1, at * lanes : (at + 1) * lanes] = strain[k][low : low + 1]
    exact = bundle[...]
    high = exact.astype(jnp.bfloat16).astype(jnp.float32)
    both = jnp.concatenate([high, exact - high], axis=0).astype(jnp.bfloat16)

    def route_copy(other, mine):
        return pltpu.make_async_remote_copy(
            src_ref=route_out.at[other],
            dst_ref=route_in.at[mine],
            send_sem=route_send.at[other],
            recv_sem=route_recv.at[mine],
            device_id=(a, other),
            device_id_type=MESH,
        )

    chip, core = b // 2, lax.rem(b, 2)

    def pair_rows(place):
        return pl.ds(pl.multiple_of(place * (2 * slots), 2 * slots), 2 * slots)

    def hand_out(at, carry):
        place = lax.rem(chip + pairs - at, pairs)
        moved = lax.dot_general(
            both,
            spots[pair_rows(place)],
            (((1,), (1,)), ((), ())),
            preferred_element_type=jnp.float32,
        )
        moved = moved[:8] + moved[8:]
        for k in range(2):
            other = 2 * place + k
            piece = moved[:, k * slots : (k + 1) * slots]

            @pl.when(other != b)
            def _():
                route_out[other] = piece
                route_copy(other, b).start()

            @pl.when(other == b)
            def _():
                route_in[b] = piece

        return carry

    lax.fori_loop(0, pairs, hand_out, 0)


    lame_first, lame_shear = first_ref[0], shear_ref[0]
    tall_at = lax.broadcasted_iota(jnp.int32, (tall, 2 * slots), 0)
    on_trace = jnp.where(tall_at < 3, lame_first, 0.0)
    on_strain = jnp.where(tall_at < 3, 2.0 * lame_shear, jnp.where(tall_at < 6, lame_shear, 0.0))
    base = jnp.zeros((tall, 2 * slots), jnp.float32)
    for at, (i, j) in enumerate(PAIRS):
        if i == j:
            amount = lame_first + 2.0 * lame_shear if i < 3 else lame_shear
        elif j < 3:
            amount = lame_first
        else:
            continue
        base = jnp.where(tall_at == 6 + at, amount, base)

    def back_copy(other, mine):
        return pltpu.make_async_remote_copy(
            src_ref=back_out.at[other],
            dst_ref=back_in.at[mine],
            send_sem=back_send.at[other],
            recv_sem=back_recv.at[mine],
            device_id=(a, other),
            device_id_type=MESH,
        )

    def solve(at, carry):
        place = lax.rem(chip + at, pairs)
        taken = []
        for k in range(2):
            other = 2 * place + k

            @pl.when(other != b)
            def _():
                route_copy(b, other).wait_recv()

            taken.append(route_in[other])
        points_in = jnp.concatenate(taken, axis=1)
        sweeps = points_in[6:7]
        strain_in = points_in.astype(jnp.bfloat16)
        strain_in = jnp.concatenate([strain_in, strain_in], axis=0)

        def mapped(at):
            return jnp.dot(
                maps[pl.ds(at * size, size)], strain_in, preferred_element_type=jnp.float32
            )

        modes, misfit, modal_load = mapped(0), mapped(1), mapped(2)
        for sweep in range(1, ITMAX):
            if sweep > 1:
                misfit = jnp.dot(
                    stiff[...], modes.astype(jnp.bfloat16), preferred_element_type=jnp.float32
                )
                misfit = misfit - modal_load
            misfit = (misfit + BETA * jnp.tanh(modes)).astype(jnp.bfloat16)
            change = jnp.dot(pre[...], misfit, preferred_element_type=jnp.float32)
            modes = modes - jnp.where(sweeps > sweep, OMEGA, 0.0) * change
        bent = jnp.tanh(modes)
        slope = 1.0 - bent * bent
        trace = points_in[0:1] + points_in[1:2] + points_in[2:3]
        padded = jnp.concatenate(
            [points_in, jnp.zeros((tall - 8, 2 * slots), jnp.float32)], axis=0
        )
        answer = on_trace * trace + on_strain * padded + base
        answer = answer + jnp.dot(
            couple[...], modes.astype(jnp.bfloat16), preferred_element_type=jnp.float32
        )
        answer = answer + jnp.dot(
            products[...], slope.astype(jnp.bfloat16), preferred_element_type=jnp.float32
        )
        for k in range(2):
            other = 2 * place + k
            piece = answer[:, k * slots : (k + 1) * slots]

            @pl.when(other != b)
            def _():
                back_out[other] = piece
                back_copy(other, b).start()

            @pl.when(other == b)
            def _():
                back_in[b] = piece

        return carry

    lax.fori_loop(0, pairs, solve, 0)

    def take_back(at, carry):
        place = lax.rem(chip + pairs - at, pairs)
        taken = []
        for k in range(2):
            other = 2 * place + k

            @pl.when(other != b)
            def _():
                back_copy(b, other).wait_recv()

            taken.append(back_in[other])
        exact = jnp.concatenate(taken, axis=1)
        high = exact.astype(jnp.bfloat16).astype(jnp.float32)
        both = jnp.concatenate([high, exact - high], axis=0).astype(jnp.bfloat16)
        moved = jnp.dot(both, spots[pair_rows(place)], preferred_element_type=jnp.float32)
        values[...] += moved[:tall] + moved[tall:]
        return carry

    lax.fori_loop(0, pairs, take_back, 0)

    def side_copy(at):
        (dx, dy), place, _ = handed[at]
        low = column_at[place] * lanes
        return pltpu.make_async_remote_copy(
            src_ref=values.at[:, pl.ds(low, lanes)],
            dst_ref=beside.at[at],
            send_sem=side_send.at[at],
            recv_sem=side_recv.at[at],
            device_id=(a + dx, b + dy),
            device_id_type=MESH,
        )

    for at, ((dx, dy), _, _) in enumerate(handed):

        @pl.when(inside(dx, dy))
        def _():
            side_copy(at).start()

    def put_column(read, row):
        for v in range(6 + len(PAIRS)):
            elem[v, pl.ds(row, 1)] = read(v)

    for at, (i, j) in enumerate(owned):
        put_column(
            lambda v: values[v : v + 1, at * lanes : (at + 1) * lanes], (i + 1) * wide + j + 1
        )
    for at, ((dx, dy), _, (i, j)) in enumerate(handed):

        @pl.when(inside(dx, dy))
        def _():
            side_copy(at).wait_send()

        @pl.when(inside(-dx, -dy))
        def _():
            pltpu.make_async_remote_copy(
                src_ref=values.at[:, pl.ds(0, lanes)],
                dst_ref=beside.at[at],
                send_sem=side_send.at[at],
                recv_sem=side_recv.at[at],
                device_id=(a - dx, b - dy),
                device_id_type=MESH,
            ).wait_recv()

        put_column(lambda v: beside[at, v : v + 1], i * wide + j)

    def near(step, count):
        return {0: list(range(1, count + 1)), -1: [1], 1: [count]}[step]

    def far(step, count):
        return {0: list(range(1, count + 1)), -1: [0], 1: [count + 1]}[step]

    def places(at, pick):
        dx, dy = AROUND[at]
        return [i * wide + j for i in pick(dx, count_x) for j in pick(dy, count_y)]

    def hop(it, at):
        dx, dy = AROUND[at]
        other = len(AROUND) - 1 - at
        return pltpu.make_async_remote_copy(
            src_ref=send_halo.at[it, at],
            dst_ref=halo.at[it, other],
            send_sem=send_sem.at[it, at],
            recv_sem=recv_sem.at[it, other],
            device_id=(a + dx, b + dy),
            device_id_type=MESH,
        )

    def halo_start(it):
        for at, (dx, dy) in enumerate(AROUND):

            @pl.when(inside(dx, dy))
            def _():
                mine = places(at, near)
                for c in range(3):
                    for k, row in enumerate(mine):
                        send_halo[it, at, pl.ds(c * len(mine) + k, 1)] = basis[it, c, pl.ds(row, 1)]
                hop(it, at).start()

    def halo_finish(it):
        for at, (dx, dy) in enumerate(AROUND):

            @pl.when(inside(dx, dy))
            def _():
                hop(it, at).wait_send()
                pltpu.make_async_remote_copy(
                    src_ref=send_halo.at[it, at],
                    dst_ref=halo.at[it, at],
                    send_sem=send_sem.at[it, at],
                    recv_sem=recv_sem.at[it, at],
                    device_id=(a + dx, b + dy),
                    device_id_type=MESH,
                ).wait_recv()

        for at in range(len(AROUND)):
            theirs = places(at, far)
            for c in range(3):
                for k, row in enumerate(theirs):
                    basis[it, c, pl.ds(row, 1)] = halo[it, at, pl.ds(c * len(theirs) + k, 1)]

    def force_of(stress, c):
        first, second, third = (stress[VOIGT[c][d]] for d in range(3))
        first = first + down(first, 2)
        second = second + down(second, 2)
        third = down(third, 2) - third
        first = first + down(first, 1)
        rest = down(second, 1) - second + third + down(third, 1)
        return 0.25 * (down(first, 0) - first + rest + down(rest, 0))

    def applied(it):
        strain = strain_of(it)
        stress = []
        for i in range(6):
            value = None
            for j in range(6):
                term = elem[6 + PAIR_AT[(min(i, j), max(i, j))]] * strain[j]
                value = term if value is None else value + term
            stress.append(value)
        return [
            jnp.where(own, MASS * basis[it, c] + force_of(stress, c), 0.0) for c in range(3)
        ]

    def product(first, second):
        total = None
        for c in range(3):
            term = first[c] * second[c]
            total = term if total is None else total + term
        total = jnp.sum(jnp.where(own, total, 0.0), axis=0, keepdims=True)
        value = total[:, :128]
        for at in range(128, lanes, 128):
            value = value + total[:, at : at + 128]
        return value

    def stacked(pieces):
        tile_row = lax.broadcasted_iota(jnp.int32, (16, 128), 0)
        value = jnp.zeros((16, 128), jnp.float32)
        for at, piece in enumerate(pieces):
            value = jnp.where(tile_row == at, piece, value)
        return value

    def gather_start(src, dst, count, mine, send, recv, device):
        copies = []
        for step in range(1, count):
            copy = pltpu.make_async_remote_copy(
                src_ref=src,
                dst_ref=dst.at[mine],
                send_sem=send.at[step - 1],
                recv_sem=recv.at[step - 1],
                device_id=device(lax.rem(mine + step, count)),
                device_id_type=MESH,
            )
            copy.start()
            copies.append(copy)
        dst[mine] = src[...]
        return copies

    def gather_finish(copies, dst, count):
        for copy in copies:
            copy.wait()
        total = dst[0]
        for at in range(1, count):
            total = total + dst[at]
        return total

    stress = [elem[i] for i in range(6)]
    zero = jnp.zeros((rows, lanes), jnp.float32)
    for c in range(3):
        padded = jnp.concatenate(
            [jnp.zeros((wide + 1, lanes), jnp.float32)]
            + [
                piece
                for i in range(count_x)
                for piece in (load_ref[c, i], jnp.zeros((2, lanes), jnp.float32))
            ]
            + [jnp.zeros((rows - 1 - wide * (count_x + 1), lanes), jnp.float32)],
            axis=0,
        )
        basis[0, c] = jnp.where(own, padded - force_of(stress, c), zero)
    halo_start(0)
    halo_finish(0)
    grown = applied(0)
    for c in range(3):
        basis[1, c] = grown[c]
    halo_start(1)
    start = [basis[0, c] for c in range(3)]
    part[...] = stacked([product(start, start), product(grown, grown)])
    copies = gather_start(
        part, got_micro, n_micro, b, micro_send, micro_recv, lambda other: (a, other)
    )
    halo_finish(1)
    grown = applied(1)
    for c in range(3):
        basis[2, c] = grown[c]
    halo_start(2)
    middle[...] = gather_finish(copies, got_micro, n_micro)
    copies = gather_start(
        middle, got_macro, n_macro, a, macro_send, macro_recv, lambda other: (other, b)
    )
    halo_finish(2)
    totals = jnp.sum(gather_finish(copies, got_macro, n_macro), axis=1, keepdims=True)
    shift = jnp.sqrt(totals[1:2] / totals[0:1])
    scale = 1.0 / shift
    for c in range(3):
        u0, w1, w2 = basis[0, c], basis[1, c] * scale, basis[2, c] * (scale * scale)
        basis[1, c] = w1 - u0
        basis[2, c] = (w2 - w1) - (w1 - u0)

    def field(it):
        return [basis[it, c] for c in range(3)]

    def step(it):
        grown = applied(it)
        return [grown[c] * scale - jnp.where(own, basis[it, c], 0.0) for c in range(3)]

    moments = []
    for it in range(2, ITERS):
        grown = step(it)
        if it + 1 < ITERS:
            for c in range(3):
                basis[it + 1, c] = grown[c]
            halo_start(it + 1)
            if it == 2:
                for k in range(3):
                    moments.append(product(field(k), field(k)))
                    moments.append(product(field(k), field(k + 1)))
            else:
                moments.append(product(field(it), field(it)))
                moments.append(product(field(it), field(it + 1)))
            halo_finish(it + 1)
    moments.append(product(field(ITERS - 1), field(ITERS - 1)))
    moments.append(product(field(ITERS - 1), grown))
    sums = jnp.sum(stacked(moments), axis=1, keepdims=True)
    diagonal = lax.broadcasted_iota(jnp.int32, (16, 128), 0) == lax.broadcasted_iota(
        jnp.int32, (16, 128), 1
    )
    last_part[...] = jnp.sum(jnp.where(diagonal, sums, 0.0), axis=0, keepdims=True)

    def last_copy(step, other):
        return pltpu.make_async_remote_copy(
            src_ref=last_part,
            dst_ref=last_all.at[me],
            send_sem=last_send.at[step],
            recv_sem=last_recv.at[step],
            device_id=device(other),
            device_id_type=MESH,
        )

    def last_start(step, carry):
        last_copy(step, lax.rem(me + step, total)).start()
        return carry

    def last_wait(step, carry):
        last_copy(step, lax.rem(me + step, total)).wait()
        return carry

    lax.fori_loop(1, total, last_start, 0)
    last_all[me] = last_part[...]
    lax.fori_loop(1, total, last_wait, 0)
    totals = jnp.sum(last_all[...], axis=0)
    held = [totals[:, k : k + 1] for k in range(2 * ITERS)]

    def inner(first, second, extra=0):
        gathered = {}
        for i, x in enumerate(first):
            for j, y in enumerate(second):
                gathered.setdefault(i + j, []).append(x * y)
        value = None
        for degree, terms in gathered.items():
            total = terms[0]
            for term in terms[1:]:
                total = total + term
            total = total * held[degree + extra]
            value = total if value is None else value + total
        return value

    one = jnp.ones((1, 1), jnp.float32)
    left, toward, done = [one], [one], []
    norm = held[0]
    for it in range(ITERS):
        energy = inner(toward, toward) + inner(toward, toward, 1)
        length = norm / energy
        done = [x + length * scale * p for x, p in zip(done + [0.0], toward)]
        raised = [
            (toward[k] if k < len(toward) else 0.0) + (toward[k - 1] if k > 0 else 0.0)
            for k in range(len(toward) + 1)
        ]
        left = [
            (left[k] if k < len(left) else 0.0) - length * raised[k] for k in range(len(raised))
        ]
        if it + 1 < ITERS:
            fresh = inner(left, left)
            ratio = fresh / norm
            toward = [
                left[k] + (ratio * toward[k] if k < len(toward) else 0.0)
                for k in range(len(left))
            ]
            norm = fresh
    for c in range(3):
        fields = [basis[k, c] for k in range(ITERS)] + [grown[c]]
        moved, rest = None, None
        for k in range(ITERS + 1):
            if k < len(done):
                term = done[k] * fields[k]
                moved = term if moved is None else moved + term
            term = left[k] * fields[k]
            rest = term if rest is None else rest + term
        for i in range(count_x):
            low = (i + 1) * wide + 1
            inc_ref[c, i] = moved[low : low + count_y]
            res_ref[c, i] = rest[low : low + count_y]

    def sent(step, carry):
        other = lax.rem(b + step, n_micro)
        route_copy(other, b).wait_send()
        back_copy(other, b).wait_send()
        return carry

    lax.fori_loop(1, n_micro, sent, 0)


def shards(
    displacement,
    load,
    routes,
    counts,
    stiffness,
    precond,
    forcing,
    coupling,
    lame_first,
    lame_shear,
):
    _, count_x, count_y, lanes = displacement.shape
    points = count_x * count_y * lanes
    n_macro, n_micro = lax.axis_size("macro"), lax.axis_size("micro")
    capacity = max(2, 2 * points // n_micro)
    slots = -(-capacity // 128) * 128
    size = stiffness.shape[1]
    tall = -(-(6 + len(PAIRS)) // 8) * 8
    rows = -(-(count_x + 2) * (count_y + 2) // 8) * 8
    side = -(-3 * max(count_x, count_y) // 8) * 8
    total = n_macro * n_micro
    sides = count_x + count_y + 1
    vmem = pl.BlockSpec(memory_space=pltpu.VMEM)
    smem = pl.BlockSpec(memory_space=pltpu.SMEM)
    anywhere = pl.BlockSpec(memory_space=pl.ANY)
    dma = pltpu.SemaphoreType.DMA

    def held(*shape):
        return pltpu.VMEM(shape, jnp.float32)

    def half(*shape):
        return pltpu.VMEM(shape, jnp.bfloat16)

    def body(*refs):
        newton_kernel((count_x, count_y, lanes, n_macro, n_micro), *refs)

    return tuple(
        pl.pallas_call(
            body,
            out_shape=[jax.ShapeDtypeStruct(load.shape, jnp.float32)] * 2,
            in_specs=[vmem] * 4 + [anywhere] * 2 + [vmem] * 2 + [smem] * 2,
            out_specs=[vmem, vmem],
            scratch_shapes=[
                half(size, size),
                half(size, size),
                half(3 * size, 16),
                half(tall, size),
                half(tall, size),
                held(tall, size),
                half(n_micro * slots, points),
                held(3, *displacement.shape),
                held(8, points),
                held(n_micro, 8, slots),
                held(n_micro, 8, slots),
                held(n_micro, tall, slots),
                held(n_micro, tall, slots),
                held(tall, points),
                held(sides, tall, lanes),
                held(6 + len(PAIRS), rows, lanes),
                held(ITERS, 3, rows, lanes),
                held(ITERS, len(AROUND), side, lanes),
                held(ITERS, len(AROUND), side, lanes),
                held(16, 128),
                held(n_micro, 16, 128),
                held(16, 128),
                held(n_macro, 16, 128),
                held(1, 128),
                held(total, 1, 128),
                dma((2,)),
                dma((3,)),
                dma((3,)),
                dma((n_micro,)),
                dma((n_micro,)),
                dma((n_micro,)),
                dma((n_micro,)),
                dma((sides,)),
                dma((sides,)),
                dma((ITERS, len(AROUND))),
                dma((ITERS, len(AROUND))),
                dma((n_micro - 1,)),
                dma((n_micro - 1,)),
                dma((n_macro - 1,)),
                dma((n_macro - 1,)),
                dma((total,)),
                dma((total,)),
            ],
            compiler_params=pltpu.CompilerParams(collective_id=0, has_side_effects=True),
            name="newton_step",
        )(
            displacement,
            load,
            routes.reshape(points // 128, 128),
            counts.reshape(points // 128, 128),
            stiffness[0],
            precond[0],
            forcing[0],
            coupling[0].T,
            lame_first,
            lame_shear,
        )
    )


def solution(mesh):
    in_specs = (
        P(None, "macro", "micro", None),
        P(None, "macro", "micro", None),
        P("macro", "micro", None, None),
        P("macro", "micro", None),
        P("micro", None, None),
        P("micro", None, None),
        P("micro", None, None),
        P("micro", None, None),
        P("micro"),
        P("micro"),
    )
    out_specs = (P(None, "macro", "micro", None), P(None, "macro", "micro", None))
    return jax.shard_map(shards, mesh=mesh, in_specs=in_specs, out_specs=out_specs, check_vma=False)
```

```python
import jax
import jax.numpy as jnp
from jax import lax
from jax.experimental import pallas as pl
from jax.experimental.pallas import tpu as pltpu
from jax.sharding import PartitionSpec as P

ITMAX = 4
ITERS = 5


BETA = 0.1
OMEGA = 0.8
MASS = 0.1
VOIGT = ((0, 5, 4), (5, 1, 3), (4, 3, 2))
PAIRS = tuple((first, second) for first in range(6) for second in range(first, 6))
PAIR_AT = {pair: at for at, pair in enumerate(PAIRS)}
AROUND = tuple((dx, dy) for dx in (-1, 0, 1) for dy in (-1, 0, 1) if (dx, dy) != (0, 0))
MESH = pl.DeviceIdType.MESH


def newton_kernel(
    sizes,
    disp_in,
    load_in,
    routes_in,
    counts_in,
    stiff_in,
    pre_in,
    force_in,
    couple_in,
    first_ref,
    shear_ref,
    inc_ref,
    res_ref,
    disp_ref,
    load_ref,
    routes_ref,
    counts_ref,
    stiff,
    pre,
    force_ref,
    couple_ref,
    maps,
    couple,
    products,
    wide_products,
    spots,
    near_disp,
    bundle,
    route_out,
    route_in,
    back_out,
    back_in,
    values,
    beside,
    elem,
    basis,
    send_halo,
    halo,
    part,
    got_micro,
    middle,
    got_macro,
    last_part,
    last_all,
    input_sem,
    disp_send,
    disp_recv,
    route_send,
    route_recv,
    back_send,
    back_recv,
    side_send,
    side_recv,
    send_sem,
    recv_sem,
    micro_send,
    micro_recv,
    macro_send,
    macro_recv,
    last_send,
    last_recv,
):
    count_x, count_y, lanes, n_macro, n_micro = sizes
    wide = count_y + 2
    rows = basis.shape[2]
    points = spots.shape[1]
    slots = spots.shape[0] // n_micro
    pairs = n_micro // 2
    groups = points // 128
    size = stiff.shape[0]
    tall = couple.shape[0]
    total = n_macro * n_micro
    a, b = lax.axis_index("macro"), lax.axis_index("micro")
    me = a * n_micro + b

    def device(other):
        return (other // n_micro, lax.rem(other, n_micro))

    def inside(dx, dy):
        test = None
        for place, step, count in ((a, dx, n_macro), (b, dy, n_micro)):
            if step != 0:
                good = (place > 0) if step < 0 else (place < count - 1)
                test = good if test is None else jnp.logical_and(test, good)
        return test

    barrier = pltpu.get_barrier_semaphore()

    def every(count, act):
        if count <= 32:
            for step in range(1, count):
                act(step)
        else:
            lax.fori_loop(1, count, lambda step, carry: (act(step), carry)[1], 0)

    def greet(row, column):
        pl.semaphore_signal(barrier, inc=1, device_id=(row, column), device_id_type=MESH)

    for step in range(1, n_macro):
        for aside in range(3):
            greet(lax.rem(a + step, n_macro), lax.rem(b + n_micro - 1 + aside, n_micro))
    every(n_micro, lambda step: greet(a, lax.rem(b + step, n_micro)))
    greeted = 3 * (n_macro - 1) + n_micro - 1
    inputs = {}
    for at, (name, source, target) in enumerate(
        (
            ("routes", routes_in, routes_ref),
            ("force", force_in, force_ref),
            ("couple", couple_in, couple_ref),
            ("counts", counts_in, counts_ref),
            ("disp", disp_in, disp_ref),
            ("load", load_in, load_ref),
            ("pre", pre_in, pre),
            ("stiff", stiff_in, stiff),
        )
    ):
        inputs[name] = pltpu.make_async_copy(source, target, input_sem.at[at])
        inputs[name].start()

    for name in ("routes", "force", "couple", "counts", "disp"):
        inputs[name].wait()
    force = force_ref[...].astype(jnp.float32)
    force = jnp.concatenate([force, jnp.zeros((2, size), jnp.float32)], axis=0)
    load_map = force.T
    wide_products[...] = jnp.zeros((tall, size), jnp.float32)
    coupling = couple_ref[...].astype(jnp.float32)
    wide_products[pl.ds(0, 6)] = coupling
    couple[...] = wide_products[...].astype(jnp.bfloat16)
    wide_products[pl.ds(0, 6)] = jnp.zeros((6, size), jnp.float32)
    for at, (first, second) in enumerate(PAIRS):
        wide_products[pl.ds(6 + at, 1)] = coupling[first : first + 1] * coupling[second : second + 1]
    products[...] = wide_products[...].astype(jnp.bfloat16)

    route = routes_ref[...]
    row_of = lax.broadcasted_iota(jnp.int32, (128, 128), 0)
    column_of = lax.broadcasted_iota(jnp.int32, (128, 128), 1)
    until = jnp.where(row_of <= column_of, 1.0, 0.0).astype(jnp.bfloat16)
    named = [jnp.where(route == owner, 1.0, 0.0) for owner in range(n_micro)]
    named = jnp.concatenate(named, axis=0).astype(jnp.bfloat16)
    inner_rank = jnp.dot(named, until, preferred_element_type=jnp.float32)
    whole = jnp.dot(
        named, jnp.ones((128, 128), jnp.bfloat16), preferred_element_type=jnp.float32
    ).astype(jnp.bfloat16)
    span = n_micro * groups
    row_of = lax.broadcasted_iota(jnp.int32, (span, span), 0)
    column_of = lax.broadcasted_iota(jnp.int32, (span, span), 1)
    ahead = jnp.logical_and(column_of < row_of, column_of // groups == row_of // groups)
    before = jnp.dot(
        jnp.where(ahead, 1.0, 0.0).astype(jnp.bfloat16), whole, preferred_element_type=jnp.float32
    )
    ranks = inner_rank + before - 1.0
    rank = jnp.zeros((groups, 128), jnp.float32)
    for owner in range(n_micro):
        rank = jnp.where(route == owner, ranks[owner * groups : (owner + 1) * groups], rank)
    slot_at = lax.broadcasted_iota(jnp.int32, (slots, 128), 0).astype(jnp.float32)

    def spot(owner, carry):
        local = jnp.where(route == owner, rank, -1.0)
        for g in range(groups):
            hit = jnp.where(local[g : g + 1] == slot_at, 1.0, 0.0)
            low = pl.multiple_of(owner * slots, slots)
            spots[pl.ds(low, slots), g * 128 : (g + 1) * 128] = hit.astype(jnp.bfloat16)
        return carry

    lax.fori_loop(0, n_micro, spot, 0)

    for it in range(basis.shape[0]):
        for c in range(3):
            basis[it, c] = jnp.zeros((rows, lanes), jnp.float32)
    elem[...] = jnp.zeros(elem.shape, jnp.float32)
    values[...] = jnp.zeros(values.shape, jnp.float32)
    bundle[...] = jnp.zeros(bundle.shape, jnp.float32)
    for g in range(groups):
        bundle[6:7, g * 128 : (g + 1) * 128] = counts_ref[g : g + 1].astype(jnp.float32)

    for at, (dx, dy) in enumerate(AROUND):

        @pl.when(jnp.logical_not(inside(dx, dy)))
        def _():
            for it in range(ITERS):
                halo[it, at] = jnp.zeros(halo.shape[2:], jnp.float32)

    after = ((1, 0), (0, 1), (1, 1))
    for at, (dx, dy) in enumerate(after):

        @pl.when(jnp.logical_not(inside(dx, dy)))
        def _():
            near_disp[at] = jnp.zeros(near_disp.shape[1:], jnp.float32)

    owned = [(i, j) for i in range(count_x) for j in range(count_y)]
    column_at = {place: at for at, place in enumerate(owned)}
    handed = [((1, 0), (count_x - 1, j), (0, j + 1)) for j in range(count_y)]
    handed += [((0, 1), (i, count_y - 1), (i + 1, 0)) for i in range(count_x)]
    handed += [((1, 1), (count_x - 1, count_y - 1), (0, 0))]
    for at, ((dx, dy), _, _) in enumerate(handed):

        @pl.when(jnp.logical_not(inside(-dx, -dy)))
        def _():
            beside[at] = jnp.zeros(beside.shape[1:], jnp.float32)

    pl.semaphore_wait(barrier, greeted)

    def show(at):
        dx, dy = after[at]
        return pltpu.make_async_remote_copy(
            src_ref=disp_ref,
            dst_ref=near_disp.at[at],
            send_sem=disp_send.at[at],
            recv_sem=disp_recv.at[at],
            device_id=(a - dx, b - dy),
            device_id_type=MESH,
        )

    for at, (dx, dy) in enumerate(after):

        @pl.when(inside(-dx, -dy))
        def _():
            show(at).start()

    for name in ("pre", "stiff", "load"):
        inputs[name].wait()

    def split(exact):
        high = exact.astype(jnp.bfloat16)
        return jnp.concatenate([high, (exact - high.astype(jnp.float32)).astype(jnp.bfloat16)], axis=1)

    def through(matrix, exact):
        moved = jnp.dot(matrix[...], split(exact), preferred_element_type=jnp.float32)
        return moved[:, :8] + moved[:, 8:]

    first_map = OMEGA * through(pre, load_map)
    misfit_map = through(stiff, first_map) - load_map
    for at, exact in enumerate((first_map, misfit_map, load_map)):
        maps[pl.ds(at * size, size)] = split(exact)
    for c in range(3):
        for i, j in owned:
            basis[0, c, pl.ds((i + 1) * wide + j + 1, 1)] = disp_ref[c, i, j : j + 1]
    for at, (dx, dy) in enumerate(after):

        @pl.when(inside(-dx, -dy))
        def _():
            show(at).wait_send()

        @pl.when(inside(dx, dy))
        def _():
            pltpu.make_async_remote_copy(
                src_ref=disp_ref,
                dst_ref=near_disp.at[at],
                send_sem=disp_send.at[at],
                recv_sem=disp_recv.at[at],
                device_id=(a + dx, b + dy),
                device_id_type=MESH,
            ).wait_recv()

    for c in range(3):
        for j in range(count_y):
            basis[0, c, pl.ds((count_x + 1) * wide + j + 1, 1)] = near_disp[0, c, 0, j : j + 1]
        for i in range(count_x):
            basis[0, c, pl.ds((i + 1) * wide + count_y + 1, 1)] = near_disp[1, c, i, 0:1]
        basis[0, c, pl.ds((count_x + 1) * wide + count_y + 1, 1)] = near_disp[2, c, 0, 0:1]

    row_at = lax.broadcasted_iota(jnp.int32, (rows, lanes), 0)
    lane_at = lax.broadcasted_iota(jnp.int32, (rows, lanes), 1)
    own = row_at < 0
    for i in range(1, count_x + 1):
        low = i * wide + 1
        own = jnp.logical_or(own, jnp.logical_and(row_at >= low, row_at < low + count_y))

    def up(value, axis):
        if axis == 2:
            moved = pltpu.roll(value, lanes - 1, 1)
            return jnp.where(lane_at == lanes - 1, 0.0, moved)
        return pltpu.roll(value, rows - (wide if axis == 0 else 1), 0)

    def down(value, axis):
        if axis == 2:
            return jnp.where(lane_at == 0, 0.0, pltpu.roll(value, 1, 1))
        return pltpu.roll(value, wide if axis == 0 else 1, 0)

    def strain_of(it):
        grads = []
        for c in range(3):
            value = basis[it, c]
            moved = up(value, 2)
            total, gap = value + moved, moved - value
            total_up, gap_up = up(total, 1), up(gap, 1)
            flat, slope_y, slope_z = total + total_up, total_up - total, gap + gap_up
            grads.append(
                (
                    0.25 * (up(flat, 0) - flat),
                    0.25 * (up(slope_y, 0) + slope_y),
                    0.25 * (up(slope_z, 0) + slope_z),
                )
            )
        return [
            grads[0][0],
            grads[1][1],
            grads[2][2],
            grads[1][2] + grads[2][1],
            grads[0][2] + grads[2][0],
            grads[0][1] + grads[1][0],
        ]

    strain = strain_of(0)
    for at, (i, j) in enumerate(owned):
        low = (i + 1) * wide + j + 1
        for k in range(6):
            bundle[k : k + 1, at * lanes : (at + 1) * lanes] = strain[k][low : low + 1]
    exact = bundle[...]
    high = exact.astype(jnp.bfloat16).astype(jnp.float32)
    both = jnp.concatenate([high, exact - high], axis=0).astype(jnp.bfloat16)

    def route_copy(other, mine):
        return pltpu.make_async_remote_copy(
            src_ref=route_out.at[other],
            dst_ref=route_in.at[mine],
            send_sem=route_send.at[other],
            recv_sem=route_recv.at[mine],
            device_id=(a, other),
            device_id_type=MESH,
        )

    chip, core = b // 2, lax.rem(b, 2)

    def pair_rows(place):
        return pl.ds(pl.multiple_of(place * (2 * slots), 2 * slots), 2 * slots)

    def hand_out(at, carry):
        place = lax.rem(chip + pairs - at, pairs)
        moved = lax.dot_general(
            both,
            spots[pair_rows(place)],
            (((1,), (1,)), ((), ())),
            preferred_element_type=jnp.float32,
        )
        moved = moved[:8] + moved[8:]
        for k in range(2):
            other = 2 * place + k
            piece = moved[:, k * slots : (k + 1) * slots]

            @pl.when(other != b)
            def _():
                route_out[other] = piece
                route_copy(other, b).start()

            @pl.when(other == b)
            def _():
                route_in[b] = piece

        return carry

    lax.fori_loop(0, pairs, hand_out, 0)


    lame_first, lame_shear = first_ref[0], shear_ref[0]
    tall_at = lax.broadcasted_iota(jnp.int32, (tall, 2 * slots), 0)
    on_trace = jnp.where(tall_at < 3, lame_first, 0.0)
    on_strain = jnp.where(tall_at < 3, 2.0 * lame_shear, jnp.where(tall_at < 6, lame_shear, 0.0))
    base = jnp.zeros((tall, 2 * slots), jnp.float32)
    for at, (i, j) in enumerate(PAIRS):
        if i == j:
            amount = lame_first + 2.0 * lame_shear if i < 3 else lame_shear
        elif j < 3:
            amount = lame_first
        else:
            continue
        base = jnp.where(tall_at == 6 + at, amount, base)

    def back_copy(other, mine):
        return pltpu.make_async_remote_copy(
            src_ref=back_out.at[other],
            dst_ref=back_in.at[mine],
            send_sem=back_send.at[other],
            recv_sem=back_recv.at[mine],
            device_id=(a, other),
            device_id_type=MESH,
        )

    def solve(at, carry):
        place = lax.rem(chip + at, pairs)
        taken = []
        for k in range(2):
            other = 2 * place + k

            @pl.when(other != b)
            def _():
                route_copy(b, other).wait_recv()

            taken.append(route_in[other])
        points_in = jnp.concatenate(taken, axis=1)
        sweeps = points_in[6:7]
        strain_in = points_in.astype(jnp.bfloat16)
        strain_in = jnp.concatenate([strain_in, strain_in], axis=0)

        def mapped(at):
            return jnp.dot(
                maps[pl.ds(at * size, size)], strain_in, preferred_element_type=jnp.float32
            )

        modes, misfit, modal_load = mapped(0), mapped(1), mapped(2)
        for sweep in range(1, ITMAX):
            if sweep > 1:
                misfit = jnp.dot(
                    stiff[...], modes.astype(jnp.bfloat16), preferred_element_type=jnp.float32
                )
                misfit = misfit - modal_load
            misfit = (misfit + BETA * jnp.tanh(modes)).astype(jnp.bfloat16)
            change = jnp.dot(pre[...], misfit, preferred_element_type=jnp.float32)
            modes = modes - jnp.where(sweeps > sweep, OMEGA, 0.0) * change
        bent = jnp.tanh(modes)
        slope = 1.0 - bent * bent
        trace = points_in[0:1] + points_in[1:2] + points_in[2:3]
        padded = jnp.concatenate(
            [points_in, jnp.zeros((tall - 8, 2 * slots), jnp.float32)], axis=0
        )
        answer = on_trace * trace + on_strain * padded + base
        answer = answer + jnp.dot(
            couple[...], modes.astype(jnp.bfloat16), preferred_element_type=jnp.float32
        )
        answer = answer + jnp.dot(
            products[...], slope.astype(jnp.bfloat16), preferred_element_type=jnp.float32
        )
        for k in range(2):
            other = 2 * place + k
            piece = answer[:, k * slots : (k + 1) * slots]

            @pl.when(other != b)
            def _():
                back_out[other] = piece
                back_copy(other, b).start()

            @pl.when(other == b)
            def _():
                back_in[b] = piece

        return carry

    lax.fori_loop(0, pairs, solve, 0)

    def take_back(at, carry):
        place = lax.rem(chip + pairs - at, pairs)
        taken = []
        for k in range(2):
            other = 2 * place + k

            @pl.when(other != b)
            def _():
                back_copy(b, other).wait_recv()

            taken.append(back_in[other])
        exact = jnp.concatenate(taken, axis=1)
        high = exact.astype(jnp.bfloat16).astype(jnp.float32)
        both = jnp.concatenate([high, exact - high], axis=0).astype(jnp.bfloat16)
        moved = jnp.dot(both, spots[pair_rows(place)], preferred_element_type=jnp.float32)
        values[...] += moved[:tall] + moved[tall:]
        return carry

    lax.fori_loop(0, pairs, take_back, 0)

    def side_copy(at):
        (dx, dy), place, _ = handed[at]
        low = column_at[place] * lanes
        return pltpu.make_async_remote_copy(
            src_ref=values.at[:, pl.ds(low, lanes)],
            dst_ref=beside.at[at],
            send_sem=side_send.at[at],
            recv_sem=side_recv.at[at],
            device_id=(a + dx, b + dy),
            device_id_type=MESH,
        )

    for at, ((dx, dy), _, _) in enumerate(handed):

        @pl.when(inside(dx, dy))
        def _():
            side_copy(at).start()

    def put_column(read, row):
        for v in range(6 + len(PAIRS)):
            elem[v, pl.ds(row, 1)] = read(v)

    for at, (i, j) in enumerate(owned):
        put_column(
            lambda v: values[v : v + 1, at * lanes : (at + 1) * lanes], (i + 1) * wide + j + 1
        )
    for at, ((dx, dy), _, (i, j)) in enumerate(handed):

        @pl.when(inside(dx, dy))
        def _():
            side_copy(at).wait_send()

        @pl.when(inside(-dx, -dy))
        def _():
            pltpu.make_async_remote_copy(
                src_ref=values.at[:, pl.ds(0, lanes)],
                dst_ref=beside.at[at],
                send_sem=side_send.at[at],
                recv_sem=side_recv.at[at],
                device_id=(a - dx, b - dy),
                device_id_type=MESH,
            ).wait_recv()

        put_column(lambda v: beside[at, v : v + 1], i * wide + j)

    def near(step, count):
        return {0: list(range(1, count + 1)), -1: [1], 1: [count]}[step]

    def far(step, count):
        return {0: list(range(1, count + 1)), -1: [0], 1: [count + 1]}[step]

    def places(at, pick):
        dx, dy = AROUND[at]
        return [i * wide + j for i in pick(dx, count_x) for j in pick(dy, count_y)]

    def hop(it, at):
        dx, dy = AROUND[at]
        other = len(AROUND) - 1 - at
        return pltpu.make_async_remote_copy(
            src_ref=send_halo.at[it, at],
            dst_ref=halo.at[it, other],
            send_sem=send_sem.at[it, at],
            recv_sem=recv_sem.at[it, other],
            device_id=(a + dx, b + dy),
            device_id_type=MESH,
        )

    def halo_start(it):
        for at, (dx, dy) in enumerate(AROUND):

            @pl.when(inside(dx, dy))
            def _():
                mine = places(at, near)
                for c in range(3):
                    for k, row in enumerate(mine):
                        send_halo[it, at, pl.ds(c * len(mine) + k, 1)] = basis[it, c, pl.ds(row, 1)]
                hop(it, at).start()

    def halo_finish(it):
        for at, (dx, dy) in enumerate(AROUND):

            @pl.when(inside(dx, dy))
            def _():
                hop(it, at).wait_send()
                pltpu.make_async_remote_copy(
                    src_ref=send_halo.at[it, at],
                    dst_ref=halo.at[it, at],
                    send_sem=send_sem.at[it, at],
                    recv_sem=recv_sem.at[it, at],
                    device_id=(a + dx, b + dy),
                    device_id_type=MESH,
                ).wait_recv()

        for at in range(len(AROUND)):
            theirs = places(at, far)
            for c in range(3):
                for k, row in enumerate(theirs):
                    basis[it, c, pl.ds(row, 1)] = halo[it, at, pl.ds(c * len(theirs) + k, 1)]

    def force_of(stress, c):
        first, second, third = (stress[VOIGT[c][d]] for d in range(3))
        first = first + down(first, 2)
        second = second + down(second, 2)
        third = down(third, 2) - third
        first = first + down(first, 1)
        rest = down(second, 1) - second + third + down(third, 1)
        return 0.25 * (down(first, 0) - first + rest + down(rest, 0))

    def applied(it):
        strain = strain_of(it)
        stress = []
        for i in range(6):
            value = None
            for j in range(6):
                term = elem[6 + PAIR_AT[(min(i, j), max(i, j))]] * strain[j]
                value = term if value is None else value + term
            stress.append(value)
        return [
            jnp.where(own, MASS * basis[it, c] + force_of(stress, c), 0.0) for c in range(3)
        ]

    def product(first, second):
        total = None
        for c in range(3):
            term = first[c] * second[c]
            total = term if total is None else total + term
        total = jnp.sum(jnp.where(own, total, 0.0), axis=0, keepdims=True)
        value = total[:, :128]
        for at in range(128, lanes, 128):
            value = value + total[:, at : at + 128]
        return value

    def stacked(pieces):
        tile_row = lax.broadcasted_iota(jnp.int32, (16, 128), 0)
        value = jnp.zeros((16, 128), jnp.float32)
        for at, piece in enumerate(pieces):
            value = jnp.where(tile_row == at, piece, value)
        return value

    def gather_start(src, dst, count, mine, send, recv, device):
        copies = []
        for step in range(1, count):
            copy = pltpu.make_async_remote_copy(
                src_ref=src,
                dst_ref=dst.at[mine],
                send_sem=send.at[step - 1],
                recv_sem=recv.at[step - 1],
                device_id=device(lax.rem(mine + step, count)),
                device_id_type=MESH,
            )
            copy.start()
            copies.append(copy)
        dst[mine] = src[...]
        return copies

    def gather_finish(copies, dst, count):
        for copy in copies:
            copy.wait()
        total = dst[0]
        for at in range(1, count):
            total = total + dst[at]
        return total

    stress = [elem[i] for i in range(6)]
    zero = jnp.zeros((rows, lanes), jnp.float32)
    for c in range(3):
        padded = jnp.concatenate(
            [jnp.zeros((wide + 1, lanes), jnp.float32)]
            + [
                piece
                for i in range(count_x)
                for piece in (load_ref[c, i], jnp.zeros((2, lanes), jnp.float32))
            ]
            + [jnp.zeros((rows - 1 - wide * (count_x + 1), lanes), jnp.float32)],
            axis=0,
        )
        basis[0, c] = jnp.where(own, padded - force_of(stress, c), zero)
    halo_start(0)
    halo_finish(0)
    grown = applied(0)
    for c in range(3):
        basis[1, c] = grown[c]
    halo_start(1)
    start = [basis[0, c] for c in range(3)]
    part[...] = stacked([product(start, start), product(grown, grown)])
    copies = gather_start(
        part, got_micro, n_micro, b, micro_send, micro_recv, lambda other: (a, other)
    )
    halo_finish(1)
    grown = applied(1)
    for c in range(3):
        basis[2, c] = grown[c]
    halo_start(2)
    middle[...] = gather_finish(copies, got_micro, n_micro)
    copies = gather_start(
        middle, got_macro, n_macro, a, macro_send, macro_recv, lambda other: (other, b)
    )
    halo_finish(2)
    totals = jnp.sum(gather_finish(copies, got_macro, n_macro), axis=1, keepdims=True)
    shift = jnp.sqrt(totals[1:2] / totals[0:1])
    scale = 1.0 / shift
    for c in range(3):
        u0, w1, w2 = basis[0, c], basis[1, c] * scale, basis[2, c] * (scale * scale)
        basis[1, c] = w1 - u0
        basis[2, c] = (w2 - w1) - (w1 - u0)

    def field(it):
        return [basis[it, c] for c in range(3)]

    def step(it):
        grown = applied(it)
        return [grown[c] * scale - jnp.where(own, basis[it, c], 0.0) for c in range(3)]

    moments = []
    for it in range(2, ITERS):
        grown = step(it)
        if it + 1 < ITERS:
            for c in range(3):
                basis[it + 1, c] = grown[c]
            halo_start(it + 1)
            if it == 2:
                for k in range(3):
                    moments.append(product(field(k), field(k)))
                    moments.append(product(field(k), field(k + 1)))
            else:
                moments.append(product(field(it), field(it)))
                moments.append(product(field(it), field(it + 1)))
            halo_finish(it + 1)
    moments.append(product(field(ITERS - 1), field(ITERS - 1)))
    moments.append(product(field(ITERS - 1), grown))
    sums = jnp.sum(stacked(moments), axis=1, keepdims=True)
    diagonal = lax.broadcasted_iota(jnp.int32, (16, 128), 0) == lax.broadcasted_iota(
        jnp.int32, (16, 128), 1
    )
    last_part[...] = jnp.sum(jnp.where(diagonal, sums, 0.0), axis=0, keepdims=True)

    def last_copy(step, other):
        return pltpu.make_async_remote_copy(
            src_ref=last_part,
            dst_ref=last_all.at[me],
            send_sem=last_send.at[step],
            recv_sem=last_recv.at[step],
            device_id=device(other),
            device_id_type=MESH,
        )

    every(total, lambda step: last_copy(step, lax.rem(me + step, total)).start())
    last_all[me] = last_part[...]
    every(total, lambda step: last_copy(step, lax.rem(me + step, total)).wait())
    totals = jnp.sum(last_all[...], axis=0)
    held = [totals[:, k : k + 1] for k in range(2 * ITERS)]

    def inner(first, second, extra=0):
        gathered = {}
        for i, x in enumerate(first):
            for j, y in enumerate(second):
                gathered.setdefault(i + j, []).append(x * y)
        value = None
        for degree, terms in gathered.items():
            total = terms[0]
            for term in terms[1:]:
                total = total + term
            total = total * held[degree + extra]
            value = total if value is None else value + total
        return value

    one = jnp.ones((1, 1), jnp.float32)
    left, toward, done = [one], [one], []
    norm = held[0]
    for it in range(ITERS):
        energy = inner(toward, toward) + inner(toward, toward, 1)
        length = norm / energy
        done = [x + length * scale * p for x, p in zip(done + [0.0], toward)]
        raised = [
            (toward[k] if k < len(toward) else 0.0) + (toward[k - 1] if k > 0 else 0.0)
            for k in range(len(toward) + 1)
        ]
        left = [
            (left[k] if k < len(left) else 0.0) - length * raised[k] for k in range(len(raised))
        ]
        if it + 1 < ITERS:
            fresh = inner(left, left)
            ratio = fresh / norm
            toward = [
                left[k] + (ratio * toward[k] if k < len(toward) else 0.0)
                for k in range(len(left))
            ]
            norm = fresh
    for c in range(3):
        fields = [basis[k, c] for k in range(ITERS)] + [grown[c]]
        moved, rest = None, None
        for k in range(ITERS + 1):
            if k < len(done):
                term = done[k] * fields[k]
                moved = term if moved is None else moved + term
            term = left[k] * fields[k]
            rest = term if rest is None else rest + term
        for i in range(count_x):
            low = (i + 1) * wide + 1
            inc_ref[c, i] = moved[low : low + count_y]
            res_ref[c, i] = rest[low : low + count_y]

    def sent(step, carry):
        other = lax.rem(b + step, n_micro)
        route_copy(other, b).wait_send()
        back_copy(other, b).wait_send()
        return carry

    lax.fori_loop(1, n_micro, sent, 0)


def shards(
    displacement,
    load,
    routes,
    counts,
    stiffness,
    precond,
    forcing,
    coupling,
    lame_first,
    lame_shear,
):
    _, count_x, count_y, lanes = displacement.shape
    points = count_x * count_y * lanes
    n_macro, n_micro = lax.axis_size("macro"), lax.axis_size("micro")
    capacity = max(2, 2 * points // n_micro)
    slots = -(-capacity // 128) * 128
    size = stiffness.shape[1]
    tall = -(-(6 + len(PAIRS)) // 8) * 8
    rows = -(-(count_x + 2) * (count_y + 2) // 8) * 8
    side = -(-3 * max(count_x, count_y) // 8) * 8
    total = n_macro * n_micro
    sides = count_x + count_y + 1
    vmem = pl.BlockSpec(memory_space=pltpu.VMEM)
    smem = pl.BlockSpec(memory_space=pltpu.SMEM)
    anywhere = pl.BlockSpec(memory_space=pl.ANY)
    dma = pltpu.SemaphoreType.DMA

    def held(*shape):
        return pltpu.VMEM(shape, jnp.float32)

    def half(*shape):
        return pltpu.VMEM(shape, jnp.bfloat16)

    def body(*refs):
        newton_kernel((count_x, count_y, lanes, n_macro, n_micro), *refs)

    return tuple(
        pl.pallas_call(
            body,
            out_shape=[jax.ShapeDtypeStruct(load.shape, jnp.float32)] * 2,
            in_specs=[anywhere] * 8 + [smem] * 2,
            out_specs=[vmem, vmem],
            scratch_shapes=[
                held(*displacement.shape),
                held(*load.shape),
                pltpu.VMEM((points // 128, 128), jnp.int32),
                pltpu.VMEM((points // 128, 128), jnp.int32),
                half(size, size),
                half(size, size),
                half(6, size),
                half(6, size),
                half(3 * size, 16),
                half(tall, size),
                half(tall, size),
                held(tall, size),
                half(n_micro * slots, points),
                held(3, *displacement.shape),
                held(8, points),
                held(n_micro, 8, slots),
                held(n_micro, 8, slots),
                held(n_micro, tall, slots),
                held(n_micro, tall, slots),
                held(tall, points),
                held(sides, tall, lanes),
                held(6 + len(PAIRS), rows, lanes),
                held(ITERS, 3, rows, lanes),
                held(ITERS, len(AROUND), side, lanes),
                held(ITERS, len(AROUND), side, lanes),
                held(16, 128),
                held(n_micro, 16, 128),
                held(16, 128),
                held(n_macro, 16, 128),
                held(1, 128),
                held(total, 1, 128),
                dma((8,)),
                dma((3,)),
                dma((3,)),
                dma((n_micro,)),
                dma((n_micro,)),
                dma((n_micro,)),
                dma((n_micro,)),
                dma((sides,)),
                dma((sides,)),
                dma((ITERS, len(AROUND))),
                dma((ITERS, len(AROUND))),
                dma((n_micro - 1,)),
                dma((n_micro - 1,)),
                dma((n_macro - 1,)),
                dma((n_macro - 1,)),
                dma((total,)),
                dma((total,)),
            ],
            compiler_params=pltpu.CompilerParams(collective_id=0, has_side_effects=True),
            name="newton_step",
        )(
            displacement,
            load,
            routes.reshape(points // 128, 128),
            counts.reshape(points // 128, 128),
            stiffness[0],
            precond[0],
            forcing[0],
            coupling[0].T,
            lame_first,
            lame_shear,
        )
    )


def solution(mesh):
    in_specs = (
        P(None, "macro", "micro", None),
        P(None, "macro", "micro", None),
        P("macro", "micro", None, None),
        P("macro", "micro", None),
        P("micro", None, None),
        P("micro", None, None),
        P("micro", None, None),
        P("micro", None, None),
        P("micro"),
        P("micro"),
    )
    out_specs = (P(None, "macro", "micro", None), P(None, "macro", "micro", None))
    return jax.shard_map(shards, mesh=mesh, in_specs=in_specs, out_specs=out_specs, check_vma=False)
```

```python
import functools
import itertools

import jax
import jax.numpy as jnp
from jax import lax
from jax.experimental import pallas as pl
from jax.experimental.pallas import tpu as pltpu
from jax.sharding import PartitionSpec as P

ITMAX = 4
ITERS = 5


BETA = 0.1
OMEGA = 0.8
MASS = 0.1
VOIGT = ((0, 5, 4), (5, 1, 3), (4, 3, 2))
PAIRS = tuple((first, second) for first in range(6) for second in range(first, 6))
PAIR_AT = {pair: at for at, pair in enumerate(PAIRS)}
AROUND = tuple((dx, dy) for dx in (-1, 0, 1) for dy in (-1, 0, 1) if (dx, dy) != (0, 0))
MESH = pl.DeviceIdType.MESH


def newton_kernel(
    sizes,
    disp_in,
    load_in,
    routes_in,
    counts_in,
    stiff_in,
    pre_in,
    force_in,
    couple_in,
    first_ref,
    shear_ref,
    inc_ref,
    res_ref,
    disp_ref,
    load_ref,
    routes_ref,
    counts_ref,
    stiff,
    pre,
    force_ref,
    couple_ref,
    maps,
    couple,
    products,
    wide_products,
    spots,
    load_here,
    values_here,
    packed,
    home,
    near_disp,
    bundle,
    route_out,
    route_in,
    back_out,
    back_in,
    values,
    beside,
    elem,
    basis,
    send_halo,
    halo,
    part,
    got_micro,
    middle,
    got_macro,
    last_part,
    last_all,
    input_sem,
    disp_send,
    disp_recv,
    route_send,
    route_recv,
    back_send,
    back_recv,
    side_send,
    side_recv,
    send_sem,
    recv_sem,
    micro_send,
    micro_recv,
    macro_send,
    macro_recv,
    last_send,
    last_recv,
    seat_send,
    seat_recv,
    home_send,
    home_recv,
):
    count_x, count_y, lanes, n_macro, n_micro, line = sizes
    wide = count_y + 2
    rows = basis.shape[2]
    points = spots.shape[1]
    slots = spots.shape[0] // n_micro
    pairs = n_micro // 2
    groups = points // 128
    size = stiff.shape[0]
    tall = couple.shape[0]
    total = n_macro * n_micro
    a, b = lax.axis_index("macro"), lax.axis_index("micro")
    me = a * n_micro + b

    def pick(table, index):
        value = table[0]
        for at, entry in enumerate(table[1:], 1):
            value = jnp.where(index == at, entry, value)
        return value

    level = pick([line.index(at) for at in range(n_macro)], a)
    seat = pick(line, a)
    moved_rows = list(line) != list(range(n_macro))

    def device(other):
        return (other // n_micro, lax.rem(other, n_micro))

    def inside(dx, dy, start=None):
        test = None
        for place, step, count in ((a if start is None else start, dx, n_macro), (b, dy, n_micro)):
            if step != 0:
                good = (place > 0) if step < 0 else (place < count - 1)
                test = good if test is None else jnp.logical_and(test, good)
        return test

    barrier = pltpu.get_barrier_semaphore()

    def every(count, act):
        if count <= 32:
            for step in range(1, count):
                act(step)
        else:
            lax.fori_loop(1, count, lambda step, carry: (act(step), carry)[1], 0)

    def greet(row, column):
        pl.semaphore_signal(barrier, inc=1, device_id=(row, column), device_id_type=MESH)

    for step in range(1, n_macro):
        for aside in range(3):
            greet(lax.rem(a + step, n_macro), lax.rem(b + n_micro - 1 + aside, n_micro))
    every(n_micro, lambda step: greet(a, lax.rem(b + step, n_micro)))
    greeted = 3 * (n_macro - 1) + n_micro - 1
    inputs = {}
    for at, (name, source, target) in enumerate(
        (
            ("routes", routes_in, routes_ref),
            ("force", force_in, force_ref),
            ("couple", couple_in, couple_ref),
            ("counts", counts_in, counts_ref),
            ("disp", disp_in, disp_ref),
            ("load", load_in, load_ref),
            ("pre", pre_in, pre),
            ("stiff", stiff_in, stiff),
        )
    ):
        inputs[name] = pltpu.make_async_copy(source, target, input_sem.at[at])
        inputs[name].start()

    for name in ("routes", "force", "couple", "counts", "disp"):
        inputs[name].wait()
    force = force_ref[...].astype(jnp.float32)
    force = jnp.concatenate([force, jnp.zeros((2, size), jnp.float32)], axis=0)
    load_map = force.T
    wide_products[...] = jnp.zeros((tall, size), jnp.float32)
    coupling = couple_ref[...].astype(jnp.float32)
    wide_products[pl.ds(0, 6)] = coupling
    couple[...] = wide_products[...].astype(jnp.bfloat16)
    wide_products[pl.ds(0, 6)] = jnp.zeros((6, size), jnp.float32)
    for at, (first, second) in enumerate(PAIRS):
        wide_products[pl.ds(6 + at, 1)] = coupling[first : first + 1] * coupling[second : second + 1]
    products[...] = wide_products[...].astype(jnp.bfloat16)

    route = routes_ref[...]
    row_of = lax.broadcasted_iota(jnp.int32, (128, 128), 0)
    column_of = lax.broadcasted_iota(jnp.int32, (128, 128), 1)
    until = jnp.where(row_of <= column_of, 1.0, 0.0).astype(jnp.bfloat16)
    named = [jnp.where(route == owner, 1.0, 0.0) for owner in range(n_micro)]
    named = jnp.concatenate(named, axis=0).astype(jnp.bfloat16)
    inner_rank = jnp.dot(named, until, preferred_element_type=jnp.float32)
    whole = jnp.dot(
        named, jnp.ones((128, 128), jnp.bfloat16), preferred_element_type=jnp.float32
    ).astype(jnp.bfloat16)
    span = n_micro * groups
    row_of = lax.broadcasted_iota(jnp.int32, (span, span), 0)
    column_of = lax.broadcasted_iota(jnp.int32, (span, span), 1)
    ahead = jnp.logical_and(column_of < row_of, column_of // groups == row_of // groups)
    before = jnp.dot(
        jnp.where(ahead, 1.0, 0.0).astype(jnp.bfloat16), whole, preferred_element_type=jnp.float32
    )
    ranks = inner_rank + before - 1.0
    rank = jnp.zeros((groups, 128), jnp.float32)
    for owner in range(n_micro):
        rank = jnp.where(route == owner, ranks[owner * groups : (owner + 1) * groups], rank)
    slot_at = lax.broadcasted_iota(jnp.int32, (slots, 128), 0).astype(jnp.float32)

    def spot(owner, carry):
        local = jnp.where(route == owner, rank, -1.0)
        for g in range(groups):
            hit = jnp.where(local[g : g + 1] == slot_at, 1.0, 0.0)
            low = pl.multiple_of(owner * slots, slots)
            spots[pl.ds(low, slots), g * 128 : (g + 1) * 128] = hit.astype(jnp.bfloat16)
        return carry

    lax.fori_loop(0, n_micro, spot, 0)

    for it in range(basis.shape[0]):
        for c in range(3):
            basis[it, c] = jnp.zeros((rows, lanes), jnp.float32)
    elem[...] = jnp.zeros(elem.shape, jnp.float32)
    values[...] = jnp.zeros(values.shape, jnp.float32)
    bundle[...] = jnp.zeros(bundle.shape, jnp.float32)
    for g in range(groups):
        bundle[6:7, g * 128 : (g + 1) * 128] = counts_ref[g : g + 1].astype(jnp.float32)

    for at, (dx, dy) in enumerate(AROUND):

        @pl.when(jnp.logical_not(inside(dx, dy, level)))
        def _():
            for it in range(ITERS):
                halo[it, at] = jnp.zeros(halo.shape[2:], jnp.float32)

    after = ((1, 0), (0, 1), (1, 1))
    for at, (dx, dy) in enumerate(after):

        @pl.when(jnp.logical_not(inside(dx, dy)))
        def _():
            near_disp[at] = jnp.zeros(near_disp.shape[1:], jnp.float32)

    owned = [(i, j) for i in range(count_x) for j in range(count_y)]
    column_at = {place: at for at, place in enumerate(owned)}
    handed = [((1, 0), (count_x - 1, j), (0, j + 1)) for j in range(count_y)]
    handed += [((0, 1), (i, count_y - 1), (i + 1, 0)) for i in range(count_x)]
    handed += [((1, 1), (count_x - 1, count_y - 1), (0, 0))]
    for at, ((dx, dy), _, _) in enumerate(handed):

        @pl.when(jnp.logical_not(inside(-dx, -dy, level)))
        def _():
            beside[at] = jnp.zeros(beside.shape[1:], jnp.float32)

    pl.semaphore_wait(barrier, greeted)

    def show(at):
        dx, dy = after[at]
        return pltpu.make_async_remote_copy(
            src_ref=disp_ref,
            dst_ref=near_disp.at[at],
            send_sem=disp_send.at[at],
            recv_sem=disp_recv.at[at],
            device_id=(a - dx, b - dy),
            device_id_type=MESH,
        )

    for at, (dx, dy) in enumerate(after):

        @pl.when(inside(-dx, -dy))
        def _():
            show(at).start()

    def at_seat(source, target, at):
        return pltpu.make_async_remote_copy(
            src_ref=source,
            dst_ref=target,
            send_sem=seat_send.at[at],
            recv_sem=seat_recv.at[at],
            device_id=(seat, b),
            device_id_type=MESH,
        )

    def at_home(at):
        return pltpu.make_async_remote_copy(
            src_ref=packed.at[at],
            dst_ref=home.at[at],
            send_sem=home_send.at[at],
            recv_sem=home_recv.at[at],
            device_id=(level, b),
            device_id_type=MESH,
        )

    def when_moved(act, stay):
        if not moved_rows:
            stay()
            return

        @pl.when(seat != a)
        def _():
            act()

        @pl.when(seat == a)
        def _():
            stay()

    for name in ("pre", "stiff", "load"):
        inputs[name].wait()

    def load_stays():
        load_here[...] = load_ref[...]

    when_moved(at_seat(load_ref, load_here, 0).start if moved_rows else None, load_stays)

    def split(exact):
        high = exact.astype(jnp.bfloat16)
        return jnp.concatenate([high, (exact - high.astype(jnp.float32)).astype(jnp.bfloat16)], axis=1)

    def through(matrix, exact):
        moved = jnp.dot(matrix[...], split(exact), preferred_element_type=jnp.float32)
        return moved[:, :8] + moved[:, 8:]

    first_map = OMEGA * through(pre, load_map)
    misfit_map = through(stiff, first_map) - load_map
    for at, exact in enumerate((first_map, misfit_map, load_map)):
        maps[pl.ds(at * size, size)] = split(exact)
    for c in range(3):
        for i, j in owned:
            basis[0, c, pl.ds((i + 1) * wide + j + 1, 1)] = disp_ref[c, i, j : j + 1]
    for at, (dx, dy) in enumerate(after):

        @pl.when(inside(-dx, -dy))
        def _():
            show(at).wait_send()

        @pl.when(inside(dx, dy))
        def _():
            pltpu.make_async_remote_copy(
                src_ref=disp_ref,
                dst_ref=near_disp.at[at],
                send_sem=disp_send.at[at],
                recv_sem=disp_recv.at[at],
                device_id=(a + dx, b + dy),
                device_id_type=MESH,
            ).wait_recv()

    for c in range(3):
        for j in range(count_y):
            basis[0, c, pl.ds((count_x + 1) * wide + j + 1, 1)] = near_disp[0, c, 0, j : j + 1]
        for i in range(count_x):
            basis[0, c, pl.ds((i + 1) * wide + count_y + 1, 1)] = near_disp[1, c, i, 0:1]
        basis[0, c, pl.ds((count_x + 1) * wide + count_y + 1, 1)] = near_disp[2, c, 0, 0:1]

    row_at = lax.broadcasted_iota(jnp.int32, (rows, lanes), 0)
    lane_at = lax.broadcasted_iota(jnp.int32, (rows, lanes), 1)
    own = row_at < 0
    for i in range(1, count_x + 1):
        low = i * wide + 1
        own = jnp.logical_or(own, jnp.logical_and(row_at >= low, row_at < low + count_y))

    def up(value, axis):
        if axis == 2:
            moved = pltpu.roll(value, lanes - 1, 1)
            return jnp.where(lane_at == lanes - 1, 0.0, moved)
        return pltpu.roll(value, rows - (wide if axis == 0 else 1), 0)

    def down(value, axis):
        if axis == 2:
            return jnp.where(lane_at == 0, 0.0, pltpu.roll(value, 1, 1))
        return pltpu.roll(value, wide if axis == 0 else 1, 0)

    def strain_of(it):
        grads = []
        for c in range(3):
            value = basis[it, c]
            moved = up(value, 2)
            total, gap = value + moved, moved - value
            total_up, gap_up = up(total, 1), up(gap, 1)
            flat, slope_y, slope_z = total + total_up, total_up - total, gap + gap_up
            grads.append(
                (
                    0.25 * (up(flat, 0) - flat),
                    0.25 * (up(slope_y, 0) + slope_y),
                    0.25 * (up(slope_z, 0) + slope_z),
                )
            )
        return [
            grads[0][0],
            grads[1][1],
            grads[2][2],
            grads[1][2] + grads[2][1],
            grads[0][2] + grads[2][0],
            grads[0][1] + grads[1][0],
        ]

    strain = strain_of(0)
    for at, (i, j) in enumerate(owned):
        low = (i + 1) * wide + j + 1
        for k in range(6):
            bundle[k : k + 1, at * lanes : (at + 1) * lanes] = strain[k][low : low + 1]
    exact = bundle[...]
    high = exact.astype(jnp.bfloat16).astype(jnp.float32)
    both = jnp.concatenate([high, exact - high], axis=0).astype(jnp.bfloat16)

    def route_copy(other, mine):
        return pltpu.make_async_remote_copy(
            src_ref=route_out.at[other],
            dst_ref=route_in.at[mine],
            send_sem=route_send.at[other],
            recv_sem=route_recv.at[mine],
            device_id=(a, other),
            device_id_type=MESH,
        )

    chip, core = b // 2, lax.rem(b, 2)

    def pair_rows(place):
        return pl.ds(pl.multiple_of(place * (2 * slots), 2 * slots), 2 * slots)

    def hand_out(at, carry):
        place = lax.rem(chip + pairs - at, pairs)
        moved = lax.dot_general(
            both,
            spots[pair_rows(place)],
            (((1,), (1,)), ((), ())),
            preferred_element_type=jnp.float32,
        )
        moved = moved[:8] + moved[8:]
        for k in range(2):
            other = 2 * place + k
            piece = moved[:, k * slots : (k + 1) * slots]

            @pl.when(other != b)
            def _():
                route_out[other] = piece
                route_copy(other, b).start()

            @pl.when(other == b)
            def _():
                route_in[b] = piece

        return carry

    lax.fori_loop(0, pairs, hand_out, 0)


    lame_first, lame_shear = first_ref[0], shear_ref[0]
    tall_at = lax.broadcasted_iota(jnp.int32, (tall, 2 * slots), 0)
    on_trace = jnp.where(tall_at < 3, lame_first, 0.0)
    on_strain = jnp.where(tall_at < 3, 2.0 * lame_shear, jnp.where(tall_at < 6, lame_shear, 0.0))
    base = jnp.zeros((tall, 2 * slots), jnp.float32)
    for at, (i, j) in enumerate(PAIRS):
        if i == j:
            amount = lame_first + 2.0 * lame_shear if i < 3 else lame_shear
        elif j < 3:
            amount = lame_first
        else:
            continue
        base = jnp.where(tall_at == 6 + at, amount, base)

    def back_copy(other, mine):
        return pltpu.make_async_remote_copy(
            src_ref=back_out.at[other],
            dst_ref=back_in.at[mine],
            send_sem=back_send.at[other],
            recv_sem=back_recv.at[mine],
            device_id=(a, other),
            device_id_type=MESH,
        )

    def solve(at, carry):
        place = lax.rem(chip + at, pairs)
        taken = []
        for k in range(2):
            other = 2 * place + k

            @pl.when(other != b)
            def _():
                route_copy(b, other).wait_recv()

            taken.append(route_in[other])
        points_in = jnp.concatenate(taken, axis=1)
        sweeps = points_in[6:7]
        strain_in = points_in.astype(jnp.bfloat16)
        strain_in = jnp.concatenate([strain_in, strain_in], axis=0)

        def mapped(at):
            return jnp.dot(
                maps[pl.ds(at * size, size)], strain_in, preferred_element_type=jnp.float32
            )

        modes, misfit, modal_load = mapped(0), mapped(1), mapped(2)
        for sweep in range(1, ITMAX):
            if sweep > 1:
                misfit = jnp.dot(
                    stiff[...], modes.astype(jnp.bfloat16), preferred_element_type=jnp.float32
                )
                misfit = misfit - modal_load
            misfit = (misfit + BETA * jnp.tanh(modes)).astype(jnp.bfloat16)
            change = jnp.dot(pre[...], misfit, preferred_element_type=jnp.float32)
            modes = modes - jnp.where(sweeps > sweep, OMEGA, 0.0) * change
        bent = jnp.tanh(modes)
        slope = 1.0 - bent * bent
        trace = points_in[0:1] + points_in[1:2] + points_in[2:3]
        padded = jnp.concatenate(
            [points_in, jnp.zeros((tall - 8, 2 * slots), jnp.float32)], axis=0
        )
        answer = on_trace * trace + on_strain * padded + base
        answer = answer + jnp.dot(
            couple[...], modes.astype(jnp.bfloat16), preferred_element_type=jnp.float32
        )
        answer = answer + jnp.dot(
            products[...], slope.astype(jnp.bfloat16), preferred_element_type=jnp.float32
        )
        for k in range(2):
            other = 2 * place + k
            piece = answer[:, k * slots : (k + 1) * slots]

            @pl.when(other != b)
            def _():
                back_out[other] = piece
                back_copy(other, b).start()

            @pl.when(other == b)
            def _():
                back_in[b] = piece

        return carry

    lax.fori_loop(0, pairs, solve, 0)

    def take_back(at, carry):
        place = lax.rem(chip + pairs - at, pairs)
        taken = []
        for k in range(2):
            other = 2 * place + k

            @pl.when(other != b)
            def _():
                back_copy(b, other).wait_recv()

            taken.append(back_in[other])
        exact = jnp.concatenate(taken, axis=1)
        high = exact.astype(jnp.bfloat16).astype(jnp.float32)
        both = jnp.concatenate([high, exact - high], axis=0).astype(jnp.bfloat16)
        moved = jnp.dot(both, spots[pair_rows(place)], preferred_element_type=jnp.float32)
        values[...] += moved[:tall] + moved[tall:]
        return carry

    lax.fori_loop(0, pairs, take_back, 0)

    def side_copy(at):
        (dx, dy), place, _ = handed[at]
        low = column_at[place] * lanes
        return pltpu.make_async_remote_copy(
            src_ref=values.at[:, pl.ds(low, lanes)],
            dst_ref=beside.at[at],
            send_sem=side_send.at[at],
            recv_sem=side_recv.at[at],
            device_id=(pick(line, a + dx), b + dy),
            device_id_type=MESH,
        )

    def values_stay():
        values_here[...] = values[...]

    def side_test(at, leaves, same):
        (dx, dy), _, _ = handed[at]
        test = inside(dx, dy) if leaves else inside(-dx, -dy, level)
        if dy != 0 or not moved_rows:
            return None if same else test
        itself = (pick(line, a + dx) if leaves else level - dx) == a
        return jnp.logical_and(test, itself if same else jnp.logical_not(itself))

    when_moved(at_seat(values, values_here, 1).start if moved_rows else None, values_stay)
    for at, (_, place, _) in enumerate(handed):

        @pl.when(side_test(at, True, False))
        def _():
            side_copy(at).start()

        test = side_test(at, True, True)
        if test is not None:

            @pl.when(test)
            def _():
                low = column_at[place] * lanes
                beside[at] = values[:, low : low + lanes]

    def put_column(read, row):
        for v in range(6 + len(PAIRS)):
            elem[v, pl.ds(row, 1)] = read(v)

    def put_own():
        for at, (i, j) in enumerate(owned):
            put_column(
                lambda v: values_here[v : v + 1, at * lanes : (at + 1) * lanes],
                (i + 1) * wide + j + 1,
            )

    when_moved(lambda: None, put_own)
    for at, ((dx, dy), _, (i, j)) in enumerate(handed):

        @pl.when(side_test(at, True, False))
        def _():
            side_copy(at).wait_send()

        @pl.when(side_test(at, False, False))
        def _():
            side_copy(at).wait_recv()

        put_column(lambda v: beside[at, v : v + 1], i * wide + j)

    def guest():
        at_seat(load_ref, load_here, 0).wait()
        at_seat(values, values_here, 1).wait()
        put_own()

    when_moved(guest, lambda: None)

    def near(step, count):
        return {0: list(range(1, count + 1)), -1: [1], 1: [count]}[step]

    def far(step, count):
        return {0: list(range(1, count + 1)), -1: [0], 1: [count + 1]}[step]

    def places(at, pick):
        dx, dy = AROUND[at]
        return [i * wide + j for i in pick(dx, count_x) for j in pick(dy, count_y)]

    def hop(it, at):
        dx, dy = AROUND[at]
        other = len(AROUND) - 1 - at
        return pltpu.make_async_remote_copy(
            src_ref=send_halo.at[it, at],
            dst_ref=halo.at[it, other],
            send_sem=send_sem.at[it, at],
            recv_sem=recv_sem.at[it, other],
            device_id=(pick(line, level + dx), b + dy),
            device_id_type=MESH,
        )

    def halo_start(it):
        for at, (dx, dy) in enumerate(AROUND):

            @pl.when(inside(dx, dy, level))
            def _():
                mine = places(at, near)
                for c in range(3):
                    for k, row in enumerate(mine):
                        send_halo[it, at, pl.ds(c * len(mine) + k, 1)] = basis[it, c, pl.ds(row, 1)]
                hop(it, at).start()

    def halo_finish(it):
        for at, (dx, dy) in enumerate(AROUND):

            @pl.when(inside(dx, dy, level))
            def _():
                hop(it, at).wait_send()
                pltpu.make_async_remote_copy(
                    src_ref=send_halo.at[it, at],
                    dst_ref=halo.at[it, at],
                    send_sem=send_sem.at[it, at],
                    recv_sem=recv_sem.at[it, at],
                    device_id=(pick(line, level + dx), b + dy),
                    device_id_type=MESH,
                ).wait_recv()

        for at in range(len(AROUND)):
            theirs = places(at, far)
            for c in range(3):
                for k, row in enumerate(theirs):
                    basis[it, c, pl.ds(row, 1)] = halo[it, at, pl.ds(c * len(theirs) + k, 1)]

    def keep(it, read):
        for target, there in ((packed, True), (home, False)) if moved_rows else ((home, None),):

            def put():
                for c in range(3):
                    for at, (i, j) in enumerate(owned):
                        place = (i + 1) * wide + j + 1
                        target[it, pl.ds(c * len(owned) + at, 1)] = read(c, place)
                if there:
                    at_home(it).start()

            if there is None:
                put()
            else:
                pl.when((seat != a) if there else (seat == a))(put)

    def kept(it):
        keep(it, lambda c, place: basis[it, c, pl.ds(place, 1)])

    def force_of(stress, c):
        first, second, third = (stress[VOIGT[c][d]] for d in range(3))
        first = first + down(first, 2)
        second = second + down(second, 2)
        third = down(third, 2) - third
        first = first + down(first, 1)
        rest = down(second, 1) - second + third + down(third, 1)
        return 0.25 * (down(first, 0) - first + rest + down(rest, 0))

    def applied(it):
        strain = strain_of(it)
        stress = []
        for i in range(6):
            value = None
            for j in range(6):
                term = elem[6 + PAIR_AT[(min(i, j), max(i, j))]] * strain[j]
                value = term if value is None else value + term
            stress.append(value)
        return [
            jnp.where(own, MASS * basis[it, c] + force_of(stress, c), 0.0) for c in range(3)
        ]

    def product(first, second):
        total = None
        for c in range(3):
            term = first[c] * second[c]
            total = term if total is None else total + term
        total = jnp.sum(jnp.where(own, total, 0.0), axis=0, keepdims=True)
        value = total[:, :128]
        for at in range(128, lanes, 128):
            value = value + total[:, at : at + 128]
        return value

    def stacked(pieces):
        tile_row = lax.broadcasted_iota(jnp.int32, (16, 128), 0)
        value = jnp.zeros((16, 128), jnp.float32)
        for at, piece in enumerate(pieces):
            value = jnp.where(tile_row == at, piece, value)
        return value

    def gather_start(src, dst, count, mine, send, recv, device):
        copies = []
        for step in range(1, count):
            copy = pltpu.make_async_remote_copy(
                src_ref=src,
                dst_ref=dst.at[mine],
                send_sem=send.at[step - 1],
                recv_sem=recv.at[step - 1],
                device_id=device(lax.rem(mine + step, count)),
                device_id_type=MESH,
            )
            copy.start()
            copies.append(copy)
        dst[mine] = src[...]
        return copies

    def gather_finish(copies, dst, count):
        for copy in copies:
            copy.wait()
        total = dst[0]
        for at in range(1, count):
            total = total + dst[at]
        return total

    stress = [elem[i] for i in range(6)]
    zero = jnp.zeros((rows, lanes), jnp.float32)
    for c in range(3):
        padded = jnp.concatenate(
            [jnp.zeros((wide + 1, lanes), jnp.float32)]
            + [
                piece
                for i in range(count_x)
                for piece in (load_here[c, i], jnp.zeros((2, lanes), jnp.float32))
            ]
            + [jnp.zeros((rows - 1 - wide * (count_x + 1), lanes), jnp.float32)],
            axis=0,
        )
        basis[0, c] = jnp.where(own, padded - force_of(stress, c), zero)
    halo_start(0)
    kept(0)
    halo_finish(0)
    grown = applied(0)
    for c in range(3):
        basis[1, c] = grown[c]
    halo_start(1)
    kept(1)
    start = [basis[0, c] for c in range(3)]
    part[...] = stacked([product(start, start), product(grown, grown)])
    copies = gather_start(
        part, got_micro, n_micro, b, micro_send, micro_recv, lambda other: (a, other)
    )
    halo_finish(1)
    grown = applied(1)
    for c in range(3):
        basis[2, c] = grown[c]
    halo_start(2)
    kept(2)
    middle[...] = gather_finish(copies, got_micro, n_micro)
    copies = gather_start(
        middle, got_macro, n_macro, a, macro_send, macro_recv, lambda other: (other, b)
    )
    halo_finish(2)
    totals = jnp.sum(gather_finish(copies, got_macro, n_macro), axis=1, keepdims=True)
    shift = jnp.sqrt(totals[1:2] / totals[0:1])
    scale = 1.0 / shift
    for c in range(3):
        u0, w1, w2 = basis[0, c], basis[1, c] * scale, basis[2, c] * (scale * scale)
        basis[1, c] = w1 - u0
        basis[2, c] = (w2 - w1) - (w1 - u0)

    def field(it):
        return [basis[it, c] for c in range(3)]

    def step(it):
        grown = applied(it)
        return [grown[c] * scale - jnp.where(own, basis[it, c], 0.0) for c in range(3)]

    moments = []
    for it in range(2, ITERS):
        grown = step(it)
        if it + 1 < ITERS:
            for c in range(3):
                basis[it + 1, c] = grown[c]
            halo_start(it + 1)
            kept(it + 1)
            if it == 2:
                for k in range(3):
                    moments.append(product(field(k), field(k)))
                    moments.append(product(field(k), field(k + 1)))
            else:
                moments.append(product(field(it), field(it)))
                moments.append(product(field(it), field(it + 1)))
            halo_finish(it + 1)
    keep(ITERS, lambda c, place: grown[c][place : place + 1])
    moments.append(product(field(ITERS - 1), field(ITERS - 1)))
    moments.append(product(field(ITERS - 1), grown))
    sums = jnp.sum(stacked(moments), axis=1, keepdims=True)
    diagonal = lax.broadcasted_iota(jnp.int32, (16, 128), 0) == lax.broadcasted_iota(
        jnp.int32, (16, 128), 1
    )
    last_part[...] = jnp.sum(jnp.where(diagonal, sums, 0.0), axis=0, keepdims=True)

    def last_copy(step, other):
        return pltpu.make_async_remote_copy(
            src_ref=last_part,
            dst_ref=last_all.at[me],
            send_sem=last_send.at[step],
            recv_sem=last_recv.at[step],
            device_id=device(other),
            device_id_type=MESH,
        )

    every(total, lambda step: last_copy(step, lax.rem(me + step, total)).start())
    last_all[me] = last_part[...]
    every(total, lambda step: last_copy(step, lax.rem(me + step, total)).wait())
    totals = jnp.sum(last_all[...], axis=0)
    held = [totals[:, k : k + 1] for k in range(2 * ITERS)]

    def inner(first, second, extra=0):
        gathered = {}
        for i, x in enumerate(first):
            for j, y in enumerate(second):
                gathered.setdefault(i + j, []).append(x * y)
        value = None
        for degree, terms in gathered.items():
            total = terms[0]
            for term in terms[1:]:
                total = total + term
            total = total * held[degree + extra]
            value = total if value is None else value + total
        return value

    one = jnp.ones((1, 1), jnp.float32)
    left, toward, done = [one], [one], []
    norm = held[0]
    for it in range(ITERS):
        energy = inner(toward, toward) + inner(toward, toward, 1)
        length = norm / energy
        done = [x + length * scale * p for x, p in zip(done + [0.0], toward)]
        raised = [
            (toward[k] if k < len(toward) else 0.0) + (toward[k - 1] if k > 0 else 0.0)
            for k in range(len(toward) + 1)
        ]
        left = [
            (left[k] if k < len(left) else 0.0) - length * raised[k] for k in range(len(raised))
        ]
        if it + 1 < ITERS:
            fresh = inner(left, left)
            ratio = fresh / norm
            toward = [
                left[k] + (ratio * toward[k] if k < len(toward) else 0.0)
                for k in range(len(left))
            ]
            norm = fresh
    def landed():
        for at in range(ITERS + 1):
            at_home(at).wait()

    when_moved(landed, lambda: None)
    fields = [home[k] for k in range(ITERS + 1)]
    u0, w1, w2 = fields[0], fields[1] * scale, fields[2] * (scale * scale)
    fields[1] = w1 - u0
    fields[2] = (w2 - w1) - (w1 - u0)
    moved, rest = None, None
    for k in range(ITERS + 1):
        if k < len(done):
            term = done[k] * fields[k]
            moved = term if moved is None else moved + term
        term = left[k] * fields[k]
        rest = term if rest is None else rest + term
    for c in range(3):
        for i in range(count_x):
            low = c * len(owned) + i * count_y
            inc_ref[c, i] = moved[low : low + count_y]
            res_ref[c, i] = rest[low : low + count_y]

    def sent(step, carry):
        other = lax.rem(b + step, n_micro)
        route_copy(other, b).wait_send()
        back_copy(other, b).wait_send()
        return carry

    lax.fori_loop(1, n_micro, sent, 0)


def line_of(mesh):
    places = [tuple(getattr(device, "coords", ())) for device in mesh.devices[:, 0]]

    def cost(order):
        hops = sum(
            sum(abs(x - y) for x, y in zip(places[p], places[q]))
            for p, q in zip(order, order[1:])
        )
        return hops, sum(p != at for at, p in enumerate(order)), order

    if len(places) > 6:
        return list(range(len(places)))
    return list(min(itertools.permutations(range(len(places))), key=cost))


def shards(
    line,
    displacement,
    load,
    routes,
    counts,
    stiffness,
    precond,
    forcing,
    coupling,
    lame_first,
    lame_shear,
):
    _, count_x, count_y, lanes = displacement.shape
    points = count_x * count_y * lanes
    n_macro, n_micro = lax.axis_size("macro"), lax.axis_size("micro")
    capacity = max(2, 2 * points // n_micro)
    slots = -(-capacity // 128) * 128
    size = stiffness.shape[1]
    tall = -(-(6 + len(PAIRS)) // 8) * 8
    rows = -(-(count_x + 2) * (count_y + 2) // 8) * 8
    side = -(-3 * max(count_x, count_y) // 8) * 8
    total = n_macro * n_micro
    fields = -(-3 * count_x * count_y // 8) * 8
    sides = count_x + count_y + 1
    vmem = pl.BlockSpec(memory_space=pltpu.VMEM)
    smem = pl.BlockSpec(memory_space=pltpu.SMEM)
    anywhere = pl.BlockSpec(memory_space=pl.ANY)
    dma = pltpu.SemaphoreType.DMA

    def held(*shape):
        return pltpu.VMEM(shape, jnp.float32)

    def half(*shape):
        return pltpu.VMEM(shape, jnp.bfloat16)

    def body(*refs):
        newton_kernel((count_x, count_y, lanes, n_macro, n_micro, line), *refs)

    return tuple(
        pl.pallas_call(
            body,
            out_shape=[jax.ShapeDtypeStruct(load.shape, jnp.float32)] * 2,
            in_specs=[anywhere] * 8 + [smem] * 2,
            out_specs=[vmem, vmem],
            scratch_shapes=[
                held(*displacement.shape),
                held(*load.shape),
                pltpu.VMEM((points // 128, 128), jnp.int32),
                pltpu.VMEM((points // 128, 128), jnp.int32),
                half(size, size),
                half(size, size),
                half(6, size),
                half(6, size),
                half(3 * size, 16),
                half(tall, size),
                half(tall, size),
                held(tall, size),
                half(n_micro * slots, points),
                held(*load.shape),
                held(tall, points),
                held(ITERS + 1, fields, lanes),
                held(ITERS + 1, fields, lanes),
                held(3, *displacement.shape),
                held(8, points),
                held(n_micro, 8, slots),
                held(n_micro, 8, slots),
                held(n_micro, tall, slots),
                held(n_micro, tall, slots),
                held(tall, points),
                held(sides, tall, lanes),
                held(6 + len(PAIRS), rows, lanes),
                held(ITERS, 3, rows, lanes),
                held(ITERS, len(AROUND), side, lanes),
                held(ITERS, len(AROUND), side, lanes),
                held(16, 128),
                held(n_micro, 16, 128),
                held(16, 128),
                held(n_macro, 16, 128),
                held(1, 128),
                held(total, 1, 128),
                dma((8,)),
                dma((3,)),
                dma((3,)),
                dma((n_micro,)),
                dma((n_micro,)),
                dma((n_micro,)),
                dma((n_micro,)),
                dma((sides,)),
                dma((sides,)),
                dma((ITERS, len(AROUND))),
                dma((ITERS, len(AROUND))),
                dma((n_micro - 1,)),
                dma((n_micro - 1,)),
                dma((n_macro - 1,)),
                dma((n_macro - 1,)),
                dma((total,)),
                dma((total,)),
                dma((2,)),
                dma((2,)),
                dma((ITERS + 1,)),
                dma((ITERS + 1,)),
            ],
            compiler_params=pltpu.CompilerParams(collective_id=0, has_side_effects=True),
            name="newton_step",
        )(
            displacement,
            load,
            routes.reshape(points // 128, 128),
            counts.reshape(points // 128, 128),
            stiffness[0],
            precond[0],
            forcing[0],
            coupling[0].T,
            lame_first,
            lame_shear,
        )
    )


def solution(mesh):
    in_specs = (
        P(None, "macro", "micro", None),
        P(None, "macro", "micro", None),
        P("macro", "micro", None, None),
        P("macro", "micro", None),
        P("micro", None, None),
        P("micro", None, None),
        P("micro", None, None),
        P("micro", None, None),
        P("micro"),
        P("micro"),
    )
    out_specs = (P(None, "macro", "micro", None), P(None, "macro", "micro", None))
    return jax.shard_map(functools.partial(shards, line_of(mesh)), mesh=mesh, in_specs=in_specs, out_specs=out_specs, check_vma=False)
```

```python
import jax
import jax.numpy as jnp
from jax import lax
from jax.experimental import pallas as pl
from jax.experimental.pallas import tpu as pltpu
from jax.sharding import PartitionSpec as P

ITMAX = 4
ITERS = 5


BETA = 0.1
OMEGA = 0.8
MASS = 0.1
VOIGT = ((0, 5, 4), (5, 1, 3), (4, 3, 2))
PAIRS = tuple((first, second) for first in range(6) for second in range(first, 6))
PAIR_AT = {pair: at for at, pair in enumerate(PAIRS)}
AROUND = tuple((dx, dy) for dx in (-1, 0, 1) for dy in (-1, 0, 1) if (dx, dy) != (0, 0))
MESH = pl.DeviceIdType.MESH


def newton_kernel(
    sizes,
    disp_in,
    load_in,
    routes_in,
    counts_in,
    stiff_in,
    pre_in,
    force_in,
    couple_in,
    first_ref,
    shear_ref,
    inc_ref,
    res_ref,
    disp_ref,
    load_ref,
    routes_ref,
    counts_ref,
    stiff,
    pre,
    force_ref,
    couple_ref,
    maps,
    couple,
    products,
    wide_products,
    spots,
    near_disp,
    bundle,
    route_out,
    route_in,
    back_out,
    back_in,
    values,
    beside,
    elem,
    basis,
    send_halo,
    halo,
    part,
    got_micro,
    middle,
    got_macro,
    last_part,
    last_all,
    input_sem,
    disp_send,
    disp_recv,
    route_send,
    route_recv,
    back_send,
    back_recv,
    side_send,
    side_recv,
    send_sem,
    recv_sem,
    micro_send,
    micro_recv,
    macro_send,
    macro_recv,
    last_send,
    last_recv,
):
    count_x, count_y, lanes, n_macro, n_micro = sizes
    wide = count_y + 2
    rows = basis.shape[2]
    points = spots.shape[1]
    slots = spots.shape[0] // n_micro
    pairs = n_micro // 2
    groups = points // 128
    size = stiff.shape[0]
    tall = couple.shape[0]
    total = n_macro * n_micro
    a, b = lax.axis_index("macro"), lax.axis_index("micro")
    me = a * n_micro + b

    def device(other):
        return (other // n_micro, lax.rem(other, n_micro))

    def inside(dx, dy):
        test = None
        for place, step, count in ((a, dx, n_macro), (b, dy, n_micro)):
            if step != 0:
                good = (place > 0) if step < 0 else (place < count - 1)
                test = good if test is None else jnp.logical_and(test, good)
        return test

    barrier = pltpu.get_barrier_semaphore()

    def every(count, act):
        if count <= 32:
            for step in range(1, count):
                act(step)
        else:
            lax.fori_loop(1, count, lambda step, carry: (act(step), carry)[1], 0)

    def greet(row, column):
        pl.semaphore_signal(barrier, inc=1, device_id=(row, column), device_id_type=MESH)

    for step in range(1, n_macro):
        for aside in range(3):
            greet(lax.rem(a + step, n_macro), lax.rem(b + n_micro - 1 + aside, n_micro))
    every(n_micro, lambda step: greet(a, lax.rem(b + step, n_micro)))
    greeted = 3 * (n_macro - 1) + n_micro - 1
    inputs = {}
    for at, (name, source, target) in enumerate(
        (
            ("routes", routes_in, routes_ref),
            ("force", force_in, force_ref),
            ("couple", couple_in, couple_ref),
            ("counts", counts_in, counts_ref),
            ("disp", disp_in, disp_ref),
            ("load", load_in, load_ref),
            ("pre", pre_in, pre),
            ("stiff", stiff_in, stiff),
        )
    ):
        inputs[name] = pltpu.make_async_copy(source, target, input_sem.at[at])
        inputs[name].start()

    inputs["disp"].wait()
    after = ((1, 0), (0, 1), (1, 1))
    pl.semaphore_wait(barrier, greeted)

    def show(at):
        dx, dy = after[at]
        return pltpu.make_async_remote_copy(
            src_ref=disp_ref,
            dst_ref=near_disp.at[at],
            send_sem=disp_send.at[at],
            recv_sem=disp_recv.at[at],
            device_id=(a - dx, b - dy),
            device_id_type=MESH,
        )

    for at, (dx, dy) in enumerate(after):

        @pl.when(inside(-dx, -dy))
        def _():
            show(at).start()

    for name in ("routes", "force", "couple", "counts"):
        inputs[name].wait()
    force = force_ref[...].astype(jnp.float32)
    force = jnp.concatenate([force, jnp.zeros((2, size), jnp.float32)], axis=0)
    load_map = force.T
    wide_products[...] = jnp.zeros((tall, size), jnp.float32)
    coupling = couple_ref[...].astype(jnp.float32)
    wide_products[pl.ds(0, 6)] = coupling
    couple[...] = wide_products[...].astype(jnp.bfloat16)
    wide_products[pl.ds(0, 6)] = jnp.zeros((6, size), jnp.float32)
    for at, (first, second) in enumerate(PAIRS):
        wide_products[pl.ds(6 + at, 1)] = coupling[first : first + 1] * coupling[second : second + 1]
    products[...] = wide_products[...].astype(jnp.bfloat16)

    route = routes_ref[...]
    row_of = lax.broadcasted_iota(jnp.int32, (128, 128), 0)
    column_of = lax.broadcasted_iota(jnp.int32, (128, 128), 1)
    until = jnp.where(row_of <= column_of, 1.0, 0.0).astype(jnp.bfloat16)
    named = [jnp.where(route == owner, 1.0, 0.0) for owner in range(n_micro)]
    named = jnp.concatenate(named, axis=0).astype(jnp.bfloat16)
    inner_rank = jnp.dot(named, until, preferred_element_type=jnp.float32)
    whole = jnp.dot(
        named, jnp.ones((128, 128), jnp.bfloat16), preferred_element_type=jnp.float32
    ).astype(jnp.bfloat16)
    span = n_micro * groups
    row_of = lax.broadcasted_iota(jnp.int32, (span, span), 0)
    column_of = lax.broadcasted_iota(jnp.int32, (span, span), 1)
    ahead = jnp.logical_and(column_of < row_of, column_of // groups == row_of // groups)
    before = jnp.dot(
        jnp.where(ahead, 1.0, 0.0).astype(jnp.bfloat16), whole, preferred_element_type=jnp.float32
    )
    ranks = inner_rank + before - 1.0
    rank = jnp.zeros((groups, 128), jnp.float32)
    for owner in range(n_micro):
        rank = jnp.where(route == owner, ranks[owner * groups : (owner + 1) * groups], rank)
    slot_at = lax.broadcasted_iota(jnp.int32, (slots, 128), 0).astype(jnp.float32)

    def spot(owner, carry):
        local = jnp.where(route == owner, rank, -1.0)
        for g in range(groups):
            hit = jnp.where(local[g : g + 1] == slot_at, 1.0, 0.0)
            low = pl.multiple_of(owner * slots, slots)
            spots[pl.ds(low, slots), g * 128 : (g + 1) * 128] = hit.astype(jnp.bfloat16)
        return carry

    lax.fori_loop(0, n_micro, spot, 0)

    for it in range(basis.shape[0]):
        for c in range(3):
            basis[it, c] = jnp.zeros((rows, lanes), jnp.float32)
    elem[...] = jnp.zeros(elem.shape, jnp.float32)
    values[...] = jnp.zeros(values.shape, jnp.float32)
    bundle[...] = jnp.zeros(bundle.shape, jnp.float32)
    for g in range(groups):
        bundle[6:7, g * 128 : (g + 1) * 128] = counts_ref[g : g + 1].astype(jnp.float32)

    for at, (dx, dy) in enumerate(AROUND):

        @pl.when(jnp.logical_not(inside(dx, dy)))
        def _():
            for it in range(ITERS):
                halo[it, at] = jnp.zeros(halo.shape[2:], jnp.float32)

    for at, (dx, dy) in enumerate(after):

        @pl.when(jnp.logical_not(inside(dx, dy)))
        def _():
            near_disp[at] = jnp.zeros(near_disp.shape[1:], jnp.float32)

    owned = [(i, j) for i in range(count_x) for j in range(count_y)]
    column_at = {place: at for at, place in enumerate(owned)}
    handed = [((1, 0), (count_x - 1, j), (0, j + 1)) for j in range(count_y)]
    handed += [((0, 1), (i, count_y - 1), (i + 1, 0)) for i in range(count_x)]
    handed += [((1, 1), (count_x - 1, count_y - 1), (0, 0))]
    for at, ((dx, dy), _, _) in enumerate(handed):

        @pl.when(jnp.logical_not(inside(-dx, -dy)))
        def _():
            beside[at] = jnp.zeros(beside.shape[1:], jnp.float32)

    for name in ("pre", "stiff", "load"):
        inputs[name].wait()

    def split(exact):
        high = exact.astype(jnp.bfloat16)
        return jnp.concatenate([high, (exact - high.astype(jnp.float32)).astype(jnp.bfloat16)], axis=1)

    def through(matrix, exact):
        moved = jnp.dot(matrix[...], split(exact), preferred_element_type=jnp.float32)
        return moved[:, :8] + moved[:, 8:]

    first_map = OMEGA * through(pre, load_map)
    misfit_map = through(stiff, first_map) - load_map
    for at, exact in enumerate((first_map, misfit_map, load_map)):
        maps[pl.ds(at * size, size)] = split(exact)
    for c in range(3):
        for i, j in owned:
            basis[0, c, pl.ds((i + 1) * wide + j + 1, 1)] = disp_ref[c, i, j : j + 1]
    for at, (dx, dy) in enumerate(after):

        @pl.when(inside(-dx, -dy))
        def _():
            show(at).wait_send()

        @pl.when(inside(dx, dy))
        def _():
            pltpu.make_async_remote_copy(
                src_ref=disp_ref,
                dst_ref=near_disp.at[at],
                send_sem=disp_send.at[at],
                recv_sem=disp_recv.at[at],
                device_id=(a + dx, b + dy),
                device_id_type=MESH,
            ).wait_recv()

    for c in range(3):
        for j in range(count_y):
            basis[0, c, pl.ds((count_x + 1) * wide + j + 1, 1)] = near_disp[0, c, 0, j : j + 1]
        for i in range(count_x):
            basis[0, c, pl.ds((i + 1) * wide + count_y + 1, 1)] = near_disp[1, c, i, 0:1]
        basis[0, c, pl.ds((count_x + 1) * wide + count_y + 1, 1)] = near_disp[2, c, 0, 0:1]

    row_at = lax.broadcasted_iota(jnp.int32, (rows, lanes), 0)
    lane_at = lax.broadcasted_iota(jnp.int32, (rows, lanes), 1)
    own = row_at < 0
    for i in range(1, count_x + 1):
        low = i * wide + 1
        own = jnp.logical_or(own, jnp.logical_and(row_at >= low, row_at < low + count_y))

    def up(value, axis):
        if axis == 2:
            moved = pltpu.roll(value, lanes - 1, 1)
            return jnp.where(lane_at == lanes - 1, 0.0, moved)
        return pltpu.roll(value, rows - (wide if axis == 0 else 1), 0)

    def down(value, axis):
        if axis == 2:
            return jnp.where(lane_at == 0, 0.0, pltpu.roll(value, 1, 1))
        return pltpu.roll(value, wide if axis == 0 else 1, 0)

    def strain_of(it):
        grads = []
        for c in range(3):
            value = basis[it, c]
            moved = up(value, 2)
            total, gap = value + moved, moved - value
            total_up, gap_up = up(total, 1), up(gap, 1)
            flat, slope_y, slope_z = total + total_up, total_up - total, gap + gap_up
            grads.append(
                (
                    0.25 * (up(flat, 0) - flat),
                    0.25 * (up(slope_y, 0) + slope_y),
                    0.25 * (up(slope_z, 0) + slope_z),
                )
            )
        return [
            grads[0][0],
            grads[1][1],
            grads[2][2],
            grads[1][2] + grads[2][1],
            grads[0][2] + grads[2][0],
            grads[0][1] + grads[1][0],
        ]

    strain = strain_of(0)
    for at, (i, j) in enumerate(owned):
        low = (i + 1) * wide + j + 1
        for k in range(6):
            bundle[k : k + 1, at * lanes : (at + 1) * lanes] = strain[k][low : low + 1]
    exact = bundle[...]
    high = exact.astype(jnp.bfloat16).astype(jnp.float32)
    both = jnp.concatenate([high, exact - high], axis=0).astype(jnp.bfloat16)

    def route_copy(other, mine):
        return pltpu.make_async_remote_copy(
            src_ref=route_out.at[other],
            dst_ref=route_in.at[mine],
            send_sem=route_send.at[other],
            recv_sem=route_recv.at[mine],
            device_id=(a, other),
            device_id_type=MESH,
        )

    chip, core = b // 2, lax.rem(b, 2)

    def pair_rows(place):
        return pl.ds(pl.multiple_of(place * (2 * slots), 2 * slots), 2 * slots)

    def hand_out(at, carry):
        place = lax.rem(chip + pairs - at, pairs)
        moved = lax.dot_general(
            both,
            spots[pair_rows(place)],
            (((1,), (1,)), ((), ())),
            preferred_element_type=jnp.float32,
        )
        moved = moved[:8] + moved[8:]
        for k in range(2):
            other = 2 * place + k
            piece = moved[:, k * slots : (k + 1) * slots]

            @pl.when(other != b)
            def _():
                route_out[other] = piece
                route_copy(other, b).start()

            @pl.when(other == b)
            def _():
                route_in[b] = piece

        return carry

    lax.fori_loop(0, pairs, hand_out, 0)


    lame_first, lame_shear = first_ref[0], shear_ref[0]
    tall_at = lax.broadcasted_iota(jnp.int32, (tall, 2 * slots), 0)
    on_trace = jnp.where(tall_at < 3, lame_first, 0.0)
    on_strain = jnp.where(tall_at < 3, 2.0 * lame_shear, jnp.where(tall_at < 6, lame_shear, 0.0))
    base = jnp.zeros((tall, 2 * slots), jnp.float32)
    for at, (i, j) in enumerate(PAIRS):
        if i == j:
            amount = lame_first + 2.0 * lame_shear if i < 3 else lame_shear
        elif j < 3:
            amount = lame_first
        else:
            continue
        base = jnp.where(tall_at == 6 + at, amount, base)

    def back_copy(other, mine):
        return pltpu.make_async_remote_copy(
            src_ref=back_out.at[other],
            dst_ref=back_in.at[mine],
            send_sem=back_send.at[other],
            recv_sem=back_recv.at[mine],
            device_id=(a, other),
            device_id_type=MESH,
        )

    def solve(at, carry):
        place = lax.rem(chip + at, pairs)
        taken = []
        for k in range(2):
            other = 2 * place + k

            @pl.when(other != b)
            def _():
                route_copy(b, other).wait_recv()

            taken.append(route_in[other])
        points_in = jnp.concatenate(taken, axis=1)
        sweeps = points_in[6:7]
        strain_in = points_in.astype(jnp.bfloat16)
        strain_in = jnp.concatenate([strain_in, strain_in], axis=0)

        def mapped(at):
            return jnp.dot(
                maps[pl.ds(at * size, size)], strain_in, preferred_element_type=jnp.float32
            )

        modes, misfit, modal_load = mapped(0), mapped(1), mapped(2)
        for sweep in range(1, ITMAX):
            if sweep > 1:
                misfit = jnp.dot(
                    stiff[...], modes.astype(jnp.bfloat16), preferred_element_type=jnp.float32
                )
                misfit = misfit - modal_load
            misfit = (misfit + BETA * jnp.tanh(modes)).astype(jnp.bfloat16)
            change = jnp.dot(pre[...], misfit, preferred_element_type=jnp.float32)
            modes = modes - jnp.where(sweeps > sweep, OMEGA, 0.0) * change
        bent = jnp.tanh(modes)
        slope = 1.0 - bent * bent
        trace = points_in[0:1] + points_in[1:2] + points_in[2:3]
        padded = jnp.concatenate(
            [points_in, jnp.zeros((tall - 8, 2 * slots), jnp.float32)], axis=0
        )
        answer = on_trace * trace + on_strain * padded + base
        answer = answer + jnp.dot(
            couple[...], modes.astype(jnp.bfloat16), preferred_element_type=jnp.float32
        )
        answer = answer + jnp.dot(
            products[...], slope.astype(jnp.bfloat16), preferred_element_type=jnp.float32
        )
        for k in range(2):
            other = 2 * place + k
            piece = answer[:, k * slots : (k + 1) * slots]

            @pl.when(other != b)
            def _():
                back_out[other] = piece
                back_copy(other, b).start()

            @pl.when(other == b)
            def _():
                back_in[b] = piece

        return carry

    lax.fori_loop(0, pairs, solve, 0)

    def take_back(at, carry):
        place = lax.rem(chip + pairs - at, pairs)
        taken = []
        for k in range(2):
            other = 2 * place + k

            @pl.when(other != b)
            def _():
                back_copy(b, other).wait_recv()

            taken.append(back_in[other])
        exact = jnp.concatenate(taken, axis=1)
        high = exact.astype(jnp.bfloat16).astype(jnp.float32)
        both = jnp.concatenate([high, exact - high], axis=0).astype(jnp.bfloat16)
        moved = jnp.dot(both, spots[pair_rows(place)], preferred_element_type=jnp.float32)
        values[...] += moved[:tall] + moved[tall:]
        return carry

    lax.fori_loop(0, pairs, take_back, 0)

    def side_copy(at):
        (dx, dy), place, _ = handed[at]
        low = column_at[place] * lanes
        return pltpu.make_async_remote_copy(
            src_ref=values.at[:, pl.ds(low, lanes)],
            dst_ref=beside.at[at],
            send_sem=side_send.at[at],
            recv_sem=side_recv.at[at],
            device_id=(a + dx, b + dy),
            device_id_type=MESH,
        )

    for at, ((dx, dy), _, _) in enumerate(handed):

        @pl.when(inside(dx, dy))
        def _():
            side_copy(at).start()

    def put_column(read, row):
        for v in range(6 + len(PAIRS)):
            elem[v, pl.ds(row, 1)] = read(v)

    for at, (i, j) in enumerate(owned):
        put_column(
            lambda v: values[v : v + 1, at * lanes : (at + 1) * lanes], (i + 1) * wide + j + 1
        )
    for at, ((dx, dy), _, (i, j)) in enumerate(handed):

        @pl.when(inside(dx, dy))
        def _():
            side_copy(at).wait_send()

        @pl.when(inside(-dx, -dy))
        def _():
            pltpu.make_async_remote_copy(
                src_ref=values.at[:, pl.ds(0, lanes)],
                dst_ref=beside.at[at],
                send_sem=side_send.at[at],
                recv_sem=side_recv.at[at],
                device_id=(a - dx, b - dy),
                device_id_type=MESH,
            ).wait_recv()

        put_column(lambda v: beside[at, v : v + 1], i * wide + j)

    def near(step, count):
        return {0: list(range(1, count + 1)), -1: [1], 1: [count]}[step]

    def far(step, count):
        return {0: list(range(1, count + 1)), -1: [0], 1: [count + 1]}[step]

    def places(at, pick):
        dx, dy = AROUND[at]
        return [i * wide + j for i in pick(dx, count_x) for j in pick(dy, count_y)]

    def hop(it, at):
        dx, dy = AROUND[at]
        other = len(AROUND) - 1 - at
        return pltpu.make_async_remote_copy(
            src_ref=send_halo.at[it, at],
            dst_ref=halo.at[it, other],
            send_sem=send_sem.at[it, at],
            recv_sem=recv_sem.at[it, other],
            device_id=(a + dx, b + dy),
            device_id_type=MESH,
        )

    def halo_start(it):
        for at, (dx, dy) in enumerate(AROUND):

            @pl.when(inside(dx, dy))
            def _():
                mine = places(at, near)
                for c in range(3):
                    for k, row in enumerate(mine):
                        send_halo[it, at, pl.ds(c * len(mine) + k, 1)] = basis[it, c, pl.ds(row, 1)]
                hop(it, at).start()

    def halo_finish(it):
        for at, (dx, dy) in enumerate(AROUND):

            @pl.when(inside(dx, dy))
            def _():
                hop(it, at).wait_send()
                pltpu.make_async_remote_copy(
                    src_ref=send_halo.at[it, at],
                    dst_ref=halo.at[it, at],
                    send_sem=send_sem.at[it, at],
                    recv_sem=recv_sem.at[it, at],
                    device_id=(a + dx, b + dy),
                    device_id_type=MESH,
                ).wait_recv()

        for at in range(len(AROUND)):
            theirs = places(at, far)
            for c in range(3):
                for k, row in enumerate(theirs):
                    basis[it, c, pl.ds(row, 1)] = halo[it, at, pl.ds(c * len(theirs) + k, 1)]

    def force_of(stress, c):
        first, second, third = (stress[VOIGT[c][d]] for d in range(3))
        first = first + down(first, 2)
        second = second + down(second, 2)
        third = down(third, 2) - third
        first = first + down(first, 1)
        rest = down(second, 1) - second + third + down(third, 1)
        return 0.25 * (down(first, 0) - first + rest + down(rest, 0))

    def applied(it):
        strain = strain_of(it)
        stress = []
        for i in range(6):
            value = None
            for j in range(6):
                term = elem[6 + PAIR_AT[(min(i, j), max(i, j))]] * strain[j]
                value = term if value is None else value + term
            stress.append(value)
        return [
            jnp.where(own, MASS * basis[it, c] + force_of(stress, c), 0.0) for c in range(3)
        ]

    def product(first, second):
        total = None
        for c in range(3):
            term = first[c] * second[c]
            total = term if total is None else total + term
        total = jnp.sum(jnp.where(own, total, 0.0), axis=0, keepdims=True)
        value = total[:, :128]
        for at in range(128, lanes, 128):
            value = value + total[:, at : at + 128]
        return value

    def stacked(pieces):
        tile_row = lax.broadcasted_iota(jnp.int32, (16, 128), 0)
        value = jnp.zeros((16, 128), jnp.float32)
        for at, piece in enumerate(pieces):
            value = jnp.where(tile_row == at, piece, value)
        return value

    def gather_start(src, dst, count, mine, send, recv, device):
        copies = []
        for step in range(1, count):
            copy = pltpu.make_async_remote_copy(
                src_ref=src,
                dst_ref=dst.at[mine],
                send_sem=send.at[step - 1],
                recv_sem=recv.at[step - 1],
                device_id=device(lax.rem(mine + step, count)),
                device_id_type=MESH,
            )
            copy.start()
            copies.append(copy)
        dst[mine] = src[...]
        return copies

    def gather_finish(copies, dst, count):
        for copy in copies:
            copy.wait()
        total = dst[0]
        for at in range(1, count):
            total = total + dst[at]
        return total

    stress = [elem[i] for i in range(6)]
    zero = jnp.zeros((rows, lanes), jnp.float32)
    for c in range(3):
        padded = jnp.concatenate(
            [jnp.zeros((wide + 1, lanes), jnp.float32)]
            + [
                piece
                for i in range(count_x)
                for piece in (load_ref[c, i], jnp.zeros((2, lanes), jnp.float32))
            ]
            + [jnp.zeros((rows - 1 - wide * (count_x + 1), lanes), jnp.float32)],
            axis=0,
        )
        basis[0, c] = jnp.where(own, padded - force_of(stress, c), zero)
    halo_start(0)
    halo_finish(0)
    grown = applied(0)
    for c in range(3):
        basis[1, c] = grown[c]
    halo_start(1)
    start = [basis[0, c] for c in range(3)]
    part[...] = stacked([product(start, start), product(grown, grown)])
    copies = gather_start(
        part, got_micro, n_micro, b, micro_send, micro_recv, lambda other: (a, other)
    )
    halo_finish(1)
    grown = applied(1)
    for c in range(3):
        basis[2, c] = grown[c]
    halo_start(2)
    middle[...] = gather_finish(copies, got_micro, n_micro)
    copies = gather_start(
        middle, got_macro, n_macro, a, macro_send, macro_recv, lambda other: (other, b)
    )
    halo_finish(2)
    totals = jnp.sum(gather_finish(copies, got_macro, n_macro), axis=1, keepdims=True)
    shift = jnp.sqrt(totals[1:2] / totals[0:1])
    scale = 1.0 / shift
    for c in range(3):
        u0, w1, w2 = basis[0, c], basis[1, c] * scale, basis[2, c] * (scale * scale)
        basis[1, c] = w1 - u0
        basis[2, c] = (w2 - w1) - (w1 - u0)

    def field(it):
        return [basis[it, c] for c in range(3)]

    def step(it):
        grown = applied(it)
        return [grown[c] * scale - jnp.where(own, basis[it, c], 0.0) for c in range(3)]

    moments = []
    for it in range(2, ITERS):
        grown = step(it)
        if it + 1 < ITERS:
            for c in range(3):
                basis[it + 1, c] = grown[c]
            halo_start(it + 1)
            if it == 2:
                for k in range(3):
                    moments.append(product(field(k), field(k)))
                    moments.append(product(field(k), field(k + 1)))
            else:
                moments.append(product(field(it), field(it)))
                moments.append(product(field(it), field(it + 1)))
            halo_finish(it + 1)
    moments.append(product(field(ITERS - 1), field(ITERS - 1)))
    moments.append(product(field(ITERS - 1), grown))
    sums = jnp.sum(stacked(moments), axis=1, keepdims=True)
    diagonal = lax.broadcasted_iota(jnp.int32, (16, 128), 0) == lax.broadcasted_iota(
        jnp.int32, (16, 128), 1
    )
    last_part[...] = jnp.sum(jnp.where(diagonal, sums, 0.0), axis=0, keepdims=True)

    def last_copy(step, other):
        return pltpu.make_async_remote_copy(
            src_ref=last_part,
            dst_ref=last_all.at[me],
            send_sem=last_send.at[step],
            recv_sem=last_recv.at[step],
            device_id=device(other),
            device_id_type=MESH,
        )

    every(total, lambda step: last_copy(step, lax.rem(me + step, total)).start())
    last_all[me] = last_part[...]
    every(total, lambda step: last_copy(step, lax.rem(me + step, total)).wait())
    totals = jnp.sum(last_all[...], axis=0)
    held = [totals[:, k : k + 1] for k in range(2 * ITERS)]

    def inner(first, second, extra=0):
        gathered = {}
        for i, x in enumerate(first):
            for j, y in enumerate(second):
                gathered.setdefault(i + j, []).append(x * y)
        value = None
        for degree, terms in gathered.items():
            total = terms[0]
            for term in terms[1:]:
                total = total + term
            total = total * held[degree + extra]
            value = total if value is None else value + total
        return value

    one = jnp.ones((1, 1), jnp.float32)
    left, toward, done = [one], [one], []
    norm = held[0]
    for it in range(ITERS):
        energy = inner(toward, toward) + inner(toward, toward, 1)
        length = norm / energy
        done = [x + length * scale * p for x, p in zip(done + [0.0], toward)]
        raised = [
            (toward[k] if k < len(toward) else 0.0) + (toward[k - 1] if k > 0 else 0.0)
            for k in range(len(toward) + 1)
        ]
        left = [
            (left[k] if k < len(left) else 0.0) - length * raised[k] for k in range(len(raised))
        ]
        if it + 1 < ITERS:
            fresh = inner(left, left)
            ratio = fresh / norm
            toward = [
                left[k] + (ratio * toward[k] if k < len(toward) else 0.0)
                for k in range(len(left))
            ]
            norm = fresh
    for c in range(3):
        fields = [basis[k, c] for k in range(ITERS)] + [grown[c]]
        moved, rest = None, None
        for k in range(ITERS + 1):
            if k < len(done):
                term = done[k] * fields[k]
                moved = term if moved is None else moved + term
            term = left[k] * fields[k]
            rest = term if rest is None else rest + term
        for i in range(count_x):
            low = (i + 1) * wide + 1
            inc_ref[c, i] = moved[low : low + count_y]
            res_ref[c, i] = rest[low : low + count_y]

    def sent(step, carry):
        other = lax.rem(b + step, n_micro)
        route_copy(other, b).wait_send()
        back_copy(other, b).wait_send()
        return carry

    lax.fori_loop(1, n_micro, sent, 0)


def shards(
    displacement,
    load,
    routes,
    counts,
    stiffness,
    precond,
    forcing,
    coupling,
    lame_first,
    lame_shear,
):
    _, count_x, count_y, lanes = displacement.shape
    points = count_x * count_y * lanes
    n_macro, n_micro = lax.axis_size("macro"), lax.axis_size("micro")
    capacity = max(2, 2 * points // n_micro)
    slots = -(-capacity // 128) * 128
    size = stiffness.shape[1]
    tall = -(-(6 + len(PAIRS)) // 8) * 8
    rows = -(-(count_x + 2) * (count_y + 2) // 8) * 8
    side = -(-3 * max(count_x, count_y) // 8) * 8
    total = n_macro * n_micro
    sides = count_x + count_y + 1
    vmem = pl.BlockSpec(memory_space=pltpu.VMEM)
    smem = pl.BlockSpec(memory_space=pltpu.SMEM)
    anywhere = pl.BlockSpec(memory_space=pl.ANY)
    dma = pltpu.SemaphoreType.DMA

    def held(*shape):
        return pltpu.VMEM(shape, jnp.float32)

    def half(*shape):
        return pltpu.VMEM(shape, jnp.bfloat16)

    def body(*refs):
        newton_kernel((count_x, count_y, lanes, n_macro, n_micro), *refs)

    return tuple(
        pl.pallas_call(
            body,
            out_shape=[jax.ShapeDtypeStruct(load.shape, jnp.float32)] * 2,
            in_specs=[anywhere] * 8 + [smem] * 2,
            out_specs=[vmem, vmem],
            scratch_shapes=[
                held(*displacement.shape),
                held(*load.shape),
                pltpu.VMEM((points // 128, 128), jnp.int32),
                pltpu.VMEM((points // 128, 128), jnp.int32),
                half(size, size),
                half(size, size),
                half(6, size),
                half(6, size),
                half(3 * size, 16),
                half(tall, size),
                half(tall, size),
                held(tall, size),
                half(n_micro * slots, points),
                held(3, *displacement.shape),
                held(8, points),
                held(n_micro, 8, slots),
                held(n_micro, 8, slots),
                held(n_micro, tall, slots),
                held(n_micro, tall, slots),
                held(tall, points),
                held(sides, tall, lanes),
                held(6 + len(PAIRS), rows, lanes),
                held(ITERS, 3, rows, lanes),
                held(ITERS, len(AROUND), side, lanes),
                held(ITERS, len(AROUND), side, lanes),
                held(16, 128),
                held(n_micro, 16, 128),
                held(16, 128),
                held(n_macro, 16, 128),
                held(1, 128),
                held(total, 1, 128),
                dma((8,)),
                dma((3,)),
                dma((3,)),
                dma((n_micro,)),
                dma((n_micro,)),
                dma((n_micro,)),
                dma((n_micro,)),
                dma((sides,)),
                dma((sides,)),
                dma((ITERS, len(AROUND))),
                dma((ITERS, len(AROUND))),
                dma((n_micro - 1,)),
                dma((n_micro - 1,)),
                dma((n_macro - 1,)),
                dma((n_macro - 1,)),
                dma((total,)),
                dma((total,)),
            ],
            compiler_params=pltpu.CompilerParams(collective_id=0, has_side_effects=True),
            name="newton_step",
        )(
            displacement,
            load,
            routes.reshape(points // 128, 128),
            counts.reshape(points // 128, 128),
            stiffness[0],
            precond[0],
            forcing[0],
            coupling[0].T,
            lame_first,
            lame_shear,
        )
    )


def solution(mesh):
    in_specs = (
        P(None, "macro", "micro", None),
        P(None, "macro", "micro", None),
        P("macro", "micro", None, None),
        P("macro", "micro", None),
        P("micro", None, None),
        P("micro", None, None),
        P("micro", None, None),
        P("micro", None, None),
        P("micro"),
        P("micro"),
    )
    out_specs = (P(None, "macro", "micro", None), P(None, "macro", "micro", None))
    return jax.shard_map(shards, mesh=mesh, in_specs=in_specs, out_specs=out_specs, check_vma=False)
```

```python
import jax
import jax.numpy as jnp
from jax import lax
from jax.experimental import pallas as pl
from jax.experimental.pallas import tpu as pltpu
from jax.sharding import PartitionSpec as P

ITMAX = 4
ITERS = 5


BETA = 0.1
OMEGA = 0.8
MASS = 0.1
VOIGT = ((0, 5, 4), (5, 1, 3), (4, 3, 2))
PAIRS = tuple((first, second) for first in range(6) for second in range(first, 6))
PAIR_AT = {pair: at for at, pair in enumerate(PAIRS)}
AROUND = tuple((dx, dy) for dx in (-1, 0, 1) for dy in (-1, 0, 1) if (dx, dy) != (0, 0))
MESH = pl.DeviceIdType.MESH


def strips_of(count_x, count_y):
    strips = []
    for dx, dy in AROUND:
        across = range(count_x if dx >= 0 else 1)
        if dy >= 0:
            strips.append(((dx, dy), 0, len(across) * count_y))
        else:
            strips += [((dx, dy), i * count_y, 1) for i in across]
    return strips


def newton_kernel(
    sizes,
    disp_in,
    load_in,
    routes_in,
    counts_in,
    stiff_in,
    pre_in,
    force_in,
    couple_in,
    first_ref,
    shear_ref,
    inc_ref,
    res_ref,
    disp_ref,
    load_ref,
    routes_ref,
    counts_ref,
    stiff,
    pre,
    force_ref,
    couple_ref,
    maps,
    couple,
    products,
    wide_products,
    spots,
    near_load,
    near_stress,
    outer,
    loads,
    near_disp,
    bundle,
    route_out,
    route_in,
    back_out,
    back_in,
    values,
    beside,
    elem,
    basis,
    send_halo,
    halo,
    part,
    got_micro,
    middle,
    got_macro,
    last_part,
    last_all,
    input_sem,
    disp_send,
    disp_recv,
    route_send,
    route_recv,
    back_send,
    back_recv,
    side_send,
    side_recv,
    send_sem,
    recv_sem,
    micro_send,
    micro_recv,
    macro_send,
    macro_recv,
    last_send,
    last_recv,
    load_send,
    load_recv,
    strip_send,
    strip_recv,
):
    count_x, count_y, lanes, n_macro, n_micro = sizes
    wide = count_y + 2
    rows = basis.shape[2]
    points = spots.shape[1]
    slots = spots.shape[0] // n_micro
    pairs = n_micro // 2
    groups = points // 128
    size = stiff.shape[0]
    tall = couple.shape[0]
    total = n_macro * n_micro
    a, b = lax.axis_index("macro"), lax.axis_index("micro")
    me = a * n_micro + b

    def device(other):
        return (other // n_micro, lax.rem(other, n_micro))

    def inside(dx, dy):
        test = None
        for place, step, count in ((a, dx, n_macro), (b, dy, n_micro)):
            if step != 0:
                good = (place > 0) if step < 0 else (place < count - 1)
                test = good if test is None else jnp.logical_and(test, good)
        return test

    barrier = pltpu.get_barrier_semaphore()

    def every(count, act):
        if count <= 32:
            for step in range(1, count):
                act(step)
        else:
            lax.fori_loop(1, count, lambda step, carry: (act(step), carry)[1], 0)

    def greet(row, column):
        pl.semaphore_signal(barrier, inc=1, device_id=(row, column), device_id_type=MESH)

    for step in range(1, n_macro):
        for aside in range(3):
            greet(lax.rem(a + step, n_macro), lax.rem(b + n_micro - 1 + aside, n_micro))
    every(n_micro, lambda step: greet(a, lax.rem(b + step, n_micro)))
    greeted = 3 * (n_macro - 1) + n_micro - 1
    inputs = {}
    for at, (name, source, target) in enumerate(
        (
            ("routes", routes_in, routes_ref),
            ("force", force_in, force_ref),
            ("couple", couple_in, couple_ref),
            ("counts", counts_in, counts_ref),
            ("disp", disp_in, disp_ref),
            ("load", load_in, load_ref),
            ("pre", pre_in, pre),
            ("stiff", stiff_in, stiff),
        )
    ):
        inputs[name] = pltpu.make_async_copy(source, target, input_sem.at[at])
        inputs[name].start()

    inputs["disp"].wait()
    after = ((1, 0), (0, 1), (1, 1))
    pl.semaphore_wait(barrier, greeted)

    def show(at):
        dx, dy = after[at]
        return pltpu.make_async_remote_copy(
            src_ref=disp_ref,
            dst_ref=near_disp.at[at],
            send_sem=disp_send.at[at],
            recv_sem=disp_recv.at[at],
            device_id=(a - dx, b - dy),
            device_id_type=MESH,
        )

    for at, (dx, dy) in enumerate(after):

        @pl.when(inside(-dx, -dy))
        def _():
            show(at).start()

    inputs["load"].wait()

    def load_copy(at):
        dx, dy = AROUND[at]
        other = len(AROUND) - 1 - at
        return pltpu.make_async_remote_copy(
            src_ref=load_ref,
            dst_ref=near_load.at[other],
            send_sem=load_send.at[at],
            recv_sem=load_recv.at[other],
            device_id=(a + dx, b + dy),
            device_id_type=MESH,
        )

    def load_arrival(at):
        dx, dy = AROUND[at]
        return pltpu.make_async_remote_copy(
            src_ref=load_ref,
            dst_ref=near_load.at[at],
            send_sem=load_send.at[at],
            recv_sem=load_recv.at[at],
            device_id=(a + dx, b + dy),
            device_id_type=MESH,
        )

    for at, (dx, dy) in enumerate(AROUND):

        @pl.when(inside(dx, dy))
        def _():
            load_copy(at).start()

        @pl.when(jnp.logical_not(inside(dx, dy)))
        def _():
            near_load[at] = jnp.zeros(near_load.shape[1:], jnp.float32)
            near_stress[at] = jnp.zeros(near_stress.shape[1:], jnp.float32)

    outer[...] = jnp.zeros(outer.shape, jnp.float32)
    loads[...] = jnp.zeros(loads.shape, jnp.float32)
    for name in ("routes", "force", "couple", "counts"):
        inputs[name].wait()
    force = force_ref[...].astype(jnp.float32)
    force = jnp.concatenate([force, jnp.zeros((2, size), jnp.float32)], axis=0)
    load_map = force.T
    wide_products[...] = jnp.zeros((tall, size), jnp.float32)
    coupling = couple_ref[...].astype(jnp.float32)
    wide_products[pl.ds(0, 6)] = coupling
    couple[...] = wide_products[...].astype(jnp.bfloat16)
    wide_products[pl.ds(0, 6)] = jnp.zeros((6, size), jnp.float32)
    for at, (first, second) in enumerate(PAIRS):
        wide_products[pl.ds(6 + at, 1)] = coupling[first : first + 1] * coupling[second : second + 1]
    products[...] = wide_products[...].astype(jnp.bfloat16)

    route = routes_ref[...]
    row_of = lax.broadcasted_iota(jnp.int32, (128, 128), 0)
    column_of = lax.broadcasted_iota(jnp.int32, (128, 128), 1)
    until = jnp.where(row_of <= column_of, 1.0, 0.0).astype(jnp.bfloat16)
    named = [jnp.where(route == owner, 1.0, 0.0) for owner in range(n_micro)]
    named = jnp.concatenate(named, axis=0).astype(jnp.bfloat16)
    inner_rank = jnp.dot(named, until, preferred_element_type=jnp.float32)
    whole = jnp.dot(
        named, jnp.ones((128, 128), jnp.bfloat16), preferred_element_type=jnp.float32
    ).astype(jnp.bfloat16)
    span = n_micro * groups
    row_of = lax.broadcasted_iota(jnp.int32, (span, span), 0)
    column_of = lax.broadcasted_iota(jnp.int32, (span, span), 1)
    ahead = jnp.logical_and(column_of < row_of, column_of // groups == row_of // groups)
    before = jnp.dot(
        jnp.where(ahead, 1.0, 0.0).astype(jnp.bfloat16), whole, preferred_element_type=jnp.float32
    )
    ranks = inner_rank + before - 1.0
    rank = jnp.zeros((groups, 128), jnp.float32)
    for owner in range(n_micro):
        rank = jnp.where(route == owner, ranks[owner * groups : (owner + 1) * groups], rank)
    slot_at = lax.broadcasted_iota(jnp.int32, (slots, 128), 0).astype(jnp.float32)

    def spot(owner, carry):
        local = jnp.where(route == owner, rank, -1.0)
        for g in range(groups):
            hit = jnp.where(local[g : g + 1] == slot_at, 1.0, 0.0)
            low = pl.multiple_of(owner * slots, slots)
            spots[pl.ds(low, slots), g * 128 : (g + 1) * 128] = hit.astype(jnp.bfloat16)
        return carry

    lax.fori_loop(0, n_micro, spot, 0)

    for it in range(basis.shape[0]):
        for c in range(3):
            basis[it, c] = jnp.zeros((rows, lanes), jnp.float32)
    elem[...] = jnp.zeros(elem.shape, jnp.float32)
    values[...] = jnp.zeros(values.shape, jnp.float32)
    bundle[...] = jnp.zeros(bundle.shape, jnp.float32)
    for g in range(groups):
        bundle[6:7, g * 128 : (g + 1) * 128] = counts_ref[g : g + 1].astype(jnp.float32)

    for at, (dx, dy) in enumerate(AROUND):

        @pl.when(jnp.logical_not(inside(dx, dy)))
        def _():
            for it in range(1, ITERS):
                halo[it, at] = jnp.zeros(halo.shape[2:], jnp.float32)

    for at, (dx, dy) in enumerate(after):

        @pl.when(jnp.logical_not(inside(dx, dy)))
        def _():
            near_disp[at] = jnp.zeros(near_disp.shape[1:], jnp.float32)

    owned = [(i, j) for i in range(count_x) for j in range(count_y)]
    column_at = {place: at for at, place in enumerate(owned)}
    handed = [((1, 0), (count_x - 1, j), (0, j + 1)) for j in range(count_y)]
    handed += [((0, 1), (i, count_y - 1), (i + 1, 0)) for i in range(count_x)]
    handed += [((1, 1), (count_x - 1, count_y - 1), (0, 0))]
    for at, ((dx, dy), _, _) in enumerate(handed):

        @pl.when(jnp.logical_not(inside(-dx, -dy)))
        def _():
            beside[at] = jnp.zeros(beside.shape[1:], jnp.float32)

    for name in ("pre", "stiff"):
        inputs[name].wait()

    def split(exact):
        high = exact.astype(jnp.bfloat16)
        return jnp.concatenate([high, (exact - high.astype(jnp.float32)).astype(jnp.bfloat16)], axis=1)

    def through(matrix, exact):
        moved = jnp.dot(matrix[...], split(exact), preferred_element_type=jnp.float32)
        return moved[:, :8] + moved[:, 8:]

    first_map = OMEGA * through(pre, load_map)
    misfit_map = through(stiff, first_map) - load_map
    for at, exact in enumerate((first_map, misfit_map, load_map)):
        maps[pl.ds(at * size, size)] = split(exact)
    for c in range(3):
        for i, j in owned:
            basis[0, c, pl.ds((i + 1) * wide + j + 1, 1)] = disp_ref[c, i, j : j + 1]
    for at, (dx, dy) in enumerate(after):

        @pl.when(inside(-dx, -dy))
        def _():
            show(at).wait_send()

        @pl.when(inside(dx, dy))
        def _():
            pltpu.make_async_remote_copy(
                src_ref=disp_ref,
                dst_ref=near_disp.at[at],
                send_sem=disp_send.at[at],
                recv_sem=disp_recv.at[at],
                device_id=(a + dx, b + dy),
                device_id_type=MESH,
            ).wait_recv()

    for c in range(3):
        for j in range(count_y):
            basis[0, c, pl.ds((count_x + 1) * wide + j + 1, 1)] = near_disp[0, c, 0, j : j + 1]
        for i in range(count_x):
            basis[0, c, pl.ds((i + 1) * wide + count_y + 1, 1)] = near_disp[1, c, i, 0:1]
        basis[0, c, pl.ds((count_x + 1) * wide + count_y + 1, 1)] = near_disp[2, c, 0, 0:1]

    row_at = lax.broadcasted_iota(jnp.int32, (rows, lanes), 0)
    lane_at = lax.broadcasted_iota(jnp.int32, (rows, lanes), 1)
    own = row_at < 0
    for i in range(1, count_x + 1):
        low = i * wide + 1
        own = jnp.logical_or(own, jnp.logical_and(row_at >= low, row_at < low + count_y))

    def up(value, axis):
        if axis == 2:
            moved = pltpu.roll(value, lanes - 1, 1)
            return jnp.where(lane_at == lanes - 1, 0.0, moved)
        return pltpu.roll(value, rows - (wide if axis == 0 else 1), 0)

    def down(value, axis):
        if axis == 2:
            return jnp.where(lane_at == 0, 0.0, pltpu.roll(value, 1, 1))
        return pltpu.roll(value, wide if axis == 0 else 1, 0)

    def strain_of(it):
        grads = []
        for c in range(3):
            value = basis[it, c]
            moved = up(value, 2)
            total, gap = value + moved, moved - value
            total_up, gap_up = up(total, 1), up(gap, 1)
            flat, slope_y, slope_z = total + total_up, total_up - total, gap + gap_up
            grads.append(
                (
                    0.25 * (up(flat, 0) - flat),
                    0.25 * (up(slope_y, 0) + slope_y),
                    0.25 * (up(slope_z, 0) + slope_z),
                )
            )
        return [
            grads[0][0],
            grads[1][1],
            grads[2][2],
            grads[1][2] + grads[2][1],
            grads[0][2] + grads[2][0],
            grads[0][1] + grads[1][0],
        ]

    strain = strain_of(0)
    for at, (i, j) in enumerate(owned):
        low = (i + 1) * wide + j + 1
        for k in range(6):
            bundle[k : k + 1, at * lanes : (at + 1) * lanes] = strain[k][low : low + 1]
    exact = bundle[...]
    high = exact.astype(jnp.bfloat16).astype(jnp.float32)
    both = jnp.concatenate([high, exact - high], axis=0).astype(jnp.bfloat16)

    def route_copy(other, mine):
        return pltpu.make_async_remote_copy(
            src_ref=route_out.at[other],
            dst_ref=route_in.at[mine],
            send_sem=route_send.at[other],
            recv_sem=route_recv.at[mine],
            device_id=(a, other),
            device_id_type=MESH,
        )

    chip, core = b // 2, lax.rem(b, 2)

    def pair_rows(place):
        return pl.ds(pl.multiple_of(place * (2 * slots), 2 * slots), 2 * slots)

    def hand_out(at, carry):
        place = lax.rem(chip + pairs - at, pairs)
        moved = lax.dot_general(
            both,
            spots[pair_rows(place)],
            (((1,), (1,)), ((), ())),
            preferred_element_type=jnp.float32,
        )
        moved = moved[:8] + moved[8:]
        for k in range(2):
            other = 2 * place + k
            piece = moved[:, k * slots : (k + 1) * slots]

            @pl.when(other != b)
            def _():
                route_out[other] = piece
                route_copy(other, b).start()

            @pl.when(other == b)
            def _():
                route_in[b] = piece

        return carry

    lax.fori_loop(0, pairs, hand_out, 0)


    lame_first, lame_shear = first_ref[0], shear_ref[0]
    tall_at = lax.broadcasted_iota(jnp.int32, (tall, 2 * slots), 0)
    on_trace = jnp.where(tall_at < 3, lame_first, 0.0)
    on_strain = jnp.where(tall_at < 3, 2.0 * lame_shear, jnp.where(tall_at < 6, lame_shear, 0.0))
    base = jnp.zeros((tall, 2 * slots), jnp.float32)
    for at, (i, j) in enumerate(PAIRS):
        if i == j:
            amount = lame_first + 2.0 * lame_shear if i < 3 else lame_shear
        elif j < 3:
            amount = lame_first
        else:
            continue
        base = jnp.where(tall_at == 6 + at, amount, base)

    def back_copy(other, mine):
        return pltpu.make_async_remote_copy(
            src_ref=back_out.at[other],
            dst_ref=back_in.at[mine],
            send_sem=back_send.at[other],
            recv_sem=back_recv.at[mine],
            device_id=(a, other),
            device_id_type=MESH,
        )

    def solve(at, carry):
        place = lax.rem(chip + at, pairs)
        taken = []
        for k in range(2):
            other = 2 * place + k

            @pl.when(other != b)
            def _():
                route_copy(b, other).wait_recv()

            taken.append(route_in[other])
        points_in = jnp.concatenate(taken, axis=1)
        sweeps = points_in[6:7]
        strain_in = points_in.astype(jnp.bfloat16)
        strain_in = jnp.concatenate([strain_in, strain_in], axis=0)

        def mapped(at):
            return jnp.dot(
                maps[pl.ds(at * size, size)], strain_in, preferred_element_type=jnp.float32
            )

        modes, misfit, modal_load = mapped(0), mapped(1), mapped(2)
        for sweep in range(1, ITMAX):
            if sweep > 1:
                misfit = jnp.dot(
                    stiff[...], modes.astype(jnp.bfloat16), preferred_element_type=jnp.float32
                )
                misfit = misfit - modal_load
            misfit = (misfit + BETA * jnp.tanh(modes)).astype(jnp.bfloat16)
            change = jnp.dot(pre[...], misfit, preferred_element_type=jnp.float32)
            modes = modes - jnp.where(sweeps > sweep, OMEGA, 0.0) * change
        bent = jnp.tanh(modes)
        slope = 1.0 - bent * bent
        trace = points_in[0:1] + points_in[1:2] + points_in[2:3]
        padded = jnp.concatenate(
            [points_in, jnp.zeros((tall - 8, 2 * slots), jnp.float32)], axis=0
        )
        answer = on_trace * trace + on_strain * padded + base
        answer = answer + jnp.dot(
            couple[...], modes.astype(jnp.bfloat16), preferred_element_type=jnp.float32
        )
        answer = answer + jnp.dot(
            products[...], slope.astype(jnp.bfloat16), preferred_element_type=jnp.float32
        )
        for k in range(2):
            other = 2 * place + k
            piece = answer[:, k * slots : (k + 1) * slots]

            @pl.when(other != b)
            def _():
                back_out[other] = piece
                back_copy(other, b).start()

            @pl.when(other == b)
            def _():
                back_in[b] = piece

        return carry

    lax.fori_loop(0, pairs, solve, 0)

    def take_back(at, carry):
        place = lax.rem(chip + pairs - at, pairs)
        taken = []
        for k in range(2):
            other = 2 * place + k

            @pl.when(other != b)
            def _():
                back_copy(b, other).wait_recv()

            taken.append(back_in[other])
        exact = jnp.concatenate(taken, axis=1)
        high = exact.astype(jnp.bfloat16).astype(jnp.float32)
        both = jnp.concatenate([high, exact - high], axis=0).astype(jnp.bfloat16)
        moved = jnp.dot(both, spots[pair_rows(place)], preferred_element_type=jnp.float32)
        values[...] += moved[:tall] + moved[tall:]
        return carry

    lax.fori_loop(0, pairs, take_back, 0)

    def side_copy(at):
        (dx, dy), place, _ = handed[at]
        low = column_at[place] * lanes
        return pltpu.make_async_remote_copy(
            src_ref=values.at[pl.ds(8, tall - 8), pl.ds(low, lanes)],
            dst_ref=beside.at[at],
            send_sem=side_send.at[at],
            recv_sem=side_recv.at[at],
            device_id=(a + dx, b + dy),
            device_id_type=MESH,
        )

    strips = strips_of(count_x, count_y)

    def strip_copy(at):
        (dx, dy), first, count = strips[at]
        columns = pl.ds(first * lanes, count * lanes)
        return pltpu.make_async_remote_copy(
            src_ref=values.at[pl.ds(0, 8), columns],
            dst_ref=near_stress.at[len(AROUND) - 1 - AROUND.index((dx, dy)), pl.ds(0, 8), columns],
            send_sem=strip_send.at[at],
            recv_sem=strip_recv.at[at],
            device_id=(a + dx, b + dy),
            device_id_type=MESH,
        )

    for at, ((dx, dy), _, _) in enumerate(strips):

        @pl.when(inside(dx, dy))
        def _():
            strip_copy(at).start()

    for at, ((dx, dy), _, _) in enumerate(handed):

        @pl.when(inside(dx, dy))
        def _():
            side_copy(at).start()

    for at, (dx, dy) in enumerate(AROUND):

        @pl.when(inside(dx, dy))
        def _():
            load_copy(at).wait_send()
            load_arrival(at).wait_recv()

    def span(step, count, below):
        if step == 0:
            return [(k, k) for k in range(count)]
        if step > 0:
            return [(count, 0)]
        return [(k - below, count + k - below) for k in range(below)]

    for c in range(3):
        for i in range(count_x):
            loads[c, pl.ds((i + 1) * wide + 1, count_y)] = load_ref[c, i]
        for at, (dx, dy) in enumerate(AROUND):
            for i, from_i in span(dx, count_x, 1):
                for j, from_j in span(dy, count_y, 1):
                    loads[c, pl.ds((i + 1) * wide + j + 1, 1)] = near_load[
                        at, c, from_i, from_j : from_j + 1
                    ]

    broad = count_y + 3

    def put_stress(read, i, j):
        for v in range(6):
            outer[v, pl.ds((i + 2) * broad + j + 2, 1)] = read(v)

    def put_tangent(read, row, first=6):
        for v in range(first, 6 + len(PAIRS)):
            elem[v, pl.ds(row, 1)] = read(v)

    for at, (i, j) in enumerate(owned):
        put_stress(lambda v: values[v : v + 1, at * lanes : (at + 1) * lanes], i, j)
        put_tangent(
            lambda v: values[v : v + 1, at * lanes : (at + 1) * lanes], (i + 1) * wide + j + 1
        )
    for at, ((dx, dy), _, _) in enumerate(strips):

        @pl.when(inside(dx, dy))
        def _():
            strip_copy(at).wait_send()

        @pl.when(inside(-dx, -dy))
        def _():
            strip_copy(at).wait_recv()

    for at, (dx, dy) in enumerate(AROUND):
        for i, from_i in span(dx, count_x, 2):
            for j, from_j in span(dy, count_y, 2):
                low = column_at[from_i, from_j] * lanes
                put_stress(lambda v: near_stress[at, v : v + 1, low : low + lanes], i, j)
    for at, ((dx, dy), place, (i, j)) in enumerate(handed):
        low = column_at[place] * lanes
        source = AROUND.index((-dx, -dy))
        for v in (6, 7):
            elem[v, pl.ds(i * wide + j, 1)] = near_stress[source, v : v + 1, low : low + lanes]
    for at, ((dx, dy), _, (i, j)) in enumerate(handed):

        @pl.when(inside(dx, dy))
        def _():
            side_copy(at).wait_send()

        @pl.when(inside(-dx, -dy))
        def _():
            side_copy(at).wait_recv()

        put_tangent(lambda v: beside[at, v - 8 : v - 7], i * wide + j, 8)

    def near(step, count):
        return {0: list(range(1, count + 1)), -1: [1], 1: [count]}[step]

    def far(step, count):
        return {0: list(range(1, count + 1)), -1: [0], 1: [count + 1]}[step]

    def places(at, pick):
        dx, dy = AROUND[at]
        return [i * wide + j for i in pick(dx, count_x) for j in pick(dy, count_y)]

    def hop(it, at):
        dx, dy = AROUND[at]
        other = len(AROUND) - 1 - at
        return pltpu.make_async_remote_copy(
            src_ref=send_halo.at[it, at],
            dst_ref=halo.at[it, other],
            send_sem=send_sem.at[it, at],
            recv_sem=recv_sem.at[it, other],
            device_id=(a + dx, b + dy),
            device_id_type=MESH,
        )

    def halo_start(it):
        for at, (dx, dy) in enumerate(AROUND):

            @pl.when(inside(dx, dy))
            def _():
                mine = places(at, near)
                for c in range(3):
                    for k, row in enumerate(mine):
                        send_halo[it, at, pl.ds(c * len(mine) + k, 1)] = basis[it, c, pl.ds(row, 1)]
                hop(it, at).start()

    def halo_finish(it):
        for at, (dx, dy) in enumerate(AROUND):

            @pl.when(inside(dx, dy))
            def _():
                hop(it, at).wait_send()
                pltpu.make_async_remote_copy(
                    src_ref=send_halo.at[it, at],
                    dst_ref=halo.at[it, at],
                    send_sem=send_sem.at[it, at],
                    recv_sem=recv_sem.at[it, at],
                    device_id=(a + dx, b + dy),
                    device_id_type=MESH,
                ).wait_recv()

        for at in range(len(AROUND)):
            theirs = places(at, far)
            for c in range(3):
                for k, row in enumerate(theirs):
                    basis[it, c, pl.ds(row, 1)] = halo[it, at, pl.ds(c * len(theirs) + k, 1)]

    def force_of(stress, c, down=down):
        first, second, third = (stress[VOIGT[c][d]] for d in range(3))
        first = first + down(first, 2)
        second = second + down(second, 2)
        third = down(third, 2) - third
        first = first + down(first, 1)
        rest = down(second, 1) - second + third + down(third, 1)
        return 0.25 * (down(first, 0) - first + rest + down(rest, 0))

    def applied(it):
        strain = strain_of(it)
        stress = []
        for i in range(6):
            value = None
            for j in range(6):
                term = elem[6 + PAIR_AT[(min(i, j), max(i, j))]] * strain[j]
                value = term if value is None else value + term
            stress.append(value)
        return [
            jnp.where(own, MASS * basis[it, c] + force_of(stress, c), 0.0) for c in range(3)
        ]

    def product(first, second):
        total = None
        for c in range(3):
            term = first[c] * second[c]
            total = term if total is None else total + term
        total = jnp.sum(jnp.where(own, total, 0.0), axis=0, keepdims=True)
        value = total[:, :128]
        for at in range(128, lanes, 128):
            value = value + total[:, at : at + 128]
        return value

    def stacked(pieces):
        tile_row = lax.broadcasted_iota(jnp.int32, (16, 128), 0)
        value = jnp.zeros((16, 128), jnp.float32)
        for at, piece in enumerate(pieces):
            value = jnp.where(tile_row == at, piece, value)
        return value

    def gather_start(src, dst, count, mine, send, recv, device):
        copies = []
        for step in range(1, count):
            copy = pltpu.make_async_remote_copy(
                src_ref=src,
                dst_ref=dst.at[mine],
                send_sem=send.at[step - 1],
                recv_sem=recv.at[step - 1],
                device_id=device(lax.rem(mine + step, count)),
                device_id_type=MESH,
            )
            copy.start()
            copies.append(copy)
        dst[mine] = src[...]
        return copies

    def gather_finish(copies, dst, count):
        for copy in copies:
            copy.wait()
        total = dst[0]
        for at in range(1, count):
            total = total + dst[at]
        return total

    broad_lane = lax.broadcasted_iota(jnp.int32, outer.shape[1:], 1)

    def back(value, axis):
        if axis == 2:
            return jnp.where(broad_lane == 0, 0.0, pltpu.roll(value, 1, 1))
        return pltpu.roll(value, broad if axis == 0 else 1, 0)

    row_x, row_y = row_at // wide, row_at % wide
    real = jnp.logical_and(
        jnp.logical_and(
            row_x >= jnp.where(a > 0, 0, 1),
            row_x <= jnp.where(a < n_macro - 1, count_x + 1, count_x),
        ),
        jnp.logical_and(
            row_y >= jnp.where(b > 0, 0, 1),
            row_y <= jnp.where(b < n_micro - 1, count_y + 1, count_y),
        ),
    )
    stress = [outer[v] for v in range(6)]
    for c in range(3):
        pushed = force_of(stress, c, back)
        for i in range(count_x + 2):
            low = (i + 1) * broad + 1
            basis[0, c, pl.ds(i * wide, wide)] = pushed[low : low + wide]
        basis[0, c] = jnp.where(real, loads[c] - basis[0, c], 0.0)
    grown = applied(0)
    for c in range(3):
        basis[1, c] = grown[c]
    halo_start(1)
    start = [basis[0, c] for c in range(3)]
    part[...] = stacked([product(start, start), product(grown, grown)])
    copies = gather_start(
        part, got_micro, n_micro, b, micro_send, micro_recv, lambda other: (a, other)
    )
    halo_finish(1)
    grown = applied(1)
    for c in range(3):
        basis[2, c] = grown[c]
    halo_start(2)
    middle[...] = gather_finish(copies, got_micro, n_micro)
    copies = gather_start(
        middle, got_macro, n_macro, a, macro_send, macro_recv, lambda other: (other, b)
    )
    halo_finish(2)
    totals = jnp.sum(gather_finish(copies, got_macro, n_macro), axis=1, keepdims=True)
    shift = jnp.sqrt(totals[1:2] / totals[0:1])
    scale = 1.0 / shift
    for c in range(3):
        u0, w1, w2 = basis[0, c], basis[1, c] * scale, basis[2, c] * (scale * scale)
        basis[1, c] = w1 - u0
        basis[2, c] = (w2 - w1) - (w1 - u0)

    def field(it):
        return [basis[it, c] for c in range(3)]

    def step(it):
        grown = applied(it)
        return [grown[c] * scale - jnp.where(own, basis[it, c], 0.0) for c in range(3)]

    moments = []
    for it in range(2, ITERS):
        grown = step(it)
        if it + 1 < ITERS:
            for c in range(3):
                basis[it + 1, c] = grown[c]
            halo_start(it + 1)
            if it == 2:
                for k in range(3):
                    moments.append(product(field(k), field(k)))
                    moments.append(product(field(k), field(k + 1)))
            else:
                moments.append(product(field(it), field(it)))
                moments.append(product(field(it), field(it + 1)))
            halo_finish(it + 1)
    moments.append(product(field(ITERS - 1), field(ITERS - 1)))
    moments.append(product(field(ITERS - 1), grown))
    sums = jnp.sum(stacked(moments), axis=1, keepdims=True)
    diagonal = lax.broadcasted_iota(jnp.int32, (16, 128), 0) == lax.broadcasted_iota(
        jnp.int32, (16, 128), 1
    )
    last_part[...] = jnp.sum(jnp.where(diagonal, sums, 0.0), axis=0, keepdims=True)

    def last_copy(step, other):
        return pltpu.make_async_remote_copy(
            src_ref=last_part,
            dst_ref=last_all.at[me],
            send_sem=last_send.at[step],
            recv_sem=last_recv.at[step],
            device_id=device(other),
            device_id_type=MESH,
        )

    every(total, lambda step: last_copy(step, lax.rem(me + step, total)).start())
    last_all[me] = last_part[...]
    every(total, lambda step: last_copy(step, lax.rem(me + step, total)).wait())
    totals = jnp.sum(last_all[...], axis=0)
    held = [totals[:, k : k + 1] for k in range(2 * ITERS)]

    def inner(first, second, extra=0):
        gathered = {}
        for i, x in enumerate(first):
            for j, y in enumerate(second):
                gathered.setdefault(i + j, []).append(x * y)
        value = None
        for degree, terms in gathered.items():
            total = terms[0]
            for term in terms[1:]:
                total = total + term
            total = total * held[degree + extra]
            value = total if value is None else value + total
        return value

    one = jnp.ones((1, 1), jnp.float32)
    left, toward, done = [one], [one], []
    norm = held[0]
    for it in range(ITERS):
        energy = inner(toward, toward) + inner(toward, toward, 1)
        length = norm / energy
        done = [x + length * scale * p for x, p in zip(done + [0.0], toward)]
        raised = [
            (toward[k] if k < len(toward) else 0.0) + (toward[k - 1] if k > 0 else 0.0)
            for k in range(len(toward) + 1)
        ]
        left = [
            (left[k] if k < len(left) else 0.0) - length * raised[k] for k in range(len(raised))
        ]
        if it + 1 < ITERS:
            fresh = inner(left, left)
            ratio = fresh / norm
            toward = [
                left[k] + (ratio * toward[k] if k < len(toward) else 0.0)
                for k in range(len(left))
            ]
            norm = fresh
    for c in range(3):
        fields = [basis[k, c] for k in range(ITERS)] + [grown[c]]
        moved, rest = None, None
        for k in range(ITERS + 1):
            if k < len(done):
                term = done[k] * fields[k]
                moved = term if moved is None else moved + term
            term = left[k] * fields[k]
            rest = term if rest is None else rest + term
        for i in range(count_x):
            low = (i + 1) * wide + 1
            inc_ref[c, i] = moved[low : low + count_y]
            res_ref[c, i] = rest[low : low + count_y]

    def sent(step, carry):
        other = lax.rem(b + step, n_micro)
        route_copy(other, b).wait_send()
        back_copy(other, b).wait_send()
        return carry

    lax.fori_loop(1, n_micro, sent, 0)


def shards(
    displacement,
    load,
    routes,
    counts,
    stiffness,
    precond,
    forcing,
    coupling,
    lame_first,
    lame_shear,
):
    _, count_x, count_y, lanes = displacement.shape
    points = count_x * count_y * lanes
    n_macro, n_micro = lax.axis_size("macro"), lax.axis_size("micro")
    capacity = max(2, 2 * points // n_micro)
    slots = -(-capacity // 128) * 128
    size = stiffness.shape[1]
    tall = -(-(6 + len(PAIRS)) // 8) * 8
    rows = -(-(count_x + 2) * (count_y + 2) // 8) * 8
    side = -(-3 * max(count_x, count_y) // 8) * 8
    total = n_macro * n_micro
    sides = count_x + count_y + 1
    outer_rows = -(-(count_x + 3) * (count_y + 3) // 8) * 8
    strips = len(strips_of(count_x, count_y))
    vmem = pl.BlockSpec(memory_space=pltpu.VMEM)
    smem = pl.BlockSpec(memory_space=pltpu.SMEM)
    anywhere = pl.BlockSpec(memory_space=pl.ANY)
    dma = pltpu.SemaphoreType.DMA

    def held(*shape):
        return pltpu.VMEM(shape, jnp.float32)

    def half(*shape):
        return pltpu.VMEM(shape, jnp.bfloat16)

    def body(*refs):
        newton_kernel((count_x, count_y, lanes, n_macro, n_micro), *refs)

    return tuple(
        pl.pallas_call(
            body,
            out_shape=[jax.ShapeDtypeStruct(load.shape, jnp.float32)] * 2,
            in_specs=[anywhere] * 8 + [smem] * 2,
            out_specs=[vmem, vmem],
            scratch_shapes=[
                held(*displacement.shape),
                held(*load.shape),
                pltpu.VMEM((points // 128, 128), jnp.int32),
                pltpu.VMEM((points // 128, 128), jnp.int32),
                half(size, size),
                half(size, size),
                half(6, size),
                half(6, size),
                half(3 * size, 16),
                half(tall, size),
                half(tall, size),
                held(tall, size),
                half(n_micro * slots, points),
                held(len(AROUND), *load.shape),
                held(len(AROUND), 8, points),
                held(6, outer_rows, lanes),
                held(3, rows, lanes),
                held(3, *displacement.shape),
                held(8, points),
                held(n_micro, 8, slots),
                held(n_micro, 8, slots),
                held(n_micro, tall, slots),
                held(n_micro, tall, slots),
                held(tall, points),
                held(sides, tall - 8, lanes),
                held(6 + len(PAIRS), rows, lanes),
                held(ITERS, 3, rows, lanes),
                held(ITERS, len(AROUND), side, lanes),
                held(ITERS, len(AROUND), side, lanes),
                held(16, 128),
                held(n_micro, 16, 128),
                held(16, 128),
                held(n_macro, 16, 128),
                held(1, 128),
                held(total, 1, 128),
                dma((8,)),
                dma((3,)),
                dma((3,)),
                dma((n_micro,)),
                dma((n_micro,)),
                dma((n_micro,)),
                dma((n_micro,)),
                dma((sides,)),
                dma((sides,)),
                dma((ITERS, len(AROUND))),
                dma((ITERS, len(AROUND))),
                dma((n_micro - 1,)),
                dma((n_micro - 1,)),
                dma((n_macro - 1,)),
                dma((n_macro - 1,)),
                dma((total,)),
                dma((total,)),
                dma((len(AROUND),)),
                dma((len(AROUND),)),
                dma((strips,)),
                dma((strips,)),
            ],
            compiler_params=pltpu.CompilerParams(collective_id=0, has_side_effects=True),
            name="newton_step",
        )(
            displacement,
            load,
            routes.reshape(points // 128, 128),
            counts.reshape(points // 128, 128),
            stiffness[0],
            precond[0],
            forcing[0],
            coupling[0].T,
            lame_first,
            lame_shear,
        )
    )


def solution(mesh):
    in_specs = (
        P(None, "macro", "micro", None),
        P(None, "macro", "micro", None),
        P("macro", "micro", None, None),
        P("macro", "micro", None),
        P("micro", None, None),
        P("micro", None, None),
        P("micro", None, None),
        P("micro", None, None),
        P("micro"),
        P("micro"),
    )
    out_specs = (P(None, "macro", "micro", None), P(None, "macro", "micro", None))
    return jax.shard_map(shards, mesh=mesh, in_specs=in_specs, out_specs=out_specs, check_vma=False)
```

```python
import jax
import jax.numpy as jnp
from jax import lax
from jax.experimental import pallas as pl
from jax.experimental.pallas import tpu as pltpu
from jax.sharding import PartitionSpec as P

ITMAX = 4
ITERS = 5


BETA = 0.1
OMEGA = 0.8
MASS = 0.1
VOIGT = ((0, 5, 4), (5, 1, 3), (4, 3, 2))
PAIRS = tuple((first, second) for first in range(6) for second in range(first, 6))
PAIR_AT = {pair: at for at, pair in enumerate(PAIRS)}
AROUND = tuple((dx, dy) for dx in (-1, 0, 1) for dy in (-1, 0, 1) if (dx, dy) != (0, 0))
MESH = pl.DeviceIdType.MESH


def strips_of(count_x, count_y):
    strips = []
    for dx, dy in AROUND:
        across = range(count_x if dx >= 0 else 1)
        if dy >= 0:
            strips.append(((dx, dy), 0, len(across) * count_y))
        else:
            strips += [((dx, dy), i * count_y, 1) for i in across]
    return strips


def newton_kernel(
    sizes,
    disp_in,
    load_in,
    routes_in,
    counts_in,
    stiff_in,
    pre_in,
    force_in,
    couple_in,
    first_ref,
    shear_ref,
    inc_ref,
    res_ref,
    disp_ref,
    load_ref,
    routes_ref,
    counts_ref,
    stiff,
    pre,
    force_ref,
    couple_ref,
    maps,
    couple,
    products,
    wide_products,
    spots,
    near_load,
    near_stress,
    outer,
    loads,
    near_disp,
    bundle,
    route_out,
    route_in,
    back_out,
    back_in,
    values,
    beside,
    elem,
    basis,
    send_halo,
    halo,
    part,
    got_micro,
    middle,
    got_macro,
    last_part,
    last_all,
    input_sem,
    disp_send,
    disp_recv,
    route_send,
    route_recv,
    back_send,
    back_recv,
    side_send,
    side_recv,
    send_sem,
    recv_sem,
    sum_send,
    sum_recv,
):
    count_x, count_y, lanes, n_macro, n_micro = sizes
    wide = count_y + 2
    rows = basis.shape[2]
    points = spots.shape[1]
    slots = spots.shape[0] // n_micro
    pairs = n_micro // 2
    groups = points // 128
    size = stiff.shape[0]
    tall = couple.shape[0]
    total = n_macro * n_micro
    a, b = lax.axis_index("macro"), lax.axis_index("micro")
    me = a * n_micro + b

    def device(other):
        return (other // n_micro, lax.rem(other, n_micro))

    def inside(dx, dy):
        test = None
        for place, step, count in ((a, dx, n_macro), (b, dy, n_micro)):
            if step != 0:
                good = (place > 0) if step < 0 else (place < count - 1)
                test = good if test is None else jnp.logical_and(test, good)
        return test

    barrier = pltpu.get_barrier_semaphore()

    def every(count, act):
        if count <= 32:
            for step in range(1, count):
                act(step)
        else:
            lax.fori_loop(1, count, lambda step, carry: (act(step), carry)[1], 0)

    def greet(row, column):
        pl.semaphore_signal(barrier, inc=1, device_id=(row, column), device_id_type=MESH)

    for step in range(1, n_macro):
        for aside in range(3):
            greet(lax.rem(a + step, n_macro), lax.rem(b + n_micro - 1 + aside, n_micro))
    every(n_micro, lambda step: greet(a, lax.rem(b + step, n_micro)))
    greeted = 3 * (n_macro - 1) + n_micro - 1
    inputs = {}
    for at, (name, source, target) in enumerate(
        (
            ("routes", routes_in, routes_ref),
            ("force", force_in, force_ref),
            ("couple", couple_in, couple_ref),
            ("counts", counts_in, counts_ref),
            ("disp", disp_in, disp_ref),
            ("load", load_in, load_ref),
            ("pre", pre_in, pre),
            ("stiff", stiff_in, stiff),
        )
    ):
        inputs[name] = pltpu.make_async_copy(source, target, input_sem.at[at])
        inputs[name].start()

    inputs["disp"].wait()
    after = ((1, 0), (0, 1), (1, 1))
    pl.semaphore_wait(barrier, greeted)

    def show(at):
        dx, dy = after[at]
        return pltpu.make_async_remote_copy(
            src_ref=disp_ref,
            dst_ref=near_disp.at[at],
            send_sem=disp_send.at[at],
            recv_sem=disp_recv.at[at],
            device_id=(a - dx, b - dy),
            device_id_type=MESH,
        )

    for at, (dx, dy) in enumerate(after):

        @pl.when(inside(-dx, -dy))
        def _():
            show(at).start()

    inputs["load"].wait()

    def load_copy(at):
        dx, dy = AROUND[at]
        other = len(AROUND) - 1 - at
        return pltpu.make_async_remote_copy(
            src_ref=load_ref,
            dst_ref=near_load.at[other],
            send_sem=send_sem.at[0, at],
            recv_sem=recv_sem.at[0, other],
            device_id=(a + dx, b + dy),
            device_id_type=MESH,
        )

    def load_arrival(at):
        dx, dy = AROUND[at]
        return pltpu.make_async_remote_copy(
            src_ref=load_ref,
            dst_ref=near_load.at[at],
            send_sem=send_sem.at[0, at],
            recv_sem=recv_sem.at[0, at],
            device_id=(a + dx, b + dy),
            device_id_type=MESH,
        )

    for at, (dx, dy) in enumerate(AROUND):

        @pl.when(inside(dx, dy))
        def _():
            load_copy(at).start()

        @pl.when(jnp.logical_not(inside(dx, dy)))
        def _():
            near_load[at] = jnp.zeros(near_load.shape[1:], jnp.float32)
            near_stress[at] = jnp.zeros(near_stress.shape[1:], jnp.float32)

    outer[...] = jnp.zeros(outer.shape, jnp.float32)
    loads[...] = jnp.zeros(loads.shape, jnp.float32)
    for name in ("routes", "force", "couple", "counts"):
        inputs[name].wait()
    force = force_ref[...].astype(jnp.float32)
    force = jnp.concatenate([force, jnp.zeros((2, size), jnp.float32)], axis=0)
    load_map = force.T
    wide_products[...] = jnp.zeros((tall, size), jnp.float32)
    coupling = couple_ref[...].astype(jnp.float32)
    wide_products[pl.ds(0, 6)] = coupling
    couple[...] = wide_products[...].astype(jnp.bfloat16)
    wide_products[pl.ds(0, 6)] = jnp.zeros((6, size), jnp.float32)
    for at, (first, second) in enumerate(PAIRS):
        wide_products[pl.ds(6 + at, 1)] = coupling[first : first + 1] * coupling[second : second + 1]
    products[...] = wide_products[...].astype(jnp.bfloat16)

    route = routes_ref[...]
    row_of = lax.broadcasted_iota(jnp.int32, (128, 128), 0)
    column_of = lax.broadcasted_iota(jnp.int32, (128, 128), 1)
    until = jnp.where(row_of <= column_of, 1.0, 0.0).astype(jnp.bfloat16)
    named = [jnp.where(route == owner, 1.0, 0.0) for owner in range(n_micro)]
    named = jnp.concatenate(named, axis=0).astype(jnp.bfloat16)
    inner_rank = jnp.dot(named, until, preferred_element_type=jnp.float32)
    whole = jnp.dot(
        named, jnp.ones((128, 128), jnp.bfloat16), preferred_element_type=jnp.float32
    ).astype(jnp.bfloat16)
    span = n_micro * groups
    row_of = lax.broadcasted_iota(jnp.int32, (span, span), 0)
    column_of = lax.broadcasted_iota(jnp.int32, (span, span), 1)
    ahead = jnp.logical_and(column_of < row_of, column_of // groups == row_of // groups)
    before = jnp.dot(
        jnp.where(ahead, 1.0, 0.0).astype(jnp.bfloat16), whole, preferred_element_type=jnp.float32
    )
    ranks = inner_rank + before - 1.0
    rank = jnp.zeros((groups, 128), jnp.float32)
    for owner in range(n_micro):
        rank = jnp.where(route == owner, ranks[owner * groups : (owner + 1) * groups], rank)
    slot_at = lax.broadcasted_iota(jnp.int32, (slots, 128), 0).astype(jnp.float32)

    def spot(owner, carry):
        local = jnp.where(route == owner, rank, -1.0)
        for g in range(groups):
            hit = jnp.where(local[g : g + 1] == slot_at, 1.0, 0.0)
            low = pl.multiple_of(owner * slots, slots)
            spots[pl.ds(low, slots), g * 128 : (g + 1) * 128] = hit.astype(jnp.bfloat16)
        return carry

    lax.fori_loop(0, n_micro, spot, 0)

    for it in range(basis.shape[0]):
        for c in range(3):
            basis[it, c] = jnp.zeros((rows, lanes), jnp.float32)
    elem[...] = jnp.zeros(elem.shape, jnp.float32)
    values[...] = jnp.zeros(values.shape, jnp.float32)
    bundle[...] = jnp.zeros(bundle.shape, jnp.float32)
    for g in range(groups):
        bundle[6:7, g * 128 : (g + 1) * 128] = counts_ref[g : g + 1].astype(jnp.float32)

    for at, (dx, dy) in enumerate(AROUND):

        @pl.when(jnp.logical_not(inside(dx, dy)))
        def _():
            for it in range(1, ITERS):
                halo[it, at] = jnp.zeros(halo.shape[2:], jnp.float32)

    for at, (dx, dy) in enumerate(after):

        @pl.when(jnp.logical_not(inside(dx, dy)))
        def _():
            near_disp[at] = jnp.zeros(near_disp.shape[1:], jnp.float32)

    owned = [(i, j) for i in range(count_x) for j in range(count_y)]
    column_at = {place: at for at, place in enumerate(owned)}
    handed = [((1, 0), (count_x - 1, j), (0, j + 1)) for j in range(count_y)]
    handed += [((0, 1), (i, count_y - 1), (i + 1, 0)) for i in range(count_x)]
    handed += [((1, 1), (count_x - 1, count_y - 1), (0, 0))]
    for at, ((dx, dy), _, _) in enumerate(handed):

        @pl.when(jnp.logical_not(inside(-dx, -dy)))
        def _():
            beside[at] = jnp.zeros(beside.shape[1:], jnp.float32)

    for name in ("pre", "stiff"):
        inputs[name].wait()

    def split(exact):
        high = exact.astype(jnp.bfloat16)
        return jnp.concatenate([high, (exact - high.astype(jnp.float32)).astype(jnp.bfloat16)], axis=1)

    def through(matrix, exact):
        moved = jnp.dot(matrix[...], split(exact), preferred_element_type=jnp.float32)
        return moved[:, :8] + moved[:, 8:]

    first_map = OMEGA * through(pre, load_map)
    misfit_map = through(stiff, first_map) - load_map
    for at, exact in enumerate((first_map, misfit_map, load_map)):
        maps[pl.ds(at * size, size)] = split(exact)
    for c in range(3):
        for i, j in owned:
            basis[0, c, pl.ds((i + 1) * wide + j + 1, 1)] = disp_ref[c, i, j : j + 1]
    for at, (dx, dy) in enumerate(after):

        @pl.when(inside(-dx, -dy))
        def _():
            show(at).wait_send()

        @pl.when(inside(dx, dy))
        def _():
            pltpu.make_async_remote_copy(
                src_ref=disp_ref,
                dst_ref=near_disp.at[at],
                send_sem=disp_send.at[at],
                recv_sem=disp_recv.at[at],
                device_id=(a + dx, b + dy),
                device_id_type=MESH,
            ).wait_recv()

    for c in range(3):
        for j in range(count_y):
            basis[0, c, pl.ds((count_x + 1) * wide + j + 1, 1)] = near_disp[0, c, 0, j : j + 1]
        for i in range(count_x):
            basis[0, c, pl.ds((i + 1) * wide + count_y + 1, 1)] = near_disp[1, c, i, 0:1]
        basis[0, c, pl.ds((count_x + 1) * wide + count_y + 1, 1)] = near_disp[2, c, 0, 0:1]

    row_at = lax.broadcasted_iota(jnp.int32, (rows, lanes), 0)
    lane_at = lax.broadcasted_iota(jnp.int32, (rows, lanes), 1)
    own = row_at < 0
    for i in range(1, count_x + 1):
        low = i * wide + 1
        own = jnp.logical_or(own, jnp.logical_and(row_at >= low, row_at < low + count_y))

    def up(value, axis):
        if axis == 2:
            moved = pltpu.roll(value, lanes - 1, 1)
            return jnp.where(lane_at == lanes - 1, 0.0, moved)
        return pltpu.roll(value, rows - (wide if axis == 0 else 1), 0)

    def down(value, axis):
        if axis == 2:
            return jnp.where(lane_at == 0, 0.0, pltpu.roll(value, 1, 1))
        return pltpu.roll(value, wide if axis == 0 else 1, 0)

    def strain_of(it):
        grads = []
        for c in range(3):
            value = basis[it, c]
            moved = up(value, 2)
            total, gap = value + moved, moved - value
            total_up, gap_up = up(total, 1), up(gap, 1)
            flat, slope_y, slope_z = total + total_up, total_up - total, gap + gap_up
            grads.append(
                (
                    0.25 * (up(flat, 0) - flat),
                    0.25 * (up(slope_y, 0) + slope_y),
                    0.25 * (up(slope_z, 0) + slope_z),
                )
            )
        return [
            grads[0][0],
            grads[1][1],
            grads[2][2],
            grads[1][2] + grads[2][1],
            grads[0][2] + grads[2][0],
            grads[0][1] + grads[1][0],
        ]

    strain = strain_of(0)
    for at, (i, j) in enumerate(owned):
        low = (i + 1) * wide + j + 1
        for k in range(6):
            bundle[k : k + 1, at * lanes : (at + 1) * lanes] = strain[k][low : low + 1]
    exact = bundle[...]
    high = exact.astype(jnp.bfloat16).astype(jnp.float32)
    both = jnp.concatenate([high, exact - high], axis=0).astype(jnp.bfloat16)

    def route_copy(other, mine):
        return pltpu.make_async_remote_copy(
            src_ref=route_out.at[other],
            dst_ref=route_in.at[mine],
            send_sem=route_send.at[0],
            recv_sem=route_recv.at[mine],
            device_id=(a, other),
            device_id_type=MESH,
        )

    chip, core = b // 2, lax.rem(b, 2)

    def pair_rows(place):
        return pl.ds(pl.multiple_of(place * (2 * slots), 2 * slots), 2 * slots)

    def hand_out(at, carry):
        place = lax.rem(chip + pairs - at, pairs)
        moved = lax.dot_general(
            both,
            spots[pair_rows(place)],
            (((1,), (1,)), ((), ())),
            preferred_element_type=jnp.float32,
        )
        moved = moved[:8] + moved[8:]
        for k in range(2):
            other = 2 * place + k
            piece = moved[:, k * slots : (k + 1) * slots]

            @pl.when(other != b)
            def _():
                route_out[other] = piece
                route_copy(other, b).start()

            @pl.when(other == b)
            def _():
                route_in[b] = piece

        return carry

    lax.fori_loop(0, pairs, hand_out, 0)


    lame_first, lame_shear = first_ref[...], shear_ref[...]
    tall_at = lax.broadcasted_iota(jnp.int32, (tall, 2 * slots), 0)
    on_trace = jnp.where(tall_at < 3, lame_first, 0.0)
    on_strain = jnp.where(tall_at < 3, 2.0 * lame_shear, jnp.where(tall_at < 6, lame_shear, 0.0))
    base = jnp.zeros((tall, 2 * slots), jnp.float32)
    for at, (i, j) in enumerate(PAIRS):
        if i == j:
            amount = lame_first + 2.0 * lame_shear if i < 3 else lame_shear
        elif j < 3:
            amount = lame_first
        else:
            continue
        base = jnp.where(tall_at == 6 + at, amount, base)

    def back_copy(other, mine):
        return pltpu.make_async_remote_copy(
            src_ref=back_out.at[other],
            dst_ref=back_in.at[mine],
            send_sem=back_send.at[0],
            recv_sem=back_recv.at[mine],
            device_id=(a, other),
            device_id_type=MESH,
        )

    def solve(at, carry):
        place = lax.rem(chip + at, pairs)
        taken = []
        for k in range(2):
            other = 2 * place + k

            @pl.when(other != b)
            def _():
                route_copy(b, other).wait_recv()

            taken.append(route_in[other])
        points_in = jnp.concatenate(taken, axis=1)
        sweeps = points_in[6:7]
        strain_in = points_in.astype(jnp.bfloat16)
        strain_in = jnp.concatenate([strain_in, strain_in], axis=0)

        def mapped(at):
            return jnp.dot(
                maps[pl.ds(at * size, size)], strain_in, preferred_element_type=jnp.float32
            )

        modes, misfit, modal_load = mapped(0), mapped(1), mapped(2)
        for sweep in range(1, ITMAX):
            if sweep > 1:
                misfit = jnp.dot(
                    stiff[...], modes.astype(jnp.bfloat16), preferred_element_type=jnp.float32
                )
                misfit = misfit - modal_load
            misfit = (misfit + BETA * jnp.tanh(modes)).astype(jnp.bfloat16)
            change = jnp.dot(pre[...], misfit, preferred_element_type=jnp.float32)
            modes = modes - jnp.where(sweeps > sweep, OMEGA, 0.0) * change
        bent = jnp.tanh(modes)
        slope = 1.0 - bent * bent
        trace = points_in[0:1] + points_in[1:2] + points_in[2:3]
        padded = jnp.concatenate(
            [points_in, jnp.zeros((tall - 8, 2 * slots), jnp.float32)], axis=0
        )
        answer = on_trace * trace + on_strain * padded + base
        answer = answer + jnp.dot(
            couple[...], modes.astype(jnp.bfloat16), preferred_element_type=jnp.float32
        )
        answer = answer + jnp.dot(
            products[...], slope.astype(jnp.bfloat16), preferred_element_type=jnp.float32
        )
        for k in range(2):
            other = 2 * place + k
            piece = answer[:, k * slots : (k + 1) * slots]

            @pl.when(other != b)
            def _():
                back_out[other] = piece
                back_copy(other, b).start()

            @pl.when(other == b)
            def _():
                back_in[b] = piece

        return carry

    lax.fori_loop(0, pairs, solve, 0)

    def take_back(at, carry):
        place = lax.rem(chip + pairs - at, pairs)
        taken = []
        for k in range(2):
            other = 2 * place + k

            @pl.when(other != b)
            def _():
                back_copy(b, other).wait_recv()

            taken.append(back_in[other])
        exact = jnp.concatenate(taken, axis=1)
        high = exact.astype(jnp.bfloat16).astype(jnp.float32)
        both = jnp.concatenate([high, exact - high], axis=0).astype(jnp.bfloat16)
        moved = jnp.dot(both, spots[pair_rows(place)], preferred_element_type=jnp.float32)
        values[...] += moved[:tall] + moved[tall:]
        return carry

    lax.fori_loop(0, pairs, take_back, 0)

    def side_copy(at):
        (dx, dy), place, _ = handed[at]
        low = column_at[place] * lanes
        return pltpu.make_async_remote_copy(
            src_ref=values.at[pl.ds(8, tall - 8), pl.ds(low, lanes)],
            dst_ref=beside.at[at],
            send_sem=side_send.at[after.index((dx, dy))],
            recv_sem=side_recv.at[after.index((dx, dy))],
            device_id=(a + dx, b + dy),
            device_id_type=MESH,
        )

    strips = strips_of(count_x, count_y)

    def strip_copy(at):
        (dx, dy), first, count = strips[at]
        columns = pl.ds(first * lanes, count * lanes)
        way = AROUND.index((dx, dy))
        other = len(AROUND) - 1 - way
        return pltpu.make_async_remote_copy(
            src_ref=values.at[pl.ds(0, 8), columns],
            dst_ref=near_stress.at[other, pl.ds(0, 8), columns],
            send_sem=send_sem.at[1, way],
            recv_sem=recv_sem.at[1, other],
            device_id=(a + dx, b + dy),
            device_id_type=MESH,
        )

    def strips_moved(way, sent):
        dx, dy = AROUND[way]
        offset = (dx, dy) if sent else (-dx, -dy)
        count = sum(count for place, _, count in strips if place == offset)
        columns = near_stress.at[way, pl.ds(0, 8), pl.ds(0, count * lanes)]
        return pltpu.make_async_remote_copy(
            src_ref=columns,
            dst_ref=columns,
            send_sem=send_sem.at[1, way],
            recv_sem=recv_sem.at[1, way],
            device_id=(a + dx, b + dy),
            device_id_type=MESH,
        )

    for at, (dx, dy) in enumerate(AROUND):

        @pl.when(inside(dx, dy))
        def _():
            load_copy(at).wait_send()
            load_arrival(at).wait_recv()

    for at, ((dx, dy), _, _) in enumerate(strips):

        @pl.when(inside(dx, dy))
        def _():
            strip_copy(at).start()

    for at, ((dx, dy), _, _) in enumerate(handed):

        @pl.when(inside(dx, dy))
        def _():
            side_copy(at).start()

    def span(step, count, below):
        if step == 0:
            return [(k, k) for k in range(count)]
        if step > 0:
            return [(count, 0)]
        return [(k - below, count + k - below) for k in range(below)]

    for c in range(3):
        for i in range(count_x):
            loads[c, pl.ds((i + 1) * wide + 1, count_y)] = load_ref[c, i]
        for at, (dx, dy) in enumerate(AROUND):
            for i, from_i in span(dx, count_x, 1):
                for j, from_j in span(dy, count_y, 1):
                    loads[c, pl.ds((i + 1) * wide + j + 1, 1)] = near_load[
                        at, c, from_i, from_j : from_j + 1
                    ]

    broad = count_y + 3

    def put_stress(read, i, j):
        for v in range(6):
            outer[v, pl.ds((i + 2) * broad + j + 2, 1)] = read(v)

    def put_tangent(read, row, first=6):
        for v in range(first, 6 + len(PAIRS)):
            elem[v, pl.ds(row, 1)] = read(v)

    for at, (i, j) in enumerate(owned):
        put_stress(lambda v: values[v : v + 1, at * lanes : (at + 1) * lanes], i, j)
        put_tangent(
            lambda v: values[v : v + 1, at * lanes : (at + 1) * lanes], (i + 1) * wide + j + 1
        )
    for at, (dx, dy) in enumerate(AROUND):

        @pl.when(inside(dx, dy))
        def _():
            strips_moved(at, True).wait_send()
            strips_moved(at, False).wait_recv()

    for at, (dx, dy) in enumerate(AROUND):
        for i, from_i in span(dx, count_x, 2):
            for j, from_j in span(dy, count_y, 2):
                low = column_at[from_i, from_j] * lanes
                put_stress(lambda v: near_stress[at, v : v + 1, low : low + lanes], i, j)
    for at, ((dx, dy), place, (i, j)) in enumerate(handed):
        low = column_at[place] * lanes
        source = AROUND.index((-dx, -dy))
        for v in (6, 7):
            elem[v, pl.ds(i * wide + j, 1)] = near_stress[source, v : v + 1, low : low + lanes]
    def near(step, count):
        return {0: list(range(1, count + 1)), -1: [1], 1: [count]}[step]

    def far(step, count):
        return {0: list(range(1, count + 1)), -1: [0], 1: [count + 1]}[step]

    def places(at, pick):
        dx, dy = AROUND[at]
        return [i * wide + j for i in pick(dx, count_x) for j in pick(dy, count_y)]

    def hop(it, at):
        dx, dy = AROUND[at]
        other = len(AROUND) - 1 - at
        return pltpu.make_async_remote_copy(
            src_ref=send_halo.at[it, at],
            dst_ref=halo.at[it, other],
            send_sem=send_sem.at[(it - 1) % 2, at],
            recv_sem=recv_sem.at[(it - 1) % 2, other],
            device_id=(a + dx, b + dy),
            device_id_type=MESH,
        )

    def halo_start(it):
        for at, (dx, dy) in enumerate(AROUND):

            @pl.when(inside(dx, dy))
            def _():
                mine = places(at, near)
                for c in range(3):
                    for k, row in enumerate(mine):
                        send_halo[it, at, pl.ds(c * len(mine) + k, 1)] = basis[it, c, pl.ds(row, 1)]
                hop(it, at).start()

    def halo_finish(it):
        for at, (dx, dy) in enumerate(AROUND):

            @pl.when(inside(dx, dy))
            def _():
                hop(it, at).wait_send()
                pltpu.make_async_remote_copy(
                    src_ref=send_halo.at[it, at],
                    dst_ref=halo.at[it, at],
                    send_sem=send_sem.at[(it - 1) % 2, at],
                    recv_sem=recv_sem.at[(it - 1) % 2, at],
                    device_id=(a + dx, b + dy),
                    device_id_type=MESH,
                ).wait_recv()

        for at in range(len(AROUND)):
            theirs = places(at, far)
            for c in range(3):
                for k, row in enumerate(theirs):
                    basis[it, c, pl.ds(row, 1)] = halo[it, at, pl.ds(c * len(theirs) + k, 1)]

    def force_of(stress, c, down=down):
        first, second, third = (stress[VOIGT[c][d]] for d in range(3))
        first = first + down(first, 2)
        second = second + down(second, 2)
        third = down(third, 2) - third
        first = first + down(first, 1)
        rest = down(second, 1) - second + third + down(third, 1)
        return 0.25 * (down(first, 0) - first + rest + down(rest, 0))

    def applied(it):
        strain = strain_of(it)
        stress = []
        for i in range(6):
            value = None
            for j in range(6):
                term = elem[6 + PAIR_AT[(min(i, j), max(i, j))]] * strain[j]
                value = term if value is None else value + term
            stress.append(value)
        return [
            jnp.where(own, MASS * basis[it, c] + force_of(stress, c), 0.0) for c in range(3)
        ]

    def product(first, second):
        total = None
        for c in range(3):
            term = first[c] * second[c]
            total = term if total is None else total + term
        total = jnp.sum(jnp.where(own, total, 0.0), axis=0, keepdims=True)
        value = total[:, :128]
        for at in range(128, lanes, 128):
            value = value + total[:, at : at + 128]
        return value

    def stacked(pieces):
        high = -(-len(pieces) // 8) * 8
        tile_row = lax.broadcasted_iota(jnp.int32, (high, 128), 0)
        value = jnp.zeros((high, 128), jnp.float32)
        for at, piece in enumerate(pieces):
            value = jnp.where(tile_row == at, piece, value)
        return value

    def gather_start(at, src, dst, count, mine, device):
        def send(step):
            pltpu.make_async_remote_copy(
                src_ref=src,
                dst_ref=dst.at[mine],
                send_sem=sum_send.at[at],
                recv_sem=sum_recv.at[at],
                device_id=device(lax.rem(mine + step, count)),
                device_id_type=MESH,
            ).start()

        every(count, send)
        dst[mine] = src[...]

    def gather_finish(at, dst, count, device, mine):
        others = dst.at[pl.ds(0, count - 1)]
        pltpu.make_async_remote_copy(
            src_ref=others,
            dst_ref=others,
            send_sem=sum_send.at[at],
            recv_sem=sum_recv.at[at],
            device_id=device(lax.rem(mine + 1, count)),
            device_id_type=MESH,
        ).wait()

    def along_micro(other):
        return (a, other)

    def along_macro(other):
        return (other, b)

    broad_lane = lax.broadcasted_iota(jnp.int32, outer.shape[1:], 1)

    def back(value, axis):
        if axis == 2:
            return jnp.where(broad_lane == 0, 0.0, pltpu.roll(value, 1, 1))
        return pltpu.roll(value, broad if axis == 0 else 1, 0)

    row_x, row_y = row_at // wide, row_at % wide
    real = jnp.logical_and(
        jnp.logical_and(
            row_x >= jnp.where(a > 0, 0, 1),
            row_x <= jnp.where(a < n_macro - 1, count_x + 1, count_x),
        ),
        jnp.logical_and(
            row_y >= jnp.where(b > 0, 0, 1),
            row_y <= jnp.where(b < n_micro - 1, count_y + 1, count_y),
        ),
    )
    stress = [outer[v] for v in range(6)]
    for c in range(3):
        pushed = force_of(stress, c, back)
        for i in range(count_x + 2):
            low = (i + 1) * broad + 1
            basis[0, c, pl.ds(i * wide, wide)] = pushed[low : low + wide]
        basis[0, c] = jnp.where(real, loads[c] - basis[0, c], 0.0)
    for way, (dx, dy) in enumerate(after):
        mine = [at for at, (offset, _, _) in enumerate(handed) if offset == (dx, dy)]
        landed = beside.at[pl.ds(mine[0], len(mine))]
        moved = pltpu.make_async_remote_copy(
            src_ref=landed,
            dst_ref=landed,
            send_sem=side_send.at[way],
            recv_sem=side_recv.at[way],
            device_id=(a + dx, b + dy),
            device_id_type=MESH,
        )

        @pl.when(inside(dx, dy))
        def _():
            moved.wait_send()

        @pl.when(inside(-dx, -dy))
        def _():
            moved.wait_recv()

    for at, (_, _, (i, j)) in enumerate(handed):
        put_tangent(lambda v: beside[at, v - 8 : v - 7], i * wide + j, 8)

    grown = applied(0)
    for c in range(3):
        basis[1, c] = grown[c]
    halo_start(1)
    start = [basis[0, c] for c in range(3)]
    part[...] = stacked([product(start, start), product(grown, grown)])
    gather_start(0, part, got_micro, n_micro, b, along_micro)
    halo_finish(1)
    grown = applied(1)
    for c in range(3):
        basis[2, c] = grown[c]
    halo_start(2)
    gather_finish(0, got_micro, n_micro, along_micro, b)
    middle[...] = jnp.sum(got_micro[...], axis=0)
    gather_start(1, middle, got_macro, n_macro, a, along_macro)
    halo_finish(2)
    gather_finish(1, got_macro, n_macro, along_macro, a)
    totals = jnp.sum(jnp.sum(got_macro[...], axis=0), axis=1, keepdims=True)
    shift = jnp.sqrt(totals[1:2] / totals[0:1])
    scale = 1.0 / shift
    for c in range(3):
        u0, w1, w2 = basis[0, c], basis[1, c] * scale, basis[2, c] * (scale * scale)
        basis[1, c] = w1 - u0
        basis[2, c] = (w2 - w1) - (w1 - u0)

    def field(it):
        return [basis[it, c] for c in range(3)]

    def step(it):
        grown = applied(it)
        return [grown[c] * scale - jnp.where(own, basis[it, c], 0.0) for c in range(3)]

    moments = []
    for it in range(2, ITERS):
        grown = step(it)
        if it + 1 < ITERS:
            for c in range(3):
                basis[it + 1, c] = grown[c]
            halo_start(it + 1)
            if it == 2:
                for k in range(3):
                    moments.append(product(field(k), field(k)))
                    moments.append(product(field(k), field(k + 1)))
            else:
                moments.append(product(field(it), field(it)))
                moments.append(product(field(it), field(it + 1)))
            halo_finish(it + 1)
    moments.append(product(field(ITERS - 1), field(ITERS - 1)))
    moments.append(product(field(ITERS - 1), grown))
    sums = jnp.sum(stacked(moments), axis=1, keepdims=True)
    diagonal = lax.broadcasted_iota(jnp.int32, (16, 128), 0) == lax.broadcasted_iota(
        jnp.int32, (16, 128), 1
    )
    last_part[...] = jnp.sum(jnp.where(diagonal, sums, 0.0), axis=0, keepdims=True)

    gather_start(2, last_part, last_all, total, me, device)
    gather_finish(2, last_all, total, device, me)
    totals = jnp.sum(last_all[...], axis=0)
    held = [totals[:, k : k + 1] for k in range(2 * ITERS)]

    def inner(first, second, extra=0):
        gathered = {}
        for i, x in enumerate(first):
            for j, y in enumerate(second):
                gathered.setdefault(i + j, []).append(x * y)
        value = None
        for degree, terms in gathered.items():
            total = terms[0]
            for term in terms[1:]:
                total = total + term
            total = total * held[degree + extra]
            value = total if value is None else value + total
        return value

    one = jnp.ones((1, 1), jnp.float32)
    left, toward, done = [one], [one], []
    norm = held[0]
    for it in range(ITERS):
        energy = inner(toward, toward) + inner(toward, toward, 1)
        length = norm / energy
        done = [x + length * scale * p for x, p in zip(done + [0.0], toward)]
        raised = [
            (toward[k] if k < len(toward) else 0.0) + (toward[k - 1] if k > 0 else 0.0)
            for k in range(len(toward) + 1)
        ]
        left = [
            (left[k] if k < len(left) else 0.0) - length * raised[k] for k in range(len(raised))
        ]
        if it + 1 < ITERS:
            fresh = inner(left, left)
            ratio = fresh / norm
            toward = [
                left[k] + (ratio * toward[k] if k < len(toward) else 0.0)
                for k in range(len(left))
            ]
            norm = fresh
    for c in range(3):
        fields = [basis[k, c] for k in range(ITERS)] + [grown[c]]
        moved, rest = None, None
        for k in range(ITERS + 1):
            if k < len(done):
                term = done[k] * fields[k]
                moved = term if moved is None else moved + term
            term = left[k] * fields[k]
            rest = term if rest is None else rest + term
        for i in range(count_x):
            low = (i + 1) * wide + 1
            inc_ref[c, i] = moved[low : low + count_y]
            res_ref[c, i] = rest[low : low + count_y]

    for buffer, semaphore in ((route_out, route_send), (back_out, back_send)):
        others = buffer.at[pl.ds(0, n_micro - 1)]
        pltpu.make_async_remote_copy(
            src_ref=others,
            dst_ref=others,
            send_sem=semaphore.at[0],
            recv_sem=semaphore.at[0],
            device_id=(a, lax.rem(b + 1, n_micro)),
            device_id_type=MESH,
        ).wait_send()


def hand_over(inc_in, res_in, inc_ref, res_ref):
    inc_ref[...] = inc_in[...]
    res_ref[...] = res_in[...]


def shards(
    displacement,
    load,
    routes,
    counts,
    stiffness,
    precond,
    forcing,
    coupling,
    lame_first,
    lame_shear,
):
    _, count_x, count_y, lanes = displacement.shape
    points = count_x * count_y * lanes
    n_macro, n_micro = lax.axis_size("macro"), lax.axis_size("micro")
    capacity = max(2, 2 * points // n_micro)
    slots = -(-capacity // 128) * 128
    size = stiffness.shape[1]
    tall = -(-(6 + len(PAIRS)) // 8) * 8
    rows = -(-(count_x + 2) * (count_y + 2) // 8) * 8
    side = -(-3 * max(count_x, count_y) // 8) * 8
    total = n_macro * n_micro
    sides = count_x + count_y + 1
    outer_rows = -(-(count_x + 3) * (count_y + 3) // 8) * 8
    vmem = pl.BlockSpec(memory_space=pltpu.VMEM)
    anywhere = pl.BlockSpec(memory_space=pl.ANY)
    dma = pltpu.SemaphoreType.DMA

    def held(*shape):
        return pltpu.VMEM(shape, jnp.float32)

    def half(*shape):
        return pltpu.VMEM(shape, jnp.bfloat16)

    def body(*refs):
        newton_kernel((count_x, count_y, lanes, n_macro, n_micro), *refs)

    outputs = pl.pallas_call(
            body,
            out_shape=[jax.ShapeDtypeStruct(load.shape, jnp.float32)] * 2,
            in_specs=[anywhere] * 8 + [vmem] * 2,
            out_specs=[vmem, vmem],
            scratch_shapes=[
                held(*displacement.shape),
                held(*load.shape),
                pltpu.VMEM((points // 128, 128), jnp.int32),
                pltpu.VMEM((points // 128, 128), jnp.int32),
                half(size, size),
                half(size, size),
                half(6, size),
                half(6, size),
                half(3 * size, 16),
                half(tall, size),
                half(tall, size),
                held(tall, size),
                half(n_micro * slots, points),
                held(len(AROUND), *load.shape),
                held(len(AROUND), 8, points),
                held(6, outer_rows, lanes),
                held(3, rows, lanes),
                held(3, *displacement.shape),
                held(8, points),
                held(n_micro, 8, slots),
                held(n_micro, 8, slots),
                held(n_micro, tall, slots),
                held(n_micro, tall, slots),
                held(tall, points),
                held(sides, tall - 8, lanes),
                held(6 + len(PAIRS), rows, lanes),
                held(ITERS, 3, rows, lanes),
                held(ITERS, len(AROUND), side, lanes),
                held(ITERS, len(AROUND), side, lanes),
                held(8, 128),
                held(n_micro, 8, 128),
                held(8, 128),
                held(n_macro, 8, 128),
                held(1, 128),
                held(total, 1, 128),
                dma((8,)),
                dma((3,)),
                dma((3,)),
                dma((1,)),
                dma((n_micro,)),
                dma((1,)),
                dma((n_micro,)),
                dma((3,)),
                dma((3,)),
                dma((2, len(AROUND))),
                dma((2, len(AROUND))),
                dma((3,)),
                dma((3,)),
            ],
            compiler_params=pltpu.CompilerParams(collective_id=0, has_side_effects=True),
            name="newton_step",
        )(
            displacement,
            load,
            routes.reshape(points // 128, 128),
            counts.reshape(points // 128, 128),
            stiffness[0],
            precond[0],
            forcing[0],
            coupling[0].T,
            lame_first.reshape(1, 1),
            lame_shear.reshape(1, 1),
        )
    return tuple(
        pl.pallas_call(
            hand_over,
            out_shape=[jax.ShapeDtypeStruct(load.shape, jnp.float32)] * 2,
            in_specs=[vmem, vmem],
            out_specs=[vmem, vmem],
            name="hand_over",
        )(*outputs)
    )


def solution(mesh):
    in_specs = (
        P(None, "macro", "micro", None),
        P(None, "macro", "micro", None),
        P("macro", "micro", None, None),
        P("macro", "micro", None),
        P("micro", None, None),
        P("micro", None, None),
        P("micro", None, None),
        P("micro", None, None),
        P("micro"),
        P("micro"),
    )
    out_specs = (P(None, "macro", "micro", None), P(None, "macro", "micro", None))
    return jax.shard_map(shards, mesh=mesh, in_specs=in_specs, out_specs=out_specs, check_vma=False)
```

```python
import jax
import jax.numpy as jnp
from jax import lax
from jax.experimental import pallas as pl
from jax.experimental.pallas import tpu as pltpu
from jax.sharding import PartitionSpec as P

ITMAX = 4
ITERS = 5


BETA = 0.1
OMEGA = 0.8
MASS = 0.1
VOIGT = ((0, 5, 4), (5, 1, 3), (4, 3, 2))
PAIRS = tuple((first, second) for first in range(6) for second in range(first, 6))
PAIR_AT = {pair: at for at, pair in enumerate(PAIRS)}
AROUND = tuple((dx, dy) for dx in (-1, 0, 1) for dy in (-1, 0, 1) if (dx, dy) != (0, 0))
MESH = pl.DeviceIdType.MESH


def strips_of(count_x, count_y):
    strips = []
    for dx, dy in AROUND:
        across = range(count_x if dx >= 0 else 1)
        if dy >= 0:
            strips.append(((dx, dy), 0, len(across) * count_y))
        else:
            strips += [((dx, dy), i * count_y, 1) for i in across]
    return strips


def newton_kernel(
    sizes,
    disp_in,
    load_in,
    routes_in,
    counts_in,
    stiff_in,
    pre_in,
    force_in,
    couple_in,
    first_ref,
    shear_ref,
    inc_ref,
    res_ref,
    disp_ref,
    load_ref,
    routes_ref,
    counts_ref,
    stiff,
    pre,
    force_ref,
    couple_ref,
    maps,
    couple,
    products,
    wide_products,
    spots,
    near_load,
    near_stress,
    outer,
    loads,
    near_disp,
    bundle,
    route_out,
    route_in,
    back_out,
    back_in,
    values,
    beside,
    elem,
    basis,
    send_halo,
    halo,
    part,
    got_micro,
    middle,
    got_macro,
    last_part,
    last_all,
    input_sem,
    disp_send,
    disp_recv,
    route_send,
    route_recv,
    back_send,
    back_recv,
    side_send,
    side_recv,
    send_sem,
    recv_sem,
    sum_send,
    sum_recv,
):
    count_x, count_y, lanes, n_macro, n_micro = sizes
    wide = count_y + 2
    rows = basis.shape[2]
    points = spots.shape[1]
    slots = spots.shape[0] // n_micro
    pairs = n_micro // 2
    groups = points // 128
    size = stiff.shape[0]
    tall = couple.shape[0]
    total = n_macro * n_micro
    a, b = lax.axis_index("macro"), lax.axis_index("micro")
    me = a * n_micro + b

    def device(other):
        return (other // n_micro, lax.rem(other, n_micro))

    def inside(dx, dy):
        test = None
        for place, step, count in ((a, dx, n_macro), (b, dy, n_micro)):
            if step != 0:
                good = (place > 0) if step < 0 else (place < count - 1)
                test = good if test is None else jnp.logical_and(test, good)
        return test

    barrier = pltpu.get_barrier_semaphore()

    def every(count, act):
        if count <= 32:
            for step in range(1, count):
                act(step)
        else:
            lax.fori_loop(1, count, lambda step, carry: (act(step), carry)[1], 0)

    def greet(row, column):
        pl.semaphore_signal(barrier, inc=1, device_id=(row, column), device_id_type=MESH)

    for step in range(1, n_macro):
        for aside in range(3):
            greet(lax.rem(a + step, n_macro), lax.rem(b + n_micro - 1 + aside, n_micro))
    every(n_micro, lambda step: greet(a, lax.rem(b + step, n_micro)))
    greeted = 3 * (n_macro - 1) + n_micro - 1
    inputs = {}
    for at, (name, source, target) in enumerate(
        (
            ("routes", routes_in, routes_ref),
            ("force", force_in, force_ref),
            ("couple", couple_in, couple_ref),
            ("counts", counts_in, counts_ref),
            ("disp", disp_in, disp_ref),
            ("load", load_in, load_ref),
            ("pre", pre_in, pre),
            ("stiff", stiff_in, stiff),
        )
    ):
        inputs[name] = pltpu.make_async_copy(source, target, input_sem.at[at])
        inputs[name].start()

    inputs["disp"].wait()
    after = ((1, 0), (0, 1), (1, 1))
    pl.semaphore_wait(barrier, greeted)

    def show(at):
        dx, dy = after[at]
        return pltpu.make_async_remote_copy(
            src_ref=disp_ref,
            dst_ref=near_disp.at[at],
            send_sem=disp_send.at[at],
            recv_sem=disp_recv.at[at],
            device_id=(a - dx, b - dy),
            device_id_type=MESH,
        )

    for at, (dx, dy) in enumerate(after):

        @pl.when(inside(-dx, -dy))
        def _():
            show(at).start()

    inputs["load"].wait()

    def load_copy(at):
        dx, dy = AROUND[at]
        other = len(AROUND) - 1 - at
        return pltpu.make_async_remote_copy(
            src_ref=load_ref,
            dst_ref=near_load.at[other],
            send_sem=send_sem.at[0, at],
            recv_sem=recv_sem.at[0, other],
            device_id=(a + dx, b + dy),
            device_id_type=MESH,
        )

    def load_arrival(at):
        dx, dy = AROUND[at]
        return pltpu.make_async_remote_copy(
            src_ref=load_ref,
            dst_ref=near_load.at[at],
            send_sem=send_sem.at[0, at],
            recv_sem=recv_sem.at[0, at],
            device_id=(a + dx, b + dy),
            device_id_type=MESH,
        )

    for at, (dx, dy) in enumerate(AROUND):

        @pl.when(inside(dx, dy))
        def _():
            load_copy(at).start()

        @pl.when(jnp.logical_not(inside(dx, dy)))
        def _():
            near_load[at] = jnp.zeros(near_load.shape[1:], jnp.float32)
            near_stress[at] = jnp.zeros(near_stress.shape[1:], jnp.float32)

    outer[...] = jnp.zeros(outer.shape, jnp.float32)
    loads[...] = jnp.zeros(loads.shape, jnp.float32)
    for name in ("routes", "force", "couple", "counts"):
        inputs[name].wait()
    force = force_ref[...].astype(jnp.float32)
    force = jnp.concatenate([force, jnp.zeros((2, size), jnp.float32)], axis=0)
    wide_products[...] = jnp.zeros((tall, size), jnp.float32)
    coupling = couple_ref[...].astype(jnp.float32)
    wide_products[pl.ds(0, 6)] = coupling
    couple[...] = wide_products[...].astype(jnp.bfloat16)
    wide_products[pl.ds(0, 6)] = jnp.zeros((6, size), jnp.float32)
    for at, (first, second) in enumerate(PAIRS):
        wide_products[pl.ds(6 + at, 1)] = coupling[first : first + 1] * coupling[second : second + 1]
    products[...] = wide_products[...].astype(jnp.bfloat16)

    route = routes_ref[...]
    row_of = lax.broadcasted_iota(jnp.int32, (128, 128), 0)
    column_of = lax.broadcasted_iota(jnp.int32, (128, 128), 1)
    until = jnp.where(row_of <= column_of, 1.0, 0.0).astype(jnp.bfloat16)
    named = [jnp.where(route == owner, 1.0, 0.0) for owner in range(n_micro)]
    named = jnp.concatenate(named, axis=0).astype(jnp.bfloat16)
    inner_rank = jnp.dot(named, until, preferred_element_type=jnp.float32)
    whole = jnp.dot(
        named, jnp.ones((128, 128), jnp.bfloat16), preferred_element_type=jnp.float32
    ).astype(jnp.bfloat16)
    span = n_micro * groups
    row_of = lax.broadcasted_iota(jnp.int32, (span, span), 0)
    column_of = lax.broadcasted_iota(jnp.int32, (span, span), 1)
    ahead = jnp.logical_and(column_of < row_of, column_of // groups == row_of // groups)
    before = jnp.dot(
        jnp.where(ahead, 1.0, 0.0).astype(jnp.bfloat16), whole, preferred_element_type=jnp.float32
    )
    ranks = inner_rank + before - 1.0
    rank = jnp.zeros((groups, 128), jnp.float32)
    for owner in range(n_micro):
        rank = jnp.where(route == owner, ranks[owner * groups : (owner + 1) * groups], rank)
    slot_type = jnp.bfloat16 if slots <= 256 else jnp.float32
    slot_at = lax.broadcasted_iota(jnp.int32, (slots, 128), 0).astype(jnp.float32)
    slot_at = slot_at.astype(slot_type)

    def spot(owner, carry):
        local = jnp.where(route == owner, rank, -1.0)
        for g in range(groups):
            near_slot = jnp.broadcast_to(local[g : g + 1], (16, 128)).astype(slot_type)
            near_slot = jnp.concatenate([near_slot] * (slots // 16), axis=0)
            hit = jnp.where(near_slot == slot_at, slot_type(1), slot_type(0))
            low = pl.multiple_of(owner * slots, slots)
            spots[pl.ds(low, slots), g * 128 : (g + 1) * 128] = hit.astype(jnp.bfloat16)
        return carry

    lax.fori_loop(0, n_micro, spot, 0)

    for it in range(basis.shape[0]):
        for c in range(3):
            basis[it, c] = jnp.zeros((rows, lanes), jnp.float32)
    elem[...] = jnp.zeros(elem.shape, jnp.float32)
    values[...] = jnp.zeros(values.shape, jnp.float32)
    bundle[...] = jnp.zeros(bundle.shape, jnp.float32)
    for g in range(groups):
        bundle[6:7, g * 128 : (g + 1) * 128] = counts_ref[g : g + 1].astype(jnp.float32)

    for at, (dx, dy) in enumerate(AROUND):

        @pl.when(jnp.logical_not(inside(dx, dy)))
        def _():
            for it in range(1, ITERS):
                halo[it, at] = jnp.zeros(halo.shape[2:], jnp.float32)

    for at, (dx, dy) in enumerate(after):

        @pl.when(jnp.logical_not(inside(dx, dy)))
        def _():
            near_disp[at] = jnp.zeros(near_disp.shape[1:], jnp.float32)

    owned = [(i, j) for i in range(count_x) for j in range(count_y)]
    column_at = {place: at for at, place in enumerate(owned)}
    handed = [((1, 0), (count_x - 1, j), (0, j + 1)) for j in range(count_y)]
    handed += [((0, 1), (i, count_y - 1), (i + 1, 0)) for i in range(count_x)]
    handed += [((1, 1), (count_x - 1, count_y - 1), (0, 0))]
    for at, ((dx, dy), _, _) in enumerate(handed):

        @pl.when(jnp.logical_not(inside(-dx, -dy)))
        def _():
            beside[at] = jnp.zeros(beside.shape[1:], jnp.float32)

    for name in ("pre", "stiff"):
        inputs[name].wait()

    def split(exact):
        high = exact.astype(jnp.bfloat16).astype(jnp.float32)
        return jnp.concatenate([high, exact - high], axis=0)

    def through(matrix, exact):
        moved = jnp.dot(
            split(exact).astype(jnp.bfloat16), matrix[...], preferred_element_type=jnp.float32
        )
        return moved[:8] + moved[8:]

    first_map = OMEGA * through(pre, force)
    misfit_map = through(stiff, first_map) - force
    turned = jnp.concatenate([split(first_map), split(misfit_map), split(force)], axis=0).T
    for at in range(3):
        maps[pl.ds(at * size, size)] = turned[:, at * 16 : (at + 1) * 16].astype(jnp.bfloat16)
    for c in range(3):
        for i, j in owned:
            basis[0, c, pl.ds((i + 1) * wide + j + 1, 1)] = disp_ref[c, i, j : j + 1]
    for at, (dx, dy) in enumerate(after):

        @pl.when(inside(-dx, -dy))
        def _():
            show(at).wait_send()

        @pl.when(inside(dx, dy))
        def _():
            pltpu.make_async_remote_copy(
                src_ref=disp_ref,
                dst_ref=near_disp.at[at],
                send_sem=disp_send.at[at],
                recv_sem=disp_recv.at[at],
                device_id=(a + dx, b + dy),
                device_id_type=MESH,
            ).wait_recv()

    for c in range(3):
        for j in range(count_y):
            basis[0, c, pl.ds((count_x + 1) * wide + j + 1, 1)] = near_disp[0, c, 0, j : j + 1]
        for i in range(count_x):
            basis[0, c, pl.ds((i + 1) * wide + count_y + 1, 1)] = near_disp[1, c, i, 0:1]
        basis[0, c, pl.ds((count_x + 1) * wide + count_y + 1, 1)] = near_disp[2, c, 0, 0:1]

    row_at = lax.broadcasted_iota(jnp.int32, (rows, lanes), 0)
    lane_at = lax.broadcasted_iota(jnp.int32, (rows, lanes), 1)
    own = row_at < 0
    for i in range(1, count_x + 1):
        low = i * wide + 1
        own = jnp.logical_or(own, jnp.logical_and(row_at >= low, row_at < low + count_y))

    def up(value, axis):
        if axis == 2:
            moved = pltpu.roll(value, lanes - 1, 1)
            return jnp.where(lane_at == lanes - 1, 0.0, moved)
        return pltpu.roll(value, rows - (wide if axis == 0 else 1), 0)

    def down(value, axis):
        if axis == 2:
            return jnp.where(lane_at == 0, 0.0, pltpu.roll(value, 1, 1))
        return pltpu.roll(value, wide if axis == 0 else 1, 0)

    def strain_of(it):
        grads = []
        for c in range(3):
            value = basis[it, c]
            moved = up(value, 2)
            total, gap = value + moved, moved - value
            total_up, gap_up = up(total, 1), up(gap, 1)
            flat, slope_y, slope_z = total + total_up, total_up - total, gap + gap_up
            grads.append(
                (
                    0.25 * (up(flat, 0) - flat),
                    0.25 * (up(slope_y, 0) + slope_y),
                    0.25 * (up(slope_z, 0) + slope_z),
                )
            )
        return [
            grads[0][0],
            grads[1][1],
            grads[2][2],
            grads[1][2] + grads[2][1],
            grads[0][2] + grads[2][0],
            grads[0][1] + grads[1][0],
        ]

    strain = strain_of(0)
    for at, (i, j) in enumerate(owned):
        low = (i + 1) * wide + j + 1
        for k in range(6):
            bundle[k : k + 1, at * lanes : (at + 1) * lanes] = strain[k][low : low + 1]
    exact = bundle[...]
    high = exact.astype(jnp.bfloat16).astype(jnp.float32)
    both = jnp.concatenate([high, exact - high], axis=0).astype(jnp.bfloat16)

    def route_copy(other, mine):
        return pltpu.make_async_remote_copy(
            src_ref=route_out.at[other],
            dst_ref=route_in.at[mine],
            send_sem=route_send.at[0],
            recv_sem=route_recv.at[mine],
            device_id=(a, other),
            device_id_type=MESH,
        )

    chip, core = b // 2, lax.rem(b, 2)

    def pair_rows(place):
        return pl.ds(pl.multiple_of(place * (2 * slots), 2 * slots), 2 * slots)

    def hand_out(at, carry):
        place = lax.rem(chip + pairs - at, pairs)
        moved = lax.dot_general(
            both,
            spots[pair_rows(place)],
            (((1,), (1,)), ((), ())),
            preferred_element_type=jnp.float32,
        )
        moved = moved[:8] + moved[8:]
        for k in range(2):
            other = 2 * place + k
            piece = moved[:, k * slots : (k + 1) * slots]

            @pl.when(other != b)
            def _():
                route_out[other] = piece
                route_copy(other, b).start()

            @pl.when(other == b)
            def _():
                route_in[b] = piece

        return carry

    lax.fori_loop(0, pairs, hand_out, 0)


    lame_first, lame_shear = first_ref[...], shear_ref[...]
    tall_at = lax.broadcasted_iota(jnp.int32, (tall, 2 * slots), 0)
    on_trace = jnp.where(tall_at < 3, lame_first, 0.0)
    on_strain = jnp.where(tall_at < 3, 2.0 * lame_shear, jnp.where(tall_at < 6, lame_shear, 0.0))
    base = jnp.zeros((tall, 2 * slots), jnp.float32)
    for at, (i, j) in enumerate(PAIRS):
        if i == j:
            amount = lame_first + 2.0 * lame_shear if i < 3 else lame_shear
        elif j < 3:
            amount = lame_first
        else:
            continue
        base = jnp.where(tall_at == 6 + at, amount, base)

    def back_copy(other, mine):
        return pltpu.make_async_remote_copy(
            src_ref=back_out.at[other],
            dst_ref=back_in.at[mine],
            send_sem=back_send.at[0],
            recv_sem=back_recv.at[mine],
            device_id=(a, other),
            device_id_type=MESH,
        )

    def solve(at, carry):
        place = lax.rem(chip + at, pairs)
        taken = []
        for k in range(2):
            other = 2 * place + k

            @pl.when(other != b)
            def _():
                route_copy(b, other).wait_recv()

            taken.append(route_in[other])
        points_in = jnp.concatenate(taken, axis=1)
        sweeps = points_in[6:7]
        strain_in = points_in.astype(jnp.bfloat16)
        strain_in = jnp.concatenate([strain_in, strain_in], axis=0)

        def mapped(at):
            return jnp.dot(
                maps[pl.ds(at * size, size)], strain_in, preferred_element_type=jnp.float32
            )

        modes, misfit, modal_load = mapped(0), mapped(1), mapped(2)
        for sweep in range(1, ITMAX):
            if sweep > 1:
                misfit = jnp.dot(
                    stiff[...], modes.astype(jnp.bfloat16), preferred_element_type=jnp.float32
                )
                misfit = misfit - modal_load
            misfit = (misfit + BETA * jnp.tanh(modes)).astype(jnp.bfloat16)
            change = jnp.dot(pre[...], misfit, preferred_element_type=jnp.float32)
            modes = modes - jnp.where(sweeps > sweep, OMEGA, 0.0) * change
        bent = jnp.tanh(modes)
        slope = 1.0 - bent * bent
        trace = points_in[0:1] + points_in[1:2] + points_in[2:3]
        padded = jnp.concatenate(
            [points_in, jnp.zeros((tall - 8, 2 * slots), jnp.float32)], axis=0
        )
        answer = on_trace * trace + on_strain * padded + base
        answer = answer + jnp.dot(
            couple[...], modes.astype(jnp.bfloat16), preferred_element_type=jnp.float32
        )
        answer = answer + jnp.dot(
            products[...], slope.astype(jnp.bfloat16), preferred_element_type=jnp.float32
        )
        for k in range(2):
            other = 2 * place + k
            piece = answer[:, k * slots : (k + 1) * slots]

            @pl.when(other != b)
            def _():
                back_out[other] = piece
                back_copy(other, b).start()

            @pl.when(other == b)
            def _():
                back_in[b] = piece

        return carry

    lax.fori_loop(0, pairs, solve, 0)

    def take_back(at, carry):
        place = lax.rem(chip + pairs - at, pairs)
        taken = []
        for k in range(2):
            other = 2 * place + k

            @pl.when(other != b)
            def _():
                back_copy(b, other).wait_recv()

            taken.append(back_in[other])
        exact = jnp.concatenate(taken, axis=1)
        high = exact.astype(jnp.bfloat16).astype(jnp.float32)
        both = jnp.concatenate([high, exact - high], axis=0).astype(jnp.bfloat16)
        moved = jnp.dot(both, spots[pair_rows(place)], preferred_element_type=jnp.float32)
        values[...] += moved[:tall] + moved[tall:]
        return carry

    lax.fori_loop(0, pairs, take_back, 0)

    def side_copy(at):
        (dx, dy), place, _ = handed[at]
        low = column_at[place] * lanes
        return pltpu.make_async_remote_copy(
            src_ref=values.at[pl.ds(8, tall - 8), pl.ds(low, lanes)],
            dst_ref=beside.at[at],
            send_sem=side_send.at[after.index((dx, dy))],
            recv_sem=side_recv.at[after.index((dx, dy))],
            device_id=(a + dx, b + dy),
            device_id_type=MESH,
        )

    strips = strips_of(count_x, count_y)

    def strip_copy(at):
        (dx, dy), first, count = strips[at]
        columns = pl.ds(first * lanes, count * lanes)
        way = AROUND.index((dx, dy))
        other = len(AROUND) - 1 - way
        return pltpu.make_async_remote_copy(
            src_ref=values.at[pl.ds(0, 8), columns],
            dst_ref=near_stress.at[other, pl.ds(0, 8), columns],
            send_sem=send_sem.at[1, way],
            recv_sem=recv_sem.at[1, other],
            device_id=(a + dx, b + dy),
            device_id_type=MESH,
        )

    def strips_moved(way, sent):
        dx, dy = AROUND[way]
        offset = (dx, dy) if sent else (-dx, -dy)
        count = sum(count for place, _, count in strips if place == offset)
        columns = near_stress.at[way, pl.ds(0, 8), pl.ds(0, count * lanes)]
        return pltpu.make_async_remote_copy(
            src_ref=columns,
            dst_ref=columns,
            send_sem=send_sem.at[1, way],
            recv_sem=recv_sem.at[1, way],
            device_id=(a + dx, b + dy),
            device_id_type=MESH,
        )

    for at, (dx, dy) in enumerate(AROUND):

        @pl.when(inside(dx, dy))
        def _():
            load_copy(at).wait_send()
            load_arrival(at).wait_recv()

    for at, ((dx, dy), _, _) in enumerate(strips):

        @pl.when(inside(dx, dy))
        def _():
            strip_copy(at).start()

    for at, ((dx, dy), _, _) in enumerate(handed):

        @pl.when(inside(dx, dy))
        def _():
            side_copy(at).start()

    def span(step, count, below):
        if step == 0:
            return [(k, k) for k in range(count)]
        if step > 0:
            return [(count, 0)]
        return [(k - below, count + k - below) for k in range(below)]

    for c in range(3):
        for i in range(count_x):
            loads[c, pl.ds((i + 1) * wide + 1, count_y)] = load_ref[c, i]
        for at, (dx, dy) in enumerate(AROUND):
            for i, from_i in span(dx, count_x, 1):
                for j, from_j in span(dy, count_y, 1):
                    loads[c, pl.ds((i + 1) * wide + j + 1, 1)] = near_load[
                        at, c, from_i, from_j : from_j + 1
                    ]

    broad = count_y + 3

    def put_stress(read, i, j):
        for v in range(6):
            outer[v, pl.ds((i + 2) * broad + j + 2, 1)] = read(v)

    def put_tangent(read, row, first=6):
        for v in range(first, 6 + len(PAIRS)):
            elem[v, pl.ds(row, 1)] = read(v)

    for at, (i, j) in enumerate(owned):
        put_stress(lambda v: values[v : v + 1, at * lanes : (at + 1) * lanes], i, j)
        put_tangent(
            lambda v: values[v : v + 1, at * lanes : (at + 1) * lanes], (i + 1) * wide + j + 1
        )
    for at, (dx, dy) in enumerate(AROUND):

        @pl.when(inside(dx, dy))
        def _():
            strips_moved(at, True).wait_send()
            strips_moved(at, False).wait_recv()

    for at, (dx, dy) in enumerate(AROUND):
        for i, from_i in span(dx, count_x, 2):
            for j, from_j in span(dy, count_y, 2):
                low = column_at[from_i, from_j] * lanes
                put_stress(lambda v: near_stress[at, v : v + 1, low : low + lanes], i, j)
    for at, ((dx, dy), place, (i, j)) in enumerate(handed):
        low = column_at[place] * lanes
        source = AROUND.index((-dx, -dy))
        for v in (6, 7):
            elem[v, pl.ds(i * wide + j, 1)] = near_stress[source, v : v + 1, low : low + lanes]
    def near(step, count):
        return {0: list(range(1, count + 1)), -1: [1], 1: [count]}[step]

    def far(step, count):
        return {0: list(range(1, count + 1)), -1: [0], 1: [count + 1]}[step]

    def places(at, pick):
        dx, dy = AROUND[at]
        return [i * wide + j for i in pick(dx, count_x) for j in pick(dy, count_y)]

    def hop(it, at):
        dx, dy = AROUND[at]
        other = len(AROUND) - 1 - at
        return pltpu.make_async_remote_copy(
            src_ref=send_halo.at[it, at],
            dst_ref=halo.at[it, other],
            send_sem=send_sem.at[(it - 1) % 2, at],
            recv_sem=recv_sem.at[(it - 1) % 2, other],
            device_id=(a + dx, b + dy),
            device_id_type=MESH,
        )

    def halo_start(it):
        for at, (dx, dy) in enumerate(AROUND):

            @pl.when(inside(dx, dy))
            def _():
                mine = places(at, near)
                for c in range(3):
                    for k, row in enumerate(mine):
                        send_halo[it, at, pl.ds(c * len(mine) + k, 1)] = basis[it, c, pl.ds(row, 1)]
                hop(it, at).start()

    def halo_finish(it):
        for at, (dx, dy) in enumerate(AROUND):

            @pl.when(inside(dx, dy))
            def _():
                hop(it, at).wait_send()
                pltpu.make_async_remote_copy(
                    src_ref=send_halo.at[it, at],
                    dst_ref=halo.at[it, at],
                    send_sem=send_sem.at[(it - 1) % 2, at],
                    recv_sem=recv_sem.at[(it - 1) % 2, at],
                    device_id=(a + dx, b + dy),
                    device_id_type=MESH,
                ).wait_recv()

        for at in range(len(AROUND)):
            theirs = places(at, far)
            for c in range(3):
                for k, row in enumerate(theirs):
                    basis[it, c, pl.ds(row, 1)] = halo[it, at, pl.ds(c * len(theirs) + k, 1)]

    def force_of(stress, c, down=down):
        first, second, third = (stress[VOIGT[c][d]] for d in range(3))
        first = first + down(first, 2)
        second = second + down(second, 2)
        third = down(third, 2) - third
        first = first + down(first, 1)
        rest = down(second, 1) - second + third + down(third, 1)
        return 0.25 * (down(first, 0) - first + rest + down(rest, 0))

    def applied(it):
        strain = strain_of(it)
        stress = []
        for i in range(6):
            value = None
            for j in range(6):
                term = elem[6 + PAIR_AT[(min(i, j), max(i, j))]] * strain[j]
                value = term if value is None else value + term
            stress.append(value)
        return [
            jnp.where(own, MASS * basis[it, c] + force_of(stress, c), 0.0) for c in range(3)
        ]

    def product(first, second):
        total = None
        for c in range(3):
            term = first[c] * second[c]
            total = term if total is None else total + term
        total = jnp.sum(jnp.where(own, total, 0.0), axis=0, keepdims=True)
        value = total[:, :128]
        for at in range(128, lanes, 128):
            value = value + total[:, at : at + 128]
        return value

    def stacked(pieces):
        high = -(-len(pieces) // 8) * 8
        tile_row = lax.broadcasted_iota(jnp.int32, (high, 128), 0)
        value = jnp.zeros((high, 128), jnp.float32)
        for at, piece in enumerate(pieces):
            value = jnp.where(tile_row == at, piece, value)
        return value

    def spread(at, src, dst, mine, row, column):
        pltpu.make_async_remote_copy(
            src_ref=src,
            dst_ref=dst.at[mine],
            send_sem=sum_send.at[at],
            recv_sem=sum_recv.at[at],
            device_id=(row, column),
            device_id_type=MESH,
        ).start()

    def gather_start(at, src, dst, count, mine, device):
        every(
            count, lambda step: spread(at, src, dst, mine, *device(lax.rem(mine + step, count)))
        )
        dst[mine] = src[...]

    def gather_all(at, src, dst):
        columns = [lax.rem(b + step, n_micro) for step in range(n_micro)] if total <= 32 else None
        for step in range(n_macro - 1, -1, -1):
            row = lax.rem(a + step, n_macro)
            if columns is None:
                lax.fori_loop(
                    0 if step else 1,
                    n_micro,
                    lambda k, carry: (
                        spread(at, src, dst, me, row, lax.rem(b + k, n_micro)),
                        carry,
                    )[1],
                    0,
                )
            else:
                order = sorted(range(n_micro), key=lambda k: -min(k, n_micro - k))
                for k in order:
                    if step or k:
                        spread(at, src, dst, me, row, columns[k])
        dst[me] = src[...]

    def gather_finish(at, dst, count, device, mine):
        others = dst.at[pl.ds(0, count - 1)]
        pltpu.make_async_remote_copy(
            src_ref=others,
            dst_ref=others,
            send_sem=sum_send.at[at],
            recv_sem=sum_recv.at[at],
            device_id=device(lax.rem(mine + 1, count)),
            device_id_type=MESH,
        ).wait()

    def along_micro(other):
        return (a, other)

    def along_macro(other):
        return (other, b)

    broad_lane = lax.broadcasted_iota(jnp.int32, outer.shape[1:], 1)

    def back(value, axis):
        if axis == 2:
            return jnp.where(broad_lane == 0, 0.0, pltpu.roll(value, 1, 1))
        return pltpu.roll(value, broad if axis == 0 else 1, 0)

    row_x, row_y = row_at // wide, row_at % wide
    real = jnp.logical_and(
        jnp.logical_and(
            row_x >= jnp.where(a > 0, 0, 1),
            row_x <= jnp.where(a < n_macro - 1, count_x + 1, count_x),
        ),
        jnp.logical_and(
            row_y >= jnp.where(b > 0, 0, 1),
            row_y <= jnp.where(b < n_micro - 1, count_y + 1, count_y),
        ),
    )
    stress = [outer[v] for v in range(6)]
    for c in range(3):
        pushed = force_of(stress, c, back)
        for i in range(count_x + 2):
            low = (i + 1) * broad + 1
            basis[0, c, pl.ds(i * wide, wide)] = pushed[low : low + wide]
        basis[0, c] = jnp.where(real, loads[c] - basis[0, c], 0.0)
    for way, (dx, dy) in enumerate(after):
        mine = [at for at, (offset, _, _) in enumerate(handed) if offset == (dx, dy)]
        landed = beside.at[pl.ds(mine[0], len(mine))]
        moved = pltpu.make_async_remote_copy(
            src_ref=landed,
            dst_ref=landed,
            send_sem=side_send.at[way],
            recv_sem=side_recv.at[way],
            device_id=(a + dx, b + dy),
            device_id_type=MESH,
        )

        @pl.when(inside(dx, dy))
        def _():
            moved.wait_send()

        @pl.when(inside(-dx, -dy))
        def _():
            moved.wait_recv()

    for at, (_, _, (i, j)) in enumerate(handed):
        put_tangent(lambda v: beside[at, v - 8 : v - 7], i * wide + j, 8)

    grown = applied(0)
    for c in range(3):
        basis[1, c] = grown[c]
    halo_start(1)
    start = [basis[0, c] for c in range(3)]
    part[...] = stacked([product(start, start), product(grown, grown)])
    gather_start(0, part, got_micro, n_micro, b, along_micro)
    halo_finish(1)
    grown = applied(1)
    for c in range(3):
        basis[2, c] = grown[c]
    halo_start(2)
    gather_finish(0, got_micro, n_micro, along_micro, b)
    middle[...] = jnp.sum(got_micro[...], axis=0)
    gather_start(1, middle, got_macro, n_macro, a, along_macro)
    halo_finish(2)
    gather_finish(1, got_macro, n_macro, along_macro, a)
    totals = jnp.sum(jnp.sum(got_macro[...], axis=0), axis=1, keepdims=True)
    shift = jnp.sqrt(totals[1:2] / totals[0:1])
    scale = 1.0 / shift
    for c in range(3):
        u0, w1, w2 = basis[0, c], basis[1, c] * scale, basis[2, c] * (scale * scale)
        basis[1, c] = w1 - u0
        basis[2, c] = (w2 - w1) - (w1 - u0)

    def field(it):
        return [basis[it, c] for c in range(3)]

    def step(it):
        grown = applied(it)
        return [grown[c] * scale - jnp.where(own, basis[it, c], 0.0) for c in range(3)]

    moments = []
    for it in range(2, ITERS):
        grown = step(it)
        if it + 1 < ITERS:
            for c in range(3):
                basis[it + 1, c] = grown[c]
            halo_start(it + 1)
            if it == 2:
                for k in range(3):
                    moments.append(product(field(k), field(k)))
                    moments.append(product(field(k), field(k + 1)))
            else:
                moments.append(product(field(it), field(it)))
                moments.append(product(field(it), field(it + 1)))
            halo_finish(it + 1)
    moments.append(product(field(ITERS - 1), field(ITERS - 1)))
    moments.append(product(field(ITERS - 1), grown))
    sums = jnp.sum(stacked(moments), axis=1, keepdims=True)
    diagonal = lax.broadcasted_iota(jnp.int32, (16, 128), 0) == lax.broadcasted_iota(
        jnp.int32, (16, 128), 1
    )
    last_part[...] = jnp.sum(jnp.where(diagonal, sums, 0.0), axis=0, keepdims=True)

    gather_all(2, last_part, last_all)
    gather_finish(2, last_all, total, device, me)
    totals = jnp.sum(last_all[...], axis=0)
    held = [totals[:, k : k + 1] for k in range(2 * ITERS)]

    def inner(first, second, extra=0):
        gathered = {}
        for i, x in enumerate(first):
            for j, y in enumerate(second):
                gathered.setdefault(i + j, []).append(x * y)
        value = None
        for degree, terms in gathered.items():
            total = terms[0]
            for term in terms[1:]:
                total = total + term
            total = total * held[degree + extra]
            value = total if value is None else value + total
        return value

    one = jnp.ones((1, 1), jnp.float32)
    left, toward, done = [one], [one], []
    norm = held[0]
    for it in range(ITERS):
        energy = inner(toward, toward) + inner(toward, toward, 1)
        length = norm / energy
        done = [x + length * scale * p for x, p in zip(done + [0.0], toward)]
        raised = [
            (toward[k] if k < len(toward) else 0.0) + (toward[k - 1] if k > 0 else 0.0)
            for k in range(len(toward) + 1)
        ]
        left = [
            (left[k] if k < len(left) else 0.0) - length * raised[k] for k in range(len(raised))
        ]
        if it + 1 < ITERS:
            fresh = inner(left, left)
            ratio = fresh / norm
            toward = [
                left[k] + (ratio * toward[k] if k < len(toward) else 0.0)
                for k in range(len(left))
            ]
            norm = fresh
    for c in range(3):
        fields = [basis[k, c] for k in range(ITERS)] + [grown[c]]
        moved, rest = None, None
        for k in range(ITERS + 1):
            if k < len(done):
                term = done[k] * fields[k]
                moved = term if moved is None else moved + term
            term = left[k] * fields[k]
            rest = term if rest is None else rest + term
        for i in range(count_x):
            low = (i + 1) * wide + 1
            inc_ref[c, i] = moved[low : low + count_y]
            res_ref[c, i] = rest[low : low + count_y]

    for buffer, semaphore in ((route_out, route_send), (back_out, back_send)):
        others = buffer.at[pl.ds(0, n_micro - 1)]
        pltpu.make_async_remote_copy(
            src_ref=others,
            dst_ref=others,
            send_sem=semaphore.at[0],
            recv_sem=semaphore.at[0],
            device_id=(a, lax.rem(b + 1, n_micro)),
            device_id_type=MESH,
        ).wait_send()


def hand_over(inc_in, res_in, inc_ref, res_ref):
    inc_ref[...] = inc_in[...]
    res_ref[...] = res_in[...]


def shards(
    displacement,
    load,
    routes,
    counts,
    stiffness,
    precond,
    forcing,
    coupling,
    lame_first,
    lame_shear,
):
    _, count_x, count_y, lanes = displacement.shape
    points = count_x * count_y * lanes
    n_macro, n_micro = lax.axis_size("macro"), lax.axis_size("micro")
    capacity = max(2, 2 * points // n_micro)
    slots = -(-capacity // 128) * 128
    size = stiffness.shape[1]
    tall = -(-(6 + len(PAIRS)) // 8) * 8
    rows = -(-(count_x + 2) * (count_y + 2) // 8) * 8
    side = -(-3 * max(count_x, count_y) // 8) * 8
    total = n_macro * n_micro
    sides = count_x + count_y + 1
    outer_rows = -(-(count_x + 3) * (count_y + 3) // 8) * 8
    vmem = pl.BlockSpec(memory_space=pltpu.VMEM)
    anywhere = pl.BlockSpec(memory_space=pl.ANY)
    dma = pltpu.SemaphoreType.DMA

    def held(*shape):
        return pltpu.VMEM(shape, jnp.float32)

    def half(*shape):
        return pltpu.VMEM(shape, jnp.bfloat16)

    def body(*refs):
        newton_kernel((count_x, count_y, lanes, n_macro, n_micro), *refs)

    outputs = pl.pallas_call(
            body,
            out_shape=[jax.ShapeDtypeStruct(load.shape, jnp.float32)] * 2,
            in_specs=[anywhere] * 8 + [vmem] * 2,
            out_specs=[vmem, vmem],
            scratch_shapes=[
                held(*displacement.shape),
                held(*load.shape),
                pltpu.VMEM((points // 128, 128), jnp.int32),
                pltpu.VMEM((points // 128, 128), jnp.int32),
                half(size, size),
                half(size, size),
                half(6, size),
                half(6, size),
                half(3 * size, 16),
                half(tall, size),
                half(tall, size),
                held(tall, size),
                half(n_micro * slots, points),
                held(len(AROUND), *load.shape),
                held(len(AROUND), 8, points),
                held(6, outer_rows, lanes),
                held(3, rows, lanes),
                held(3, *displacement.shape),
                held(8, points),
                held(n_micro, 8, slots),
                held(n_micro, 8, slots),
                held(n_micro, tall, slots),
                held(n_micro, tall, slots),
                held(tall, points),
                held(sides, tall - 8, lanes),
                held(6 + len(PAIRS), rows, lanes),
                held(ITERS, 3, rows, lanes),
                held(ITERS, len(AROUND), side, lanes),
                held(ITERS, len(AROUND), side, lanes),
                held(8, 128),
                held(n_micro, 8, 128),
                held(8, 128),
                held(n_macro, 8, 128),
                held(1, 128),
                held(total, 1, 128),
                dma((8,)),
                dma((3,)),
                dma((3,)),
                dma((1,)),
                dma((n_micro,)),
                dma((1,)),
                dma((n_micro,)),
                dma((3,)),
                dma((3,)),
                dma((2, len(AROUND))),
                dma((2, len(AROUND))),
                dma((3,)),
                dma((3,)),
            ],
            compiler_params=pltpu.CompilerParams(collective_id=0, has_side_effects=True),
            name="newton_step",
        )(
            displacement,
            load,
            routes.reshape(points // 128, 128),
            counts.reshape(points // 128, 128),
            stiffness[0],
            precond[0],
            forcing[0],
            coupling[0].T,
            lame_first.reshape(1, 1),
            lame_shear.reshape(1, 1),
        )
    return tuple(
        pl.pallas_call(
            hand_over,
            out_shape=[jax.ShapeDtypeStruct(load.shape, jnp.float32)] * 2,
            in_specs=[vmem, vmem],
            out_specs=[vmem, vmem],
            name="hand_over",
        )(*outputs)
    )


def solution(mesh):
    in_specs = (
        P(None, "macro", "micro", None),
        P(None, "macro", "micro", None),
        P("macro", "micro", None, None),
        P("macro", "micro", None),
        P("micro", None, None),
        P("micro", None, None),
        P("micro", None, None),
        P("micro", None, None),
        P("micro"),
        P("micro"),
    )
    out_specs = (P(None, "macro", "micro", None), P(None, "macro", "micro", None))
    return jax.shard_map(shards, mesh=mesh, in_specs=in_specs, out_specs=out_specs, check_vma=False)
```

```python
import jax
import jax.numpy as jnp
from jax import lax
from jax.experimental import pallas as pl
from jax.experimental.pallas import tpu as pltpu
from jax.sharding import PartitionSpec as P

ITMAX = 4
ITERS = 5


BETA = 0.1
OMEGA = 0.8
MASS = 0.1
VOIGT = ((0, 5, 4), (5, 1, 3), (4, 3, 2))
PAIRS = tuple((first, second) for first in range(6) for second in range(first, 6))
PAIR_AT = {pair: at for at, pair in enumerate(PAIRS)}
AROUND = tuple((dx, dy) for dx in (-1, 0, 1) for dy in (-1, 0, 1) if (dx, dy) != (0, 0))
MESH = pl.DeviceIdType.MESH


def strips_of(count_x, count_y):
    strips = []
    for dx, dy in AROUND:
        across = range(count_x if dx >= 0 else 1)
        if dy >= 0:
            strips.append(((dx, dy), 0, len(across) * count_y))
        else:
            strips += [((dx, dy), i * count_y, 1) for i in across]
    return strips


def newton_kernel(
    sizes,
    disp_in,
    load_in,
    routes_in,
    counts_in,
    stiff_in,
    pre_in,
    force_in,
    couple_in,
    first_ref,
    shear_ref,
    inc_ref,
    res_ref,
    disp_ref,
    load_ref,
    routes_ref,
    counts_ref,
    stiff,
    pre,
    force_ref,
    couple_ref,
    maps,
    couple,
    products,
    wide_products,
    spots,
    near_load,
    near_stress,
    outer,
    loads,
    near_disp,
    bundle,
    route_out,
    route_in,
    back_out,
    back_in,
    values,
    beside,
    elem,
    basis,
    send_halo,
    halo,
    part,
    got_micro,
    middle,
    got_macro,
    last_part,
    last_all,
    input_sem,
    disp_send,
    disp_recv,
    route_send,
    route_recv,
    back_send,
    back_recv,
    side_send,
    side_recv,
    send_sem,
    recv_sem,
    sum_send,
    sum_recv,
):
    count_x, count_y, lanes, n_macro, n_micro = sizes
    wide = count_y + 2
    rows = basis.shape[2]
    points = spots.shape[1]
    slots = spots.shape[0] // n_micro
    pairs = n_micro // 2
    groups = points // 128
    size = stiff.shape[0]
    tall = couple.shape[0]
    total = n_macro * n_micro
    a, b = lax.axis_index("macro"), lax.axis_index("micro")
    me = a * n_micro + b

    def device(other):
        return (other // n_micro, lax.rem(other, n_micro))

    def inside(dx, dy):
        test = None
        for place, step, count in ((a, dx, n_macro), (b, dy, n_micro)):
            if step != 0:
                good = (place > 0) if step < 0 else (place < count - 1)
                test = good if test is None else jnp.logical_and(test, good)
        return test

    barrier = pltpu.get_barrier_semaphore()

    def every(count, act):
        if count <= 32:
            for step in range(1, count):
                act(step)
        else:
            lax.fori_loop(1, count, lambda step, carry: (act(step), carry)[1], 0)

    def greet(row, column):
        pl.semaphore_signal(barrier, inc=1, device_id=(row, column), device_id_type=MESH)

    for step in range(1, n_macro):
        for aside in range(3):
            greet(lax.rem(a + step, n_macro), lax.rem(b + n_micro - 1 + aside, n_micro))
    every(n_micro, lambda step: greet(a, lax.rem(b + step, n_micro)))
    greeted = 3 * (n_macro - 1) + n_micro - 1
    inputs = {}
    for at, (name, source, target) in enumerate(
        (
            ("routes", routes_in, routes_ref),
            ("force", force_in, force_ref),
            ("couple", couple_in, couple_ref),
            ("counts", counts_in, counts_ref),
            ("disp", disp_in, disp_ref),
            ("load", load_in, load_ref),
            ("pre", pre_in, pre),
            ("stiff", stiff_in, stiff),
        )
    ):
        inputs[name] = pltpu.make_async_copy(source, target, input_sem.at[at])
        inputs[name].start()

    inputs["disp"].wait()
    after = ((1, 0), (0, 1), (1, 1))
    pl.semaphore_wait(barrier, greeted)

    def show(at):
        dx, dy = after[at]
        return pltpu.make_async_remote_copy(
            src_ref=disp_ref,
            dst_ref=near_disp.at[at],
            send_sem=disp_send.at[at],
            recv_sem=disp_recv.at[at],
            device_id=(a - dx, b - dy),
            device_id_type=MESH,
        )

    for at, (dx, dy) in enumerate(after):

        @pl.when(inside(-dx, -dy))
        def _():
            show(at).start()

    inputs["load"].wait()

    def load_copy(at):
        dx, dy = AROUND[at]
        other = len(AROUND) - 1 - at
        return pltpu.make_async_remote_copy(
            src_ref=load_ref,
            dst_ref=near_load.at[other],
            send_sem=send_sem.at[0, at],
            recv_sem=recv_sem.at[0, other],
            device_id=(a + dx, b + dy),
            device_id_type=MESH,
        )

    def load_arrival(at):
        dx, dy = AROUND[at]
        return pltpu.make_async_remote_copy(
            src_ref=load_ref,
            dst_ref=near_load.at[at],
            send_sem=send_sem.at[0, at],
            recv_sem=recv_sem.at[0, at],
            device_id=(a + dx, b + dy),
            device_id_type=MESH,
        )

    for at, (dx, dy) in enumerate(AROUND):

        @pl.when(inside(dx, dy))
        def _():
            load_copy(at).start()

        @pl.when(jnp.logical_not(inside(dx, dy)))
        def _():
            near_load[at] = jnp.zeros(near_load.shape[1:], jnp.float32)
            near_stress[at] = jnp.zeros(near_stress.shape[1:], jnp.float32)

    outer[...] = jnp.zeros(outer.shape, jnp.float32)
    loads[...] = jnp.zeros(loads.shape, jnp.float32)
    for name in ("routes", "force", "couple", "counts"):
        inputs[name].wait()
    force = force_ref[...].astype(jnp.float32)
    force = jnp.concatenate([force, jnp.zeros((2, size), jnp.float32)], axis=0)
    wide_products[...] = jnp.zeros((tall, size), jnp.float32)
    coupling = couple_ref[...].astype(jnp.float32)
    wide_products[pl.ds(0, 6)] = coupling
    couple[...] = wide_products[...].astype(jnp.bfloat16)
    wide_products[pl.ds(0, 6)] = jnp.zeros((6, size), jnp.float32)
    for at, (first, second) in enumerate(PAIRS):
        wide_products[pl.ds(6 + at, 1)] = coupling[first : first + 1] * coupling[second : second + 1]
    products[...] = wide_products[...].astype(jnp.bfloat16)

    route = routes_ref[...]
    row_of = lax.broadcasted_iota(jnp.int32, (128, 128), 0)
    column_of = lax.broadcasted_iota(jnp.int32, (128, 128), 1)
    until = jnp.where(row_of <= column_of, 1.0, 0.0).astype(jnp.bfloat16)
    named = [jnp.where(route == owner, 1.0, 0.0) for owner in range(n_micro)]
    named = jnp.concatenate(named, axis=0).astype(jnp.bfloat16)
    inner_rank = jnp.dot(named, until, preferred_element_type=jnp.float32)
    whole = jnp.dot(
        named, jnp.ones((128, 128), jnp.bfloat16), preferred_element_type=jnp.float32
    ).astype(jnp.bfloat16)
    span = n_micro * groups
    row_of = lax.broadcasted_iota(jnp.int32, (span, span), 0)
    column_of = lax.broadcasted_iota(jnp.int32, (span, span), 1)
    ahead = jnp.logical_and(column_of < row_of, column_of // groups == row_of // groups)
    before = jnp.dot(
        jnp.where(ahead, 1.0, 0.0).astype(jnp.bfloat16), whole, preferred_element_type=jnp.float32
    )
    ranks = inner_rank + before - 1.0
    rank = jnp.zeros((groups, 128), jnp.float32)
    for owner in range(n_micro):
        rank = jnp.where(route == owner, ranks[owner * groups : (owner + 1) * groups], rank)
    slot_type = jnp.bfloat16 if slots <= 256 else jnp.float32
    slot_at = lax.broadcasted_iota(jnp.int32, (slots, 128), 0).astype(jnp.float32)
    slot_at = slot_at.astype(slot_type)

    def spot(owner, carry):
        local = jnp.where(route == owner, rank, -1.0)
        for g in range(groups):
            near_slot = jnp.broadcast_to(local[g : g + 1], (16, 128)).astype(slot_type)
            near_slot = jnp.concatenate([near_slot] * (slots // 16), axis=0)
            hit = jnp.where(near_slot == slot_at, slot_type(1), slot_type(0))
            low = pl.multiple_of(owner * slots, slots)
            spots[pl.ds(low, slots), g * 128 : (g + 1) * 128] = hit.astype(jnp.bfloat16)
        return carry

    lax.fori_loop(0, n_micro, spot, 0)

    for it in range(basis.shape[0]):
        for c in range(3):
            basis[it, c] = jnp.zeros((rows, lanes), jnp.float32)
    elem[...] = jnp.zeros(elem.shape, jnp.float32)
    values[...] = jnp.zeros(values.shape, jnp.float32)
    bundle[...] = jnp.zeros(bundle.shape, jnp.float32)
    for g in range(groups):
        bundle[6:7, g * 128 : (g + 1) * 128] = counts_ref[g : g + 1].astype(jnp.float32)

    for at, (dx, dy) in enumerate(AROUND):

        @pl.when(jnp.logical_not(inside(dx, dy)))
        def _():
            for it in range(1, ITERS):
                halo[it, at] = jnp.zeros(halo.shape[2:], jnp.float32)

    for at, (dx, dy) in enumerate(after):

        @pl.when(jnp.logical_not(inside(dx, dy)))
        def _():
            near_disp[at] = jnp.zeros(near_disp.shape[1:], jnp.float32)

    owned = [(i, j) for i in range(count_x) for j in range(count_y)]
    column_at = {place: at for at, place in enumerate(owned)}
    handed = [((1, 0), (count_x - 1, j), (0, j + 1)) for j in range(count_y)]
    handed += [((0, 1), (i, count_y - 1), (i + 1, 0)) for i in range(count_x)]
    handed += [((1, 1), (count_x - 1, count_y - 1), (0, 0))]
    for at, ((dx, dy), _, _) in enumerate(handed):

        @pl.when(jnp.logical_not(inside(-dx, -dy)))
        def _():
            beside[at] = jnp.zeros(beside.shape[1:], jnp.float32)

    for name in ("pre", "stiff"):
        inputs[name].wait()

    def split(exact):
        high = exact.astype(jnp.bfloat16).astype(jnp.float32)
        return jnp.concatenate([high, exact - high], axis=0)

    def through(matrix, exact):
        moved = jnp.dot(
            split(exact).astype(jnp.bfloat16), matrix[...], preferred_element_type=jnp.float32
        )
        return moved[:8] + moved[8:]

    first_map = OMEGA * through(pre, force)
    misfit_map = through(stiff, first_map) - force
    turned = jnp.concatenate([split(first_map), split(misfit_map), split(force)], axis=0).T
    for at in range(3):
        maps[pl.ds(at * size, size)] = turned[:, at * 16 : (at + 1) * 16].astype(jnp.bfloat16)
    for c in range(3):
        for i, j in owned:
            basis[0, c, pl.ds((i + 1) * wide + j + 1, 1)] = disp_ref[c, i, j : j + 1]
    for at, (dx, dy) in enumerate(after):

        @pl.when(inside(-dx, -dy))
        def _():
            show(at).wait_send()

        @pl.when(inside(dx, dy))
        def _():
            pltpu.make_async_remote_copy(
                src_ref=disp_ref,
                dst_ref=near_disp.at[at],
                send_sem=disp_send.at[at],
                recv_sem=disp_recv.at[at],
                device_id=(a + dx, b + dy),
                device_id_type=MESH,
            ).wait_recv()

    for c in range(3):
        for j in range(count_y):
            basis[0, c, pl.ds((count_x + 1) * wide + j + 1, 1)] = near_disp[0, c, 0, j : j + 1]
        for i in range(count_x):
            basis[0, c, pl.ds((i + 1) * wide + count_y + 1, 1)] = near_disp[1, c, i, 0:1]
        basis[0, c, pl.ds((count_x + 1) * wide + count_y + 1, 1)] = near_disp[2, c, 0, 0:1]

    row_at = lax.broadcasted_iota(jnp.int32, (rows, lanes), 0)
    lane_at = lax.broadcasted_iota(jnp.int32, (rows, lanes), 1)
    own = row_at < 0
    for i in range(1, count_x + 1):
        low = i * wide + 1
        own = jnp.logical_or(own, jnp.logical_and(row_at >= low, row_at < low + count_y))

    def up(value, axis):
        if axis == 2:
            moved = pltpu.roll(value, lanes - 1, 1)
            return jnp.where(lane_at == lanes - 1, 0.0, moved)
        return pltpu.roll(value, rows - (wide if axis == 0 else 1), 0)

    def down(value, axis):
        if axis == 2:
            return jnp.where(lane_at == 0, 0.0, pltpu.roll(value, 1, 1))
        return pltpu.roll(value, wide if axis == 0 else 1, 0)

    def strain_of(it):
        grads = []
        for c in range(3):
            value = basis[it, c]
            moved = up(value, 2)
            total, gap = value + moved, moved - value
            total_up, gap_up = up(total, 1), up(gap, 1)
            flat, slope_y, slope_z = total + total_up, total_up - total, gap + gap_up
            grads.append(
                (
                    0.25 * (up(flat, 0) - flat),
                    0.25 * (up(slope_y, 0) + slope_y),
                    0.25 * (up(slope_z, 0) + slope_z),
                )
            )
        return [
            grads[0][0],
            grads[1][1],
            grads[2][2],
            grads[1][2] + grads[2][1],
            grads[0][2] + grads[2][0],
            grads[0][1] + grads[1][0],
        ]

    strain = strain_of(0)
    for at, (i, j) in enumerate(owned):
        low = (i + 1) * wide + j + 1
        for k in range(6):
            bundle[k : k + 1, at * lanes : (at + 1) * lanes] = strain[k][low : low + 1]
    exact = bundle[...]
    high = exact.astype(jnp.bfloat16).astype(jnp.float32)
    both = jnp.concatenate([high, exact - high], axis=0).astype(jnp.bfloat16)

    def route_copy(other, mine):
        return pltpu.make_async_remote_copy(
            src_ref=route_out.at[other],
            dst_ref=route_in.at[mine],
            send_sem=route_send.at[0],
            recv_sem=route_recv.at[mine],
            device_id=(a, other),
            device_id_type=MESH,
        )

    chip, core = b // 2, lax.rem(b, 2)

    def pair_rows(place):
        return pl.ds(pl.multiple_of(place * (2 * slots), 2 * slots), 2 * slots)

    def hand_out(at, carry):
        place = lax.rem(chip + pairs - at, pairs)
        moved = lax.dot_general(
            both,
            spots[pair_rows(place)],
            (((1,), (1,)), ((), ())),
            preferred_element_type=jnp.float32,
        )
        moved = moved[:8] + moved[8:]
        for k in range(2):
            other = 2 * place + k
            piece = moved[:, k * slots : (k + 1) * slots]

            @pl.when(other != b)
            def _():
                route_out[other] = piece
                route_copy(other, b).start()

            @pl.when(other == b)
            def _():
                route_in[b] = piece

        return carry

    lax.fori_loop(0, pairs, hand_out, 0)


    lame_first, lame_shear = first_ref[...], shear_ref[...]
    tall_at = lax.broadcasted_iota(jnp.int32, (tall, 2 * slots), 0)
    on_trace = jnp.where(tall_at < 3, lame_first, 0.0)
    on_strain = jnp.where(tall_at < 3, 2.0 * lame_shear, jnp.where(tall_at < 6, lame_shear, 0.0))
    base = jnp.zeros((tall, 2 * slots), jnp.float32)
    for at, (i, j) in enumerate(PAIRS):
        if i == j:
            amount = lame_first + 2.0 * lame_shear if i < 3 else lame_shear
        elif j < 3:
            amount = lame_first
        else:
            continue
        base = jnp.where(tall_at == 6 + at, amount, base)

    def back_copy(other, mine):
        return pltpu.make_async_remote_copy(
            src_ref=back_out.at[other],
            dst_ref=back_in.at[mine],
            send_sem=back_send.at[0],
            recv_sem=back_recv.at[mine],
            device_id=(a, other),
            device_id_type=MESH,
        )

    def solve(at, carry):
        place = lax.rem(chip + at, pairs)
        taken = []
        for k in range(2):
            other = 2 * place + k

            @pl.when(other != b)
            def _():
                route_copy(b, other).wait_recv()

            taken.append(route_in[other])
        points_in = jnp.concatenate(taken, axis=1)
        sweeps = points_in[6:7]
        strain_in = points_in.astype(jnp.bfloat16)
        strain_in = jnp.concatenate([strain_in, strain_in], axis=0)

        def mapped(at):
            return jnp.dot(
                maps[pl.ds(at * size, size)], strain_in, preferred_element_type=jnp.float32
            )

        modes, misfit, modal_load = mapped(0), mapped(1), mapped(2)
        for sweep in range(1, ITMAX):
            if sweep > 1:
                misfit = jnp.dot(
                    stiff[...], modes.astype(jnp.bfloat16), preferred_element_type=jnp.float32
                )
                misfit = misfit - modal_load
            misfit = (misfit + BETA * jnp.tanh(modes)).astype(jnp.bfloat16)
            change = jnp.dot(pre[...], misfit, preferred_element_type=jnp.float32)
            modes = modes - jnp.where(sweeps > sweep, OMEGA, 0.0) * change
        bent = jnp.tanh(modes)
        slope = 1.0 - bent * bent
        trace = points_in[0:1] + points_in[1:2] + points_in[2:3]
        padded = jnp.concatenate(
            [points_in, jnp.zeros((tall - 8, 2 * slots), jnp.float32)], axis=0
        )
        answer = on_trace * trace + on_strain * padded + base
        answer = answer + jnp.dot(
            couple[...], modes.astype(jnp.bfloat16), preferred_element_type=jnp.float32
        )
        answer = answer + jnp.dot(
            products[...], slope.astype(jnp.bfloat16), preferred_element_type=jnp.float32
        )
        for k in range(2):
            other = 2 * place + k
            piece = answer[:, k * slots : (k + 1) * slots]

            @pl.when(other != b)
            def _():
                back_out[other] = piece
                back_copy(other, b).start()

            @pl.when(other == b)
            def _():
                back_in[b] = piece

        return carry

    lax.fori_loop(0, pairs, solve, 0)

    def take_back(at, carry):
        place = lax.rem(chip + pairs - at, pairs)
        taken = []
        for k in range(2):
            other = 2 * place + k

            @pl.when(other != b)
            def _():
                back_copy(b, other).wait_recv()

            taken.append(back_in[other])
        exact = jnp.concatenate(taken, axis=1)
        high = exact.astype(jnp.bfloat16).astype(jnp.float32)
        both = jnp.concatenate([high, exact - high], axis=0).astype(jnp.bfloat16)
        moved = jnp.dot(both, spots[pair_rows(place)], preferred_element_type=jnp.float32)
        values[...] += moved[:tall] + moved[tall:]
        return carry

    lax.fori_loop(0, pairs, take_back, 0)

    def side_copy(at):
        (dx, dy), place, _ = handed[at]
        low = column_at[place] * lanes
        return pltpu.make_async_remote_copy(
            src_ref=values.at[pl.ds(8, tall - 8), pl.ds(low, lanes)],
            dst_ref=beside.at[at],
            send_sem=side_send.at[after.index((dx, dy))],
            recv_sem=side_recv.at[after.index((dx, dy))],
            device_id=(a + dx, b + dy),
            device_id_type=MESH,
        )

    strips = strips_of(count_x, count_y)

    def strip_copy(at):
        (dx, dy), first, count = strips[at]
        columns = pl.ds(first * lanes, count * lanes)
        way = AROUND.index((dx, dy))
        other = len(AROUND) - 1 - way
        return pltpu.make_async_remote_copy(
            src_ref=values.at[pl.ds(0, 8), columns],
            dst_ref=near_stress.at[other, pl.ds(0, 8), columns],
            send_sem=send_sem.at[1, way],
            recv_sem=recv_sem.at[1, other],
            device_id=(a + dx, b + dy),
            device_id_type=MESH,
        )

    def strips_moved(way, sent):
        dx, dy = AROUND[way]
        offset = (dx, dy) if sent else (-dx, -dy)
        count = sum(count for place, _, count in strips if place == offset)
        columns = near_stress.at[way, pl.ds(0, 8), pl.ds(0, count * lanes)]
        return pltpu.make_async_remote_copy(
            src_ref=columns,
            dst_ref=columns,
            send_sem=send_sem.at[1, way],
            recv_sem=recv_sem.at[1, way],
            device_id=(a + dx, b + dy),
            device_id_type=MESH,
        )

    for at, (dx, dy) in enumerate(AROUND):

        @pl.when(inside(dx, dy))
        def _():
            load_copy(at).wait_send()
            load_arrival(at).wait_recv()

    for at, ((dx, dy), _, _) in enumerate(strips):

        @pl.when(inside(dx, dy))
        def _():
            strip_copy(at).start()

    for at, ((dx, dy), _, _) in enumerate(handed):

        @pl.when(inside(dx, dy))
        def _():
            side_copy(at).start()

    def span(step, count, below):
        if step == 0:
            return [(k, k) for k in range(count)]
        if step > 0:
            return [(count, 0)]
        return [(k - below, count + k - below) for k in range(below)]

    for c in range(3):
        for i in range(count_x):
            loads[c, pl.ds((i + 1) * wide + 1, count_y)] = load_ref[c, i]
        for at, (dx, dy) in enumerate(AROUND):
            for i, from_i in span(dx, count_x, 1):
                for j, from_j in span(dy, count_y, 1):
                    loads[c, pl.ds((i + 1) * wide + j + 1, 1)] = near_load[
                        at, c, from_i, from_j : from_j + 1
                    ]

    broad = count_y + 3

    def put_stress(read, i, j):
        for v in range(6):
            outer[v, pl.ds((i + 2) * broad + j + 2, 1)] = read(v)

    def put_tangent(read, row, first=6):
        for v in range(first, 6 + len(PAIRS)):
            elem[v, pl.ds(row, 1)] = read(v)

    for at, (i, j) in enumerate(owned):
        put_stress(lambda v: values[v : v + 1, at * lanes : (at + 1) * lanes], i, j)
        put_tangent(
            lambda v: values[v : v + 1, at * lanes : (at + 1) * lanes], (i + 1) * wide + j + 1
        )
    for at, (dx, dy) in enumerate(AROUND):

        @pl.when(inside(dx, dy))
        def _():
            strips_moved(at, True).wait_send()
            strips_moved(at, False).wait_recv()

    for at, (dx, dy) in enumerate(AROUND):
        for i, from_i in span(dx, count_x, 2):
            for j, from_j in span(dy, count_y, 2):
                low = column_at[from_i, from_j] * lanes
                put_stress(lambda v: near_stress[at, v : v + 1, low : low + lanes], i, j)
    for at, ((dx, dy), place, (i, j)) in enumerate(handed):
        low = column_at[place] * lanes
        source = AROUND.index((-dx, -dy))
        for v in (6, 7):
            elem[v, pl.ds(i * wide + j, 1)] = near_stress[source, v : v + 1, low : low + lanes]
    def near(step, count):
        return {0: list(range(1, count + 1)), -1: [1], 1: [count]}[step]

    def far(step, count):
        return {0: list(range(1, count + 1)), -1: [0], 1: [count + 1]}[step]

    def places(at, pick):
        dx, dy = AROUND[at]
        return [i * wide + j for i in pick(dx, count_x) for j in pick(dy, count_y)]

    def filled(at):
        return 3 * len(places(at, near))

    def hop(it, at):
        dx, dy = AROUND[at]
        other = len(AROUND) - 1 - at
        return pltpu.make_async_remote_copy(
            src_ref=send_halo.at[it, at, pl.ds(0, filled(at))],
            dst_ref=halo.at[it, other, pl.ds(0, filled(at))],
            send_sem=send_sem.at[(it - 1) % 2, at],
            recv_sem=recv_sem.at[(it - 1) % 2, other],
            device_id=(a + dx, b + dy),
            device_id_type=MESH,
        )

    def halo_start(it):
        for at, (dx, dy) in enumerate(AROUND):

            @pl.when(inside(dx, dy))
            def _():
                mine = places(at, near)
                for c in range(3):
                    for k, row in enumerate(mine):
                        send_halo[it, at, pl.ds(c * len(mine) + k, 1)] = basis[it, c, pl.ds(row, 1)]
                hop(it, at).start()

    def halo_finish(it):
        for at, (dx, dy) in enumerate(AROUND):

            @pl.when(inside(dx, dy))
            def _():
                hop(it, at).wait_send()
                pltpu.make_async_remote_copy(
                    src_ref=send_halo.at[it, at, pl.ds(0, filled(at))],
                    dst_ref=halo.at[it, at, pl.ds(0, filled(at))],
                    send_sem=send_sem.at[(it - 1) % 2, at],
                    recv_sem=recv_sem.at[(it - 1) % 2, at],
                    device_id=(a + dx, b + dy),
                    device_id_type=MESH,
                ).wait_recv()

        for at in range(len(AROUND)):
            theirs = places(at, far)
            for c in range(3):
                for k, row in enumerate(theirs):
                    basis[it, c, pl.ds(row, 1)] = halo[it, at, pl.ds(c * len(theirs) + k, 1)]

    def force_of(stress, c, down=down):
        first, second, third = (stress[VOIGT[c][d]] for d in range(3))
        first = first + down(first, 2)
        second = second + down(second, 2)
        third = down(third, 2) - third
        first = first + down(first, 1)
        rest = down(second, 1) - second + third + down(third, 1)
        return 0.25 * (down(first, 0) - first + rest + down(rest, 0))

    def applied(it):
        strain = strain_of(it)
        stress = []
        for i in range(6):
            value = None
            for j in range(6):
                term = elem[6 + PAIR_AT[(min(i, j), max(i, j))]] * strain[j]
                value = term if value is None else value + term
            stress.append(value)
        return [
            jnp.where(own, MASS * basis[it, c] + force_of(stress, c), 0.0) for c in range(3)
        ]

    def product(first, second):
        total = None
        for c in range(3):
            term = first[c] * second[c]
            total = term if total is None else total + term
        total = jnp.sum(jnp.where(own, total, 0.0), axis=0, keepdims=True)
        value = total[:, :128]
        for at in range(128, lanes, 128):
            value = value + total[:, at : at + 128]
        return value

    def stacked(pieces):
        high = -(-len(pieces) // 8) * 8
        tile_row = lax.broadcasted_iota(jnp.int32, (high, 128), 0)
        value = jnp.zeros((high, 128), jnp.float32)
        for at, piece in enumerate(pieces):
            value = jnp.where(tile_row == at, piece, value)
        return value

    def spread(at, src, dst, mine, row, column):
        pltpu.make_async_remote_copy(
            src_ref=src,
            dst_ref=dst.at[mine],
            send_sem=sum_send.at[at],
            recv_sem=sum_recv.at[at],
            device_id=(row, column),
            device_id_type=MESH,
        ).start()

    def gather_start(at, src, dst, count, mine, device):
        every(
            count, lambda step: spread(at, src, dst, mine, *device(lax.rem(mine + step, count)))
        )
        dst[mine] = src[...]

    def gather_all(at, src, dst):
        columns = [lax.rem(b + step, n_micro) for step in range(n_micro)] if total <= 32 else None
        for step in range(n_macro - 1, -1, -1):
            row = lax.rem(a + step, n_macro)
            if columns is None:
                lax.fori_loop(
                    0 if step else 1,
                    n_micro,
                    lambda k, carry: (
                        spread(at, src, dst, me, row, lax.rem(b + k, n_micro)),
                        carry,
                    )[1],
                    0,
                )
            else:
                order = sorted(range(n_micro), key=lambda k: -min(k, n_micro - k))
                for k in order:
                    if step or k:
                        spread(at, src, dst, me, row, columns[k])
        dst[me] = src[...]

    def gather_finish(at, dst, count, device, mine):
        others = dst.at[pl.ds(0, count - 1)]
        pltpu.make_async_remote_copy(
            src_ref=others,
            dst_ref=others,
            send_sem=sum_send.at[at],
            recv_sem=sum_recv.at[at],
            device_id=device(lax.rem(mine + 1, count)),
            device_id_type=MESH,
        ).wait()

    def along_micro(other):
        return (a, other)

    def along_macro(other):
        return (other, b)

    broad_lane = lax.broadcasted_iota(jnp.int32, outer.shape[1:], 1)

    def back(value, axis):
        if axis == 2:
            return jnp.where(broad_lane == 0, 0.0, pltpu.roll(value, 1, 1))
        return pltpu.roll(value, broad if axis == 0 else 1, 0)

    row_x, row_y = row_at // wide, row_at % wide
    real = jnp.logical_and(
        jnp.logical_and(
            row_x >= jnp.where(a > 0, 0, 1),
            row_x <= jnp.where(a < n_macro - 1, count_x + 1, count_x),
        ),
        jnp.logical_and(
            row_y >= jnp.where(b > 0, 0, 1),
            row_y <= jnp.where(b < n_micro - 1, count_y + 1, count_y),
        ),
    )
    stress = [outer[v] for v in range(6)]
    for c in range(3):
        pushed = force_of(stress, c, back)
        for i in range(count_x + 2):
            low = (i + 1) * broad + 1
            basis[0, c, pl.ds(i * wide, wide)] = pushed[low : low + wide]
        basis[0, c] = jnp.where(real, loads[c] - basis[0, c], 0.0)
    for way, (dx, dy) in enumerate(after):
        mine = [at for at, (offset, _, _) in enumerate(handed) if offset == (dx, dy)]
        landed = beside.at[pl.ds(mine[0], len(mine))]
        moved = pltpu.make_async_remote_copy(
            src_ref=landed,
            dst_ref=landed,
            send_sem=side_send.at[way],
            recv_sem=side_recv.at[way],
            device_id=(a + dx, b + dy),
            device_id_type=MESH,
        )

        @pl.when(inside(dx, dy))
        def _():
            moved.wait_send()

        @pl.when(inside(-dx, -dy))
        def _():
            moved.wait_recv()

    for at, (_, _, (i, j)) in enumerate(handed):
        put_tangent(lambda v: beside[at, v - 8 : v - 7], i * wide + j, 8)

    grown = applied(0)
    for c in range(3):
        basis[1, c] = grown[c]
    halo_start(1)
    start = [basis[0, c] for c in range(3)]
    part[...] = stacked([product(start, start), product(grown, grown)])
    gather_start(0, part, got_micro, n_micro, b, along_micro)
    halo_finish(1)
    grown = applied(1)
    for c in range(3):
        basis[2, c] = grown[c]
    halo_start(2)
    gather_finish(0, got_micro, n_micro, along_micro, b)
    middle[...] = jnp.sum(got_micro[...], axis=0)
    gather_start(1, middle, got_macro, n_macro, a, along_macro)
    halo_finish(2)
    grown = applied(2)
    for c in range(3):
        basis[3, c] = grown[c]
    halo_start(3)
    gather_finish(1, got_macro, n_macro, along_macro, a)
    totals = jnp.sum(jnp.sum(got_macro[...], axis=0), axis=1, keepdims=True)
    shift = jnp.sqrt(totals[1:2] / totals[0:1])
    scale = 1.0 / shift
    halo_finish(3)
    for c in range(3):
        powers = [basis[0, c]]
        factor = scale
        for k in range(1, 4):
            powers.append(basis[k, c] * factor)
            factor = factor * scale
        for k in range(1, 4):
            powers = [later - sooner for sooner, later in zip(powers, powers[1:])]
            basis[k, c] = powers[0]

    def field(it):
        return [basis[it, c] for c in range(3)]

    def step(it):
        grown = applied(it)
        return [grown[c] * scale - jnp.where(own, basis[it, c], 0.0) for c in range(3)]

    moments = []
    for it in range(3, ITERS):
        grown = step(it)
        if it + 1 < ITERS:
            for c in range(3):
                basis[it + 1, c] = grown[c]
            halo_start(it + 1)
            for k in range(len(moments) // 2, it + 1):
                moments.append(product(field(k), field(k)))
                moments.append(product(field(k), field(k + 1)))
            halo_finish(it + 1)
    moments.append(product(field(ITERS - 1), field(ITERS - 1)))
    moments.append(product(field(ITERS - 1), grown))
    sums = jnp.sum(stacked(moments), axis=1, keepdims=True)
    diagonal = lax.broadcasted_iota(jnp.int32, (16, 128), 0) == lax.broadcasted_iota(
        jnp.int32, (16, 128), 1
    )
    last_part[...] = jnp.sum(jnp.where(diagonal, sums, 0.0), axis=0, keepdims=True)

    gather_all(2, last_part, last_all)
    gather_finish(2, last_all, total, device, me)
    totals = jnp.sum(last_all[...], axis=0)
    held = [totals[:, k : k + 1] for k in range(2 * ITERS)]

    def inner(first, second, extra=0):
        gathered = {}
        for i, x in enumerate(first):
            for j, y in enumerate(second):
                gathered.setdefault(i + j, []).append(x * y)
        value = None
        for degree, terms in gathered.items():
            total = terms[0]
            for term in terms[1:]:
                total = total + term
            total = total * held[degree + extra]
            value = total if value is None else value + total
        return value

    one = jnp.ones((1, 1), jnp.float32)
    left, toward, done = [one], [one], []
    norm = held[0]
    for it in range(ITERS):
        energy = inner(toward, toward) + inner(toward, toward, 1)
        length = norm / energy
        done = [x + length * scale * p for x, p in zip(done + [0.0], toward)]
        raised = [
            (toward[k] if k < len(toward) else 0.0) + (toward[k - 1] if k > 0 else 0.0)
            for k in range(len(toward) + 1)
        ]
        left = [
            (left[k] if k < len(left) else 0.0) - length * raised[k] for k in range(len(raised))
        ]
        if it + 1 < ITERS:
            fresh = inner(left, left)
            ratio = fresh / norm
            toward = [
                left[k] + (ratio * toward[k] if k < len(toward) else 0.0)
                for k in range(len(left))
            ]
            norm = fresh
    for c in range(3):
        fields = [basis[k, c] for k in range(ITERS)] + [grown[c]]
        moved, rest = None, None
        for k in range(ITERS + 1):
            if k < len(done):
                term = done[k] * fields[k]
                moved = term if moved is None else moved + term
            term = left[k] * fields[k]
            rest = term if rest is None else rest + term
        for i in range(count_x):
            low = (i + 1) * wide + 1
            inc_ref[c, i] = moved[low : low + count_y]
            res_ref[c, i] = rest[low : low + count_y]

    for buffer, semaphore in ((route_out, route_send), (back_out, back_send)):
        others = buffer.at[pl.ds(0, n_micro - 1)]
        pltpu.make_async_remote_copy(
            src_ref=others,
            dst_ref=others,
            send_sem=semaphore.at[0],
            recv_sem=semaphore.at[0],
            device_id=(a, lax.rem(b + 1, n_micro)),
            device_id_type=MESH,
        ).wait_send()


def hand_over(inc_in, res_in, inc_ref, res_ref):
    inc_ref[...] = inc_in[...]
    res_ref[...] = res_in[...]


def shards(
    displacement,
    load,
    routes,
    counts,
    stiffness,
    precond,
    forcing,
    coupling,
    lame_first,
    lame_shear,
):
    _, count_x, count_y, lanes = displacement.shape
    points = count_x * count_y * lanes
    n_macro, n_micro = lax.axis_size("macro"), lax.axis_size("micro")
    capacity = max(2, 2 * points // n_micro)
    slots = -(-capacity // 128) * 128
    size = stiffness.shape[1]
    tall = -(-(6 + len(PAIRS)) // 8) * 8
    rows = -(-(count_x + 2) * (count_y + 2) // 8) * 8
    side = -(-3 * max(count_x, count_y) // 8) * 8
    total = n_macro * n_micro
    sides = count_x + count_y + 1
    outer_rows = -(-(count_x + 3) * (count_y + 3) // 8) * 8
    vmem = pl.BlockSpec(memory_space=pltpu.VMEM)
    anywhere = pl.BlockSpec(memory_space=pl.ANY)
    dma = pltpu.SemaphoreType.DMA

    def held(*shape):
        return pltpu.VMEM(shape, jnp.float32)

    def half(*shape):
        return pltpu.VMEM(shape, jnp.bfloat16)

    def body(*refs):
        newton_kernel((count_x, count_y, lanes, n_macro, n_micro), *refs)

    outputs = pl.pallas_call(
            body,
            out_shape=[jax.ShapeDtypeStruct(load.shape, jnp.float32)] * 2,
            in_specs=[anywhere] * 8 + [vmem] * 2,
            out_specs=[vmem, vmem],
            scratch_shapes=[
                held(*displacement.shape),
                held(*load.shape),
                pltpu.VMEM((points // 128, 128), jnp.int32),
                pltpu.VMEM((points // 128, 128), jnp.int32),
                half(size, size),
                half(size, size),
                half(6, size),
                half(6, size),
                half(3 * size, 16),
                half(tall, size),
                half(tall, size),
                held(tall, size),
                half(n_micro * slots, points),
                held(len(AROUND), *load.shape),
                held(len(AROUND), 8, points),
                held(6, outer_rows, lanes),
                held(3, rows, lanes),
                held(3, *displacement.shape),
                held(8, points),
                held(n_micro, 8, slots),
                held(n_micro, 8, slots),
                held(n_micro, tall, slots),
                held(n_micro, tall, slots),
                held(tall, points),
                held(sides, tall - 8, lanes),
                held(6 + len(PAIRS), rows, lanes),
                held(ITERS, 3, rows, lanes),
                held(ITERS, len(AROUND), side, lanes),
                held(ITERS, len(AROUND), side, lanes),
                held(8, 128),
                held(n_micro, 8, 128),
                held(8, 128),
                held(n_macro, 8, 128),
                held(1, 128),
                held(total, 1, 128),
                dma((8,)),
                dma((3,)),
                dma((3,)),
                dma((1,)),
                dma((n_micro,)),
                dma((1,)),
                dma((n_micro,)),
                dma((3,)),
                dma((3,)),
                dma((2, len(AROUND))),
                dma((2, len(AROUND))),
                dma((3,)),
                dma((3,)),
            ],
            compiler_params=pltpu.CompilerParams(collective_id=0, has_side_effects=True),
            name="newton_step",
        )(
            displacement,
            load,
            routes.reshape(points // 128, 128),
            counts.reshape(points // 128, 128),
            stiffness[0],
            precond[0],
            forcing[0],
            coupling[0].T,
            lame_first.reshape(1, 1),
            lame_shear.reshape(1, 1),
        )
    return tuple(
        pl.pallas_call(
            hand_over,
            out_shape=[jax.ShapeDtypeStruct(load.shape, jnp.float32)] * 2,
            in_specs=[vmem, vmem],
            out_specs=[vmem, vmem],
            name="hand_over",
        )(*outputs)
    )


def solution(mesh):
    in_specs = (
        P(None, "macro", "micro", None),
        P(None, "macro", "micro", None),
        P("macro", "micro", None, None),
        P("macro", "micro", None),
        P("micro", None, None),
        P("micro", None, None),
        P("micro", None, None),
        P("micro", None, None),
        P("micro"),
        P("micro"),
    )
    out_specs = (P(None, "macro", "micro", None), P(None, "macro", "micro", None))
    return jax.shard_map(shards, mesh=mesh, in_specs=in_specs, out_specs=out_specs, check_vma=False)
```

```python
import jax
import jax.numpy as jnp
from jax import lax
from jax.experimental import pallas as pl
from jax.experimental.pallas import tpu as pltpu
from jax.sharding import PartitionSpec as P

ITMAX = 4
ITERS = 5


BETA = 0.1
OMEGA = 0.8
MASS = 0.1
VOIGT = ((0, 5, 4), (5, 1, 3), (4, 3, 2))
PAIRS = tuple((first, second) for first in range(6) for second in range(first, 6))
PAIR_AT = {pair: at for at, pair in enumerate(PAIRS)}
AROUND = tuple((dx, dy) for dx in (-1, 0, 1) for dy in (-1, 0, 1) if (dx, dy) != (0, 0))
MESH = pl.DeviceIdType.MESH


def strips_of(count_x, count_y):
    strips = []
    for dx, dy in AROUND:
        across = range(count_x if dx >= 0 else 1)
        if dy >= 0:
            strips.append(((dx, dy), 0, len(across) * count_y))
        else:
            strips += [((dx, dy), i * count_y, 1) for i in across]
    return strips


def newton_kernel(
    sizes,
    disp_in,
    load_in,
    routes_in,
    counts_in,
    stiff_in,
    pre_in,
    force_in,
    couple_in,
    first_ref,
    shear_ref,
    inc_ref,
    res_ref,
    disp_ref,
    load_ref,
    routes_ref,
    counts_ref,
    stiff,
    pre,
    force_ref,
    couple_ref,
    maps,
    couple,
    products,
    wide_products,
    spots,
    near_load,
    near_stress,
    outer,
    loads,
    near_disp,
    bundle,
    route_out,
    route_in,
    back_out,
    back_in,
    values,
    beside,
    elem,
    basis,
    send_halo,
    halo,
    part,
    got_micro,
    middle,
    got_macro,
    last_part,
    last_all,
    input_sem,
    disp_send,
    disp_recv,
    route_send,
    route_recv,
    back_send,
    back_recv,
    side_send,
    side_recv,
    send_sem,
    recv_sem,
    sum_send,
    sum_recv,
):
    count_x, count_y, lanes, n_macro, n_micro = sizes
    wide = count_y + 2
    rows = basis.shape[2]
    points = spots.shape[1]
    slots = spots.shape[0] // n_micro
    pairs = n_micro // 2
    groups = points // 128
    size = stiff.shape[0]
    tall = couple.shape[0]
    total = n_macro * n_micro
    a, b = lax.axis_index("macro"), lax.axis_index("micro")
    me = a * n_micro + b

    def device(other):
        return (other // n_micro, lax.rem(other, n_micro))

    def inside(dx, dy):
        test = None
        for place, step, count in ((a, dx, n_macro), (b, dy, n_micro)):
            if step != 0:
                good = (place > 0) if step < 0 else (place < count - 1)
                test = good if test is None else jnp.logical_and(test, good)
        return test

    barrier = pltpu.get_barrier_semaphore()

    def every(count, act):
        if count <= 32:
            for step in range(1, count):
                act(step)
        else:
            lax.fori_loop(1, count, lambda step, carry: (act(step), carry)[1], 0)

    def greet(row, column):
        pl.semaphore_signal(barrier, inc=1, device_id=(row, column), device_id_type=MESH)

    for step in range(1, n_macro):
        for aside in range(3):
            greet(lax.rem(a + step, n_macro), lax.rem(b + n_micro - 1 + aside, n_micro))
    every(n_micro, lambda step: greet(a, lax.rem(b + step, n_micro)))
    greeted = 3 * (n_macro - 1) + n_micro - 1
    inputs = {}
    for at, (name, source, target) in enumerate(
        (
            ("routes", routes_in, routes_ref),
            ("force", force_in, force_ref),
            ("couple", couple_in, couple_ref),
            ("counts", counts_in, counts_ref),
            ("disp", disp_in, disp_ref),
            ("load", load_in, load_ref),
            ("pre", pre_in, pre),
            ("stiff", stiff_in, stiff),
        )
    ):
        inputs[name] = pltpu.make_async_copy(source, target, input_sem.at[at])
        inputs[name].start()

    inputs["disp"].wait()
    after = ((1, 0), (0, 1), (1, 1))
    pl.semaphore_wait(barrier, greeted)

    def show(at):
        dx, dy = after[at]
        return pltpu.make_async_remote_copy(
            src_ref=disp_ref,
            dst_ref=near_disp.at[at],
            send_sem=disp_send.at[at],
            recv_sem=disp_recv.at[at],
            device_id=(a - dx, b - dy),
            device_id_type=MESH,
        )

    for at, (dx, dy) in enumerate(after):

        @pl.when(inside(-dx, -dy))
        def _():
            show(at).start()

    inputs["load"].wait()

    def load_copy(at):
        dx, dy = AROUND[at]
        other = len(AROUND) - 1 - at
        return pltpu.make_async_remote_copy(
            src_ref=load_ref,
            dst_ref=near_load.at[other],
            send_sem=send_sem.at[0, at],
            recv_sem=recv_sem.at[0, other],
            device_id=(a + dx, b + dy),
            device_id_type=MESH,
        )

    def load_arrival(at):
        dx, dy = AROUND[at]
        return pltpu.make_async_remote_copy(
            src_ref=load_ref,
            dst_ref=near_load.at[at],
            send_sem=send_sem.at[0, at],
            recv_sem=recv_sem.at[0, at],
            device_id=(a + dx, b + dy),
            device_id_type=MESH,
        )

    for at, (dx, dy) in enumerate(AROUND):

        @pl.when(inside(dx, dy))
        def _():
            load_copy(at).start()

        @pl.when(jnp.logical_not(inside(dx, dy)))
        def _():
            near_load[at] = jnp.zeros(near_load.shape[1:], jnp.float32)
            near_stress[at] = jnp.zeros(near_stress.shape[1:], jnp.float32)

    outer[...] = jnp.zeros(outer.shape, jnp.float32)
    loads[...] = jnp.zeros(loads.shape, jnp.float32)
    for name in ("routes", "force", "couple", "counts"):
        inputs[name].wait()
    force = force_ref[...].astype(jnp.float32)
    force = jnp.concatenate([force, jnp.zeros((2, size), jnp.float32)], axis=0)
    wide_products[...] = jnp.zeros((tall, size), jnp.float32)
    coupling = couple_ref[...].astype(jnp.float32)
    wide_products[pl.ds(0, 6)] = coupling
    couple[...] = wide_products[...].astype(jnp.bfloat16)
    wide_products[pl.ds(0, 6)] = jnp.zeros((6, size), jnp.float32)
    for at, (first, second) in enumerate(PAIRS):
        wide_products[pl.ds(8 + at, 1)] = coupling[first : first + 1] * coupling[second : second + 1]
    products[...] = wide_products[...].astype(jnp.bfloat16)

    route = routes_ref[...]
    row_of = lax.broadcasted_iota(jnp.int32, (128, 128), 0)
    column_of = lax.broadcasted_iota(jnp.int32, (128, 128), 1)
    until = jnp.where(row_of <= column_of, 1.0, 0.0).astype(jnp.bfloat16)
    named = [jnp.where(route == owner, 1.0, 0.0) for owner in range(n_micro)]
    named = jnp.concatenate(named, axis=0).astype(jnp.bfloat16)
    inner_rank = jnp.dot(named, until, preferred_element_type=jnp.float32)
    whole = jnp.dot(
        named, jnp.ones((128, 128), jnp.bfloat16), preferred_element_type=jnp.float32
    ).astype(jnp.bfloat16)
    span = n_micro * groups
    row_of = lax.broadcasted_iota(jnp.int32, (span, span), 0)
    column_of = lax.broadcasted_iota(jnp.int32, (span, span), 1)
    ahead = jnp.logical_and(column_of < row_of, column_of // groups == row_of // groups)
    before = jnp.dot(
        jnp.where(ahead, 1.0, 0.0).astype(jnp.bfloat16), whole, preferred_element_type=jnp.float32
    )
    ranks = inner_rank + before - 1.0
    rank = jnp.zeros((groups, 128), jnp.float32)
    for owner in range(n_micro):
        rank = jnp.where(route == owner, ranks[owner * groups : (owner + 1) * groups], rank)
    slot_type = jnp.bfloat16 if slots <= 256 else jnp.float32
    slot_at = lax.broadcasted_iota(jnp.int32, (slots, 128), 0).astype(jnp.float32)
    slot_at = slot_at.astype(slot_type)

    def spot(owner, carry):
        local = jnp.where(route == owner, rank, -1.0)
        for g in range(groups):
            near_slot = jnp.broadcast_to(local[g : g + 1], (16, 128)).astype(slot_type)
            near_slot = jnp.concatenate([near_slot] * (slots // 16), axis=0)
            hit = jnp.where(near_slot == slot_at, slot_type(1), slot_type(0))
            low = pl.multiple_of(owner * slots, slots)
            spots[pl.ds(low, slots), g * 128 : (g + 1) * 128] = hit.astype(jnp.bfloat16)
        return carry

    lax.fori_loop(0, n_micro, spot, 0)

    for it in range(basis.shape[0]):
        for c in range(3):
            basis[it, c] = jnp.zeros((rows, lanes), jnp.float32)
    elem[...] = jnp.zeros(elem.shape, jnp.float32)
    values[...] = jnp.zeros(values.shape, jnp.float32)
    bundle[...] = jnp.zeros(bundle.shape, jnp.float32)
    for g in range(groups):
        bundle[6:7, g * 128 : (g + 1) * 128] = counts_ref[g : g + 1].astype(jnp.float32)

    for at, (dx, dy) in enumerate(AROUND):

        @pl.when(jnp.logical_not(inside(dx, dy)))
        def _():
            for it in range(1, ITERS):
                halo[it, at] = jnp.zeros(halo.shape[2:], jnp.float32)

    for at, (dx, dy) in enumerate(after):

        @pl.when(jnp.logical_not(inside(dx, dy)))
        def _():
            near_disp[at] = jnp.zeros(near_disp.shape[1:], jnp.float32)

    owned = [(i, j) for i in range(count_x) for j in range(count_y)]
    column_at = {place: at for at, place in enumerate(owned)}
    handed = [((1, 0), (count_x - 1, j), (0, j + 1)) for j in range(count_y)]
    handed += [((0, 1), (i, count_y - 1), (i + 1, 0)) for i in range(count_x)]
    handed += [((1, 1), (count_x - 1, count_y - 1), (0, 0))]
    for at, ((dx, dy), _, _) in enumerate(handed):

        @pl.when(jnp.logical_not(inside(-dx, -dy)))
        def _():
            beside[at] = jnp.zeros(beside.shape[1:], jnp.float32)

    for name in ("pre", "stiff"):
        inputs[name].wait()

    def split(exact):
        high = exact.astype(jnp.bfloat16).astype(jnp.float32)
        return jnp.concatenate([high, exact - high], axis=0)

    def through(matrix, exact):
        moved = jnp.dot(
            split(exact).astype(jnp.bfloat16), matrix[...], preferred_element_type=jnp.float32
        )
        return moved[:8] + moved[8:]

    first_map = OMEGA * through(pre, force)
    misfit_map = through(stiff, first_map) - force
    turned = jnp.concatenate([split(first_map), split(misfit_map), split(force)], axis=0).T
    for at in range(3):
        maps[pl.ds(at * size, size)] = turned[:, at * 16 : (at + 1) * 16].astype(jnp.bfloat16)
    for c in range(3):
        for i, j in owned:
            basis[0, c, pl.ds((i + 1) * wide + j + 1, 1)] = disp_ref[c, i, j : j + 1]
    for at, (dx, dy) in enumerate(after):

        @pl.when(inside(-dx, -dy))
        def _():
            show(at).wait_send()

        @pl.when(inside(dx, dy))
        def _():
            pltpu.make_async_remote_copy(
                src_ref=disp_ref,
                dst_ref=near_disp.at[at],
                send_sem=disp_send.at[at],
                recv_sem=disp_recv.at[at],
                device_id=(a + dx, b + dy),
                device_id_type=MESH,
            ).wait_recv()

    for c in range(3):
        for j in range(count_y):
            basis[0, c, pl.ds((count_x + 1) * wide + j + 1, 1)] = near_disp[0, c, 0, j : j + 1]
        for i in range(count_x):
            basis[0, c, pl.ds((i + 1) * wide + count_y + 1, 1)] = near_disp[1, c, i, 0:1]
        basis[0, c, pl.ds((count_x + 1) * wide + count_y + 1, 1)] = near_disp[2, c, 0, 0:1]

    row_at = lax.broadcasted_iota(jnp.int32, (rows, lanes), 0)
    lane_at = lax.broadcasted_iota(jnp.int32, (rows, lanes), 1)
    own = row_at < 0
    for i in range(1, count_x + 1):
        low = i * wide + 1
        own = jnp.logical_or(own, jnp.logical_and(row_at >= low, row_at < low + count_y))

    def up(value, axis):
        if axis == 2:
            moved = pltpu.roll(value, lanes - 1, 1)
            return jnp.where(lane_at == lanes - 1, 0.0, moved)
        return pltpu.roll(value, rows - (wide if axis == 0 else 1), 0)

    def down(value, axis):
        if axis == 2:
            return jnp.where(lane_at == 0, 0.0, pltpu.roll(value, 1, 1))
        return pltpu.roll(value, wide if axis == 0 else 1, 0)

    def strain_of(it):
        grads = []
        for c in range(3):
            value = basis[it, c]
            moved = up(value, 2)
            total, gap = value + moved, moved - value
            total_up, gap_up = up(total, 1), up(gap, 1)
            flat, slope_y, slope_z = total + total_up, total_up - total, gap + gap_up
            grads.append(
                (
                    0.25 * (up(flat, 0) - flat),
                    0.25 * (up(slope_y, 0) + slope_y),
                    0.25 * (up(slope_z, 0) + slope_z),
                )
            )
        return [
            grads[0][0],
            grads[1][1],
            grads[2][2],
            grads[1][2] + grads[2][1],
            grads[0][2] + grads[2][0],
            grads[0][1] + grads[1][0],
        ]

    strain = strain_of(0)
    for at, (i, j) in enumerate(owned):
        low = (i + 1) * wide + j + 1
        for k in range(6):
            bundle[k : k + 1, at * lanes : (at + 1) * lanes] = strain[k][low : low + 1]
    exact = bundle[...]
    high = exact.astype(jnp.bfloat16).astype(jnp.float32)
    both = jnp.concatenate([high, exact - high], axis=0).astype(jnp.bfloat16)

    def route_copy(other, mine):
        return pltpu.make_async_remote_copy(
            src_ref=route_out.at[other],
            dst_ref=route_in.at[mine],
            send_sem=route_send.at[0],
            recv_sem=route_recv.at[mine],
            device_id=(a, other),
            device_id_type=MESH,
        )

    chip, core = b // 2, lax.rem(b, 2)

    def pair_rows(place):
        return pl.ds(pl.multiple_of(place * (2 * slots), 2 * slots), 2 * slots)

    def hand_out(at, carry):
        place = lax.rem(chip + pairs - at, pairs)
        moved = lax.dot_general(
            both,
            spots[pair_rows(place)],
            (((1,), (1,)), ((), ())),
            preferred_element_type=jnp.float32,
        )
        moved = moved[:8] + moved[8:]
        for k in range(2):
            other = 2 * place + k
            piece = moved[:, k * slots : (k + 1) * slots]

            @pl.when(other != b)
            def _():
                route_out[other] = piece
                route_copy(other, b).start()

            @pl.when(other == b)
            def _():
                route_in[b] = piece

        return carry

    lax.fori_loop(0, pairs, hand_out, 0)


    lame_first, lame_shear = first_ref[...], shear_ref[...]
    tall_at = lax.broadcasted_iota(jnp.int32, (tall, 2 * slots), 0)
    on_trace = jnp.where(tall_at < 3, lame_first, 0.0)
    on_strain = jnp.where(tall_at < 3, 2.0 * lame_shear, jnp.where(tall_at < 6, lame_shear, 0.0))
    base = jnp.zeros((tall, 2 * slots), jnp.float32)
    for at, (i, j) in enumerate(PAIRS):
        if i == j:
            amount = lame_first + 2.0 * lame_shear if i < 3 else lame_shear
        elif j < 3:
            amount = lame_first
        else:
            continue
        base = jnp.where(tall_at == 8 + at, amount, base)

    def back_copy(other, mine):
        return pltpu.make_async_remote_copy(
            src_ref=back_out.at[other],
            dst_ref=back_in.at[mine],
            send_sem=back_send.at[0],
            recv_sem=back_recv.at[mine],
            device_id=(a, other),
            device_id_type=MESH,
        )

    def solve(at, carry):
        place = lax.rem(chip + at, pairs)
        taken = []
        for k in range(2):
            other = 2 * place + k

            @pl.when(other != b)
            def _():
                route_copy(b, other).wait_recv()

            taken.append(route_in[other])
        points_in = jnp.concatenate(taken, axis=1)
        sweeps = points_in[6:7]
        strain_in = points_in.astype(jnp.bfloat16)
        strain_in = jnp.concatenate([strain_in, strain_in], axis=0)

        def mapped(at):
            return jnp.dot(
                maps[pl.ds(at * size, size)], strain_in, preferred_element_type=jnp.float32
            )

        modes, misfit, modal_load = mapped(0), mapped(1), mapped(2)
        for sweep in range(1, ITMAX):
            if sweep > 1:
                misfit = jnp.dot(
                    stiff[...], modes.astype(jnp.bfloat16), preferred_element_type=jnp.float32
                )
                misfit = misfit - modal_load
            misfit = (misfit + BETA * jnp.tanh(modes)).astype(jnp.bfloat16)
            change = jnp.dot(pre[...], misfit, preferred_element_type=jnp.float32)
            modes = modes - jnp.where(sweeps > sweep, OMEGA, 0.0) * change
        bent = jnp.tanh(modes)
        slope = 1.0 - bent * bent
        trace = points_in[0:1] + points_in[1:2] + points_in[2:3]
        padded = jnp.concatenate(
            [points_in, jnp.zeros((tall - 8, 2 * slots), jnp.float32)], axis=0
        )
        answer = on_trace * trace + on_strain * padded + base
        answer = answer + jnp.dot(
            couple[...], modes.astype(jnp.bfloat16), preferred_element_type=jnp.float32
        )
        answer = answer + jnp.dot(
            products[...], slope.astype(jnp.bfloat16), preferred_element_type=jnp.float32
        )
        for k in range(2):
            other = 2 * place + k
            piece = answer[:, k * slots : (k + 1) * slots]

            @pl.when(other != b)
            def _():
                back_out[other] = piece
                back_copy(other, b).start()

            @pl.when(other == b)
            def _():
                back_in[b] = piece

        return carry

    lax.fori_loop(0, pairs, solve, 0)

    def take_back(at, carry):
        place = lax.rem(chip + pairs - at, pairs)
        taken = []
        for k in range(2):
            other = 2 * place + k

            @pl.when(other != b)
            def _():
                back_copy(b, other).wait_recv()

            taken.append(back_in[other])
        exact = jnp.concatenate(taken, axis=1)
        high = exact.astype(jnp.bfloat16).astype(jnp.float32)
        both = jnp.concatenate([high, exact - high], axis=0).astype(jnp.bfloat16)
        moved = jnp.dot(both, spots[pair_rows(place)], preferred_element_type=jnp.float32)
        values[...] += moved[:tall] + moved[tall:]
        return carry

    lax.fori_loop(0, pairs, take_back, 0)

    even = len(PAIRS) // 8 * 8
    parts = [part for part in ((0, even), (even, len(PAIRS) - even)) if part[1] > 0]

    def side_copy(at, part):
        (dx, dy), place, _ = handed[at]
        first, count = parts[part]
        low = column_at[place] * lanes
        return pltpu.make_async_remote_copy(
            src_ref=values.at[pl.ds(8 + first, count), pl.ds(low, lanes)],
            dst_ref=beside.at[at, pl.ds(first, count)],
            send_sem=side_send.at[part, after.index((dx, dy))],
            recv_sem=side_recv.at[part, after.index((dx, dy))],
            device_id=(a + dx, b + dy),
            device_id_type=MESH,
        )

    strips = strips_of(count_x, count_y)

    def strip_copy(at):
        (dx, dy), first, count = strips[at]
        columns = pl.ds(first * lanes, count * lanes)
        way = AROUND.index((dx, dy))
        other = len(AROUND) - 1 - way
        return pltpu.make_async_remote_copy(
            src_ref=values.at[pl.ds(0, 6), columns],
            dst_ref=near_stress.at[other, pl.ds(0, 6), columns],
            send_sem=send_sem.at[1, way],
            recv_sem=recv_sem.at[1, other],
            device_id=(a + dx, b + dy),
            device_id_type=MESH,
        )

    def strips_moved(way, sent):
        dx, dy = AROUND[way]
        offset = (dx, dy) if sent else (-dx, -dy)
        count = sum(count for place, _, count in strips if place == offset)
        columns = near_stress.at[way, pl.ds(0, 6), pl.ds(0, count * lanes)]
        return pltpu.make_async_remote_copy(
            src_ref=columns,
            dst_ref=columns,
            send_sem=send_sem.at[1, way],
            recv_sem=recv_sem.at[1, way],
            device_id=(a + dx, b + dy),
            device_id_type=MESH,
        )

    for at, (dx, dy) in enumerate(AROUND):

        @pl.when(inside(dx, dy))
        def _():
            load_copy(at).wait_send()
            load_arrival(at).wait_recv()

    for at, ((dx, dy), _, _) in enumerate(strips):

        @pl.when(inside(dx, dy))
        def _():
            strip_copy(at).start()

    for at, ((dx, dy), _, _) in enumerate(handed):

        @pl.when(inside(dx, dy))
        def _():
            for part in range(len(parts)):
                side_copy(at, part).start()

    def span(step, count, below):
        if step == 0:
            return [(k, k) for k in range(count)]
        if step > 0:
            return [(count, 0)]
        return [(k - below, count + k - below) for k in range(below)]

    for c in range(3):
        for i in range(count_x):
            loads[c, pl.ds((i + 1) * wide + 1, count_y)] = load_ref[c, i]
        for at, (dx, dy) in enumerate(AROUND):
            for i, from_i in span(dx, count_x, 1):
                for j, from_j in span(dy, count_y, 1):
                    loads[c, pl.ds((i + 1) * wide + j + 1, 1)] = near_load[
                        at, c, from_i, from_j : from_j + 1
                    ]

    broad = count_y + 3

    def put_stress(read, i, j):
        for v in range(6):
            outer[v, pl.ds((i + 2) * broad + j + 2, 1)] = read(v)

    def put_tangent(read, row):
        for v in range(len(PAIRS)):
            elem[v, pl.ds(row, 1)] = read(v)

    for at, (i, j) in enumerate(owned):
        put_stress(lambda v: values[v : v + 1, at * lanes : (at + 1) * lanes], i, j)
        put_tangent(
            lambda v: values[8 + v : 9 + v, at * lanes : (at + 1) * lanes],
            (i + 1) * wide + j + 1,
        )
    for at, (dx, dy) in enumerate(AROUND):

        @pl.when(inside(dx, dy))
        def _():
            strips_moved(at, True).wait_send()
            strips_moved(at, False).wait_recv()

    for at, (dx, dy) in enumerate(AROUND):
        for i, from_i in span(dx, count_x, 2):
            for j, from_j in span(dy, count_y, 2):
                low = column_at[from_i, from_j] * lanes
                put_stress(lambda v: near_stress[at, v : v + 1, low : low + lanes], i, j)
    def near(step, count):
        return {0: list(range(1, count + 1)), -1: [1], 1: [count]}[step]

    def far(step, count):
        return {0: list(range(1, count + 1)), -1: [0], 1: [count + 1]}[step]

    def places(at, pick):
        dx, dy = AROUND[at]
        return [i * wide + j for i in pick(dx, count_x) for j in pick(dy, count_y)]

    def filled(at):
        return 3 * len(places(at, near))

    def hop(it, at):
        dx, dy = AROUND[at]
        other = len(AROUND) - 1 - at
        return pltpu.make_async_remote_copy(
            src_ref=send_halo.at[it, at, pl.ds(0, filled(at))],
            dst_ref=halo.at[it, other, pl.ds(0, filled(at))],
            send_sem=send_sem.at[(it - 1) % 2, at],
            recv_sem=recv_sem.at[(it - 1) % 2, other],
            device_id=(a + dx, b + dy),
            device_id_type=MESH,
        )

    def halo_start(it):
        for at, (dx, dy) in enumerate(AROUND):

            @pl.when(inside(dx, dy))
            def _():
                mine = places(at, near)
                for c in range(3):
                    for k, row in enumerate(mine):
                        send_halo[it, at, pl.ds(c * len(mine) + k, 1)] = basis[it, c, pl.ds(row, 1)]
                hop(it, at).start()

    def halo_finish(it):
        for at, (dx, dy) in enumerate(AROUND):

            @pl.when(inside(dx, dy))
            def _():
                hop(it, at).wait_send()
                pltpu.make_async_remote_copy(
                    src_ref=send_halo.at[it, at, pl.ds(0, filled(at))],
                    dst_ref=halo.at[it, at, pl.ds(0, filled(at))],
                    send_sem=send_sem.at[(it - 1) % 2, at],
                    recv_sem=recv_sem.at[(it - 1) % 2, at],
                    device_id=(a + dx, b + dy),
                    device_id_type=MESH,
                ).wait_recv()

        for at in range(len(AROUND)):
            theirs = places(at, far)
            for c in range(3):
                for k, row in enumerate(theirs):
                    basis[it, c, pl.ds(row, 1)] = halo[it, at, pl.ds(c * len(theirs) + k, 1)]

    def force_of(stress, c, down=down):
        first, second, third = (stress[VOIGT[c][d]] for d in range(3))
        first = first + down(first, 2)
        second = second + down(second, 2)
        third = down(third, 2) - third
        first = first + down(first, 1)
        rest = down(second, 1) - second + third + down(third, 1)
        return 0.25 * (down(first, 0) - first + rest + down(rest, 0))

    def applied(it):
        strain = strain_of(it)
        stress = []
        for i in range(6):
            value = None
            for j in range(6):
                term = elem[PAIR_AT[(min(i, j), max(i, j))]] * strain[j]
                value = term if value is None else value + term
            stress.append(value)
        return [
            jnp.where(own, MASS * basis[it, c] + force_of(stress, c), 0.0) for c in range(3)
        ]

    def product(first, second):
        total = None
        for c in range(3):
            term = first[c] * second[c]
            total = term if total is None else total + term
        total = jnp.sum(jnp.where(own, total, 0.0), axis=0, keepdims=True)
        value = total[:, :128]
        for at in range(128, lanes, 128):
            value = value + total[:, at : at + 128]
        return value

    def stacked(pieces):
        high = -(-len(pieces) // 8) * 8
        tile_row = lax.broadcasted_iota(jnp.int32, (high, 128), 0)
        value = jnp.zeros((high, 128), jnp.float32)
        for at, piece in enumerate(pieces):
            value = jnp.where(tile_row == at, piece, value)
        return value

    def spread(at, src, dst, mine, row, column):
        pltpu.make_async_remote_copy(
            src_ref=src,
            dst_ref=dst.at[mine],
            send_sem=sum_send.at[at],
            recv_sem=sum_recv.at[at],
            device_id=(row, column),
            device_id_type=MESH,
        ).start()

    def gather_start(at, src, dst, count, mine, device):
        every(
            count, lambda step: spread(at, src, dst, mine, *device(lax.rem(mine + step, count)))
        )
        dst[mine] = src[...]

    def gather_all(at, src, dst):
        columns = [lax.rem(b + step, n_micro) for step in range(n_micro)] if total <= 32 else None
        for step in range(n_macro - 1, -1, -1):
            row = lax.rem(a + step, n_macro)
            if columns is None:
                lax.fori_loop(
                    0 if step else 1,
                    n_micro,
                    lambda k, carry: (
                        spread(at, src, dst, me, row, lax.rem(b + k, n_micro)),
                        carry,
                    )[1],
                    0,
                )
            else:
                order = sorted(range(n_micro), key=lambda k: -min(k, n_micro - k))
                for k in order:
                    if step or k:
                        spread(at, src, dst, me, row, columns[k])
        dst[me] = src[...]

    def gather_finish(at, dst, count, device, mine):
        others = dst.at[pl.ds(0, count - 1)]
        pltpu.make_async_remote_copy(
            src_ref=others,
            dst_ref=others,
            send_sem=sum_send.at[at],
            recv_sem=sum_recv.at[at],
            device_id=device(lax.rem(mine + 1, count)),
            device_id_type=MESH,
        ).wait()

    def along_micro(other):
        return (a, other)

    def along_macro(other):
        return (other, b)

    broad_lane = lax.broadcasted_iota(jnp.int32, outer.shape[1:], 1)

    def back(value, axis):
        if axis == 2:
            return jnp.where(broad_lane == 0, 0.0, pltpu.roll(value, 1, 1))
        return pltpu.roll(value, broad if axis == 0 else 1, 0)

    row_x, row_y = row_at // wide, row_at % wide
    real = jnp.logical_and(
        jnp.logical_and(
            row_x >= jnp.where(a > 0, 0, 1),
            row_x <= jnp.where(a < n_macro - 1, count_x + 1, count_x),
        ),
        jnp.logical_and(
            row_y >= jnp.where(b > 0, 0, 1),
            row_y <= jnp.where(b < n_micro - 1, count_y + 1, count_y),
        ),
    )
    stress = [outer[v] for v in range(6)]
    for c in range(3):
        pushed = force_of(stress, c, back)
        for i in range(count_x + 2):
            low = (i + 1) * broad + 1
            basis[0, c, pl.ds(i * wide, wide)] = pushed[low : low + wide]
        basis[0, c] = jnp.where(real, loads[c] - basis[0, c], 0.0)
    def sides_moved(way, part):
        dx, dy = after[way]
        mine = [at for at, (offset, _, _) in enumerate(handed) if offset == (dx, dy)]
        first, count = parts[part]
        landed = beside.at[pl.ds(mine[0], len(mine)), pl.ds(first, count)]
        return pltpu.make_async_remote_copy(
            src_ref=landed,
            dst_ref=landed,
            send_sem=side_send.at[part, way],
            recv_sem=side_recv.at[part, way],
            device_id=(a + dx, b + dy),
            device_id_type=MESH,
        )

    for way, (dx, dy) in enumerate(after):

        @pl.when(inside(dx, dy))
        def _():
            for part in range(len(parts)):
                sides_moved(way, part).wait_send()

        @pl.when(inside(-dx, -dy))
        def _():
            for part in range(len(parts)):
                sides_moved(way, part).wait_recv()

    for at, (_, _, (i, j)) in enumerate(handed):
        put_tangent(lambda v: beside[at, v : v + 1], i * wide + j)

    grown = applied(0)
    for c in range(3):
        basis[1, c] = grown[c]
    halo_start(1)
    start = [basis[0, c] for c in range(3)]
    part[...] = stacked([product(start, start), product(grown, grown)])
    gather_start(0, part, got_micro, n_micro, b, along_micro)
    halo_finish(1)
    grown = applied(1)
    for c in range(3):
        basis[2, c] = grown[c]
    halo_start(2)
    gather_finish(0, got_micro, n_micro, along_micro, b)
    middle[...] = jnp.sum(got_micro[...], axis=0)
    gather_start(1, middle, got_macro, n_macro, a, along_macro)
    halo_finish(2)
    grown = applied(2)
    for c in range(3):
        basis[3, c] = grown[c]
    halo_start(3)
    gather_finish(1, got_macro, n_macro, along_macro, a)
    totals = jnp.sum(jnp.sum(got_macro[...], axis=0), axis=1, keepdims=True)
    shift = jnp.sqrt(totals[1:2] / totals[0:1])
    scale = 1.0 / shift
    halo_finish(3)
    for c in range(3):
        powers = [basis[0, c]]
        factor = scale
        for k in range(1, 4):
            powers.append(basis[k, c] * factor)
            factor = factor * scale
        for k in range(1, 4):
            powers = [later - sooner for sooner, later in zip(powers, powers[1:])]
            basis[k, c] = powers[0]

    def field(it):
        return [basis[it, c] for c in range(3)]

    def step(it):
        grown = applied(it)
        return [grown[c] * scale - jnp.where(own, basis[it, c], 0.0) for c in range(3)]

    moments = []
    for it in range(3, ITERS):
        grown = step(it)
        if it + 1 < ITERS:
            for c in range(3):
                basis[it + 1, c] = grown[c]
            halo_start(it + 1)
            for k in range(len(moments) // 2, it + 1):
                moments.append(product(field(k), field(k)))
                moments.append(product(field(k), field(k + 1)))
            halo_finish(it + 1)
    moments.append(product(field(ITERS - 1), field(ITERS - 1)))
    moments.append(product(field(ITERS - 1), grown))
    sums = jnp.sum(stacked(moments), axis=1, keepdims=True)
    diagonal = lax.broadcasted_iota(jnp.int32, (16, 128), 0) == lax.broadcasted_iota(
        jnp.int32, (16, 128), 1
    )
    last_part[...] = jnp.sum(jnp.where(diagonal, sums, 0.0), axis=0, keepdims=True)

    gather_all(2, last_part, last_all)
    gather_finish(2, last_all, total, device, me)
    totals = jnp.sum(last_all[...], axis=0)
    held = [totals[:, k : k + 1] for k in range(2 * ITERS)]

    def inner(first, second, extra=0):
        gathered = {}
        for i, x in enumerate(first):
            for j, y in enumerate(second):
                gathered.setdefault(i + j, []).append(x * y)
        value = None
        for degree, terms in gathered.items():
            total = terms[0]
            for term in terms[1:]:
                total = total + term
            total = total * held[degree + extra]
            value = total if value is None else value + total
        return value

    one = jnp.ones((1, 1), jnp.float32)
    left, toward, done = [one], [one], []
    norm = held[0]
    for it in range(ITERS):
        energy = inner(toward, toward) + inner(toward, toward, 1)
        length = norm / energy
        done = [x + length * scale * p for x, p in zip(done + [0.0], toward)]
        raised = [
            (toward[k] if k < len(toward) else 0.0) + (toward[k - 1] if k > 0 else 0.0)
            for k in range(len(toward) + 1)
        ]
        left = [
            (left[k] if k < len(left) else 0.0) - length * raised[k] for k in range(len(raised))
        ]
        if it + 1 < ITERS:
            fresh = inner(left, left)
            ratio = fresh / norm
            toward = [
                left[k] + (ratio * toward[k] if k < len(toward) else 0.0)
                for k in range(len(left))
            ]
            norm = fresh
    for c in range(3):
        fields = [basis[k, c] for k in range(ITERS)] + [grown[c]]
        moved, rest = None, None
        for k in range(ITERS + 1):
            if k < len(done):
                term = done[k] * fields[k]
                moved = term if moved is None else moved + term
            term = left[k] * fields[k]
            rest = term if rest is None else rest + term
        for i in range(count_x):
            low = (i + 1) * wide + 1
            inc_ref[c, i] = moved[low : low + count_y]
            res_ref[c, i] = rest[low : low + count_y]

    for buffer, semaphore in ((route_out, route_send), (back_out, back_send)):
        others = buffer.at[pl.ds(0, n_micro - 1)]
        pltpu.make_async_remote_copy(
            src_ref=others,
            dst_ref=others,
            send_sem=semaphore.at[0],
            recv_sem=semaphore.at[0],
            device_id=(a, lax.rem(b + 1, n_micro)),
            device_id_type=MESH,
        ).wait_send()


def hand_over(inc_in, res_in, inc_ref, res_ref):
    inc_ref[...] = inc_in[...]
    res_ref[...] = res_in[...]


def shards(
    displacement,
    load,
    routes,
    counts,
    stiffness,
    precond,
    forcing,
    coupling,
    lame_first,
    lame_shear,
):
    _, count_x, count_y, lanes = displacement.shape
    points = count_x * count_y * lanes
    n_macro, n_micro = lax.axis_size("macro"), lax.axis_size("micro")
    capacity = max(2, 2 * points // n_micro)
    slots = -(-capacity // 128) * 128
    size = stiffness.shape[1]
    tall = -(-(8 + len(PAIRS)) // 8) * 8
    rows = -(-(count_x + 2) * (count_y + 2) // 8) * 8
    side = -(-3 * max(count_x, count_y) // 8) * 8
    total = n_macro * n_micro
    sides = count_x + count_y + 1
    outer_rows = -(-(count_x + 3) * (count_y + 3) // 8) * 8
    vmem = pl.BlockSpec(memory_space=pltpu.VMEM)
    anywhere = pl.BlockSpec(memory_space=pl.ANY)
    dma = pltpu.SemaphoreType.DMA

    def held(*shape):
        return pltpu.VMEM(shape, jnp.float32)

    def half(*shape):
        return pltpu.VMEM(shape, jnp.bfloat16)

    def body(*refs):
        newton_kernel((count_x, count_y, lanes, n_macro, n_micro), *refs)

    outputs = pl.pallas_call(
            body,
            out_shape=[jax.ShapeDtypeStruct(load.shape, jnp.float32)] * 2,
            in_specs=[anywhere] * 8 + [vmem] * 2,
            out_specs=[vmem, vmem],
            scratch_shapes=[
                held(*displacement.shape),
                held(*load.shape),
                pltpu.VMEM((points // 128, 128), jnp.int32),
                pltpu.VMEM((points // 128, 128), jnp.int32),
                half(size, size),
                half(size, size),
                half(6, size),
                half(6, size),
                half(3 * size, 16),
                half(tall, size),
                half(tall, size),
                held(tall, size),
                half(n_micro * slots, points),
                held(len(AROUND), *load.shape),
                held(len(AROUND), 8, points),
                held(6, outer_rows, lanes),
                held(3, rows, lanes),
                held(3, *displacement.shape),
                held(8, points),
                held(n_micro, 8, slots),
                held(n_micro, 8, slots),
                held(n_micro, tall, slots),
                held(n_micro, tall, slots),
                held(tall, points),
                held(sides, tall - 8, lanes),
                held(len(PAIRS), rows, lanes),
                held(ITERS, 3, rows, lanes),
                held(ITERS, len(AROUND), side, lanes),
                held(ITERS, len(AROUND), side, lanes),
                held(8, 128),
                held(n_micro, 8, 128),
                held(8, 128),
                held(n_macro, 8, 128),
                held(1, 128),
                held(total, 1, 128),
                dma((8,)),
                dma((3,)),
                dma((3,)),
                dma((1,)),
                dma((n_micro,)),
                dma((1,)),
                dma((n_micro,)),
                dma((2, 3)),
                dma((2, 3)),
                dma((2, len(AROUND))),
                dma((2, len(AROUND))),
                dma((3,)),
                dma((3,)),
            ],
            compiler_params=pltpu.CompilerParams(collective_id=0, has_side_effects=True),
            name="newton_step",
        )(
            displacement,
            load,
            routes.reshape(points // 128, 128),
            counts.reshape(points // 128, 128),
            stiffness[0],
            precond[0],
            forcing[0],
            coupling[0].T,
            lame_first.reshape(1, 1),
            lame_shear.reshape(1, 1),
        )
    return tuple(
        pl.pallas_call(
            hand_over,
            out_shape=[jax.ShapeDtypeStruct(load.shape, jnp.float32)] * 2,
            in_specs=[vmem, vmem],
            out_specs=[vmem, vmem],
            name="hand_over",
        )(*outputs)
    )


def solution(mesh):
    in_specs = (
        P(None, "macro", "micro", None),
        P(None, "macro", "micro", None),
        P("macro", "micro", None, None),
        P("macro", "micro", None),
        P("micro", None, None),
        P("micro", None, None),
        P("micro", None, None),
        P("micro", None, None),
        P("micro"),
        P("micro"),
    )
    out_specs = (P(None, "macro", "micro", None), P(None, "macro", "micro", None))
    return jax.shard_map(shards, mesh=mesh, in_specs=in_specs, out_specs=out_specs, check_vma=False)
```

```python
import jax
import jax.numpy as jnp
from jax import lax
from jax.experimental import pallas as pl
from jax.experimental.pallas import tpu as pltpu
from jax.sharding import PartitionSpec as P

ITMAX = 4
ITERS = 5


BETA = 0.1
OMEGA = 0.8
MASS = 0.1
VOIGT = ((0, 5, 4), (5, 1, 3), (4, 3, 2))
PAIRS = tuple((first, second) for first in range(6) for second in range(first, 6))
PAIR_AT = {pair: at for at, pair in enumerate(PAIRS)}
AROUND = tuple((dx, dy) for dx in (-1, 0, 1) for dy in (-1, 0, 1) if (dx, dy) != (0, 0))
MESH = pl.DeviceIdType.MESH


def strips_of(count_x, count_y):
    strips = []
    for dx, dy in AROUND:
        across = range(count_x if dx >= 0 else 1)
        if dy >= 0:
            strips.append(((dx, dy), 0, len(across) * count_y))
        else:
            strips += [((dx, dy), i * count_y, 1) for i in across]
    return strips


def newton_kernel(
    sizes,
    disp_in,
    load_in,
    routes_in,
    counts_in,
    stiff_in,
    pre_in,
    force_in,
    couple_in,
    first_ref,
    shear_ref,
    inc_ref,
    res_ref,
    disp_ref,
    load_ref,
    routes_ref,
    counts_ref,
    stiff,
    pre,
    force_ref,
    couple_ref,
    force_t,
    couple,
    products,
    wide_products,
    spots,
    near_load,
    near_stress,
    outer,
    loads,
    near_disp,
    bundle,
    route_out,
    route_in,
    back_out,
    back_in,
    values,
    beside,
    elem,
    basis,
    send_halo,
    halo,
    part,
    got_micro,
    middle,
    got_macro,
    last_part,
    last_all,
    input_sem,
    disp_send,
    disp_recv,
    route_send,
    route_recv,
    back_send,
    back_recv,
    side_send,
    side_recv,
    send_sem,
    recv_sem,
    sum_send,
    sum_recv,
):
    count_x, count_y, lanes, n_macro, n_micro = sizes
    wide = count_y + 2
    rows = basis.shape[2]
    points = spots.shape[1]
    slots = spots.shape[0] // n_micro
    pairs = n_micro // 2
    groups = points // 128
    size = stiff.shape[0]
    tall = couple.shape[0]
    total = n_macro * n_micro
    a, b = lax.axis_index("macro"), lax.axis_index("micro")
    me = a * n_micro + b

    def device(other):
        return (other // n_micro, lax.rem(other, n_micro))

    def inside(dx, dy):
        test = None
        for place, step, count in ((a, dx, n_macro), (b, dy, n_micro)):
            if step != 0:
                good = (place > 0) if step < 0 else (place < count - 1)
                test = good if test is None else jnp.logical_and(test, good)
        return test

    barrier = pltpu.get_barrier_semaphore()

    def every(count, act):
        if count <= 32:
            for step in range(1, count):
                act(step)
        else:
            lax.fori_loop(1, count, lambda step, carry: (act(step), carry)[1], 0)

    def greet(row, column):
        pl.semaphore_signal(barrier, inc=1, device_id=(row, column), device_id_type=MESH)

    for step in range(1, n_macro):
        for aside in range(3):
            greet(lax.rem(a + step, n_macro), lax.rem(b + n_micro - 1 + aside, n_micro))
    every(n_micro, lambda step: greet(a, lax.rem(b + step, n_micro)))
    greeted = 3 * (n_macro - 1) + n_micro - 1
    inputs = {}
    for at, (name, source, target) in enumerate(
        (
            ("routes", routes_in, routes_ref),
            ("force", force_in, force_ref),
            ("couple", couple_in, couple_ref),
            ("counts", counts_in, counts_ref),
            ("disp", disp_in, disp_ref),
            ("load", load_in, load_ref),
            ("pre", pre_in, pre),
            ("stiff", stiff_in, stiff),
        )
    ):
        inputs[name] = pltpu.make_async_copy(source, target, input_sem.at[at])
        inputs[name].start()

    inputs["disp"].wait()
    after = ((1, 0), (0, 1), (1, 1))
    pl.semaphore_wait(barrier, greeted)

    def show(at):
        dx, dy = after[at]
        return pltpu.make_async_remote_copy(
            src_ref=disp_ref,
            dst_ref=near_disp.at[at],
            send_sem=disp_send.at[at],
            recv_sem=disp_recv.at[at],
            device_id=(a - dx, b - dy),
            device_id_type=MESH,
        )

    for at, (dx, dy) in enumerate(after):

        @pl.when(inside(-dx, -dy))
        def _():
            show(at).start()

    inputs["load"].wait()

    def load_copy(at):
        dx, dy = AROUND[at]
        other = len(AROUND) - 1 - at
        return pltpu.make_async_remote_copy(
            src_ref=load_ref,
            dst_ref=near_load.at[other],
            send_sem=send_sem.at[0, at],
            recv_sem=recv_sem.at[0, other],
            device_id=(a + dx, b + dy),
            device_id_type=MESH,
        )

    def load_arrival(at):
        dx, dy = AROUND[at]
        return pltpu.make_async_remote_copy(
            src_ref=load_ref,
            dst_ref=near_load.at[at],
            send_sem=send_sem.at[0, at],
            recv_sem=recv_sem.at[0, at],
            device_id=(a + dx, b + dy),
            device_id_type=MESH,
        )

    for at, (dx, dy) in enumerate(AROUND):

        @pl.when(inside(dx, dy))
        def _():
            load_copy(at).start()

        @pl.when(jnp.logical_not(inside(dx, dy)))
        def _():
            near_load[at] = jnp.zeros(near_load.shape[1:], jnp.float32)
            near_stress[at] = jnp.zeros(near_stress.shape[1:], jnp.float32)

    outer[...] = jnp.zeros(outer.shape, jnp.float32)
    loads[...] = jnp.zeros(loads.shape, jnp.float32)
    for name in ("routes", "force", "couple", "counts"):
        inputs[name].wait()
    force = force_ref[...].astype(jnp.float32)
    force = jnp.concatenate([force, jnp.zeros((2, size), jnp.float32)], axis=0)
    wide_products[...] = jnp.zeros((tall, size), jnp.float32)
    coupling = couple_ref[...].astype(jnp.float32)
    wide_products[pl.ds(0, 6)] = coupling
    couple[...] = wide_products[...].astype(jnp.bfloat16)
    wide_products[pl.ds(0, 6)] = jnp.zeros((6, size), jnp.float32)
    for at, (first, second) in enumerate(PAIRS):
        wide_products[pl.ds(8 + at, 1)] = coupling[first : first + 1] * coupling[second : second + 1]
    products[...] = wide_products[...].astype(jnp.bfloat16)

    route = routes_ref[...]
    row_of = lax.broadcasted_iota(jnp.int32, (128, 128), 0)
    column_of = lax.broadcasted_iota(jnp.int32, (128, 128), 1)
    until = jnp.where(row_of <= column_of, 1.0, 0.0).astype(jnp.bfloat16)
    named = [jnp.where(route == owner, 1.0, 0.0) for owner in range(n_micro)]
    named = jnp.concatenate(named, axis=0).astype(jnp.bfloat16)
    inner_rank = jnp.dot(named, until, preferred_element_type=jnp.float32)
    whole = jnp.dot(
        named, jnp.ones((128, 128), jnp.bfloat16), preferred_element_type=jnp.float32
    ).astype(jnp.bfloat16)
    span = n_micro * groups
    row_of = lax.broadcasted_iota(jnp.int32, (span, span), 0)
    column_of = lax.broadcasted_iota(jnp.int32, (span, span), 1)
    ahead = jnp.logical_and(column_of < row_of, column_of // groups == row_of // groups)
    before = jnp.dot(
        jnp.where(ahead, 1.0, 0.0).astype(jnp.bfloat16), whole, preferred_element_type=jnp.float32
    )
    ranks = inner_rank + before - 1.0
    rank = jnp.zeros((groups, 128), jnp.float32)
    for owner in range(n_micro):
        rank = jnp.where(route == owner, ranks[owner * groups : (owner + 1) * groups], rank)
    slot_type = jnp.bfloat16 if slots <= 256 else jnp.float32
    slot_at = lax.broadcasted_iota(jnp.int32, (slots, 128), 0).astype(jnp.float32)
    slot_at = slot_at.astype(slot_type)

    def spot(owner, carry):
        local = jnp.where(route == owner, rank, -1.0)
        for g in range(groups):
            near_slot = jnp.broadcast_to(local[g : g + 1], (16, 128)).astype(slot_type)
            near_slot = jnp.concatenate([near_slot] * (slots // 16), axis=0)
            hit = jnp.where(near_slot == slot_at, slot_type(1), slot_type(0))
            low = pl.multiple_of(owner * slots, slots)
            spots[pl.ds(low, slots), g * 128 : (g + 1) * 128] = hit.astype(jnp.bfloat16)
        return carry

    lax.fori_loop(0, n_micro, spot, 0)

    for it in range(basis.shape[0]):
        for c in range(3):
            basis[it, c] = jnp.zeros((rows, lanes), jnp.float32)
    elem[...] = jnp.zeros(elem.shape, jnp.float32)
    values[...] = jnp.zeros(values.shape, jnp.float32)
    bundle[...] = jnp.zeros(bundle.shape, jnp.float32)
    for g in range(groups):
        bundle[6:7, g * 128 : (g + 1) * 128] = counts_ref[g : g + 1].astype(jnp.float32)

    for at, (dx, dy) in enumerate(AROUND):

        @pl.when(jnp.logical_not(inside(dx, dy)))
        def _():
            for it in range(1, ITERS):
                halo[it, at] = jnp.zeros(halo.shape[2:], jnp.float32)

    for at, (dx, dy) in enumerate(after):

        @pl.when(jnp.logical_not(inside(dx, dy)))
        def _():
            near_disp[at] = jnp.zeros(near_disp.shape[1:], jnp.float32)

    owned = [(i, j) for i in range(count_x) for j in range(count_y)]
    column_at = {place: at for at, place in enumerate(owned)}
    handed = [((1, 0), (count_x - 1, j), (0, j + 1)) for j in range(count_y)]
    handed += [((0, 1), (i, count_y - 1), (i + 1, 0)) for i in range(count_x)]
    handed += [((1, 1), (count_x - 1, count_y - 1), (0, 0))]
    for at, ((dx, dy), _, _) in enumerate(handed):

        @pl.when(jnp.logical_not(inside(-dx, -dy)))
        def _():
            beside[at] = jnp.zeros(beside.shape[1:], jnp.float32)

    for name in ("pre", "stiff"):
        inputs[name].wait()

    force_t[...] = force.T.astype(jnp.bfloat16)
    for c in range(3):
        for i, j in owned:
            basis[0, c, pl.ds((i + 1) * wide + j + 1, 1)] = disp_ref[c, i, j : j + 1]
    for at, (dx, dy) in enumerate(after):

        @pl.when(inside(-dx, -dy))
        def _():
            show(at).wait_send()

        @pl.when(inside(dx, dy))
        def _():
            pltpu.make_async_remote_copy(
                src_ref=disp_ref,
                dst_ref=near_disp.at[at],
                send_sem=disp_send.at[at],
                recv_sem=disp_recv.at[at],
                device_id=(a + dx, b + dy),
                device_id_type=MESH,
            ).wait_recv()

    for c in range(3):
        for j in range(count_y):
            basis[0, c, pl.ds((count_x + 1) * wide + j + 1, 1)] = near_disp[0, c, 0, j : j + 1]
        for i in range(count_x):
            basis[0, c, pl.ds((i + 1) * wide + count_y + 1, 1)] = near_disp[1, c, i, 0:1]
        basis[0, c, pl.ds((count_x + 1) * wide + count_y + 1, 1)] = near_disp[2, c, 0, 0:1]

    row_at = lax.broadcasted_iota(jnp.int32, (rows, lanes), 0)
    lane_at = lax.broadcasted_iota(jnp.int32, (rows, lanes), 1)
    own = row_at < 0
    for i in range(1, count_x + 1):
        low = i * wide + 1
        own = jnp.logical_or(own, jnp.logical_and(row_at >= low, row_at < low + count_y))

    def up(value, axis):
        if axis == 2:
            moved = pltpu.roll(value, lanes - 1, 1)
            return jnp.where(lane_at == lanes - 1, 0.0, moved)
        return pltpu.roll(value, rows - (wide if axis == 0 else 1), 0)

    def down(value, axis):
        if axis == 2:
            return jnp.where(lane_at == 0, 0.0, pltpu.roll(value, 1, 1))
        return pltpu.roll(value, wide if axis == 0 else 1, 0)

    def strain_of(it):
        grads = []
        for c in range(3):
            value = basis[it, c]
            moved = up(value, 2)
            total, gap = value + moved, moved - value
            total_up, gap_up = up(total, 1), up(gap, 1)
            flat, slope_y, slope_z = total + total_up, total_up - total, gap + gap_up
            grads.append(
                (
                    0.25 * (up(flat, 0) - flat),
                    0.25 * (up(slope_y, 0) + slope_y),
                    0.25 * (up(slope_z, 0) + slope_z),
                )
            )
        return [
            grads[0][0],
            grads[1][1],
            grads[2][2],
            grads[1][2] + grads[2][1],
            grads[0][2] + grads[2][0],
            grads[0][1] + grads[1][0],
        ]

    strain = strain_of(0)
    for at, (i, j) in enumerate(owned):
        low = (i + 1) * wide + j + 1
        for k in range(6):
            bundle[k : k + 1, at * lanes : (at + 1) * lanes] = strain[k][low : low + 1]
    exact = bundle[...]
    high = exact.astype(jnp.bfloat16).astype(jnp.float32)
    both = jnp.concatenate([high, exact - high], axis=0).astype(jnp.bfloat16)

    def route_copy(other, mine):
        return pltpu.make_async_remote_copy(
            src_ref=route_out.at[other],
            dst_ref=route_in.at[mine],
            send_sem=route_send.at[0],
            recv_sem=route_recv.at[mine],
            device_id=(a, other),
            device_id_type=MESH,
        )

    chip, core = b // 2, lax.rem(b, 2)

    def pair_rows(place):
        return pl.ds(pl.multiple_of(place * (2 * slots), 2 * slots), 2 * slots)

    def hand_out(at, carry):
        place = lax.rem(chip + pairs - at, pairs)
        moved = lax.dot_general(
            both,
            spots[pair_rows(place)],
            (((1,), (1,)), ((), ())),
            preferred_element_type=jnp.float32,
        )
        moved = moved[:8] + moved[8:]
        for k in range(2):
            other = 2 * place + k
            piece = moved[:, k * slots : (k + 1) * slots]

            @pl.when(other != b)
            def _():
                route_out[other] = piece
                route_copy(other, b).start()

            @pl.when(other == b)
            def _():
                route_in[b] = piece

        return carry

    lax.fori_loop(0, pairs, hand_out, 0)


    lame_first, lame_shear = first_ref[...], shear_ref[...]
    tall_at = lax.broadcasted_iota(jnp.int32, (tall, 2 * slots), 0)
    on_trace = jnp.where(tall_at < 3, lame_first, 0.0)
    on_strain = jnp.where(tall_at < 3, 2.0 * lame_shear, jnp.where(tall_at < 6, lame_shear, 0.0))
    base = jnp.zeros((tall, 2 * slots), jnp.float32)
    for at, (i, j) in enumerate(PAIRS):
        if i == j:
            amount = lame_first + 2.0 * lame_shear if i < 3 else lame_shear
        elif j < 3:
            amount = lame_first
        else:
            continue
        base = jnp.where(tall_at == 8 + at, amount, base)

    def back_copy(other, mine):
        return pltpu.make_async_remote_copy(
            src_ref=back_out.at[other],
            dst_ref=back_in.at[mine],
            send_sem=back_send.at[0],
            recv_sem=back_recv.at[mine],
            device_id=(a, other),
            device_id_type=MESH,
        )

    def solve(at, carry):
        place = lax.rem(chip + at, pairs)
        taken = []
        for k in range(2):
            other = 2 * place + k

            @pl.when(other != b)
            def _():
                route_copy(b, other).wait_recv()

            taken.append(route_in[other])
        points_in = jnp.concatenate(taken, axis=1)
        sweeps = points_in[6:7]
        modal_load = jnp.dot(
            force_t[...], points_in.astype(jnp.bfloat16), preferred_element_type=jnp.float32
        )
        modes = -OMEGA * jnp.dot(
            pre[...], (-modal_load).astype(jnp.bfloat16), preferred_element_type=jnp.float32
        )
        for sweep in range(1, ITMAX):
            misfit = jnp.dot(
                stiff[...], modes.astype(jnp.bfloat16), preferred_element_type=jnp.float32
            )
            misfit = (misfit + BETA * jnp.tanh(modes) - modal_load).astype(jnp.bfloat16)
            change = jnp.dot(pre[...], misfit, preferred_element_type=jnp.float32)
            modes = modes - jnp.where(sweeps > sweep, OMEGA, 0.0) * change
        bent = jnp.tanh(modes)
        slope = 1.0 - bent * bent
        trace = points_in[0:1] + points_in[1:2] + points_in[2:3]
        padded = jnp.concatenate(
            [points_in, jnp.zeros((tall - 8, 2 * slots), jnp.float32)], axis=0
        )
        answer = on_trace * trace + on_strain * padded + base
        answer = answer + jnp.dot(
            couple[...], modes.astype(jnp.bfloat16), preferred_element_type=jnp.float32
        )
        answer = answer + jnp.dot(
            products[...], slope.astype(jnp.bfloat16), preferred_element_type=jnp.float32
        )
        for k in range(2):
            other = 2 * place + k
            piece = answer[:, k * slots : (k + 1) * slots]

            @pl.when(other != b)
            def _():
                back_out[other] = piece
                back_copy(other, b).start()

            @pl.when(other == b)
            def _():
                back_in[b] = piece

        return carry

    lax.fori_loop(0, pairs, solve, 0)

    def take_back(at, carry):
        place = lax.rem(chip + pairs - at, pairs)
        taken = []
        for k in range(2):
            other = 2 * place + k

            @pl.when(other != b)
            def _():
                back_copy(b, other).wait_recv()

            taken.append(back_in[other])
        exact = jnp.concatenate(taken, axis=1)
        high = exact.astype(jnp.bfloat16).astype(jnp.float32)
        both = jnp.concatenate([high, exact - high], axis=0).astype(jnp.bfloat16)
        moved = jnp.dot(both, spots[pair_rows(place)], preferred_element_type=jnp.float32)
        values[...] += moved[:tall] + moved[tall:]
        return carry

    lax.fori_loop(0, pairs, take_back, 0)

    even = len(PAIRS) // 8 * 8
    parts = [part for part in ((0, even), (even, len(PAIRS) - even)) if part[1] > 0]

    def side_copy(at, part):
        (dx, dy), place, _ = handed[at]
        first, count = parts[part]
        low = column_at[place] * lanes
        return pltpu.make_async_remote_copy(
            src_ref=values.at[pl.ds(8 + first, count), pl.ds(low, lanes)],
            dst_ref=beside.at[at, pl.ds(first, count)],
            send_sem=side_send.at[part, after.index((dx, dy))],
            recv_sem=side_recv.at[part, after.index((dx, dy))],
            device_id=(a + dx, b + dy),
            device_id_type=MESH,
        )

    strips = strips_of(count_x, count_y)

    def strip_copy(at):
        (dx, dy), first, count = strips[at]
        columns = pl.ds(first * lanes, count * lanes)
        way = AROUND.index((dx, dy))
        other = len(AROUND) - 1 - way
        return pltpu.make_async_remote_copy(
            src_ref=values.at[pl.ds(0, 6), columns],
            dst_ref=near_stress.at[other, pl.ds(0, 6), columns],
            send_sem=send_sem.at[1, way],
            recv_sem=recv_sem.at[1, other],
            device_id=(a + dx, b + dy),
            device_id_type=MESH,
        )

    def strips_moved(way, sent):
        dx, dy = AROUND[way]
        offset = (dx, dy) if sent else (-dx, -dy)
        count = sum(count for place, _, count in strips if place == offset)
        columns = near_stress.at[way, pl.ds(0, 6), pl.ds(0, count * lanes)]
        return pltpu.make_async_remote_copy(
            src_ref=columns,
            dst_ref=columns,
            send_sem=send_sem.at[1, way],
            recv_sem=recv_sem.at[1, way],
            device_id=(a + dx, b + dy),
            device_id_type=MESH,
        )

    for at, (dx, dy) in enumerate(AROUND):

        @pl.when(inside(dx, dy))
        def _():
            load_copy(at).wait_send()
            load_arrival(at).wait_recv()

    for at, ((dx, dy), _, _) in enumerate(strips):

        @pl.when(inside(dx, dy))
        def _():
            strip_copy(at).start()

    for at, ((dx, dy), _, _) in enumerate(handed):

        @pl.when(inside(dx, dy))
        def _():
            for part in range(len(parts)):
                side_copy(at, part).start()

    def span(step, count, below):
        if step == 0:
            return [(k, k) for k in range(count)]
        if step > 0:
            return [(count, 0)]
        return [(k - below, count + k - below) for k in range(below)]

    for c in range(3):
        for i in range(count_x):
            loads[c, pl.ds((i + 1) * wide + 1, count_y)] = load_ref[c, i]
        for at, (dx, dy) in enumerate(AROUND):
            for i, from_i in span(dx, count_x, 1):
                for j, from_j in span(dy, count_y, 1):
                    loads[c, pl.ds((i + 1) * wide + j + 1, 1)] = near_load[
                        at, c, from_i, from_j : from_j + 1
                    ]

    broad = count_y + 3

    def put_stress(read, i, j):
        for v in range(6):
            outer[v, pl.ds((i + 2) * broad + j + 2, 1)] = read(v)

    def put_tangent(read, row):
        for v in range(len(PAIRS)):
            elem[v, pl.ds(row, 1)] = read(v)

    for at, (i, j) in enumerate(owned):
        put_stress(lambda v: values[v : v + 1, at * lanes : (at + 1) * lanes], i, j)
        put_tangent(
            lambda v: values[8 + v : 9 + v, at * lanes : (at + 1) * lanes],
            (i + 1) * wide + j + 1,
        )
    for at, (dx, dy) in enumerate(AROUND):

        @pl.when(inside(dx, dy))
        def _():
            strips_moved(at, True).wait_send()
            strips_moved(at, False).wait_recv()

    for at, (dx, dy) in enumerate(AROUND):
        for i, from_i in span(dx, count_x, 2):
            for j, from_j in span(dy, count_y, 2):
                low = column_at[from_i, from_j] * lanes
                put_stress(lambda v: near_stress[at, v : v + 1, low : low + lanes], i, j)
    def near(step, count):
        return {0: list(range(1, count + 1)), -1: [1], 1: [count]}[step]

    def far(step, count):
        return {0: list(range(1, count + 1)), -1: [0], 1: [count + 1]}[step]

    def places(at, pick):
        dx, dy = AROUND[at]
        return [i * wide + j for i in pick(dx, count_x) for j in pick(dy, count_y)]

    def filled(at):
        return 3 * len(places(at, near))

    def hop(it, at):
        dx, dy = AROUND[at]
        other = len(AROUND) - 1 - at
        return pltpu.make_async_remote_copy(
            src_ref=send_halo.at[it, at, pl.ds(0, filled(at))],
            dst_ref=halo.at[it, other, pl.ds(0, filled(at))],
            send_sem=send_sem.at[(it - 1) % 2, at],
            recv_sem=recv_sem.at[(it - 1) % 2, other],
            device_id=(a + dx, b + dy),
            device_id_type=MESH,
        )

    def halo_start(it):
        for at, (dx, dy) in enumerate(AROUND):

            @pl.when(inside(dx, dy))
            def _():
                mine = places(at, near)
                for c in range(3):
                    for k, row in enumerate(mine):
                        send_halo[it, at, pl.ds(c * len(mine) + k, 1)] = basis[it, c, pl.ds(row, 1)]
                hop(it, at).start()

    def halo_finish(it):
        for at, (dx, dy) in enumerate(AROUND):

            @pl.when(inside(dx, dy))
            def _():
                hop(it, at).wait_send()
                pltpu.make_async_remote_copy(
                    src_ref=send_halo.at[it, at, pl.ds(0, filled(at))],
                    dst_ref=halo.at[it, at, pl.ds(0, filled(at))],
                    send_sem=send_sem.at[(it - 1) % 2, at],
                    recv_sem=recv_sem.at[(it - 1) % 2, at],
                    device_id=(a + dx, b + dy),
                    device_id_type=MESH,
                ).wait_recv()

        for at in range(len(AROUND)):
            theirs = places(at, far)
            for c in range(3):
                for k, row in enumerate(theirs):
                    basis[it, c, pl.ds(row, 1)] = halo[it, at, pl.ds(c * len(theirs) + k, 1)]

    def force_of(stress, c, down=down):
        first, second, third = (stress[VOIGT[c][d]] for d in range(3))
        first = first + down(first, 2)
        second = second + down(second, 2)
        third = down(third, 2) - third
        first = first + down(first, 1)
        rest = down(second, 1) - second + third + down(third, 1)
        return 0.25 * (down(first, 0) - first + rest + down(rest, 0))

    def applied(it):
        strain = strain_of(it)
        stress = []
        for i in range(6):
            value = None
            for j in range(6):
                term = elem[PAIR_AT[(min(i, j), max(i, j))]] * strain[j]
                value = term if value is None else value + term
            stress.append(value)
        return [
            jnp.where(own, MASS * basis[it, c] + force_of(stress, c), 0.0) for c in range(3)
        ]

    def product(first, second):
        total = None
        for c in range(3):
            term = first[c] * second[c]
            total = term if total is None else total + term
        total = jnp.sum(jnp.where(own, total, 0.0), axis=0, keepdims=True)
        value = total[:, :128]
        for at in range(128, lanes, 128):
            value = value + total[:, at : at + 128]
        return value

    def stacked(pieces):
        high = -(-len(pieces) // 8) * 8
        tile_row = lax.broadcasted_iota(jnp.int32, (high, 128), 0)
        value = jnp.zeros((high, 128), jnp.float32)
        for at, piece in enumerate(pieces):
            value = jnp.where(tile_row == at, piece, value)
        return value

    def spread(at, src, dst, mine, row, column):
        pltpu.make_async_remote_copy(
            src_ref=src,
            dst_ref=dst.at[mine],
            send_sem=sum_send.at[at],
            recv_sem=sum_recv.at[at],
            device_id=(row, column),
            device_id_type=MESH,
        ).start()

    def gather_start(at, src, dst, count, mine, device):
        every(
            count, lambda step: spread(at, src, dst, mine, *device(lax.rem(mine + step, count)))
        )
        dst[mine] = src[...]

    def gather_all(at, src, dst):
        columns = [lax.rem(b + step, n_micro) for step in range(n_micro)] if total <= 32 else None
        for step in range(n_macro - 1, -1, -1):
            row = lax.rem(a + step, n_macro)
            if columns is None:
                lax.fori_loop(
                    0 if step else 1,
                    n_micro,
                    lambda k, carry: (
                        spread(at, src, dst, me, row, lax.rem(b + k, n_micro)),
                        carry,
                    )[1],
                    0,
                )
            else:
                order = sorted(range(n_micro), key=lambda k: -min(k, n_micro - k))
                for k in order:
                    if step or k:
                        spread(at, src, dst, me, row, columns[k])
        dst[me] = src[...]

    def gather_finish(at, dst, count, device, mine):
        others = dst.at[pl.ds(0, count - 1)]
        pltpu.make_async_remote_copy(
            src_ref=others,
            dst_ref=others,
            send_sem=sum_send.at[at],
            recv_sem=sum_recv.at[at],
            device_id=device(lax.rem(mine + 1, count)),
            device_id_type=MESH,
        ).wait()

    def along_micro(other):
        return (a, other)

    def along_macro(other):
        return (other, b)

    broad_lane = lax.broadcasted_iota(jnp.int32, outer.shape[1:], 1)

    def back(value, axis):
        if axis == 2:
            return jnp.where(broad_lane == 0, 0.0, pltpu.roll(value, 1, 1))
        return pltpu.roll(value, broad if axis == 0 else 1, 0)

    row_x, row_y = row_at // wide, row_at % wide
    real = jnp.logical_and(
        jnp.logical_and(
            row_x >= jnp.where(a > 0, 0, 1),
            row_x <= jnp.where(a < n_macro - 1, count_x + 1, count_x),
        ),
        jnp.logical_and(
            row_y >= jnp.where(b > 0, 0, 1),
            row_y <= jnp.where(b < n_micro - 1, count_y + 1, count_y),
        ),
    )
    stress = [outer[v] for v in range(6)]
    for c in range(3):
        pushed = force_of(stress, c, back)
        for i in range(count_x + 2):
            low = (i + 1) * broad + 1
            basis[0, c, pl.ds(i * wide, wide)] = pushed[low : low + wide]
        basis[0, c] = jnp.where(real, loads[c] - basis[0, c], 0.0)
    def sides_moved(way, part):
        dx, dy = after[way]
        mine = [at for at, (offset, _, _) in enumerate(handed) if offset == (dx, dy)]
        first, count = parts[part]
        landed = beside.at[pl.ds(mine[0], len(mine)), pl.ds(first, count)]
        return pltpu.make_async_remote_copy(
            src_ref=landed,
            dst_ref=landed,
            send_sem=side_send.at[part, way],
            recv_sem=side_recv.at[part, way],
            device_id=(a + dx, b + dy),
            device_id_type=MESH,
        )

    for way, (dx, dy) in enumerate(after):

        @pl.when(inside(dx, dy))
        def _():
            for part in range(len(parts)):
                sides_moved(way, part).wait_send()

        @pl.when(inside(-dx, -dy))
        def _():
            for part in range(len(parts)):
                sides_moved(way, part).wait_recv()

    for at, (_, _, (i, j)) in enumerate(handed):
        put_tangent(lambda v: beside[at, v : v + 1], i * wide + j)

    grown = applied(0)
    for c in range(3):
        basis[1, c] = grown[c]
    halo_start(1)
    start = [basis[0, c] for c in range(3)]
    part[...] = stacked([product(start, start), product(grown, grown)])
    gather_start(0, part, got_micro, n_micro, b, along_micro)
    halo_finish(1)
    grown = applied(1)
    for c in range(3):
        basis[2, c] = grown[c]
    halo_start(2)
    gather_finish(0, got_micro, n_micro, along_micro, b)
    middle[...] = jnp.sum(got_micro[...], axis=0)
    gather_start(1, middle, got_macro, n_macro, a, along_macro)
    halo_finish(2)
    grown = applied(2)
    for c in range(3):
        basis[3, c] = grown[c]
    halo_start(3)
    gather_finish(1, got_macro, n_macro, along_macro, a)
    totals = jnp.sum(jnp.sum(got_macro[...], axis=0), axis=1, keepdims=True)
    shift = jnp.sqrt(totals[1:2] / totals[0:1])
    scale = 1.0 / shift
    halo_finish(3)
    for c in range(3):
        powers = [basis[0, c]]
        factor = scale
        for k in range(1, 4):
            powers.append(basis[k, c] * factor)
            factor = factor * scale
        for k in range(1, 4):
            powers = [later - sooner for sooner, later in zip(powers, powers[1:])]
            basis[k, c] = powers[0]

    def field(it):
        return [basis[it, c] for c in range(3)]

    def step(it):
        grown = applied(it)
        return [grown[c] * scale - jnp.where(own, basis[it, c], 0.0) for c in range(3)]

    moments = []
    for it in range(3, ITERS):
        grown = step(it)
        if it + 1 < ITERS:
            for c in range(3):
                basis[it + 1, c] = grown[c]
            halo_start(it + 1)
            for k in range(len(moments) // 2, it + 1):
                moments.append(product(field(k), field(k)))
                moments.append(product(field(k), field(k + 1)))
            halo_finish(it + 1)
    moments.append(product(field(ITERS - 1), field(ITERS - 1)))
    moments.append(product(field(ITERS - 1), grown))
    sums = jnp.sum(stacked(moments), axis=1, keepdims=True)
    diagonal = lax.broadcasted_iota(jnp.int32, (16, 128), 0) == lax.broadcasted_iota(
        jnp.int32, (16, 128), 1
    )
    last_part[...] = jnp.sum(jnp.where(diagonal, sums, 0.0), axis=0, keepdims=True)

    gather_all(2, last_part, last_all)
    gather_finish(2, last_all, total, device, me)
    totals = jnp.sum(last_all[...], axis=0)
    held = [totals[:, k : k + 1] for k in range(2 * ITERS)]

    def inner(first, second, extra=0):
        gathered = {}
        for i, x in enumerate(first):
            for j, y in enumerate(second):
                gathered.setdefault(i + j, []).append(x * y)
        value = None
        for degree, terms in gathered.items():
            total = terms[0]
            for term in terms[1:]:
                total = total + term
            total = total * held[degree + extra]
            value = total if value is None else value + total
        return value

    one = jnp.ones((1, 1), jnp.float32)
    left, toward, done = [one], [one], []
    norm = held[0]
    for it in range(ITERS):
        energy = inner(toward, toward) + inner(toward, toward, 1)
        length = norm / energy
        done = [x + length * scale * p for x, p in zip(done + [0.0], toward)]
        raised = [
            (toward[k] if k < len(toward) else 0.0) + (toward[k - 1] if k > 0 else 0.0)
            for k in range(len(toward) + 1)
        ]
        left = [
            (left[k] if k < len(left) else 0.0) - length * raised[k] for k in range(len(raised))
        ]
        if it + 1 < ITERS:
            fresh = inner(left, left)
            ratio = fresh / norm
            toward = [
                left[k] + (ratio * toward[k] if k < len(toward) else 0.0)
                for k in range(len(left))
            ]
            norm = fresh
    for c in range(3):
        fields = [basis[k, c] for k in range(ITERS)] + [grown[c]]
        moved, rest = None, None
        for k in range(ITERS + 1):
            if k < len(done):
                term = done[k] * fields[k]
                moved = term if moved is None else moved + term
            term = left[k] * fields[k]
            rest = term if rest is None else rest + term
        for i in range(count_x):
            low = (i + 1) * wide + 1
            inc_ref[c, i] = moved[low : low + count_y]
            res_ref[c, i] = rest[low : low + count_y]

    for buffer, semaphore in ((route_out, route_send), (back_out, back_send)):
        others = buffer.at[pl.ds(0, n_micro - 1)]
        pltpu.make_async_remote_copy(
            src_ref=others,
            dst_ref=others,
            send_sem=semaphore.at[0],
            recv_sem=semaphore.at[0],
            device_id=(a, lax.rem(b + 1, n_micro)),
            device_id_type=MESH,
        ).wait_send()


def hand_over(inc_in, res_in, inc_ref, res_ref):
    inc_ref[...] = inc_in[...]
    res_ref[...] = res_in[...]


def shards(
    displacement,
    load,
    routes,
    counts,
    stiffness,
    precond,
    forcing,
    coupling,
    lame_first,
    lame_shear,
):
    _, count_x, count_y, lanes = displacement.shape
    points = count_x * count_y * lanes
    n_macro, n_micro = lax.axis_size("macro"), lax.axis_size("micro")
    capacity = max(2, 2 * points // n_micro)
    slots = -(-capacity // 128) * 128
    size = stiffness.shape[1]
    tall = -(-(8 + len(PAIRS)) // 8) * 8
    rows = -(-(count_x + 2) * (count_y + 2) // 8) * 8
    side = -(-3 * max(count_x, count_y) // 8) * 8
    total = n_macro * n_micro
    sides = count_x + count_y + 1
    outer_rows = -(-(count_x + 3) * (count_y + 3) // 8) * 8
    vmem = pl.BlockSpec(memory_space=pltpu.VMEM)
    anywhere = pl.BlockSpec(memory_space=pl.ANY)
    dma = pltpu.SemaphoreType.DMA

    def held(*shape):
        return pltpu.VMEM(shape, jnp.float32)

    def half(*shape):
        return pltpu.VMEM(shape, jnp.bfloat16)

    def body(*refs):
        newton_kernel((count_x, count_y, lanes, n_macro, n_micro), *refs)

    outputs = pl.pallas_call(
            body,
            out_shape=[jax.ShapeDtypeStruct(load.shape, jnp.float32)] * 2,
            in_specs=[anywhere] * 8 + [vmem] * 2,
            out_specs=[vmem, vmem],
            scratch_shapes=[
                held(*displacement.shape),
                held(*load.shape),
                pltpu.VMEM((points // 128, 128), jnp.int32),
                pltpu.VMEM((points // 128, 128), jnp.int32),
                half(size, size),
                half(size, size),
                half(6, size),
                half(6, size),
                half(size, 8),
                half(tall, size),
                half(tall, size),
                held(tall, size),
                half(n_micro * slots, points),
                held(len(AROUND), *load.shape),
                held(len(AROUND), 8, points),
                held(6, outer_rows, lanes),
                held(3, rows, lanes),
                held(3, *displacement.shape),
                held(8, points),
                held(n_micro, 8, slots),
                held(n_micro, 8, slots),
                held(n_micro, tall, slots),
                held(n_micro, tall, slots),
                held(tall, points),
                held(sides, tall - 8, lanes),
                held(len(PAIRS), rows, lanes),
                held(ITERS, 3, rows, lanes),
                held(ITERS, len(AROUND), side, lanes),
                held(ITERS, len(AROUND), side, lanes),
                held(8, 128),
                held(n_micro, 8, 128),
                held(8, 128),
                held(n_macro, 8, 128),
                held(1, 128),
                held(total, 1, 128),
                dma((8,)),
                dma((3,)),
                dma((3,)),
                dma((1,)),
                dma((n_micro,)),
                dma((1,)),
                dma((n_micro,)),
                dma((2, 3)),
                dma((2, 3)),
                dma((2, len(AROUND))),
                dma((2, len(AROUND))),
                dma((3,)),
                dma((3,)),
            ],
            compiler_params=pltpu.CompilerParams(collective_id=0, has_side_effects=True),
            name="newton_step",
        )(
            displacement,
            load,
            routes.reshape(points // 128, 128),
            counts.reshape(points // 128, 128),
            stiffness[0],
            precond[0],
            forcing[0],
            coupling[0].T,
            lame_first.reshape(1, 1),
            lame_shear.reshape(1, 1),
        )
    return tuple(
        pl.pallas_call(
            hand_over,
            out_shape=[jax.ShapeDtypeStruct(load.shape, jnp.float32)] * 2,
            in_specs=[vmem, vmem],
            out_specs=[vmem, vmem],
            name="hand_over",
        )(*outputs)
    )


def solution(mesh):
    in_specs = (
        P(None, "macro", "micro", None),
        P(None, "macro", "micro", None),
        P("macro", "micro", None, None),
        P("macro", "micro", None),
        P("micro", None, None),
        P("micro", None, None),
        P("micro", None, None),
        P("micro", None, None),
        P("micro"),
        P("micro"),
    )
    out_specs = (P(None, "macro", "micro", None), P(None, "macro", "micro", None))
    return jax.shard_map(shards, mesh=mesh, in_specs=in_specs, out_specs=out_specs, check_vma=False)
```
